32 devices in a mesh: dp: 8 (over z, y), mp: 4 (over x, core).
Axes of the slice: x: 2, y: 2, z: 4, core: 2. Of those that a mesh axis runs over, the one named last changes fastest.
Arguments:
- features: bfloat16 [1024, 8, 1024], P('mp', 'dp'), may hold values from -16 to 16
- w1_in: bfloat16 [1024, 4096], P(None, 'mp'), may hold values from -0.1875 to 0.1875
- w1_out: bfloat16 [4096, 1024], P('mp'), may hold values from -0.1875 to 0.1875
- gain_ffn1: bfloat16 [1024], replicated, may hold values from 0.5 to 1.5
- w_qkv: bfloat16 [1024, 3, 1024], P(None, None, 'mp'), may hold values from -0.1875 to 0.1875
- w_attn_out: bfloat16 [1024, 1024], P('mp'), may hold values from -3 to 3
- rel_table: bfloat16 [73, 64], replicated, may hold values from -4 to 4
- gain_attn: bfloat16 [1024], replicated, may hold values from 0.5 to 1.5
- w_conv_in: bfloat16 [1024, 2, 1024], P(None, None, 'mp'), may hold values from -0.1875 to 0.1875
- w_depth: bfloat16 [31, 1024], P(None, 'mp'), may hold values from -1 to 1
- gain_depth: bfloat16 [1024], P('mp'), may hold values from 0.5 to 1.5
- w_conv_out: bfloat16 [1024, 1024], P('mp'), may hold values from -0.25 to 0.25
- gain_conv: bfloat16 [1024], replicated, may hold values from 0.5 to 1.5
- w2_in: bfloat16 [1024, 4096], P(None, 'mp'), may hold values from -0.1875 to 0.1875
- w2_out: bfloat16 [4096, 1024], P('mp'), may hold values from -0.1875 to 0.1875
- gain_ffn2: bfloat16 [1024], replicated, may hold values from 0.5 to 1.5
- gain_final: bfloat16 [1024], replicated, may hold values from 0.5 to 1.5
- cotangent: bfloat16 [1024, 8, 1024], P('mp', 'dp'), may hold values from -6 to 6
Outputs:
- output: float32 [1024, 8, 1024], P('mp', 'dp')
- input_grad: float32 [1024, 8, 1024], P('mp', 'dp')
- grad_w1_in: float32 [1024, 4096], P('dp', 'mp')
- grad_w1_out: float32 [4096, 1024], P('mp', 'dp')
- grad_gain_ffn1: float32 [1024], replicated
- grad_w_qkv: float32 [1024, 3, 1024], P('dp', None, 'mp')
- grad_w_attn_out: float32 [1024, 1024], P('mp', 'dp')
- grad_rel_table: float32 [73, 64], replicated
- grad_gain_attn: float32 [1024], replicated
- grad_w_conv_in: float32 [1024, 2, 1024], P('dp', None, 'mp')
- grad_w_depth: float32 [31, 1024], P(None, 'mp')
- grad_gain_depth: float32 [1024], P('mp')
- grad_w_conv_out: float32 [1024, 1024], P('mp', 'dp')
- grad_gain_conv: float32 [1024], replicated
- grad_w2_in: float32 [1024, 4096], P('dp', 'mp')
- grad_w2_out: float32 [4096, 1024], P('mp', 'dp')
- grad_gain_ffn2: float32 [1024], replicated
- grad_gain_final: float32 [1024], replicated
- rms_stats: float32 [5], replicated
The draws below stay inside these ranges and needn't reach their ends.
All inputs are finite; a program needn't handle non-finite values.
Results may differ from the reference program's by a relative error of at most 0.03.
Values may be sent and summed in bfloat16 or wider, within the bound.
A program may use at most 192 MiB of HBM per device.

```python
import math
import jax
import jax.numpy as jnp
from jax import lax

D = 1024
FF = 4096
HEADS = 16
HEAD = 64
KERNEL = 31
REL_LEFT = 64
REL_RIGHT = 8
FRAMES = 1024
REL = 73
CLIPS = 8


def draw_features(key, part):
    base_key = jax.random.fold_in(key, 11)
    clip_pos = jnp.arange(CLIPS, dtype=jnp.float32) / max(CLIPS - 1, 1)
    clip_scale = jnp.exp(clip_pos * math.log(3.0))[None, :, None]
    values = jnp.clip(jax.random.normal(base_key, (FRAMES, CLIPS, D), jnp.float32), -4.0, 4.0)
    return (values * clip_scale).astype(jnp.bfloat16)


def with_spikes(entries, key, source, target, blocks, factor):
    def block_of(axis_at):
        return (jnp.arange(entries.shape[axis_at]) // (entries.shape[axis_at] // blocks)).reshape((-1,) + (1,) * (entries.ndim - 1 - axis_at))

    near = jax.random.permutation(key, blocks)[block_of(target)]
    far = (block_of(target) + blocks // 2) % blocks
    return jnp.where((block_of(source) == near) | (block_of(source) == far), factor * entries, entries)


def shard_levels(key, dims, split, least, largest):
    factor_of, own = 1.0, jax.random.fold_in(key, 6)
    for dim, parts in split:
        draws = jnp.exp(jax.random.uniform(jax.random.fold_in(own, dim), (parts,), jnp.float32, least / len(split), largest / len(split)))
        factor_of = factor_of * jnp.repeat(draws, dims[dim] // parts).reshape([-1 if axis == dim else 1 for axis in range(len(dims))])
    return factor_of


def scatter_about(stream_key, dims, scale, limit, shards=(), kind=jnp.bfloat16):
    array = jax.random.normal(stream_key, dims, jnp.float32) * scale
    if len(shards) > 0:
        array = shard_levels(stream_key, dims, shards, -0.22, 0.18) * array
    return jnp.clip(array, min=-limit, max=limit).astype(kind)


def heavy_noise(key, extent, scale, most, cuts, heavy, held_as=jnp.bfloat16):
    result = scale * jax.random.normal(key, extent, jnp.float32)
    if cuts:
        result = result * shard_levels(key, extent, cuts, -0.22, 0.18)
    return jnp.clip(with_spikes(result, jax.random.fold_in(key, 3), *heavy), -most, most).astype(held_as)


def setup_inputs(seed: int = 0) -> dict:
    seeds = jax.random.split(jax.random.key(seed), 19)
    return {
        "features": draw_features(jax.random.fold_in(seeds[18], 71), 0),
        "w1_in": scatter_about(seeds[1], (D, FF), D ** -0.5, 0.1875, ((1, 4),)),
        "w1_out": scatter_about(seeds[2], (FF, D), (FF // 4) ** -0.5, 0.1875, ((0, 4),)),
        "gain_ffn1": jnp.clip(1.0 + 0.1 * jax.random.normal(seeds[3], (D,), jnp.float32), 0.5, 1.5).astype(jnp.bfloat16),
        "w_qkv": scatter_about(seeds[4], (D, 3, D), D ** -0.5, 0.1875, ((2, 4),)),
        "w_attn_out": scatter_about(seeds[5], (D, D), (max(D // 256, 2)) ** -0.5, 3.0, ((0, 4),)),
        "rel_table": scatter_about(seeds[6], (REL, HEAD), 1.0, 4.0),
        "gain_attn": jnp.clip(1.0 + 0.1 * jax.random.normal(seeds[7], (D,), jnp.float32), 0.5, 1.5).astype(jnp.bfloat16),
        "w_conv_in": scatter_about(seeds[8], (D, 2, D), D ** -0.5, 0.1875, ((2, 4),)),
        "w_depth": scatter_about(seeds[9], (KERNEL, D), KERNEL ** -0.5, 1.0, ((1, 4),)),
        "gain_depth": jnp.clip(1.0 + 0.1 * jax.random.normal(seeds[10], (D,), jnp.float32), 0.5, 1.5).astype(jnp.bfloat16),
        "w_conv_out": scatter_about(seeds[11], (D, D), (D // 2) ** -0.5, 0.25, ((0, 4),)),
        "gain_conv": jnp.clip(1.0 + 0.1 * jax.random.normal(seeds[12], (D,), jnp.float32), 0.5, 1.5).astype(jnp.bfloat16),
        "w2_in": scatter_about(seeds[13], (D, FF), D ** -0.5, 0.1875, ((1, 4),)),
        "w2_out": scatter_about(seeds[14], (FF, D), (FF // 4) ** -0.5, 0.1875, ((0, 4),)),
        "gain_ffn2": jnp.clip(1.0 + 0.1 * jax.random.normal(seeds[15], (D,), jnp.float32), 0.5, 1.5).astype(jnp.bfloat16),
        "gain_final": jnp.clip(1.0 + 0.1 * jax.random.normal(seeds[16], (D,), jnp.float32), 0.5, 1.5).astype(jnp.bfloat16),
        "cotangent": heavy_noise(seeds[17], (FRAMES, CLIPS, D), 1.0, 6.0, ((0, 4), (1, 8)), (1, 2, 8, 2.0)),
    }


epsilon = 1e-05
highest = lax.Precision.HIGHEST

@jax.custom_vjp
def low(v):
    return lax.optimization_barrier(v.astype(jnp.bfloat16)).astype(jnp.float32)

@jax.custom_vjp
def low_back(v):
    return v

def low_keep(v):
    return (low(v), None)

def low_pass(kept, grad):
    return (grad,)

def back_keep(v):
    return (v, None)

def back_low(kept, grad):
    return (low(grad),)
low.defvjp(low_keep, low_pass)
low_back.defvjp(back_keep, back_low)

def swish_act(values):
    return values * jax.nn.sigmoid(values)

def norm_rows(values, gain):
    average = lax.optimization_barrier(jnp.mean(values, -1, keepdims=True))
    centred = values - average
    spread = lax.optimization_barrier(jnp.mean(centred * centred, -1, keepdims=True))
    return centred * lax.rsqrt(spread + epsilon) * gain

def relative_index(first_row, row_count, key_count):
    query_pos = first_row + jnp.arange(row_count, dtype=jnp.int32)[:, None]
    key_pos = jnp.arange(key_count, dtype=jnp.int32)[None, :]
    return (jnp.clip(key_pos - query_pos, -REL_LEFT, REL_RIGHT) + REL_LEFT).astype(jnp.int32)

def attend_clip(queries, keys_all, values_all, rel_table):
    logits = jnp.einsum('iha,jha->hij', queries, keys_all, precision=highest)
    relative = low_back(jnp.einsum('iha,ra->hir', queries, rel_table, precision=highest))
    rel_index = relative_index(0, FRAMES, FRAMES)
    rel_bias = jnp.take_along_axis(relative, jnp.broadcast_to(rel_index[None], logits.shape), axis=2)
    scores = low_back((logits + rel_bias) * 0.125)
    row_max = lax.optimization_barrier(jnp.max(scores, -1, keepdims=True))
    weights = jnp.exp(scores - row_max)
    attn_probs = weights / lax.optimization_barrier(jnp.sum(weights, -1, keepdims=True))
    return jnp.einsum('hij,jha->iha', low(attn_probs), values_all, precision=highest)

def feed_forward(stream, gain, w_in, w_out):
    normed = low(norm_rows(stream, gain))
    hidden = low_back(jnp.einsum('lgd,df->lgf', normed, w_in, precision=highest))
    active = low(swish_act(hidden))
    return low_back(jnp.einsum('lgf,fd->lgd', active, w_out, precision=highest))

def forward(stream, w1_in, w1_out, gain_ffn1, w_qkv, w_attn_out, rel_table, gain_attn, w_conv_in, w_depth, gain_depth, w_conv_out, gain_conv, w2_in, w2_out, gain_ffn2, gain_final):
    clip_count = stream.shape[1]
    branch_one = feed_forward(stream, gain_ffn1, w1_in, w1_out)
    after_one = stream + 0.5 * branch_one
    normed = low(norm_rows(after_one, gain_attn))
    projected = low(low_back(jnp.einsum('lgd,dkc->lgkc', normed, w_qkv, precision=highest)))
    heads_view = jnp.moveaxis(projected.reshape(FRAMES, clip_count, 3, HEADS, HEAD), 1, 0)
    checked = jax.checkpoint(attend_clip)
    mixed_out = lax.map(lambda clip_data: checked(clip_data[:, 0], clip_data[:, 1], clip_data[:, 2], rel_table), heads_view)
    mixed_out = low(low_back(jnp.moveaxis(mixed_out, 0, 1).reshape(FRAMES, clip_count, D)))
    branch_two = low_back(jnp.einsum('lgc,cd->lgd', mixed_out, w_attn_out, precision=highest))
    after_two = after_one + branch_two
    normed_conv = low(norm_rows(after_two, gain_conv))
    paired = low_back(jnp.einsum('lgd,dkc->lgkc', normed_conv, w_conv_in, precision=highest))
    glu_out = paired[:, :, 0] * jax.nn.sigmoid(paired[:, :, 1])
    padded = jnp.pad(glu_out, ((KERNEL - 1, 0), (0, 0), (0, 0)))
    depth_out = jnp.zeros_like(glu_out)
    for tap_index in range(KERNEL):
        depth_out = depth_out + w_depth[tap_index] * padded[tap_index:tap_index + FRAMES]
    active = low(swish_act(norm_rows(depth_out, gain_depth)))
    branch_three = low_back(jnp.einsum('lgc,cd->lgd', active, w_conv_out, precision=highest))
    after_three = after_two + branch_three
    branch_four = feed_forward(after_three, gain_ffn2, w2_in, w2_out)
    after_four = after_three + 0.5 * branch_four
    output = norm_rows(after_four, gain_final)
    squares = jnp.stack([jnp.sum(branch_one * branch_one), jnp.sum(branch_two * branch_two), jnp.sum(branch_three * branch_three), jnp.sum(branch_four * branch_four), jnp.sum(after_four * after_four)])
    return (output, squares)

def reference(features, w1_in, w1_out, gain_ffn1, w_qkv, w_attn_out, rel_table, gain_attn, w_conv_in, w_depth, gain_depth, w_conv_out, gain_conv, w2_in, w2_out, gain_ffn2, gain_final, cotangent):
    params = tuple((weight_arg.astype(jnp.float32) for weight_arg in (w1_in, w1_out, gain_ffn1, w_qkv, w_attn_out, rel_table, gain_attn, w_conv_in, w_depth, gain_depth, w_conv_out, gain_conv, w2_in, w2_out, gain_ffn2, gain_final)))
    group_size = math.gcd(CLIPS, 4)
    group_count = CLIPS // group_size

    def regroup(array_in):
        return array_in.astype(jnp.float32).reshape(FRAMES, group_count, group_size, D).transpose(1, 0, 2, 3)

    def ungroup(array_in):
        return array_in.transpose(1, 0, 2, 3).reshape(FRAMES, CLIPS, D)

    def accumulate(carried, batch_in):
        totals, squares = carried
        stream, seed_grad = batch_in
        output, pullback, part_squares = jax.vjp(forward, stream, *params, has_aux=True)
        grad_all = pullback(seed_grad)
        totals = tuple((summed + fresh for summed, fresh in zip(totals, grad_all[1:])))
        return ((totals, squares + part_squares), (output, grad_all[0]))
    initial = (tuple((jnp.zeros_like(weight_arg) for weight_arg in params)), jnp.zeros((5,), jnp.float32))
    (totals, squares), (outputs, input_grads) = lax.scan(accumulate, initial, (regroup(features), regroup(cotangent)))
    rms_stats = jnp.sqrt(squares / (FRAMES * CLIPS * D))
    return (ungroup(outputs), ungroup(input_grads), totals[0], totals[1], totals[2], totals[3], totals[4], totals[5], totals[6], totals[7], totals[8], totals[9], totals[10], totals[11], totals[12], totals[13], totals[14], totals[15], rms_stats)
```

```python
import functools

import jax
import jax.numpy as jnp
from jax import lax
from jax.experimental import pallas as pl
from jax.experimental.pallas import tpu as pltpu
from jax.sharding import PartitionSpec as P

HEAD = 64
REL_LEFT = 64
REL_RIGHT = 8
BQ = 128
WIN = 4 * BQ


epsilon = 1e-05
highest = lax.Precision.HIGHEST


def swish_act(values):
    return values * jax.nn.sigmoid(values)


def swish_slope(values):
    logistic = jax.nn.sigmoid(values)
    return logistic + values * logistic * (1.0 - logistic)


def norm_rows(values, gain):
    average = jnp.mean(values, -1, keepdims=True)
    centred = values - average
    spread = jnp.mean(centred * centred, -1, keepdims=True)
    inverse = lax.rsqrt(spread + epsilon)
    unit_rows = centred * inverse
    return (unit_rows * gain, unit_rows, inverse)


def norm_back(grad_out, unit_rows, inverse, gain):
    scaled = grad_out * gain
    first_mean = jnp.mean(scaled, -1, keepdims=True)
    second_mean = jnp.mean(scaled * unit_rows, -1, keepdims=True)
    grad_in = inverse * (scaled - first_mean - unit_rows * second_mean)
    return (grad_in, jnp.sum(grad_out * unit_rows, 0))


def contract_rows(left_mat, right_mat):
    return lax.dot_general(
        left_mat, right_mat, (((0,), (0,)), ((), ())), preferred_element_type=jnp.float32
    )


def contract_cols(left_mat, right_mat):
    return lax.dot_general(
        left_mat, right_mat, (((1,), (1,)), ((), ())), preferred_element_type=jnp.float32
    )


def spread_rows(normed):
    return lax.all_gather(normed, "mp", axis=0, tiled=True)


def fetch_grads(grad_rows):
    return lax.all_gather(grad_rows, "mp", axis=0, tiled=True)


def reduce_branch(term_fn, row_count):
    return lax.psum_scatter(
        term_fn(jnp.int32(0), lax.axis_size("mp") * row_count).astype(jnp.bfloat16),
        "mp",
        scatter_dimension=0,
        tiled=True,
    ).astype(jnp.float32)


def reduce_inputs(term_fn, row_count):
    return lax.psum_scatter(
        term_fn(jnp.int32(0), lax.axis_size("mp") * row_count).astype(jnp.bfloat16),
        "mp",
        scatter_dimension=0,
        tiled=True,
    ).astype(jnp.float32)


def settle_block(first_grad, second_grad):
    return (first_grad, second_grad)


def nt(a, b):
    return lax.dot_general(a, b, (((1,), (1,)), ((), ())), preferred_element_type=jnp.float32)
def nn(a, b):
    return lax.dot_general(a, b, (((1,), (0,)), ((), ())), preferred_element_type=jnp.float32)
def tn(a, b):
    return lax.dot_general(a, b, (((0,), (0,)), ((), ())), preferred_element_type=jnp.float32)

def split_pair(x):
    left = lax.broadcasted_iota(jnp.int32, x.shape, 1) < HEAD
    zero = jnp.zeros_like(x)
    return jnp.concatenate([jnp.where(left, x, zero), jnp.where(left, zero, x)], 0)

def join_pair(x):
    rows = x.shape[0] // 2
    left = lax.broadcasted_iota(jnp.int32, (rows, x.shape[1]), 1) < HEAD
    return jnp.where(left, x[:rows], x[rows:])

def fwd_kernel(q_ref, k_ref, v_ref, rel_ref, mixed_ref, probs_ref, bias_ref):
    ib = pl.program_id(1)
    qs = split_pair(q_ref[...] * 0.125)
    s = nt(qs, k_ref[...])
    b = nt(qs, rel_ref[...])
    rows = b.shape[0] // 2
    bias_ref[:, 0:BQ] = b[:, 3 * BQ : 4 * BQ]
    for h in range(2):
        r = pltpu.roll(b[h * rows : (h + 1) * rows, :WIN], 0, 1, stride=1, stride_axis=0)
        bias_ref[h * rows : (h + 1) * rows, BQ : 4 * BQ] = r[:, : 3 * BQ]
    bias_ref[:, 4 * BQ :] = b[:, 4 * BQ :]
    nkeys = s.shape[1] // BQ
    parts = []
    for jb in range(nkeys):
        at = pl.multiple_of(jnp.clip(jb - ib + 2, 0, 4) * BQ, BQ)
        parts.append(s[:, jb * BQ : (jb + 1) * BQ] + bias_ref[:, pl.ds(at, BQ)])
    top = functools.reduce(jnp.maximum, parts)
    m = jnp.max(top, -1, keepdims=True)
    es = [jnp.exp(p - m) for p in parts]
    tot = jnp.sum(functools.reduce(jnp.add, es), -1, keepdims=True)
    inv = 1.0 / tot
    for jb in range(nkeys):
        probs_ref[0, :, jb * BQ : (jb + 1) * BQ] = (es[jb] * inv).astype(jnp.bfloat16)
    mixed_ref[...] = join_pair(nn(probs_ref[0], v_ref[...])).astype(jnp.bfloat16)

def bwd_kernel(q_ref, k_ref, v_ref, relb_ref, hot_ref, probs_ref, do_ref, dq_ref, dk_ref, dv_ref, dt_ref,
               tot_ref, dkt, dvt, dta, dz_ref):
    pr, ib, nb = pl.program_id(0), pl.program_id(1), pl.num_programs(1)
    @pl.when(ib == 0)
    def _():
        dkt[...] = jnp.zeros_like(dkt)
        dvt[...] = jnp.zeros_like(dvt)
    @pl.when((ib == 0) & (pr == 0))
    def _():
        dta[...] = jnp.zeros_like(dta)
    qs = split_pair(q_ref[...] * 0.125)
    dos = split_pair(do_ref[...])
    p = probs_ref[0]
    dp = nt(dos, v_ref[...])
    nkeys = dp.shape[1] // BQ
    dvt[...] += tn(dos, p)
    pf = p.astype(jnp.float32)
    acc = None
    for jb in range(nkeys):
        sl = slice(jb * BQ, (jb + 1) * BQ)
        t = pf[:, sl] * dp[:, sl]
        acc = t if acc is None else acc + t
    inner = jnp.sum(acc, -1, keepdims=True)
    tot_ref[...] = jnp.zeros_like(tot_ref)
    for jb in range(nkeys):
        sl = slice(jb * BQ, (jb + 1) * BQ)
        dz = (pf[:, sl] * (dp[:, sl] - inner)).astype(jnp.bfloat16)
        dz_ref[:, sl] = dz
        at = pl.multiple_of(jnp.clip(jb - ib + 2, 0, 4) * BQ, BQ)
        tot_ref[:, pl.ds(at, BQ)] += dz.astype(jnp.float32)
    rows = BQ
    r2 = lax.broadcasted_iota(jnp.int32, (2 * rows, 2 * rows), 0)
    c2 = lax.broadcasted_iota(jnp.int32, (2 * rows, 2 * rows), 1)
    mirror = (r2 + c2 == jnp.where(r2 < rows, rows - 1, 3 * rows - 1)).astype(jnp.bfloat16)
    w = jnp.concatenate([tot_ref[:, BQ : 4 * BQ].astype(jnp.bfloat16), jnp.zeros((2 * rows, BQ), jnp.bfloat16)], 1)
    w = nn(mirror, w)
    outs = [pltpu.roll(w[h * rows : (h + 1) * rows], WIN - rows + 1, 1, stride=1, stride_axis=0) for h in range(2)]
    d = nn(mirror, jnp.concatenate(outs, 0).astype(jnp.bfloat16)).astype(jnp.bfloat16)
    drel = nn(d, hot_ref[...])
    col = lax.broadcasted_iota(jnp.int32, drel.shape, 1)
    low = jnp.sum(tot_ref[:, :BQ], -1, keepdims=True)
    high = jnp.sum(tot_ref[:, 4 * BQ :], -1, keepdims=True)
    drel = drel + jnp.where(col == 0, low, 0.0) + jnp.where(col == REL_LEFT + REL_RIGHT, high, 0.0)
    drel = drel.astype(jnp.bfloat16)
    dz = dz_ref[...]
    dq = nn(dz, k_ref[...]) + nn(drel, relb_ref[...])
    dq_ref[...] = (join_pair(dq) * 0.125).astype(jnp.bfloat16)
    dkt[...] += tn(qs, dz)
    dta[...] += tn(drel, qs)
    @pl.when(ib == nb - 1)
    def _():
        dk_ref[...] = dkt[...].T.astype(jnp.bfloat16)
        dv_ref[...] = dvt[...].T.astype(jnp.bfloat16)
        dt_ref[...] = dta[...]

def rel_tables(rel_table):
    spots = jnp.arange(5 * BQ)
    idx = jnp.where(spots < 3 * BQ, jnp.clip(spots - REL_LEFT, 0, REL_LEFT + REL_RIGHT), jnp.where(spots < 4 * BQ, 0, REL_LEFT + REL_RIGHT))
    hot = (jnp.arange(BQ)[None, :] == idx[:, None]).astype(jnp.bfloat16)
    padded = jnp.pad(rel_table, ((0, BQ - rel_table.shape[0]), (0, 0)))
    padded = jnp.concatenate([padded, padded], 1)
    ext = jnp.dot(hot, padded, preferred_element_type=jnp.float32).astype(jnp.bfloat16)
    return ext, hot[:WIN], padded

def attn_fwd(qkv, ext):
    frames, cols = qkv.shape
    pairs = cols // 3 // 128
    nb = frames // BQ
    bf = jnp.bfloat16
    return pl.pallas_call(
        fwd_kernel,
        grid=(pairs, nb),
        in_specs=[
            pl.BlockSpec((BQ, 128), lambda p, i: (i, p)),
            pl.BlockSpec((frames, 128), lambda p, i: (0, pairs + p)),
            pl.BlockSpec((frames, 128), lambda p, i: (0, 2 * pairs + p)),
            pl.BlockSpec(ext.shape, lambda p, i: (0, 0)),
        ],
        out_specs=[
            pl.BlockSpec((BQ, 128), lambda p, i: (i, p)),
            pl.BlockSpec((1, 2 * BQ, frames), lambda p, i: (p, i, 0)),
        ],
        out_shape=[jax.ShapeDtypeStruct((frames, cols // 3), bf), jax.ShapeDtypeStruct((pairs, 2 * frames, frames), bf)],
        scratch_shapes=[pltpu.VMEM((2 * BQ, 5 * BQ), jnp.float32)],
        compiler_params=pltpu.CompilerParams(vmem_limit_bytes=48 << 20),
        name="attn_fwd",
    )(qkv, qkv, qkv, ext)

def attn_bwd(qkv, padded, hot, probs, dmixed):
    frames, cols = qkv.shape
    pairs = cols // 3 // 128
    nb = frames // BQ
    bf = jnp.bfloat16
    blk = pl.BlockSpec((BQ, 128), lambda p, i: (i, p))
    full = pl.BlockSpec((frames, 128), lambda p, i: (0, p))
    return pl.pallas_call(
        bwd_kernel,
        grid=(pairs, nb),
        in_specs=[
            blk,
            pl.BlockSpec((frames, 128), lambda p, i: (0, pairs + p)),
            pl.BlockSpec((frames, 128), lambda p, i: (0, 2 * pairs + p)),
            pl.BlockSpec(padded.shape, lambda p, i: (0, 0)),
            pl.BlockSpec(hot.shape, lambda p, i: (0, 0)),
            pl.BlockSpec((1, 2 * BQ, frames), lambda p, i: (p, i, 0)),
            blk,
        ],
        out_specs=[blk, full, full, pl.BlockSpec((128, 128), lambda p, i: (0, 0))],
        out_shape=[jax.ShapeDtypeStruct((frames, cols // 3), bf)] * 3 + [jax.ShapeDtypeStruct((128, 128), jnp.float32)],
        scratch_shapes=[pltpu.VMEM((2 * BQ, 5 * BQ), jnp.float32), pltpu.VMEM((128, frames), jnp.float32), pltpu.VMEM((128, frames), jnp.float32),
                        pltpu.VMEM((128, 128), jnp.float32), pltpu.VMEM((2 * BQ, frames), bf)],
        compiler_params=pltpu.CompilerParams(vmem_limit_bytes=48 << 20),
        name="attn_bwd",
    )(qkv, qkv, qkv, padded, hot, probs, dmixed)


def feed_forward(stream, gain, w_in, w_out):
    normed, unit_rows, inverse = norm_rows(stream, gain.astype(jnp.float32))
    gathered = spread_rows(normed.astype(jnp.bfloat16))
    hidden = jnp.dot(gathered, w_in, preferred_element_type=jnp.float32)
    active = swish_act(hidden).astype(jnp.bfloat16)

    def feed_branch_rows(first_row, row_count):
        return jnp.dot(active, w_out, preferred_element_type=jnp.float32)

    branch = reduce_branch(feed_branch_rows, stream.shape[0])
    return (branch, (unit_rows, inverse, gathered, hidden, active))


def feed_back(grad_stream, kept_state, gain, w_in, w_out):
    unit_rows, inverse, gathered, hidden, active = kept_state
    grad_branch = fetch_grads((0.5 * grad_stream).astype(jnp.bfloat16))
    grad_w_out = contract_rows(active, grad_branch)
    grad_hidden = (contract_cols(grad_branch, w_out) * swish_slope(hidden)).astype(jnp.bfloat16)
    grad_w_in = contract_rows(gathered, grad_hidden)

    def feed_input_rows(first_row, row_count):
        return contract_cols(grad_hidden, w_in)

    grad_normed = reduce_inputs(feed_input_rows, grad_stream.shape[0])
    grad_in, grad_gain = norm_back(grad_normed, unit_rows, inverse, gain.astype(jnp.float32))
    return (grad_stream + grad_in, grad_w_in, grad_w_out, grad_gain)


def attention(stream, gain, w_qkv, w_attn_out, rel_table, clip_count):
    normed, unit_rows, inverse = norm_rows(stream, gain.astype(jnp.float32))
    gathered = spread_rows(normed.astype(jnp.bfloat16))
    flat_qkv = w_qkv.reshape(w_qkv.shape[0], -1)
    projected = jnp.dot(gathered, flat_qkv, preferred_element_type=jnp.float32).astype(jnp.bfloat16)
    tables = rel_tables(rel_table)
    mixed, probs = attn_fwd(projected, tables[0])

    def attention_branch_rows(first_row, row_count):
        return jnp.dot(mixed, w_attn_out, preferred_element_type=jnp.float32)

    branch = reduce_branch(attention_branch_rows, stream.shape[0])
    return (branch, (unit_rows, inverse, gathered, projected, mixed, probs, tables))


def attention_back(grad_stream, kept_state, gain, w_qkv, w_attn_out, rel_table, clip_count):
    unit_rows, inverse, gathered, projected, mixed, probs, tables = kept_state
    grad_branch = fetch_grads(grad_stream.astype(jnp.bfloat16))
    grad_w_attn_out = contract_rows(mixed, grad_branch)
    grad_mixed = contract_cols(grad_branch, w_attn_out).astype(jnp.bfloat16)
    dq, dk, dv, dt = attn_bwd(projected, tables[2], tables[1], probs, grad_mixed)
    rel = rel_table.shape[0]
    grad_table = dt[:rel, :HEAD] + dt[:rel, HEAD:]
    grad_split = jnp.concatenate([dq, dk, dv], 1)
    grad_w_qkv = contract_rows(gathered, grad_split).reshape(w_qkv.shape)
    flat_qkv = w_qkv.reshape(w_qkv.shape[0], -1)

    def attention_input_rows(first_row, row_count):
        return contract_cols(grad_split, flat_qkv)

    grad_normed = reduce_inputs(attention_input_rows, grad_stream.shape[0])
    grad_in, grad_gain = norm_back(grad_normed, unit_rows, inverse, gain.astype(jnp.float32))
    return (grad_stream + grad_in, grad_w_qkv, grad_w_attn_out, grad_gain, grad_table)


def convolve(stream, gain, w_conv_in, w_depth, gain_depth, w_conv_out, clip_count, model_width):
    normed, unit_rows, inverse = norm_rows(stream, gain.astype(jnp.float32))
    gathered = spread_rows(normed.astype(jnp.bfloat16))
    paired = jnp.einsum("rd,dkc->rkc", gathered, w_conv_in, preferred_element_type=jnp.float32)
    frames = gathered.shape[0] // clip_count
    channels = paired.shape[2]
    glu_out = (paired[:, 0] * jax.nn.sigmoid(paired[:, 1])).reshape(frames, clip_count, channels)
    tap_weights = w_depth.astype(jnp.float32)
    tap_count = tap_weights.shape[0]
    padded = jnp.pad(glu_out, ((tap_count - 1, 0), (0, 0), (0, 0)))
    depth_out = jnp.zeros_like(glu_out)
    for tap_index in range(tap_count):
        depth_out = depth_out + tap_weights[tap_index] * padded[tap_index : tap_index + frames]
    average = lax.psum(jnp.sum(depth_out, -1), "mp") / model_width
    centred = depth_out - average[..., None]
    spread = lax.psum(jnp.sum(centred * centred, -1), "mp") / model_width
    depth_inverse = lax.rsqrt(spread + epsilon)[..., None]
    depth_unit = centred * depth_inverse
    active = (
        swish_act(depth_unit * gain_depth.astype(jnp.float32))
        .astype(jnp.bfloat16)
        .reshape(frames * clip_count, channels)
    )

    def convolve_branch_rows(first_row, row_count):
        return jnp.dot(active, w_conv_out, preferred_element_type=jnp.float32)

    branch = reduce_branch(convolve_branch_rows, stream.shape[0])
    return (branch, (unit_rows, inverse, gathered, paired, depth_unit, depth_inverse, active))


def convolve_back(
    grad_stream,
    kept_state,
    gain,
    w_conv_in,
    w_depth,
    gain_depth,
    w_conv_out,
    clip_count,
    model_width,
):
    unit_rows, inverse, gathered, paired, depth_unit, depth_inverse, active = kept_state
    grad_branch = fetch_grads(grad_stream.astype(jnp.bfloat16))
    grad_w_conv_out = contract_rows(active, grad_branch)
    frames = depth_unit.shape[0]
    channels = depth_unit.shape[2]
    depth_gain = gain_depth.astype(jnp.float32)
    gated = depth_unit * depth_gain
    grad_gated = contract_cols(grad_branch, w_conv_out).reshape(
        frames, clip_count, channels
    ) * swish_slope(gated)
    grad_gain_depth = jnp.sum(grad_gated * depth_unit, (0, 1))
    grad_unit = grad_gated * depth_gain
    first_sum, second_sum = lax.psum(
        (jnp.sum(grad_unit, -1), jnp.sum(grad_unit * depth_unit, -1)), "mp"
    )
    grad_depth = depth_inverse * (
        grad_unit
        - first_sum[..., None] / model_width
        - depth_unit * second_sum[..., None] / model_width
    )
    tap_weights = w_depth.astype(jnp.float32)
    tap_count = tap_weights.shape[0]
    gate_sig = jax.nn.sigmoid(paired[:, 1])
    glu_out = (paired[:, 0] * gate_sig).reshape(frames, clip_count, channels)
    padded = jnp.pad(glu_out, ((tap_count - 1, 0), (0, 0), (0, 0)))
    padded_grad = jnp.pad(grad_depth, ((0, tap_count - 1), (0, 0), (0, 0)))
    grad_glu = jnp.zeros_like(grad_depth)
    tap_grads = []
    for tap_index in range(tap_count):
        begin_at = tap_count - 1 - tap_index
        grad_glu = grad_glu + tap_weights[tap_index] * padded_grad[begin_at : begin_at + frames]
        tap_grads.append(jnp.sum(grad_depth * padded[tap_index : tap_index + frames], (0, 1)))
    grad_w_depth = jnp.stack(tap_grads, 0)
    grad_glu = grad_glu.reshape(frames * clip_count, channels)
    grad_paired = jnp.stack(
        [grad_glu * gate_sig, grad_glu * paired[:, 0] * gate_sig * (1.0 - gate_sig)], 1
    ).astype(jnp.bfloat16)
    grad_w_conv_in = jnp.einsum(
        "rd,rkc->dkc", gathered, grad_paired, preferred_element_type=jnp.float32
    )

    def convolve_input_rows(first_row, row_count):
        return jnp.einsum("rkc,dkc->rd", grad_paired, w_conv_in, preferred_element_type=jnp.float32)

    grad_normed = reduce_inputs(convolve_input_rows, grad_stream.shape[0])
    grad_in, grad_gain = norm_back(grad_normed, unit_rows, inverse, gain.astype(jnp.float32))
    return (
        grad_stream + grad_in,
        grad_w_conv_in,
        grad_w_conv_out,
        grad_gain,
        grad_w_depth,
        grad_gain_depth,
    )


def halve_sum(grad, dim):
    count = lax.axis_size("dp")
    me = lax.axis_index("dp")
    part = grad.astype(jnp.bfloat16)
    shape = part.shape
    size = shape[dim] // count
    step = 1
    part = part.reshape(shape[:dim] + (count, size) + shape[dim + 1 :])
    while step < count:
        groups = part.shape[dim] // 2
        paired = part.reshape(part.shape[:dim] + (groups, 2) + part.shape[dim + 1 :])
        bit = (me // step) % 2
        keep = lax.dynamic_index_in_dim(paired, bit, dim + 1, keepdims=False)
        give = lax.dynamic_index_in_dim(paired, 1 - bit, dim + 1, keepdims=False)
        got = lax.ppermute(give, "dp", [(i, i ^ step) for i in range(count)])
        total = keep.astype(jnp.float32) + got.astype(jnp.float32)
        step *= 2
        part = total.astype(jnp.bfloat16) if step < count else total
    return part.reshape(shape[:dim] + (size,) + shape[dim + 1 :])


def body(
    features,
    w1_in,
    w1_out,
    gain_ffn1,
    w_qkv,
    w_attn_out,
    rel_table,
    gain_attn,
    w_conv_in,
    w_depth,
    gain_depth,
    w_conv_out,
    gain_conv,
    w2_in,
    w2_out,
    gain_ffn2,
    gain_final,
    cotangent,
):
    local_frames, clip_count, model_width = features.shape
    row_count = local_frames * clip_count
    stream = features.reshape(row_count, model_width).astype(jnp.float32)
    branch_one, kept_one = feed_forward(stream, gain_ffn1, w1_in, w1_out)
    after_one = stream + 0.5 * branch_one
    branch_two, kept_two = attention(after_one, gain_attn, w_qkv, w_attn_out, rel_table, clip_count)
    after_two = after_one + branch_two
    branch_three, kept_three = convolve(
        after_two, gain_conv, w_conv_in, w_depth, gain_depth, w_conv_out, clip_count, model_width
    )
    after_three = after_two + branch_three
    branch_four, kept_four = feed_forward(after_three, gain_ffn2, w2_in, w2_out)
    after_four = after_three + 0.5 * branch_four
    final_gain = gain_final.astype(jnp.float32)
    output, final_unit, final_inverse = norm_rows(after_four, final_gain)
    squares = jnp.stack(
        [
            jnp.sum(branch_one * branch_one),
            jnp.sum(branch_two * branch_two),
            jnp.sum(branch_three * branch_three),
            jnp.sum(branch_four * branch_four),
            jnp.sum(after_four * after_four),
        ]
    )
    seed_grad = cotangent.reshape(row_count, model_width).astype(jnp.float32)
    grad_four, grad_final = norm_back(seed_grad, final_unit, final_inverse, final_gain)
    grad_three, grad_w2_in, grad_w2_out, grad_gain_ffn2 = feed_back(
        grad_four, kept_four, gain_ffn2, w2_in, w2_out
    )
    grad_w2_in, grad_w2_out = settle_block(grad_w2_in, grad_w2_out)
    grad_two, grad_w_conv_in, grad_w_conv_out, grad_gain_conv, grad_w_depth, grad_gain_depth = (
        convolve_back(
            grad_three,
            kept_three,
            gain_conv,
            w_conv_in,
            w_depth,
            gain_depth,
            w_conv_out,
            clip_count,
            model_width,
        )
    )
    grad_w_conv_in, grad_w_conv_out = settle_block(grad_w_conv_in, grad_w_conv_out)
    grad_one, grad_w_qkv, grad_w_attn_out, grad_gain_attn, grad_table = attention_back(
        grad_two, kept_two, gain_attn, w_qkv, w_attn_out, rel_table, clip_count
    )
    grad_w_qkv, grad_w_attn_out = settle_block(grad_w_qkv, grad_w_attn_out)
    grad_input, grad_w1_in, grad_w1_out, grad_gain_ffn1 = feed_back(
        grad_one, kept_one, gain_ffn1, w1_in, w1_out
    )
    grad_w1_in, grad_w1_out = settle_block(grad_w1_in, grad_w1_out)
    summed = (
        halve_sum(grad_w1_in, 0),
        halve_sum(grad_w1_out, 1),
        halve_sum(grad_w_qkv, 0),
        halve_sum(grad_w_attn_out, 1),
        halve_sum(grad_w_conv_in, 0),
        halve_sum(grad_w_conv_out, 1),
        halve_sum(grad_w2_in, 0),
        halve_sum(grad_w2_out, 1),
    )
    gain_grads = jnp.stack(
        [grad_gain_ffn1, grad_gain_attn, grad_gain_conv, grad_gain_ffn2, grad_final]
    )
    gain_sums, table_sum, total_squares = lax.psum((gain_grads, grad_table, squares), ("dp", "mp"))
    depth_sum, depth_gain_sum = lax.psum((grad_w_depth, grad_gain_depth), "dp")
    token_total = row_count * lax.axis_size("mp") * lax.axis_size("dp")
    rms_stats = jnp.sqrt(total_squares / (token_total * model_width))
    return (
        output.reshape(local_frames, clip_count, model_width),
        grad_input.reshape(local_frames, clip_count, model_width),
        summed[0],
        summed[1],
        gain_sums[0],
        summed[2],
        summed[3],
        table_sum,
        gain_sums[1],
        summed[4],
        depth_sum,
        depth_gain_sum,
        summed[5],
        gain_sums[2],
        summed[6],
        summed[7],
        gain_sums[3],
        gain_sums[4],
        rms_stats,
    )


def solution(mesh):
    return jax.shard_map(
        body,
        mesh=mesh,
        in_specs=(
            P("mp", "dp", None),
            P(None, "mp"),
            P("mp", None),
            P(),
            P(None, None, "mp"),
            P("mp", None),
            P(),
            P(),
            P(None, None, "mp"),
            P(None, "mp"),
            P("mp"),
            P("mp", None),
            P(),
            P(None, "mp"),
            P("mp", None),
            P(),
            P(),
            P("mp", "dp", None),
        ),
        out_specs=(
            P("mp", "dp", None),
            P("mp", "dp", None),
            P("dp", "mp"),
            P("mp", "dp"),
            P(),
            P("dp", None, "mp"),
            P("mp", "dp"),
            P(),
            P(),
            P("dp", None, "mp"),
            P(None, "mp"),
            P("mp"),
            P("mp", "dp"),
            P(),
            P("dp", "mp"),
            P("mp", "dp"),
            P(),
            P(),
            P(),
        ),
        check_vma=False,
    )
```

```python
import functools

import jax
import jax.numpy as jnp
from jax import lax
from jax.experimental import pallas as pl
from jax.experimental.pallas import tpu as pltpu
from jax.sharding import PartitionSpec as P

HEAD = 64
REL_LEFT = 64
REL_RIGHT = 8
BQ = 128
WIN = 4 * BQ


epsilon = 1e-05


def nt(a, b):
    return lax.dot_general(a, b, (((1,), (1,)), ((), ())), preferred_element_type=jnp.float32)
def nn(a, b):
    return lax.dot_general(a, b, (((1,), (0,)), ((), ())), preferred_element_type=jnp.float32)
def tn(a, b):
    return lax.dot_general(a, b, (((0,), (0,)), ((), ())), preferred_element_type=jnp.float32)

def split_pair(x):
    left = lax.broadcasted_iota(jnp.int32, x.shape, 1) < HEAD
    zero = jnp.zeros_like(x)
    return jnp.concatenate([jnp.where(left, x, zero), jnp.where(left, zero, x)], 0)

def join_pair(x):
    rows = x.shape[0] // 2
    left = lax.broadcasted_iota(jnp.int32, (rows, x.shape[1]), 1) < HEAD
    return jnp.where(left, x[:rows], x[rows:])

def fwd_kernel(q_ref, k_ref, v_ref, rel_ref, mixed_ref, probs_ref, bias_ref):
    ib = pl.program_id(1)
    qs = split_pair(q_ref[...] * 0.125)
    s = nt(qs, k_ref[...])
    b = nt(qs, rel_ref[...])
    rows = b.shape[0] // 2
    bias_ref[:, 0:BQ] = b[:, 3 * BQ : 4 * BQ]
    for h in range(2):
        r = pltpu.roll(b[h * rows : (h + 1) * rows, :WIN], 0, 1, stride=1, stride_axis=0)
        bias_ref[h * rows : (h + 1) * rows, BQ : 4 * BQ] = r[:, : 3 * BQ]
    bias_ref[:, 4 * BQ :] = b[:, 4 * BQ :]
    nkeys = s.shape[1] // BQ
    parts = []
    for jb in range(nkeys):
        at = pl.multiple_of(jnp.clip(jb - ib + 2, 0, 4) * BQ, BQ)
        parts.append(s[:, jb * BQ : (jb + 1) * BQ] + bias_ref[:, pl.ds(at, BQ)])
    top = functools.reduce(jnp.maximum, parts)
    m = jnp.max(top, -1, keepdims=True)
    es = [jnp.exp(p - m) for p in parts]
    tot = jnp.sum(functools.reduce(jnp.add, es), -1, keepdims=True)
    inv = 1.0 / tot
    for jb in range(nkeys):
        probs_ref[0, :, jb * BQ : (jb + 1) * BQ] = (es[jb] * inv).astype(jnp.bfloat16)
    mixed_ref[...] = join_pair(nn(probs_ref[0], v_ref[...])).astype(jnp.bfloat16)

def bwd_kernel(q_ref, k_ref, v_ref, relb_ref, hot_ref, probs_ref, do_ref, dq_ref, dk_ref, dv_ref, dt_ref,
               tot_ref, dkt, dvt, dta, dz_ref):
    pr, ib, nb = pl.program_id(0), pl.program_id(1), pl.num_programs(1)
    @pl.when(ib == 0)
    def _():
        dkt[...] = jnp.zeros_like(dkt)
        dvt[...] = jnp.zeros_like(dvt)
    @pl.when((ib == 0) & (pr == 0))
    def _():
        dta[...] = jnp.zeros_like(dta)
    qs = split_pair(q_ref[...] * 0.125)
    dos = split_pair(do_ref[...])
    p = probs_ref[0]
    dp = nt(dos, v_ref[...])
    nkeys = dp.shape[1] // BQ
    dvt[...] += tn(dos, p)
    pf = p.astype(jnp.float32)
    acc = None
    for jb in range(nkeys):
        sl = slice(jb * BQ, (jb + 1) * BQ)
        t = pf[:, sl] * dp[:, sl]
        acc = t if acc is None else acc + t
    inner = jnp.sum(acc, -1, keepdims=True)
    tot_ref[...] = jnp.zeros_like(tot_ref)
    for jb in range(nkeys):
        sl = slice(jb * BQ, (jb + 1) * BQ)
        dz = (pf[:, sl] * (dp[:, sl] - inner)).astype(jnp.bfloat16)
        dz_ref[:, sl] = dz
        at = pl.multiple_of(jnp.clip(jb - ib + 2, 0, 4) * BQ, BQ)
        tot_ref[:, pl.ds(at, BQ)] += dz.astype(jnp.float32)
    rows = BQ
    r2 = lax.broadcasted_iota(jnp.int32, (2 * rows, 2 * rows), 0)
    c2 = lax.broadcasted_iota(jnp.int32, (2 * rows, 2 * rows), 1)
    mirror = (r2 + c2 == jnp.where(r2 < rows, rows - 1, 3 * rows - 1)).astype(jnp.bfloat16)
    w = jnp.concatenate([tot_ref[:, BQ : 4 * BQ].astype(jnp.bfloat16), jnp.zeros((2 * rows, BQ), jnp.bfloat16)], 1)
    w = nn(mirror, w)
    outs = [pltpu.roll(w[h * rows : (h + 1) * rows], WIN - rows + 1, 1, stride=1, stride_axis=0) for h in range(2)]
    d = nn(mirror, jnp.concatenate(outs, 0).astype(jnp.bfloat16)).astype(jnp.bfloat16)
    drel = nn(d, hot_ref[...])
    col = lax.broadcasted_iota(jnp.int32, drel.shape, 1)
    low = jnp.sum(tot_ref[:, :BQ], -1, keepdims=True)
    high = jnp.sum(tot_ref[:, 4 * BQ :], -1, keepdims=True)
    drel = drel + jnp.where(col == 0, low, 0.0) + jnp.where(col == REL_LEFT + REL_RIGHT, high, 0.0)
    drel = drel.astype(jnp.bfloat16)
    dz = dz_ref[...]
    dq = nn(dz, k_ref[...]) + nn(drel, relb_ref[...])
    dq_ref[...] = (join_pair(dq) * 0.125).astype(jnp.bfloat16)
    dkt[...] += tn(qs, dz)
    dta[...] += tn(drel, qs)
    @pl.when(ib == nb - 1)
    def _():
        dk_ref[...] = dkt[...].T.astype(jnp.bfloat16)
        dv_ref[...] = dvt[...].T.astype(jnp.bfloat16)
        dt_ref[...] = dta[...]

def rel_tables(rel_table):
    spots = jnp.arange(5 * BQ)
    idx = jnp.where(spots < 3 * BQ, jnp.clip(spots - REL_LEFT, 0, REL_LEFT + REL_RIGHT), jnp.where(spots < 4 * BQ, 0, REL_LEFT + REL_RIGHT))
    hot = (jnp.arange(BQ)[None, :] == idx[:, None]).astype(jnp.bfloat16)
    padded = jnp.pad(rel_table, ((0, BQ - rel_table.shape[0]), (0, 0)))
    padded = jnp.concatenate([padded, padded], 1)
    ext = jnp.dot(hot, padded, preferred_element_type=jnp.float32).astype(jnp.bfloat16)
    return ext, hot[:WIN], padded

def attn_fwd(qkv, ext):
    frames, cols = qkv.shape
    pairs = cols // 3 // 128
    nb = frames // BQ
    bf = jnp.bfloat16
    return pl.pallas_call(
        fwd_kernel,
        grid=(pairs, nb),
        in_specs=[
            pl.BlockSpec((BQ, 128), lambda p, i: (i, p)),
            pl.BlockSpec((frames, 128), lambda p, i: (0, pairs + p)),
            pl.BlockSpec((frames, 128), lambda p, i: (0, 2 * pairs + p)),
            pl.BlockSpec(ext.shape, lambda p, i: (0, 0)),
        ],
        out_specs=[
            pl.BlockSpec((BQ, 128), lambda p, i: (i, p)),
            pl.BlockSpec((1, 2 * BQ, frames), lambda p, i: (p, i, 0)),
        ],
        out_shape=[jax.ShapeDtypeStruct((frames, cols // 3), bf), jax.ShapeDtypeStruct((pairs, 2 * frames, frames), bf)],
        scratch_shapes=[pltpu.VMEM((2 * BQ, 5 * BQ), jnp.float32)],
        compiler_params=pltpu.CompilerParams(vmem_limit_bytes=20 << 20),
        name="attn_fwd",
    )(qkv, qkv, qkv, ext)

def attn_bwd(qkv, padded, hot, probs, dmixed):
    frames, cols = qkv.shape
    pairs = cols // 3 // 128
    nb = frames // BQ
    bf = jnp.bfloat16
    blk = pl.BlockSpec((BQ, 128), lambda p, i: (i, p))
    full = pl.BlockSpec((frames, 128), lambda p, i: (0, p))
    return pl.pallas_call(
        bwd_kernel,
        grid=(pairs, nb),
        in_specs=[
            blk,
            pl.BlockSpec((frames, 128), lambda p, i: (0, pairs + p)),
            pl.BlockSpec((frames, 128), lambda p, i: (0, 2 * pairs + p)),
            pl.BlockSpec(padded.shape, lambda p, i: (0, 0)),
            pl.BlockSpec(hot.shape, lambda p, i: (0, 0)),
            pl.BlockSpec((1, 2 * BQ, frames), lambda p, i: (p, i, 0)),
            blk,
        ],
        out_specs=[blk, full, full, pl.BlockSpec((128, 128), lambda p, i: (0, 0))],
        out_shape=[jax.ShapeDtypeStruct((frames, cols // 3), bf)] * 3 + [jax.ShapeDtypeStruct((128, 128), jnp.float32)],
        scratch_shapes=[pltpu.VMEM((2 * BQ, 5 * BQ), jnp.float32), pltpu.VMEM((128, frames), jnp.float32), pltpu.VMEM((128, frames), jnp.float32),
                        pltpu.VMEM((128, 128), jnp.float32), pltpu.VMEM((2 * BQ, frames), bf)],
        compiler_params=pltpu.CompilerParams(vmem_limit_bytes=20 << 20),
        name="attn_bwd",
    )(qkv, qkv, qkv, padded, hot, probs, dmixed)


MESH = pl.DeviceIdType.MESH
CHUNKS = 4


def silu_pair(h):
    sig = jax.nn.sigmoid(h)
    act = h * sig
    return act, sig + act * (1.0 - sig)


def unit_norm(s):
    centred = s - jnp.mean(s, -1, keepdims=True)
    inverse = lax.rsqrt(jnp.mean(centred * centred, -1, keepdims=True) + epsilon)
    return centred * inverse, inverse


def fold8(x):
    return jnp.sum(x.reshape(x.shape[0] // 8, 8, x.shape[1]), 0)


def norm_pull(grad, s, gain):
    unit, inverse = unit_norm(s)
    scaled = grad * gain
    first = jnp.mean(scaled, -1, keepdims=True)
    second = jnp.mean(scaled * unit, -1, keepdims=True)
    return inverse * (scaled - first - unit * second), fold8(grad * unit)


def stage(name, cid, rows, width, *, leave=None, enter=None, dws=(), junction, row_in=(), vec_in=(), row_out=(), sums=0):
    chunk = rows // CHUNKS
    frames = rows * 4
    f32, bf = jnp.float32, jnp.bfloat16
    ins, out_shape, scratch = [], [], []
    if leave:
        ins += [leave[0], leave[1]]
    if enter:
        ins += [enter[0]] + list(enter[3])
    n_dw_in = []
    for lhs, rhs in dws:
        ins += [lhs, rhs]
    ins += list(row_in) + list(vec_in)
    if enter:
        out_shape.append(jax.ShapeDtypeStruct((frames, width), bf))
        out_shape += [jax.ShapeDtypeStruct((frames, c), d) for c, d in enter[4]]
    for lhs, rhs in dws:
        out_shape.append(jax.ShapeDtypeStruct((rhs.shape[1] // 128, lhs.shape[1], 128), bf))
    out_shape += [jax.ShapeDtypeStruct((rows, width), d) for d in row_out]
    out_shape += [jax.ShapeDtypeStruct((8, width), f32)] * sums
    if leave:
        scratch += [pltpu.VMEM((rows, width), f32)] * 2
        scratch += [pltpu.VMEM((rows, width), bf)] * 6
    scratch += [pltpu.SemaphoreType.DMA((6, CHUNKS)), pltpu.SemaphoreType.DMA((6, CHUNKS))]

    def kernel(*refs):
        refs = list(refs)
        take = lambda n: [refs.pop(0) for _ in range(n)]
        if leave:
            x_ref, wl_ref = take(2)
        if enter:
            (we_ref,) = take(1)
            extra = take(len(enter[3]))
        dw_in = [take(2) for _ in dws]
        r_in, v_in = take(len(row_in)), take(len(vec_in))
        if enter:
            (all_ref,) = take(1)
            e_out = take(len(enter[4]))
        dw_out = take(len(dws))
        r_out, s_out = take(len(row_out)), take(sums)
        if leave:
            px, own, sb, sr, xs, xr, ob, orv = take(8)
        send, recv = take(2)
        dp, me = lax.axis_index("dp"), lax.axis_index("mp")
        core, chip = me % 2, me // 2
        sib = chip * 2 + 1 - core
        far = (1 - chip) * 2 + core
        diag = (1 - chip) * 2 + 1 - core

        def part(ref, block, k):
            return ref.at[pl.ds(pl.multiple_of(block * rows + k * chunk, chunk), chunk)]

        def copy(kind, k, src, dst, to):
            return pltpu.make_async_remote_copy(
                src, dst, send.at[kind, k], recv.at[kind, k], device_id=(dp, to), device_id_type=MESH
            )

        pair_send = lambda k: copy(0, k, part(sb, 0, k), part(sr, 0, k), sib)
        far_send = lambda k: copy(1, k, part(xs, 0, k), part(xr, 0, k), far)
        own_send = lambda k: copy(2, k, part(ob, 0, k), part(orv, 0, k), sib)
        all_far = lambda k: copy(3, k, part(all_ref, me, k), part(all_ref, me, k), far)
        all_sib = lambda k: copy(4, k, part(all_ref, me, k), part(all_ref, me, k), sib)
        all_fwd = lambda k: copy(5, k, part(all_ref, far, k), part(all_ref, far, k), sib)
        got_far = lambda k: copy(3, k, part(all_ref, far, k), part(all_ref, far, k), far)
        got_sib = lambda k: copy(4, k, part(all_ref, sib, k), part(all_ref, sib, k), sib)
        got_diag = lambda k: copy(5, k, part(all_ref, diag, k), part(all_ref, diag, k), sib)

        barrier = pltpu.get_barrier_semaphore()
        for to in (sib, far):
            pl.semaphore_signal(barrier, inc=1, device_id=(dp, to), device_id_type=MESH)
        pl.semaphore_wait(barrier, 2)
        for ref in s_out:
            ref[...] = jnp.zeros_like(ref)

        if leave:
            def two(k, block_a, block_b):
                lhs = jnp.concatenate([part(x_ref, block_a, k)[...], part(x_ref, block_b, k)[...]], 0)
                return leave[2](lhs, wl_ref[...])

            def push(k):
                pair_send(k).wait_recv()
                part(xs, 0, k)[...] = (part(px, 0, k)[...] + part(sr, 0, k)[...].astype(f32)).astype(bf)
                far_send(k).start()

            def out_far(k, c):
                p = two(k, far, diag)
                part(px, 0, k)[...] = p[:chunk]
                part(sb, 0, k)[...] = p[chunk:].astype(bf)
                pair_send(k).start()

                @pl.when(k > 0)
                def _():
                    push(k - 1)
                return c

            lax.fori_loop(0, CHUNKS, out_far, 0)

            def out_near(k, c):
                p = two(k, me, sib)
                part(own, 0, k)[...] = p[:chunk]
                part(ob, 0, k)[...] = p[chunk:].astype(bf)
                own_send(k).start()

                @pl.when(k == 0)
                def _():
                    push(CHUNKS - 1)
                return c

            lax.fori_loop(0, CHUNKS, out_near, 0)

        def join(k, c):
            for (lhs, rhs), out in zip(dw_in, dw_out):
                m = max(lhs.shape[1] // CHUNKS, 128)

                @pl.when(k * m < lhs.shape[1])
                def _(lhs=lhs, rhs=rhs, out=out, m=m):
                    at = pl.ds(pl.multiple_of(k * m, m), m)
                    g = tn(lhs[:, at], rhs[...]).astype(bf)
                    for u in range(out.shape[0]):
                        out[u, at, :] = g[:, u * 128 : (u + 1) * 128]
            branch = None
            if leave:
                own_send(k).wait_recv()
                far_send(k).wait_recv()
                branch = part(own, 0, k)[...] + part(orv, 0, k)[...].astype(f32) + part(xr, 0, k)[...].astype(f32)
            view = lambda ref: part(ref, 0, k)
            fresh = junction(branch, [view(r)[...] for r in r_in], [v[...] for v in v_in], [view(r) for r in r_out], s_out)
            if enter:
                part(all_ref, me, k)[...] = fresh
                all_far(k).start()
                all_sib(k).start()
            return c

        lax.fori_loop(0, CHUNKS, join, 0)

        if enter:
            def work(k, block_a, block_b):
                lhs = jnp.concatenate([part(all_ref, block_a, k)[...], part(all_ref, block_b, k)[...]], 0)
                h = enter[1](lhs, we_ref[...])
                for i, block in enumerate((block_a, block_b)):
                    view = lambda ref: part(ref, block, k)
                    enter[2](h[i * chunk : (i + 1) * chunk], [view(r)[...] for r in extra], [view(r) for r in e_out])

            def gather(k, c):
                got_sib(k).wait_recv()
                work(k, me, sib)
                got_far(k).wait_recv()
                all_fwd(k).start()
                got_diag(k).wait_recv()
                work(k, far, diag)
                return c

            lax.fori_loop(0, CHUNKS, gather, 0)

        def drain(k, c):
            if leave:
                pair_send(k).wait_send()
                far_send(k).wait_send()
                own_send(k).wait_send()
            if enter:
                all_far(k).wait_send()
                all_sib(k).wait_send()
                all_fwd(k).wait_send()
            return c

        lax.fori_loop(0, CHUNKS, drain, 0)

    flops = 0
    if leave:
        flops += 2 * frames * leave[0].shape[1] * width
    if enter:
        flops += 2 * frames * width * sum(c for c, _ in enter[4])
    flops += sum(2 * frames * a.shape[1] * b.shape[1] for a, b in dws)
    vm = pl.BlockSpec(memory_space=pltpu.VMEM)
    return pl.pallas_call(
        kernel,
        in_specs=[vm] * len(ins),
        out_specs=[vm] * len(out_shape),
        out_shape=out_shape,
        scratch_shapes=scratch,
        compiler_params=pltpu.CompilerParams(collective_id=cid, has_side_effects=True, vmem_limit_bytes=24 << 20),
        cost_estimate=pl.CostEstimate(flops=flops, bytes_accessed=60_000_000, transcendentals=0),
        name=name,
    )(*ins)


def halve_sum(part):
    count = lax.axis_size("dp")
    me = lax.axis_index("dp")
    step = 1
    while step < count:
        paired = part.reshape((part.shape[0] // 2, 2) + part.shape[1:])
        bit = (me // step) % 2
        keep = lax.dynamic_index_in_dim(paired, bit, 1, keepdims=False)
        give = lax.dynamic_index_in_dim(paired, 1 - bit, 1, keepdims=False)
        got = lax.ppermute(give, "dp", [(i, i ^ step) for i in range(count)])
        total = keep.astype(jnp.float32) + got.astype(jnp.float32)
        step *= 2
        part = total.astype(jnp.bfloat16) if step < count else total
    return part[0]


def sum_rows(units, shape):
    count = lax.axis_size("dp")
    groups, rows, lanes = units.shape
    split = units.reshape(groups, count, rows // count, lanes).transpose(1, 0, 2, 3)
    total = halve_sum(split)
    return total.transpose(1, 0, 2).reshape((rows // count,) + shape)


def sum_cols(units):
    count = lax.axis_size("dp")
    groups, rows, lanes = units.shape
    per = count // groups
    if per > 1:
        units = units.reshape(groups, rows, per, lanes // per).transpose(0, 2, 1, 3).reshape(count, rows, lanes // per)
    return halve_sum(units)


def body(
    features,
    w1_in,
    w1_out,
    gain_ffn1,
    w_qkv,
    w_attn_out,
    rel_table,
    gain_attn,
    w_conv_in,
    w_depth,
    gain_depth,
    w_conv_out,
    gain_conv,
    w2_in,
    w2_out,
    gain_ffn2,
    gain_final,
    cotangent,
):
    local_frames, clip_count, width = features.shape
    rows = local_frames * clip_count
    f32, bf = jnp.float32, jnp.bfloat16
    s0 = features.reshape(rows, width)
    seed = cotangent.reshape(rows, width)
    vec = lambda g: g.astype(f32).reshape(1, width)
    g1, ga, gc, g2, gf = vec(gain_ffn1), vec(gain_attn), vec(gain_conv), vec(gain_ffn2), vec(gain_final)
    flat_qkv = w_qkv.reshape(width, -1)
    flat_conv = w_conv_in.reshape(width, -1)
    units = w1_in.shape[1]
    chans = w_conv_out.shape[0]

    def swish_out(h, extra, outs):
        act, slope = silu_pair(h)
        outs[0][...] = act.astype(bf)
        outs[1][...] = slope.astype(bf)

    def plain_out(h, extra, outs):
        outs[0][...] = h.astype(outs[0].dtype)

    def glu_out(h, extra, outs):
        p0 = h[:, :chans]
        sig = jax.nn.sigmoid(h[:, chans:])
        glu = p0 * sig
        outs[0][...] = glu
        outs[1][...] = sig.astype(bf)
        outs[2][...] = (glu * (1.0 - sig)).astype(bf)

    def slope_out(h, extra, outs):
        outs[0][...] = (h * extra[0][...].astype(f32)).astype(bf)

    def first(branch, ins, vecs, outs, sums):
        return (unit_norm(ins[0].astype(f32))[0] * vecs[0]).astype(bf)

    def forward(scale):
        def run(branch, ins, vecs, outs, sums):
            fresh = ins[0].astype(f32) + scale * branch
            outs[0][...] = fresh
            sums[0][...] += fold8(branch * branch)
            return (unit_norm(fresh)[0] * vecs[0]).astype(bf)
        return run

    def turn(branch, ins, vecs, outs, sums):
        fresh = ins[0] + 0.5 * branch
        sums[0][...] += fold8(branch * branch)
        sums[1][...] += fold8(fresh * fresh)
        unit, inverse = unit_norm(fresh)
        outs[0][...] = unit * vecs[0]
        grad = ins[1].astype(f32)
        scaled = grad * vecs[0]
        mean_one = jnp.mean(scaled, -1, keepdims=True)
        mean_two = jnp.mean(scaled * unit, -1, keepdims=True)
        sums[2][...] += fold8(grad * unit)
        back = inverse * (scaled - mean_one - unit * mean_two)
        outs[1][...] = back
        return (0.5 * back).astype(bf)

    def backward(scale):
        def run(branch, ins, vecs, outs, sums):
            pull, grad_gain = norm_pull(branch, ins[1].astype(f32), vecs[0])
            fresh = ins[0] + pull
            outs[0][...] = fresh
            sums[0][...] += grad_gain
            return (scale * fresh).astype(bf)
        return run

    a1, act1, slope1 = stage(
        "ffn1_in", 0, rows, width, enter=(w1_in, nn, swish_out, (), ((units, bf), (units, bf))),
        junction=first, row_in=(s0,), vec_in=(g1,),
    )
    a2, qkv, s1, sq1 = stage(
        "ffn1_out", 1, rows, width, leave=(act1, w1_out, nn),
        enter=(flat_qkv, nn, plain_out, (), ((flat_qkv.shape[1], bf),)),
        junction=forward(0.5), row_in=(s0,), vec_in=(ga,), row_out=(f32,), sums=1,
    )
    ext, hot, padded = rel_tables(rel_table)
    mixed, probs = attn_fwd(qkv, ext)
    a3, glu, sig, tail, s2, sq2 = stage(
        "attn_out", 2, rows, width, leave=(mixed, w_attn_out, nn),
        enter=(flat_conv, nn, glu_out, (), ((chans, f32), (chans, bf), (chans, bf))),
        junction=forward(1.0), row_in=(s1,), vec_in=(gc,), row_out=(f32,), sums=1,
    )
    frames = glu.shape[0]
    taps = w_depth.astype(f32)
    tap_count = taps.shape[0]
    padded_glu = jnp.pad(glu, ((tap_count - 1, 0), (0, 0)))
    depth = jnp.zeros_like(glu)
    for k in range(tap_count):
        depth = depth + taps[k] * padded_glu[k : k + frames]
    average = lax.psum(jnp.sum(depth, -1, keepdims=True), "mp") / width
    centred = depth - average
    spread = lax.psum(jnp.sum(centred * centred, -1, keepdims=True), "mp") / width
    depth_inverse = lax.rsqrt(spread + epsilon)
    depth_unit = centred * depth_inverse
    depth_gain = gain_depth.astype(f32)
    act3, slope3 = silu_pair(depth_unit * depth_gain)
    act3 = act3.astype(bf)
    a4, act2, slope2, s3, sq3 = stage(
        "conv_out", 3, rows, width, leave=(act3, w_conv_out, nn),
        enter=(w2_in, nn, swish_out, (), ((units, bf), (units, bf))),
        junction=forward(1.0), row_in=(s2,), vec_in=(g2,), row_out=(f32,), sums=1,
    )
    db4, dh2, output, grad4, sq4, sq5, dgf = stage(
        "ffn2_out", 4, rows, width, leave=(act2, w2_out, nn),
        enter=(w2_out, nt, slope_out, (slope2,), ((units, bf),)),
        junction=turn, row_in=(s3, seed), vec_in=(gf,), row_out=(f32, f32), sums=3,
    )
    db3, de3, dw2_in, dw2_out, grad3, dg2 = stage(
        "ffn2_back", 5, rows, width, leave=(dh2, w2_in, nt),
        enter=(w_conv_out, nt, plain_out, (), ((chans, f32),)), dws=((a4, dh2), (act2, db4)),
        junction=backward(1.0), row_in=(grad4, s3), vec_in=(g2,), row_out=(f32,), sums=1,
    )
    grad_gated = de3 * slope3
    grad_gain_depth = jnp.sum(grad_gated * depth_unit, 0)
    grad_unit = grad_gated * depth_gain
    first_sum, second_sum = lax.psum(
        (jnp.sum(grad_unit, -1, keepdims=True), jnp.sum(grad_unit * depth_unit, -1, keepdims=True)), "mp"
    )
    grad_depth = depth_inverse * (grad_unit - first_sum / width - depth_unit * second_sum / width)
    padded_grad = jnp.pad(grad_depth, ((0, tap_count - 1), (0, 0)))
    grad_glu = jnp.zeros_like(grad_depth)
    tap_grads = []
    for k in range(tap_count):
        start = tap_count - 1 - k
        grad_glu = grad_glu + taps[k] * padded_grad[start : start + frames]
        tap_grads.append(jnp.sum(grad_depth * padded_glu[k : k + frames], 0))
    grad_w_depth = jnp.stack(tap_grads, 0)
    dpaired = jnp.concatenate([grad_glu * sig.astype(f32), grad_glu * tail.astype(f32)], 1).astype(bf)
    db2, dmixed, dw_conv_in, dw_conv_out, grad2, dgc = stage(
        "conv_back", 6, rows, width, leave=(dpaired, flat_conv, nt),
        enter=(w_attn_out, nt, plain_out, (), ((w_attn_out.shape[0], bf),)), dws=((a3, dpaired), (act3, db3)),
        junction=backward(1.0), row_in=(grad3, s2), vec_in=(gc,), row_out=(f32,), sums=1,
    )
    dq, dk, dv, dt = attn_bwd(qkv, padded, hot, probs, dmixed)
    rel = rel_table.shape[0]
    grad_table = dt[:rel, :HEAD] + dt[:rel, HEAD:]
    dqkv = jnp.concatenate([dq, dk, dv], 1)
    db1, dh1, dw_qkv, dw_attn_out, grad1, dga = stage(
        "attn_back", 7, rows, width, leave=(dqkv, flat_qkv, nt),
        enter=(w1_out, nt, slope_out, (slope1,), ((units, bf),)), dws=((a2, dqkv), (mixed, db2)),
        junction=backward(0.5), row_in=(grad2, s1), vec_in=(ga,), row_out=(f32,), sums=1,
    )
    dw1_in, dw1_out, grad0, dg1 = stage(
        "ffn1_back", 8, rows, width, leave=(dh1, w1_in, nt), dws=((a1, dh1), (act1, db1)),
        junction=backward(1.0), row_in=(grad1, s0), vec_in=(g1,), row_out=(f32,), sums=1,
    )
    gains = jnp.stack([jnp.sum(g, 0) for g in (dg1, dga, dgc, dg2, dgf)])
    squares = jnp.stack([jnp.sum(s) for s in (sq1, sq2, sq3, sq4, sq5)])
    gain_sums, table_sum, total_squares = lax.psum((gains, grad_table, squares), ("dp", "mp"))
    depth_sum, depth_gain_sum = lax.psum((grad_w_depth, grad_gain_depth), "dp")
    token_total = rows * lax.axis_size("mp") * lax.axis_size("dp")
    rms_stats = jnp.sqrt(total_squares / (token_total * width))
    whole = lambda x: x.reshape(local_frames, clip_count, width)
    return (
        whole(output),
        whole(grad0),
        sum_rows(dw1_in, (units,)),
        sum_cols(dw1_out),
        gain_sums[0],
        sum_rows(dw_qkv, (3, w_qkv.shape[2])),
        sum_cols(dw_attn_out),
        table_sum,
        gain_sums[1],
        sum_rows(dw_conv_in, (2, chans)),
        depth_sum,
        depth_gain_sum,
        sum_cols(dw_conv_out),
        gain_sums[2],
        sum_rows(dw2_in, (units,)),
        sum_cols(dw2_out),
        gain_sums[3],
        gain_sums[4],
        rms_stats,
    )


def solution(mesh):
    return jax.shard_map(
        body,
        mesh=mesh,
        in_specs=(
            P("mp", "dp", None),
            P(None, "mp"),
            P("mp", None),
            P(),
            P(None, None, "mp"),
            P("mp", None),
            P(),
            P(),
            P(None, None, "mp"),
            P(None, "mp"),
            P("mp"),
            P("mp", None),
            P(),
            P(None, "mp"),
            P("mp", None),
            P(),
            P(),
            P("mp", "dp", None),
        ),
        out_specs=(
            P("mp", "dp", None),
            P("mp", "dp", None),
            P("dp", "mp"),
            P("mp", "dp"),
            P(),
            P("dp", None, "mp"),
            P("mp", "dp"),
            P(),
            P(),
            P("dp", None, "mp"),
            P(None, "mp"),
            P("mp"),
            P("mp", "dp"),
            P(),
            P("dp", "mp"),
            P("mp", "dp"),
            P(),
            P(),
            P(),
        ),
        check_vma=False,
    )
```

```python
import functools

import jax
import jax.numpy as jnp
from jax import lax
from jax.experimental import pallas as pl
from jax.experimental.pallas import tpu as pltpu
from jax.sharding import PartitionSpec as P

HEAD = 64
REL_LEFT = 64
REL_RIGHT = 8
BQ = 128
WIN = 4 * BQ


epsilon = 1e-05


def nt(a, b):
    return lax.dot_general(a, b, (((1,), (1,)), ((), ())), preferred_element_type=jnp.float32)
def nn(a, b):
    return lax.dot_general(a, b, (((1,), (0,)), ((), ())), preferred_element_type=jnp.float32)
def tn(a, b):
    return lax.dot_general(a, b, (((0,), (0,)), ((), ())), preferred_element_type=jnp.float32)

MESH = pl.DeviceIdType.MESH
CHUNKS = 4
PIECE = 256


def silu_pair(h):
    sig = jax.nn.sigmoid(h)
    act = h * sig
    return act, sig + act * (1.0 - sig)


def unit_norm(s):
    centred = s - jnp.mean(s, -1, keepdims=True)
    inverse = lax.rsqrt(jnp.mean(centred * centred, -1, keepdims=True) + epsilon)
    return centred * inverse, inverse


def fold8(x):
    return jnp.sum(x.reshape(x.shape[0] // 8, 8, x.shape[1]), 0)


def norm_pull(grad, s, gain):
    unit, inverse = unit_norm(s)
    scaled = grad * gain
    first = jnp.mean(scaled, -1, keepdims=True)
    second = jnp.mean(scaled * unit, -1, keepdims=True)
    return inverse * (scaled - first - unit * second), fold8(grad * unit)


class Grad:
    def __init__(self, array, bit, turned):
        self.array, self.bit, self.turned = array, bit, turned


def halved(shape, turned):
    pieces, pairs, _, block, cols = shape
    if pairs > 1:
        return jax.ShapeDtypeStruct((pieces, pairs // 2, 2, block, cols), jnp.bfloat16)
    if turned and block % 128 == 0:
        return jax.ShapeDtypeStruct((pieces * cols, block), jnp.float32)
    return jax.ShapeDtypeStruct((block, pieces * cols), jnp.float32)


def arriving(shape):
    return pltpu.VMEM((shape[0], shape[1]) + tuple(shape[3:]), jnp.bfloat16)


def place(dp, bit):
    own = (dp // 2**bit) % 2
    return own, dp + 2**bit * (1 - 2 * own)


def halving_copy(src, landing, piece, bit, send, recv, slot):
    dp, mp = lax.axis_index("dp"), lax.axis_index("mp")
    own, partner = place(dp, bit)
    return pltpu.make_async_remote_copy(
        src.at[piece, :, 1 - own], landing.at[piece], send.at[slot], recv.at[slot],
        device_id=(partner, mp), device_id_type=MESH,
    )


def halving_add(src, landing, out, piece, bit, turned):
    own, _ = place(lax.axis_index("dp"), bit)
    pairs, block, cols = landing.shape[1:]
    f32 = jnp.float32
    if pairs == 1:
        total = src[piece, 0, own].astype(f32) + landing[piece, 0].astype(f32)
        at = slice(piece * cols, (piece + 1) * cols)
        if turned and block % 128 == 0:
            out[at, :] = total.T
        else:
            out[:, at] = total
        return

    def add(j, c):
        total = src[piece, j, own].astype(f32) + landing[piece, j].astype(f32)
        out[piece, j // 2, j % 2] = total.astype(jnp.bfloat16)
        return c

    lax.fori_loop(0, pairs, add, 0)


def greet(targets):
    barrier = pltpu.get_barrier_semaphore()
    for to in targets:
        pl.semaphore_signal(barrier, inc=1, device_id=to, device_id_type=MESH)
    pl.semaphore_wait(barrier, len(targets))


def stage(name, cid, rows, width, count, *, leave=None, enter=None, dws=(), grads=(), small=None, junction, row_in=(), vec_in=(), row_out=(), sums=0):
    chunk = rows // CHUNKS
    frames = rows * 4
    steps = count.bit_length() - 1
    last = small is not None
    f32, bf = jnp.float32, jnp.bfloat16
    ins, out_shape, scratch = [], [], []
    if leave:
        ins += [leave[0], leave[1]]
        scratch += [pltpu.VMEM((rows, width), f32)] * 2 + [pltpu.VMEM((rows, width), bf)] * 6
        if leave[2]:
            scratch.append(pltpu.VMEM(leave[1].shape[::-1], bf))
    if enter:
        ins += [enter[0]] + list(enter[3])
        out_shape.append(jax.ShapeDtypeStruct((frames, width), bf))
        out_shape += [jax.ShapeDtypeStruct((frames, c), d) for c, d in enter[4]]
        if enter[1]:
            scratch.append(pltpu.VMEM(enter[0].shape[::-1], bf))
    ins += list(row_in) + list(vec_in)
    out_shape += [jax.ShapeDtypeStruct((rows, width), d) for d in row_out]
    out_shape += [jax.ShapeDtypeStruct((8, width), f32)] * sums
    fixed_out = len(out_shape)
    plan, dw_shapes = [], []
    for lhs, rhs, where, turned in dws:
        ins += [lhs, rhs]
        shape = (rhs.shape[1] // PIECE, count // 2, 2, width // count, PIECE)
        dw_shapes.append(shape)
        if where == "join":
            out_shape.append(jax.ShapeDtypeStruct(shape, bf))
        else:
            scratch.append(pltpu.VMEM(shape, bf))
            plan.append((shape, 0, turned))
    for g in grads:
        ins.append(g.array)
        plan.append((g.array.shape, g.bit, g.turned))
    chains = []
    slots = 0
    for shape, bit, turned in plan:
        links = []
        for b in range(bit, steps if last else bit + 1):
            nxt = halved(shape, turned)
            final = b == (steps if last else bit + 1) - 1
            scratch.append(arriving(shape))
            if final:
                out_shape.append(nxt)
            else:
                scratch.append(pltpu.VMEM(nxt.shape, nxt.dtype))
            links.append((b, final, slots))
            slots += shape[0]
            shape = nxt.shape
        chains.append((plan[len(chains)][0][0], turned, links))
    if last:
        ins += small
        small_shapes = [(16, width), small[-3].shape, (small[-2].shape[0] + 1, small[-2].shape[1])]
        small_steps = [steps + 2, steps + 2, steps]
        out_shape += [jax.ShapeDtypeStruct(s, f32) for s in small_shapes]
        scratch += [pltpu.VMEM((n,) + s, f32) for s, n in zip(small_shapes, small_steps)]
        scratch += [pltpu.SemaphoreType.DMA((3, steps + 2))] * 2
    if slots:
        scratch += [pltpu.SemaphoreType.DMA((slots,))] * 2
    scratch += [pltpu.SemaphoreType.DMA((6, CHUNKS))] * 2

    def kernel(*refs):
        i_refs = list(refs[: len(ins)])
        o_refs = list(refs[len(ins) : len(ins) + len(out_shape)])
        t_refs = list(refs[len(ins) + len(out_shape) :])
        take = lambda pool, n: [pool.pop(0) for _ in range(n)]
        if leave:
            x_ref, wl_raw = take(i_refs, 2)
            px, own, sb, sr, xs, xr, ob, orv = take(t_refs, 8)
            wl_ref = take(t_refs, 1)[0] if leave[2] else wl_raw
        if enter:
            (we_raw,) = take(i_refs, 1)
            extra = take(i_refs, len(enter[3]))
            (all_ref,) = take(o_refs, 1)
            e_out = take(o_refs, len(enter[4]))
            we_ref = take(t_refs, 1)[0] if enter[1] else we_raw
        r_in, v_in = take(i_refs, len(row_in)), take(i_refs, len(vec_in))
        r_out, s_out = take(o_refs, len(row_out)), take(o_refs, sums)
        dw_refs, sources = [], []
        for (lhs, rhs, where, turned) in dws:
            a, b = take(i_refs, 2)
            dw = take(o_refs if where == "join" else t_refs, 1)[0]
            dw_refs.append((a, b, dw, None if where == "join" else len(sources)))
            if where != "join":
                sources.append(dw)
        first_grad = len(sources)
        sources += take(i_refs, len(grads))
        runs = []
        for (pieces, turned, links), src in zip(chains, sources):
            run = []
            for b, final, slot in links:
                landing = take(t_refs, 1)[0]
                out = take(o_refs if final else t_refs, 1)[0]
                run.append((b, slot, src, landing, out))
                src = out
            runs.append((pieces, turned, run))
        if last:
            small_in = take(i_refs, len(small))
            small_out = take(o_refs, 3)
            small_land = take(t_refs, 3)
            ssend, srecv = take(t_refs, 2)
        if slots:
            gsend, grecv = take(t_refs, 2)
        send, recv = take(t_refs, 2)
        dp, me = lax.axis_index("dp"), lax.axis_index("mp")
        core, chip = me % 2, me // 2
        sib = chip * 2 + 1 - core
        far = (1 - chip) * 2 + core
        diag = (1 - chip) * 2 + 1 - core

        def part(ref, block, k):
            return ref.at[pl.ds(pl.multiple_of(block * rows + k * chunk, chunk), chunk)]

        def copy(kind, k, src, dst, to):
            return pltpu.make_async_remote_copy(
                src, dst, send.at[kind, k], recv.at[kind, k], device_id=(dp, to), device_id_type=MESH
            )

        pair_send = lambda k: copy(0, k, part(sb, 0, k), part(sr, 0, k), sib)
        far_send = lambda k: copy(1, k, part(xs, 0, k), part(xr, 0, k), far)
        own_send = lambda k: copy(2, k, part(ob, 0, k), part(orv, 0, k), sib)
        all_far = lambda k: copy(3, k, part(all_ref, me, k), part(all_ref, me, k), far)
        all_sib = lambda k: copy(4, k, part(all_ref, me, k), part(all_ref, me, k), sib)
        all_fwd = lambda k: copy(5, k, part(all_ref, far, k), part(all_ref, far, k), sib)
        got_far = lambda k: copy(3, k, part(all_ref, far, k), part(all_ref, far, k), far)
        got_sib = lambda k: copy(4, k, part(all_ref, sib, k), part(all_ref, sib, k), sib)
        got_diag = lambda k: copy(5, k, part(all_ref, diag, k), part(all_ref, diag, k), sib)

        def hop(chain, step, piece):
            b, slot, src, landing, out = runs[chain][2][step]
            return halving_copy(src, landing, piece, b, gsend, grecv, slot + piece)

        def settle(chain, step, piece):
            b, slot, src, landing, out = runs[chain][2][step]
            hop(chain, step, piece).wait_recv()
            halving_add(src, landing, out, piece, b, runs[chain][1])

        bits = sorted({r[0] for _, _, run in runs for r in run})
        greet([(dp, sib), (dp, far)] + [(place(dp, b)[1], me) for b in bits])
        for c in range(first_grad, len(runs)):
            for p in range(runs[c][0]):
                hop(c, 0, p).start()
        for ref in s_out:
            ref[...] = jnp.zeros_like(ref)

        def fill(k, where):
            for (lhs, rhs, at_loop, turned), (a, b, dw, chain) in zip(dws, dw_refs):
                if at_loop != where:
                    continue

                @pl.when(k < dw.shape[0])
                def _(a=a, b=b, dw=dw, chain=chain):
                    g = tn(a[...], b[:, pl.ds(pl.multiple_of(k * PIECE, PIECE), PIECE)])
                    dw[k] = g.astype(bf).reshape(dw.shape[1:])
                    if chain is not None:
                        hop(chain, 0, k).start()

        if leave:
            if leave[2]:
                wl_ref[...] = wl_raw[...].T

            def two(k, block_a, block_b):
                lhs = jnp.concatenate([part(x_ref, block_a, k)[...], part(x_ref, block_b, k)[...]], 0)
                return nn(lhs, wl_ref[...])

            def push(k):
                pair_send(k).wait_recv()
                part(xs, 0, k)[...] = (part(px, 0, k)[...] + part(sr, 0, k)[...].astype(f32)).astype(bf)
                far_send(k).start()

            def out_far(k, c):
                p = two(k, far, diag)
                part(px, 0, k)[...] = p[:chunk]
                part(sb, 0, k)[...] = p[chunk:].astype(bf)
                pair_send(k).start()

                @pl.when(k > 0)
                def _():
                    push(k - 1)

                fill(k, "far")
                return c

            lax.fori_loop(0, CHUNKS, out_far, 0)

            def out_near(k, c):
                p = two(k, me, sib)
                part(own, 0, k)[...] = p[:chunk]
                part(ob, 0, k)[...] = p[chunk:].astype(bf)
                own_send(k).start()

                @pl.when(k == 0)
                def _():
                    push(CHUNKS - 1)

                fill(k, "near")
                return c

            lax.fori_loop(0, CHUNKS, out_near, 0)
        if enter and enter[1]:
            we_ref[...] = we_raw[...].T

        def join(k, c):
            fill(k, "join")
            branch = None
            if leave:
                own_send(k).wait_recv()
                far_send(k).wait_recv()
                branch = part(own, 0, k)[...] + part(orv, 0, k)[...].astype(f32) + part(xr, 0, k)[...].astype(f32)
            view = lambda ref: part(ref, 0, k)
            fresh = junction(branch, [view(r)[...] for r in r_in], [v[...] for v in v_in], [view(r) for r in r_out], s_out)
            if enter:
                part(all_ref, me, k)[...] = fresh
                all_far(k).start()
                all_sib(k).start()
            return c

        lax.fori_loop(0, CHUNKS, join, 0)

        if enter:
            def work(k, block_a, block_b):
                lhs = jnp.concatenate([part(all_ref, block_a, k)[...], part(all_ref, block_b, k)[...]], 0)
                h = nn(lhs, we_ref[...])
                for i, block in enumerate((block_a, block_b)):
                    view = lambda ref: part(ref, block, k)
                    enter[2](h[i * chunk : (i + 1) * chunk], [view(r)[...] for r in extra], [view(r) for r in e_out])

            def gather(k, c):
                got_sib(k).wait_recv()
                work(k, me, sib)
                got_far(k).wait_recv()
                all_fwd(k).start()
                got_diag(k).wait_recv()
                work(k, far, diag)
                return c

            lax.fori_loop(0, CHUNKS, gather, 0)

        if last:
            *vectors, table, taps, tap_gain = small_in
            small_out[0][...] = jnp.zeros_like(small_out[0])
            for i, v in enumerate([s_out[0]] + vectors):
                small_out[0][i : i + 1, :] = jnp.sum(v[...], 0, keepdims=True)
            small_out[1][...] = table[...]
            small_out[2][: taps.shape[0], :] = taps[...]
            small_out[2][taps.shape[0] :, :] = tap_gain[...]

            def double(step):
                if step < steps:
                    to = (place(dp, step)[1], me)
                else:
                    to = (dp, sib if step == steps else far)
                return [
                    pltpu.make_async_remote_copy(
                        o, l.at[step], ssend.at[i, step], srecv.at[i, step], device_id=to, device_id_type=MESH
                    )
                    for i, (o, l, n) in enumerate(zip(small_out, small_land, small_steps))
                    if step < n
                ]

            for cp in double(0):
                cp.start()

        pieces = [(c, p) for c, (count_p, _, _) in enumerate(runs) for p in range(count_p)]
        order = [x for x in pieces if x[0] >= first_grad] + [x for x in pieces if x[0] < first_grad]
        deepest = max([len(run) for _, _, run in runs] + [0])
        total_slots = max(len(order) + deepest - 1, (steps + 2) if last else 0)
        for t in range(total_slots):
            if last and t < steps + 2:
                for cp in double(t):
                    cp.wait()
                for o, l, n in zip(small_out, small_land, small_steps):
                    if t < n:
                        o[...] += l[t]
                if t + 1 < steps + 2:
                    for cp in double(t + 1):
                        cp.start()
            for s in reversed(range(deepest)):
                if 0 <= t - s < len(order) and s < len(runs[order[t - s][0]][2]):
                    c, p = order[t - s]
                    settle(c, s, p)
                    if s + 1 < len(runs[c][2]):
                        hop(c, s + 1, p).start()
        for c, (count_p, _, run) in enumerate(runs):
            for s in range(len(run)):
                for p in range(count_p):
                    hop(c, s, p).wait_send()

        def drain(k, c):
            if leave:
                pair_send(k).wait_send()
                far_send(k).wait_send()
                own_send(k).wait_send()
            if enter:
                all_far(k).wait_send()
                all_sib(k).wait_send()
                all_fwd(k).wait_send()
            return c

        lax.fori_loop(0, CHUNKS, drain, 0)

    flops = 0
    if leave:
        flops += 2 * frames * leave[0].shape[1] * width
    if enter:
        flops += 2 * frames * width * sum(c for c, _ in enter[4])
    flops += sum(2 * frames * d[0].shape[1] * d[1].shape[1] for d in dws)
    vm = pl.BlockSpec(memory_space=pltpu.VMEM)
    outs = pl.pallas_call(
        kernel,
        in_specs=[vm] * len(ins),
        out_specs=[vm] * len(out_shape),
        out_shape=out_shape,
        scratch_shapes=scratch,
        compiler_params=pltpu.CompilerParams(
            collective_id=cid, has_side_effects=True, vmem_limit_bytes=(40 if last else 28) << 20
        ),
        cost_estimate=pl.CostEstimate(flops=flops, bytes_accessed=60_000_000, transcendentals=0),
        name=name,
    )(*ins)
    fixed, rest = list(outs[:fixed_out]), list(outs[fixed_out:])
    fresh = [Grad(rest.pop(0), 0, d[3]) for d in dws if d[2] == "join"]
    for (shape, bit, turned) in plan:
        fresh.append(Grad(rest.pop(0), steps if last else bit + 1, turned))
    return fixed + [fresh] + rest


def split_pair(x):
    left = lax.broadcasted_iota(jnp.int32, x.shape, 1) < HEAD
    zero = jnp.zeros_like(x)
    return jnp.concatenate([jnp.where(left, x, zero), jnp.where(left, zero, x)], 0)

def join_pair(x):
    rows = x.shape[0] // 2
    left = lax.broadcasted_iota(jnp.int32, (rows, x.shape[1]), 1) < HEAD
    return jnp.where(left, x[:rows], x[rows:])

def fwd_kernel(q_ref, k_ref, v_ref, rel_ref, mixed_ref, probs_ref, bias_ref):
    ib = pl.program_id(1)
    qs = split_pair(q_ref[...] * 0.125)
    s = nt(qs, k_ref[...])
    b = nt(qs, rel_ref[...])
    rows = b.shape[0] // 2
    bias_ref[:, 0:BQ] = b[:, 3 * BQ : 4 * BQ]
    for h in range(2):
        r = pltpu.roll(b[h * rows : (h + 1) * rows, :WIN], 0, 1, stride=1, stride_axis=0)
        bias_ref[h * rows : (h + 1) * rows, BQ : 4 * BQ] = r[:, : 3 * BQ]
    bias_ref[:, 4 * BQ :] = b[:, 4 * BQ :]
    nkeys = s.shape[1] // BQ
    parts = []
    for jb in range(nkeys):
        at = pl.multiple_of(jnp.clip(jb - ib + 2, 0, 4) * BQ, BQ)
        parts.append(s[:, jb * BQ : (jb + 1) * BQ] + bias_ref[:, pl.ds(at, BQ)])
    top = functools.reduce(jnp.maximum, parts)
    m = jnp.max(top, -1, keepdims=True)
    es = [jnp.exp(p - m) for p in parts]
    tot = jnp.sum(functools.reduce(jnp.add, es), -1, keepdims=True)
    inv = 1.0 / tot
    for jb in range(nkeys):
        probs_ref[0, :, jb * BQ : (jb + 1) * BQ] = (es[jb] * inv).astype(jnp.bfloat16)
    mixed_ref[...] = join_pair(nn(probs_ref[0], v_ref[...])).astype(jnp.bfloat16)

def bwd_kernel(plan, *refs):
    n = len(plan)
    pairs_in, refs = refs[7 : 7 + n], refs[:7] + refs[7 + n :]
    q_ref, k_ref, v_ref, relb_ref, hot_ref, probs_ref, do_ref, dq_ref, dk_ref, dv_ref, dt_ref = refs[:11]
    grads_out, refs = refs[11 : 11 + n], refs[11 + n :]
    tot_ref, dkt, dvt, dta, dz_ref = refs[:5]
    landings, sems = refs[5 : 5 + n], refs[5 + n :]
    pr, ib, nb = pl.program_id(0), pl.program_id(1), pl.num_programs(1)
    dp, mp = lax.axis_index("dp"), lax.axis_index("mp")
    hops, slot = [], 0
    for (pieces, bit, turned), src, landing, out in zip(plan, pairs_in, landings, grads_out):
        for p in range(pieces):
            hops.append((halving_copy(src, landing, p, bit, *sems, slot), src, landing, out, p, bit, turned))
            slot += 1

    if hops:

        @pl.when((ib == 0) & (pr == 0))
        def _():
            greet([(place(dp, b)[1], mp) for b in sorted({x[1] for x in plan})])
            for hop in hops:
                hop[0].start()

    @pl.when(ib == 0)
    def _():
        dkt[...] = jnp.zeros_like(dkt)
        dvt[...] = jnp.zeros_like(dvt)
    @pl.when((ib == 0) & (pr == 0))
    def _():
        dta[...] = jnp.zeros_like(dta)
    qs = split_pair(q_ref[...] * 0.125)
    dos = split_pair(do_ref[...])
    p = probs_ref[0]
    dp = nt(dos, v_ref[...])
    nkeys = dp.shape[1] // BQ
    dvt[...] += tn(dos, p)
    pf = p.astype(jnp.float32)
    acc = None
    for jb in range(nkeys):
        sl = slice(jb * BQ, (jb + 1) * BQ)
        t = pf[:, sl] * dp[:, sl]
        acc = t if acc is None else acc + t
    inner = jnp.sum(acc, -1, keepdims=True)
    tot_ref[...] = jnp.zeros_like(tot_ref)
    for jb in range(nkeys):
        sl = slice(jb * BQ, (jb + 1) * BQ)
        dz = (pf[:, sl] * (dp[:, sl] - inner)).astype(jnp.bfloat16)
        dz_ref[:, sl] = dz
        at = pl.multiple_of(jnp.clip(jb - ib + 2, 0, 4) * BQ, BQ)
        tot_ref[:, pl.ds(at, BQ)] += dz.astype(jnp.float32)
    rows = BQ
    r2 = lax.broadcasted_iota(jnp.int32, (2 * rows, 2 * rows), 0)
    c2 = lax.broadcasted_iota(jnp.int32, (2 * rows, 2 * rows), 1)
    mirror = (r2 + c2 == jnp.where(r2 < rows, rows - 1, 3 * rows - 1)).astype(jnp.bfloat16)
    w = jnp.concatenate([tot_ref[:, BQ : 4 * BQ].astype(jnp.bfloat16), jnp.zeros((2 * rows, BQ), jnp.bfloat16)], 1)
    w = nn(mirror, w)
    outs = [pltpu.roll(w[h * rows : (h + 1) * rows], WIN - rows + 1, 1, stride=1, stride_axis=0) for h in range(2)]
    d = nn(mirror, jnp.concatenate(outs, 0).astype(jnp.bfloat16)).astype(jnp.bfloat16)
    drel = nn(d, hot_ref[...])
    col = lax.broadcasted_iota(jnp.int32, drel.shape, 1)
    low = jnp.sum(tot_ref[:, :BQ], -1, keepdims=True)
    high = jnp.sum(tot_ref[:, 4 * BQ :], -1, keepdims=True)
    drel = drel + jnp.where(col == 0, low, 0.0) + jnp.where(col == REL_LEFT + REL_RIGHT, high, 0.0)
    drel = drel.astype(jnp.bfloat16)
    dz = dz_ref[...]
    dq = nn(dz, k_ref[...]) + nn(drel, relb_ref[...])
    dq_ref[...] = (join_pair(dq) * 0.125).astype(jnp.bfloat16)
    dkt[...] += tn(qs, dz)
    dta[...] += tn(drel, qs)
    @pl.when(ib == nb - 1)
    def _():
        dk_ref[...] = dkt[...].T.astype(jnp.bfloat16)
        dv_ref[...] = dvt[...].T.astype(jnp.bfloat16)
        dt_ref[...] = dta[...]

    if hops:

        @pl.when((ib == nb - 1) & (pr == pl.num_programs(0) - 1))
        def _():
            for hop in hops:
                hop[0].wait_recv()
                halving_add(*hop[1:])
            for hop in hops:
                hop[0].wait_send()

def rel_tables(rel_table):
    spots = jnp.arange(5 * BQ)
    idx = jnp.where(spots < 3 * BQ, jnp.clip(spots - REL_LEFT, 0, REL_LEFT + REL_RIGHT), jnp.where(spots < 4 * BQ, 0, REL_LEFT + REL_RIGHT))
    hot = (jnp.arange(BQ)[None, :] == idx[:, None]).astype(jnp.bfloat16)
    padded = jnp.pad(rel_table, ((0, BQ - rel_table.shape[0]), (0, 0)))
    padded = jnp.concatenate([padded, padded], 1)
    ext = jnp.dot(hot, padded, preferred_element_type=jnp.float32).astype(jnp.bfloat16)
    return ext, hot[:WIN], padded

def attn_fwd(qkv, ext):
    frames, cols = qkv.shape
    pairs = cols // 3 // 128
    nb = frames // BQ
    bf = jnp.bfloat16
    return pl.pallas_call(
        fwd_kernel,
        grid=(pairs, nb),
        in_specs=[
            pl.BlockSpec((BQ, 128), lambda p, i: (i, p)),
            pl.BlockSpec((frames, 128), lambda p, i: (0, pairs + p)),
            pl.BlockSpec((frames, 128), lambda p, i: (0, 2 * pairs + p)),
            pl.BlockSpec(ext.shape, lambda p, i: (0, 0)),
        ],
        out_specs=[
            pl.BlockSpec((BQ, 128), lambda p, i: (i, p)),
            pl.BlockSpec((1, 2 * BQ, frames), lambda p, i: (p, i, 0)),
        ],
        out_shape=[jax.ShapeDtypeStruct((frames, cols // 3), bf), jax.ShapeDtypeStruct((pairs, 2 * frames, frames), bf)],
        scratch_shapes=[pltpu.VMEM((2 * BQ, 5 * BQ), jnp.float32)],
        compiler_params=pltpu.CompilerParams(vmem_limit_bytes=20 << 20),
        name="attn_fwd",
    )(qkv, qkv, qkv, ext)

def attn_bwd(qkv, padded, hot, probs, dmixed, grads, cid):
    frames, cols = qkv.shape
    pairs = cols // 3 // 128
    nb = frames // BQ
    bf = jnp.bfloat16
    blk = pl.BlockSpec((BQ, 128), lambda p, i: (i, p))
    full = pl.BlockSpec((frames, 128), lambda p, i: (0, p))
    plan = [(g.array.shape[0], g.bit, g.turned) for g in grads]
    after = [halved(g.array.shape, g.turned) for g in grads]
    still = lambda shape: pl.BlockSpec(shape, lambda p, i: (0,) * len(shape), pipeline_mode=pl.Buffered(1))
    slots = sum(x[0] for x in plan)
    outs = pl.pallas_call(
        functools.partial(bwd_kernel, plan),
        grid=(pairs, nb),
        in_specs=[
            blk,
            pl.BlockSpec((frames, 128), lambda p, i: (0, pairs + p)),
            pl.BlockSpec((frames, 128), lambda p, i: (0, 2 * pairs + p)),
            pl.BlockSpec(padded.shape, lambda p, i: (0, 0)),
            pl.BlockSpec(hot.shape, lambda p, i: (0, 0)),
            pl.BlockSpec((1, 2 * BQ, frames), lambda p, i: (p, i, 0)),
            blk,
        ]
        + [still(g.array.shape) for g in grads],
        out_specs=[blk, full, full, pl.BlockSpec((128, 128), lambda p, i: (0, 0))] + [still(a.shape) for a in after],
        out_shape=[jax.ShapeDtypeStruct((frames, cols // 3), bf)] * 3 + [jax.ShapeDtypeStruct((128, 128), jnp.float32)] + after,
        scratch_shapes=[pltpu.VMEM((2 * BQ, 5 * BQ), jnp.float32), pltpu.VMEM((128, frames), jnp.float32), pltpu.VMEM((128, frames), jnp.float32),
                        pltpu.VMEM((128, 128), jnp.float32), pltpu.VMEM((2 * BQ, frames), bf)]
        + [arriving(g.array.shape) for g in grads]
        + ([pltpu.SemaphoreType.DMA((slots,))] * 2 if grads else []),
        compiler_params=pltpu.CompilerParams(
            vmem_limit_bytes=32 << 20, collective_id=cid, has_side_effects=True
        ),
        cost_estimate=pl.CostEstimate(flops=20 * frames * frames * 128 * pairs, bytes_accessed=20_000_000, transcendentals=0),
        name="attn_bwd",
    )(qkv, qkv, qkv, padded, hot, probs, dmixed, *[g.array for g in grads])
    return list(outs[:4]) + [[Grad(a, b + 1, t) for a, (_, b, t) in zip(outs[4:], plan)]]


def body(
    features,
    w1_in,
    w1_out,
    gain_ffn1,
    w_qkv,
    w_attn_out,
    rel_table,
    gain_attn,
    w_conv_in,
    w_depth,
    gain_depth,
    w_conv_out,
    gain_conv,
    w2_in,
    w2_out,
    gain_ffn2,
    gain_final,
    cotangent,
):
    local_frames, clip_count, width = features.shape
    rows = local_frames * clip_count
    f32, bf = jnp.float32, jnp.bfloat16
    s0 = features.reshape(rows, width)
    seed = cotangent.reshape(rows, width)
    vec = lambda g: g.astype(f32).reshape(1, width)
    g1, ga, gc, g2, gf = vec(gain_ffn1), vec(gain_attn), vec(gain_conv), vec(gain_ffn2), vec(gain_final)
    flat_qkv = w_qkv.reshape(width, -1)
    flat_conv = w_conv_in.reshape(width, -1)
    units = w1_in.shape[1]
    dp_count = lax.axis_size("dp")
    done = dp_count.bit_length() - 1
    pending = lambda items: [g for g in items if g.bit < done]
    chans = w_conv_out.shape[0]

    def swish_out(h, extra, outs):
        act, slope = silu_pair(h)
        outs[0][...] = act.astype(bf)
        outs[1][...] = slope.astype(bf)

    def plain_out(h, extra, outs):
        outs[0][...] = h.astype(outs[0].dtype)

    def glu_out(h, extra, outs):
        p0 = h[:, :chans]
        sig = jax.nn.sigmoid(h[:, chans:])
        glu = p0 * sig
        outs[0][...] = glu
        outs[1][...] = sig.astype(bf)
        outs[2][...] = (glu * (1.0 - sig)).astype(bf)

    def slope_out(h, extra, outs):
        outs[0][...] = (h * extra[0][...].astype(f32)).astype(bf)

    def first(branch, ins, vecs, outs, sums):
        return (unit_norm(ins[0].astype(f32))[0] * vecs[0]).astype(bf)

    def forward(scale):
        def run(branch, ins, vecs, outs, sums):
            fresh = ins[0].astype(f32) + scale * branch
            outs[0][...] = fresh
            sums[0][...] += fold8(branch * branch)
            return (unit_norm(fresh)[0] * vecs[0]).astype(bf)
        return run

    def turn(branch, ins, vecs, outs, sums):
        fresh = ins[0] + 0.5 * branch
        sums[0][...] += fold8(branch * branch)
        sums[1][...] += fold8(fresh * fresh)
        unit, inverse = unit_norm(fresh)
        outs[0][...] = unit * vecs[0]
        grad = ins[1].astype(f32)
        scaled = grad * vecs[0]
        mean_one = jnp.mean(scaled, -1, keepdims=True)
        mean_two = jnp.mean(scaled * unit, -1, keepdims=True)
        sums[2][...] += fold8(grad * unit)
        back = inverse * (scaled - mean_one - unit * mean_two)
        outs[1][...] = back
        return (0.5 * back).astype(bf)

    def backward(scale):
        def run(branch, ins, vecs, outs, sums):
            pull, grad_gain = norm_pull(branch, ins[1].astype(f32), vecs[0])
            fresh = ins[0] + pull
            outs[0][...] = fresh
            sums[0][...] += grad_gain
            return (scale * fresh).astype(bf)
        return run

    a1, act1, slope1, _ = stage(
        "ffn1_in", 0, rows, width, dp_count, enter=(w1_in, False, swish_out, (), ((units, bf), (units, bf))),
        junction=first, row_in=(s0,), vec_in=(g1,),
    )
    a2, qkv, s1, sq1, _ = stage(
        "ffn1_out", 1, rows, width, dp_count, leave=(act1, w1_out, False),
        enter=(flat_qkv, False, plain_out, (), ((flat_qkv.shape[1], bf),)),
        junction=forward(0.5), row_in=(s0,), vec_in=(ga,), row_out=(f32,), sums=1,
    )
    ext, hot, padded = rel_tables(rel_table)
    mixed, probs = attn_fwd(qkv, ext)
    a3, glu, sig, tail, s2, sq2, _ = stage(
        "attn_out", 2, rows, width, dp_count, leave=(mixed, w_attn_out, False),
        enter=(flat_conv, False, glu_out, (), ((chans, f32), (chans, bf), (chans, bf))),
        junction=forward(1.0), row_in=(s1,), vec_in=(gc,), row_out=(f32,), sums=1,
    )
    frames = glu.shape[0]
    taps = w_depth.astype(f32)
    tap_count = taps.shape[0]
    padded_glu = jnp.pad(glu, ((tap_count - 1, 0), (0, 0)))
    depth = jnp.zeros_like(glu)
    for k in range(tap_count):
        depth = depth + taps[k] * padded_glu[k : k + frames]
    average = lax.psum(jnp.sum(depth, -1, keepdims=True), "mp") / width
    centred = depth - average
    spread = lax.psum(jnp.sum(centred * centred, -1, keepdims=True), "mp") / width
    depth_inverse = lax.rsqrt(spread + epsilon)
    depth_unit = centred * depth_inverse
    depth_gain = gain_depth.astype(f32)
    act3, slope3 = silu_pair(depth_unit * depth_gain)
    act3 = act3.astype(bf)
    a4, act2, slope2, s3, sq3, _ = stage(
        "conv_out", 3, rows, width, dp_count, leave=(act3, w_conv_out, False),
        enter=(w2_in, False, swish_out, (), ((units, bf), (units, bf))),
        junction=forward(1.0), row_in=(s2,), vec_in=(g2,), row_out=(f32,), sums=1,
    )
    db4, dh2, output, grad4, sq4, sq5, dgf, _ = stage(
        "ffn2_out", 4, rows, width, dp_count, leave=(act2, w2_out, False),
        enter=(w2_out, True, slope_out, (slope2,), ((units, bf),)),
        junction=turn, row_in=(s3, seed), vec_in=(gf,), row_out=(f32, f32), sums=3,
    )
    db3, de3, grad3, dg2, (gw2_in, gw2_out) = stage(
        "ffn2_back", 5, rows, width, dp_count, leave=(dh2, w2_in, True),
        enter=(w_conv_out, True, plain_out, (), ((chans, f32),)), dws=((a4, dh2, "join", False), (db4, act2, "far", True)),
        junction=backward(1.0), row_in=(grad4, s3), vec_in=(g2,), row_out=(f32,), sums=1,
    )
    grad_gated = de3 * slope3
    grad_gain_depth = jnp.sum(grad_gated * depth_unit, 0)
    grad_unit = grad_gated * depth_gain
    first_sum, second_sum = lax.psum(
        (jnp.sum(grad_unit, -1, keepdims=True), jnp.sum(grad_unit * depth_unit, -1, keepdims=True)), "mp"
    )
    grad_depth = depth_inverse * (grad_unit - first_sum / width - depth_unit * second_sum / width)
    padded_grad = jnp.pad(grad_depth, ((0, tap_count - 1), (0, 0)))
    grad_glu = jnp.zeros_like(grad_depth)
    tap_grads = []
    for k in range(tap_count):
        start = tap_count - 1 - k
        grad_glu = grad_glu + taps[k] * padded_grad[start : start + frames]
        tap_grads.append(jnp.sum(grad_depth * padded_glu[k : k + frames], 0))
    grad_w_depth = jnp.stack(tap_grads, 0)
    dpaired = jnp.concatenate([grad_glu * sig.astype(f32), grad_glu * tail.astype(f32)], 1).astype(bf)
    db2, dmixed, grad2, dgc, (gconv_in, gconv_out, gw2_in, gw2_out) = stage(
        "conv_back", 6, rows, width, dp_count, leave=(dpaired, flat_conv, True),
        enter=(w_attn_out, True, plain_out, (), ((w_attn_out.shape[0], bf),)), dws=((a3, dpaired, "join", False), (db3, act3, "join", True)), grads=(gw2_in, gw2_out),
        junction=backward(1.0), row_in=(grad3, s2), vec_in=(gc,), row_out=(f32,), sums=1,
    )
    dq, dk, dv, dt, (gconv_in, gconv_out, gw2_in, gw2_out) = attn_bwd(
        qkv, padded, hot, probs, dmixed, [gconv_in, gconv_out, gw2_in, gw2_out], 9
    )
    dqkv = jnp.concatenate([dq, dk, dv], 1)
    db1, dh1, grad1, dga, (gqkv, gattn, gconv_in, gconv_out, gw2_in) = stage(
        "attn_back", 7, rows, width, dp_count, leave=(dqkv, flat_qkv, True),
        enter=(w1_out, True, slope_out, (slope1,), ((units, bf),)), dws=((a2, dqkv, "far", False), (db2, mixed, "far", True)), grads=(gconv_in, gconv_out, gw2_in),
        junction=backward(0.5), row_in=(grad2, s1), vec_in=(ga,), row_out=(f32,), sums=1,
    )
    early = [gqkv, gattn, gconv_in, gconv_out, gw2_in, gw2_out]
    waiting = pending(early)
    grad0, dg1, ends, small_rows, table, taps_end = stage(
        "ffn1_back", 8, rows, width, dp_count, leave=(dh1, w1_in, True),
        dws=((db1, act1, "far", True), (a1, dh1, "near", False)), grads=waiting,
        small=[dga, dgc, dg2, dgf, sq1, sq2, sq3, sq4, sq5, dt, grad_w_depth, grad_gain_depth[None]],
        junction=backward(1.0), row_in=(grad1, s0), vec_in=(g1,), row_out=(f32,), sums=1,
    )
    gw1_out, gw1_in = ends[:2]
    for item, end in zip(waiting, ends[2:]):
        item.array = end.array

    def finish(item):
        flip = item.turned and item.array.shape[0] * dp_count == width and (width // dp_count) % 128 != 0
        return item.array.T if flip else item.array

    rel = rel_table.shape[0]
    table_sum = table[:rel, :HEAD] + table[:rel, HEAD:]
    depth_sum, depth_gain_sum = taps_end[:-1], taps_end[-1]
    total_squares = jnp.sum(small_rows[5:10], -1)
    token_total = rows * lax.axis_size("mp") * lax.axis_size("dp")
    rms_stats = jnp.sqrt(total_squares / (token_total * width))
    whole = lambda x: x.reshape(local_frames, clip_count, width)
    return (
        whole(output),
        whole(grad0),
        finish(gw1_in),
        finish(gw1_out),
        small_rows[0],
        finish(gqkv).reshape(-1, 3, w_qkv.shape[2]),
        finish(gattn),
        table_sum,
        small_rows[1],
        finish(gconv_in).reshape(-1, 2, chans),
        depth_sum,
        depth_gain_sum,
        finish(gconv_out),
        small_rows[2],
        finish(gw2_in),
        finish(gw2_out),
        small_rows[3],
        small_rows[4],
        rms_stats,
    )


def solution(mesh):
    return jax.shard_map(
        body,
        mesh=mesh,
        in_specs=(
            P("mp", "dp", None),
            P(None, "mp"),
            P("mp", None),
            P(),
            P(None, None, "mp"),
            P("mp", None),
            P(),
            P(),
            P(None, None, "mp"),
            P(None, "mp"),
            P("mp"),
            P("mp", None),
            P(),
            P(None, "mp"),
            P("mp", None),
            P(),
            P(),
            P("mp", "dp", None),
        ),
        out_specs=(
            P("mp", "dp", None),
            P("mp", "dp", None),
            P("dp", "mp"),
            P("mp", "dp"),
            P(),
            P("dp", None, "mp"),
            P("mp", "dp"),
            P(),
            P(),
            P("dp", None, "mp"),
            P(None, "mp"),
            P("mp"),
            P("mp", "dp"),
            P(),
            P("dp", "mp"),
            P("mp", "dp"),
            P(),
            P(),
            P(),
        ),
        check_vma=False,
    )
```

```python
import functools

import jax
import jax.numpy as jnp
from jax import lax
from jax.experimental import pallas as pl
from jax.experimental.pallas import tpu as pltpu
from jax.sharding import PartitionSpec as P

HEAD = 64
REL_LEFT = 64
REL_RIGHT = 8
BQ = 128
WIN = 4 * BQ


epsilon = 1e-05


def nt(a, b):
    return lax.dot_general(a, b, (((1,), (1,)), ((), ())), preferred_element_type=jnp.float32)
def nn(a, b):
    return lax.dot_general(a, b, (((1,), (0,)), ((), ())), preferred_element_type=jnp.float32)
def tn(a, b):
    return lax.dot_general(a, b, (((0,), (0,)), ((), ())), preferred_element_type=jnp.float32)

MESH = pl.DeviceIdType.MESH
CHUNKS = 4
PIECE = 256
VMEM_LIMIT = 58 << 20


def silu_pair(h):
    sig = jax.nn.sigmoid(h)
    act = h * sig
    return act, sig + act * (1.0 - sig)


def unit_norm(s):
    centred = s - jnp.mean(s, -1, keepdims=True)
    inverse = lax.rsqrt(jnp.mean(centred * centred, -1, keepdims=True) + epsilon)
    return centred * inverse, inverse


def fold8(x):
    return jnp.sum(x.reshape(x.shape[0] // 8, 8, x.shape[1]), 0)


def norm_pull(grad, s, gain):
    unit, inverse = unit_norm(s)
    scaled = grad * gain
    first = jnp.mean(scaled, -1, keepdims=True)
    second = jnp.mean(scaled * unit, -1, keepdims=True)
    return inverse * (scaled - first - unit * second), fold8(grad * unit)


def in_hbm():
    return pl.BlockSpec(memory_space=pltpu.HBM)


class Grad:
    def __init__(self, array, bit, turned):
        self.array, self.bit, self.turned = array, bit, turned


def halved(shape, turned):
    pieces, pairs, _, block, cols = shape
    if pairs > 1:
        return jax.ShapeDtypeStruct((pieces, pairs // 2, 2, block, cols), jnp.bfloat16)
    if turned and block % 128 == 0:
        return jax.ShapeDtypeStruct((pieces * cols, block), jnp.float32)
    return jax.ShapeDtypeStruct((block, pieces * cols), jnp.float32)


def arriving(shape):
    return pltpu.VMEM((shape[0], shape[1]) + tuple(shape[3:]), jnp.bfloat16)


def place(dp, bit):
    own = (dp // 2**bit) % 2
    return own, dp + 2**bit * (1 - 2 * own)


def halving_copy(src, landing, piece, bit, send, recv, slot):
    dp, mp = lax.axis_index("dp"), lax.axis_index("mp")
    own, partner = place(dp, bit)
    return pltpu.make_async_remote_copy(
        src.at[piece, :, 1 - own], landing.at[piece], send.at[slot], recv.at[slot],
        device_id=(partner, mp), device_id_type=MESH,
    )


def halving_keep(src, kept, bit, sem):
    own, _ = place(lax.axis_index("dp"), bit)
    return pltpu.make_async_copy(src.at[:, :, own], kept, sem)


def region(ref, piece, cols, turned):
    if len(ref.shape) > 2:
        return ref.at[piece]
    at = pl.ds(piece * cols, cols)
    return ref.at[at, :] if turned else ref.at[:, at]


def halving_add(held, landing, out, piece, turned):
    pairs, block, cols = landing.shape[1:]
    f32 = jnp.float32
    if pairs == 1:
        total = held(piece, 0).astype(f32) + landing[piece, 0].astype(f32)
        turned = turned and block % 128 == 0
        region(out, piece, cols, turned)[...] = total.T if turned else total
        return

    def add(j, c):
        total = held(piece, j).astype(f32) + landing[piece, j].astype(f32)
        out[piece, j // 2, j % 2] = total.astype(jnp.bfloat16)
        return c

    lax.fori_loop(0, pairs, add, 0)


def greet(targets):
    barrier = pltpu.get_barrier_semaphore()
    for to in targets:
        pl.semaphore_signal(barrier, inc=1, device_id=to, device_id_type=MESH)
    return lambda: pl.semaphore_wait(barrier, len(targets))


def stage(name, cid, rows, width, count, gains, *, leave=None, enter=None, dws=(), grads=(), small=None, junction, row_in=(), row_out=(), sums=0):
    chunk = rows // CHUNKS
    frames = rows * 4
    bits_all = count.bit_length() - 1
    last = small is not None
    f32, bf = jnp.float32, jnp.bfloat16
    ins, vm_ins, out_shape, scratch = [], [], [], []
    known = {}

    def add_in(array, direct=False):
        if direct:
            ins.append(array)
            vm_ins.append(None)
            return len(ins) - 1
        if id(array) not in known:
            known[id(array)] = len(ins)
            ins.append(array)
            vm_ins.append(pltpu.VMEM(array.shape, array.dtype))
        return known[id(array)]

    out_slots = [0]

    def add_out(shape, dtype, slots):
        out_shape.append(jax.ShapeDtypeStruct(shape, dtype))
        first = out_slots[0]
        out_slots[0] += slots
        return len(out_shape) - 1, first

    def add_scratch(item):
        scratch.append(item)
        return len(scratch) - 1

    if leave:
        x_i, wl_i = add_in(leave[0]), add_in(leave[1])
        leave_s = [add_scratch(pltpu.VMEM((rows, width), f32)) for _ in range(2)]
        leave_s += [add_scratch(pltpu.VMEM((rows, width), bf)) for _ in range(6)]
        wl_s = add_scratch(pltpu.VMEM(leave[1].shape[::-1], bf)) if leave[2] else None
    dw_in = [(add_in(d[0]), add_in(d[1])) for d in dws if d[2] != "join"]
    gains_i = add_in(gains)
    row_i = [add_in(r) for r in row_in]
    dw_join = [(add_in(d[0]), add_in(d[1])) for d in dws if d[2] == "join"]
    if enter:
        we_i = add_in(enter[0])
        extra_i = [add_in(e) for e in enter[3]]
        we_s = add_scratch(pltpu.VMEM(enter[0].shape[::-1], bf)) if enter[1] else None
        all_o = add_out((frames, width), bf, 4 * CHUNKS)
        e_o = [add_out((frames, c), d, 4 * CHUNKS) for c, d in enter[4]]
    r_o = [add_out((rows, width), d, CHUNKS) for d in row_out]
    s_o = [add_out((8, width), f32, 1) for _ in range(sums)]
    fixed_out = len(out_shape)
    plan, join_o = [], []
    for lhs, rhs, where, turned, deep in dws:
        shape = (rhs.shape[1] // PIECE, count // 2, 2, width // count, PIECE)
        if where == "join":
            join_o.append(add_out(shape, bf, shape[0]))
        else:
            plan.append((shape, 0, turned, bits_all if last else min(deep, bits_all), add_scratch(pltpu.VMEM(shape, bf)), None, None))
    first_grad = len(plan)
    for g in grads:
        shape = g.array.shape
        plan.append((shape, g.bit, g.turned, bits_all if last else g.bit + 1, None, add_in(g.array, True), add_scratch(arriving(shape))))
    chains = []
    slots = 0
    for shape, bit, turned, end, src_s, src_i, keep_s in plan:
        links = []
        pieces = shape[0]
        for b in range(bit, end):
            nxt = halved(shape, turned)
            final = b == end - 1
            land_s = add_scratch(arriving(shape))
            if final:
                links.append((b, slots, land_s, None, add_out(nxt.shape, nxt.dtype, pieces)))
            else:
                links.append((b, slots, land_s, add_scratch(pltpu.VMEM(nxt.shape, nxt.dtype)), None))
            slots += pieces
            shape = nxt.shape
        chains.append((pieces, turned, src_s, src_i, keep_s, links))
    if last:
        small_i = [add_in(s) for s in small]
        small_shapes = [(16, width), small[-2].shape, small[-1].shape]
        small_o = [add_out(s, f32, 1) for s in small_shapes]
        hops = bits_all + 2
        land_small = [add_scratch(pltpu.VMEM((hops,) + s, f32)) for s in small_shapes]
        small_sems = [add_scratch(pltpu.SemaphoreType.DMA((3, hops))) for _ in range(2)]
    if slots:
        grad_sems = [add_scratch(pltpu.SemaphoreType.DMA((slots,))) for _ in range(2)]
    ring_sems = [add_scratch(pltpu.SemaphoreType.DMA((6, CHUNKS))) for _ in range(2)]
    load_sem = add_scratch(pltpu.SemaphoreType.DMA((len(ins),)))
    store_sem = add_scratch(pltpu.SemaphoreType.DMA((out_slots[0],)))
    n_in, n_out, n_scratch = len(ins), len(out_shape), len(scratch)
    vm_at = {}
    for i, item in enumerate(vm_ins):
        if item is not None:
            vm_at[i] = add_scratch(item)
    vo_at = [add_scratch(pltpu.VMEM(o.shape, o.dtype)) for o in out_shape]

    def kernel(*refs):
        hbm_in, hbm_out, t = refs[:n_in], refs[n_in : n_in + n_out], refs[n_in + n_out :]
        vin = lambda i: t[vm_at[i]]
        vout = lambda i: t[vo_at[i]]
        load = lambda i: pltpu.make_async_copy(hbm_in[i], vin(i), t[load_sem].at[i])
        waited = set()

        def need(*items):
            for i in items:
                if i not in waited:
                    waited.add(i)
                    load(i).wait()

        dp, me = lax.axis_index("dp"), lax.axis_index("mp")
        core, chip = me % 2, me // 2
        sib = chip * 2 + 1 - core
        far = (1 - chip) * 2 + core
        diag = (1 - chip) * 2 + 1 - core
        bits = sorted({link[0] for ch in chains for link in ch[5]})
        meet = greet([(dp, sib), (dp, far)] + [(place(dp, b)[1], me) for b in bits])
        for i in range(n_in):
            if i in vm_at:
                load(i).start()

        def part(ref, block, k):
            return ref.at[pl.ds(pl.multiple_of(block * rows + k * chunk, chunk), chunk)]

        def store_rows(o, block, k):
            i, first = o
            return pltpu.make_async_copy(part(vout(i), block, k), part(hbm_out[i], block, k), t[store_sem].at[first + block * CHUNKS + k])

        def store_whole(o):
            i, first = o
            return pltpu.make_async_copy(vout(i), hbm_out[i], t[store_sem].at[first])

        def store_piece(o, piece, cols, turned):
            i, first = o
            return pltpu.make_async_copy(
                region(vout(i), piece, cols, turned), region(hbm_out[i], piece, cols, turned), t[store_sem].at[first + piece]
            )

        def copy(kind, k, src, dst, to):
            return pltpu.make_async_remote_copy(
                src, dst, t[ring_sems[0]].at[kind, k], t[ring_sems[1]].at[kind, k], device_id=(dp, to), device_id_type=MESH
            )

        if leave:
            px, own, sb, sr, xs, xr, ob, orv = [t[s] for s in leave_s]
            x_ref = vin(x_i)
            wl_ref = t[wl_s] if leave[2] else vin(wl_i)
        if enter:
            all_ref = vout(all_o[0])
            we_ref = t[we_s] if enter[1] else vin(we_i)
        pair_send = lambda k: copy(0, k, part(sb, 0, k), part(sr, 0, k), sib)
        far_send = lambda k: copy(1, k, part(xs, 0, k), part(xr, 0, k), far)
        own_send = lambda k: copy(2, k, part(ob, 0, k), part(orv, 0, k), sib)
        all_far = lambda k: copy(3, k, part(all_ref, me, k), part(all_ref, me, k), far)
        all_sib = lambda k: copy(4, k, part(all_ref, me, k), part(all_ref, me, k), sib)
        all_fwd = lambda k: copy(5, k, part(all_ref, far, k), part(all_ref, far, k), sib)
        got_far = lambda k: copy(3, k, part(all_ref, far, k), part(all_ref, far, k), far)
        got_sib = lambda k: copy(4, k, part(all_ref, sib, k), part(all_ref, sib, k), sib)
        got_diag = lambda k: copy(5, k, part(all_ref, diag, k), part(all_ref, diag, k), sib)

        def source(c, step):
            pieces, turned, src_s, src_i, keep_s, links = chains[c]
            if step:
                return t[links[step - 1][3]]
            return t[src_s] if src_s is not None else hbm_in[src_i]

        def hop(c, step, piece):
            b, slot, land_s, _, _ = chains[c][5][step]
            return halving_copy(source(c, step), t[land_s], piece, b, t[grad_sems[0]], t[grad_sems[1]], slot + piece)

        def keep(c):
            return halving_keep(hbm_in[chains[c][3]], t[chains[c][4]], chains[c][5][0][0], t[load_sem].at[chains[c][3]])

        kept = set()

        def settle(c, step, piece):
            pieces, turned, src_s, src_i, keep_s, links = chains[c]
            b, slot, land_s, out_s, out_o = links[step]
            hop(c, step, piece).wait_recv()
            if step == 0 and src_s is None:
                if c not in kept:
                    kept.add(c)
                    keep(c).wait()
                held = lambda p, j: t[keep_s][p, j]
            else:
                own_bit, _ = place(dp, b)
                src = source(c, step)
                held = lambda p, j: src[p, j, own_bit]
            landing = t[land_s]
            out = t[out_s] if out_o is None else vout(out_o[0])
            halving_add(held, landing, out, piece, turned)
            if out_o is not None:
                store_piece(out_o, piece, PIECE, turned and landing.shape[2] % 128 == 0).start()

        for c in range(first_grad, len(chains)):
            keep(c).start()
        meet()
        for c in range(first_grad, len(chains)):
            for p in range(chains[c][0]):
                hop(c, 0, p).start()
        for o in s_o:
            vout(o[0])[...] = jnp.zeros((8, width), f32)

        def fill(k, where):
            n_far, n_join = 0, 0
            for lhs, rhs, at_loop, turned, deep in dws:
                if at_loop == "join":
                    (a, b), o, c = dw_join[n_join], join_o[n_join], None
                    n_join += 1
                else:
                    (a, b), c = dw_in[n_far], n_far
                    n_far += 1
                if at_loop != where:
                    continue
                dw = vout(o[0]) if c is None else t[chains[c][2]]

                @pl.when(k < dw.shape[0])
                def _(a=a, b=b, dw=dw, c=c, o=o if c is None else None):
                    g = tn(vin(a)[...], vin(b)[:, pl.ds(pl.multiple_of(k * PIECE, PIECE), PIECE)])
                    dw[k] = g.astype(bf).reshape(dw.shape[1:])
                    if c is None:
                        store_piece(o, k, PIECE, False).start()
                    else:
                        hop(c, 0, k).start()

        if leave:
            need(x_i, wl_i)
            if leave[2]:
                wl_ref[...] = vin(wl_i)[...].T
            for a, b in dw_in:
                need(a, b)

            def two(k, block_a, block_b):
                lhs = jnp.concatenate([part(x_ref, block_a, k)[...], part(x_ref, block_b, k)[...]], 0)
                return nn(lhs, wl_ref[...])

            def push(k):
                pair_send(k).wait_recv()
                part(xs, 0, k)[...] = (part(px, 0, k)[...] + part(sr, 0, k)[...].astype(f32)).astype(bf)
                far_send(k).start()

            def out_far(k, c):
                p = two(k, far, diag)
                part(px, 0, k)[...] = p[:chunk]
                part(sb, 0, k)[...] = p[chunk:].astype(bf)
                pair_send(k).start()

                @pl.when(k > 0)
                def _():
                    push(k - 1)

                fill(k, "far")
                return c

            lax.fori_loop(0, CHUNKS, out_far, 0)

            def out_near(k, c):
                p = two(k, me, sib)
                part(own, 0, k)[...] = p[:chunk]
                part(ob, 0, k)[...] = p[chunk:].astype(bf)
                own_send(k).start()

                @pl.when(k == 0)
                def _():
                    push(CHUNKS - 1)

                fill(k, "near")
                return c

            lax.fori_loop(0, CHUNKS, out_near, 0)
        need(gains_i, *row_i)
        for a, b in dw_join:
            need(a, b)
        if enter and enter[1]:
            need(we_i)
            we_ref[...] = vin(we_i)[...].T

        def join(k, c):
            fill(k, "join")
            branch = None
            if leave:
                own_send(k).wait_recv()
                far_send(k).wait_recv()
                branch = part(own, 0, k)[...] + part(orv, 0, k)[...].astype(f32) + part(xr, 0, k)[...].astype(f32)
            fresh = junction(
                branch, [part(vin(r), 0, k)[...] for r in row_i], vin(gains_i), [part(vout(o[0]), 0, k) for o in r_o], [vout(o[0]) for o in s_o]
            )
            if enter:
                part(all_ref, me, k)[...] = fresh
                all_far(k).start()
                all_sib(k).start()
            for o in r_o:
                store_rows(o, 0, k).start()
            return c

        lax.fori_loop(0, CHUNKS, join, 0)
        for o in s_o:
            store_whole(o).start()

        lead = [c for c in range(first_grad) if len(chains[c][5]) == 2] if enter else []
        if enter:
            need(we_i, *extra_i)

            def work(k, block_a, block_b):
                lhs = jnp.concatenate([part(all_ref, block_a, k)[...], part(all_ref, block_b, k)[...]], 0)
                h = nn(lhs, we_ref[...])
                for i, block in enumerate((block_a, block_b)):
                    view = lambda ref: part(ref, block, k)
                    enter[2](h[i * chunk : (i + 1) * chunk], [view(vin(r))[...] for r in extra_i], [view(vout(o[0])) for o in e_o])
                    for o in [all_o] + e_o:
                        store_rows(o, block, k).start()

            def gather(k, c):
                got_sib(k).wait_recv()
                work(k, me, sib)
                got_far(k).wait_recv()
                all_fwd(k).start()
                got_diag(k).wait_recv()
                work(k, far, diag)
                if lead:

                    @pl.when(k == CHUNKS - 2)
                    def _():
                        for ch in lead:
                            for p in range(chains[ch][0]):
                                settle(ch, 0, p)
                                hop(ch, 1, p).start()

                return c

            lax.fori_loop(0, CHUNKS, gather, 0)

        if last:
            need(*small_i)
            *vectors, table, taps = [vin(i) for i in small_i]
            rows_ref, table_ref, taps_ref = [vout(o[0]) for o in small_o]
            rows_ref[...] = jnp.zeros(rows_ref.shape, f32)
            for i, v in enumerate([vout(s_o[0][0])] + vectors):
                rows_ref[i : i + 1, :] = jnp.sum(v[...], 0, keepdims=True)
            table_ref[...] = table[...]
            taps_ref[...] = taps[...]
            course = ["sib", "far"] + list(range(bits_all - 1, -1, -1))

            def double(n):
                at = course[n]
                to = (dp, sib) if at == "sib" else (dp, far) if at == "far" else (place(dp, at)[1], me)
                return [
                    (
                        pltpu.make_async_remote_copy(
                            r, t[l].at[n], t[small_sems[0]].at[i, n], t[small_sems[1]].at[i, n], device_id=to, device_id_type=MESH
                        ),
                        r,
                        t[l].at[n],
                    )
                    for i, (r, l) in enumerate(zip((rows_ref, table_ref, taps_ref), land_small))
                    if i < 2 or n > 1
                ]

            def finish_double(n):
                for cp, r, l in double(n):
                    cp.wait()
                    r[...] += l[...]

            for cp, _, _ in double(0):
                cp.start()

        pieces = [(c, p) for c in range(len(chains)) for p in range(chains[c][0])]
        order = [x for x in pieces if x[0] >= first_grad] + [x for x in pieces if x[0] < first_grad]
        depth = lambda c: len(chains[c][5])
        begin = lambda c: 1 if c in lead else 0
        deepest = max([depth(c) - begin(c) for c in range(len(chains))] + [0])
        total_slots = max(len(order) + deepest - 1, len(course) if last else 0)
        for slot in range(total_slots):
            if last:
                for n in range(len(course) - 1):
                    if slot == (n if n < 2 else min(3 * n - 3, total_slots - 1)):
                        finish_double(n)
                        for cp, _, _ in double(n + 1):
                            cp.start()
            for s in reversed(range(deepest)):
                if 0 <= slot - s < len(order):
                    c, p = order[slot - s]
                    step = s + begin(c)
                    if step < depth(c):
                        settle(c, step, p)
                        if step + 1 < depth(c):
                            hop(c, step + 1, p).start()
        if last:
            finish_double(len(course) - 1)
            for o in small_o:
                store_whole(o).start()
        for c in range(len(chains)):
            for s in range(depth(c)):
                for p in range(chains[c][0]):
                    hop(c, s, p).wait_send()
            out_o = chains[c][5][-1][4]
            block = chains[c][5][-1][2]
            for p in range(chains[c][0]):
                store_piece(out_o, p, PIECE, chains[c][1] and t[block].shape[2] % 128 == 0).wait()

        def drain(k, c):
            if leave:
                pair_send(k).wait_send()
                far_send(k).wait_send()
                own_send(k).wait_send()
            if enter:
                all_far(k).wait_send()
                all_sib(k).wait_send()
                all_fwd(k).wait_send()
                for block in range(4):
                    for o in [all_o] + e_o:
                        store_rows(o, block, k).wait()
            for o in r_o:
                store_rows(o, 0, k).wait()
            return c

        lax.fori_loop(0, CHUNKS, drain, 0)
        for o in s_o + (small_o if last else []):
            store_whole(o).wait()
        for o in join_o:
            for p in range(out_shape[o[0]].shape[0]):
                store_piece(o, p, PIECE, False).wait()

    flops = 0
    if leave:
        flops += 2 * frames * leave[0].shape[1] * width
    if enter:
        flops += 2 * frames * width * sum(c for c, _ in enter[4])
    flops += sum(2 * frames * d[0].shape[1] * d[1].shape[1] for d in dws)
    outs = pl.pallas_call(
        kernel,
        in_specs=[in_hbm()] * n_in,
        out_specs=[in_hbm()] * n_out,
        out_shape=out_shape,
        scratch_shapes=scratch,
        compiler_params=pltpu.CompilerParams(collective_id=cid, has_side_effects=True, vmem_limit_bytes=VMEM_LIMIT),
        cost_estimate=pl.CostEstimate(flops=flops, bytes_accessed=60_000_000, transcendentals=0),
        name=name,
    )(*ins)
    fixed, rest = list(outs[:fixed_out]), list(outs[fixed_out:])
    fresh = [Grad(rest.pop(0), 0, d[3]) for d in dws if d[2] == "join"]
    for item in plan:
        fresh.append(Grad(rest.pop(0), item[3], item[2]))
    return fixed + [fresh] + rest


def publish(arrays, thirds):
    out_shape, scratch = [], []
    for i, a in enumerate(arrays):
        if i in thirds:
            shape = (a.shape[0], thirds[i], a.shape[1] // thirds[i])
            scratch += [pltpu.VMEM(a.shape, a.dtype), pltpu.VMEM(shape, a.dtype)]
            out_shape.append(jax.ShapeDtypeStruct(shape, a.dtype))
        else:
            out_shape.append(jax.ShapeDtypeStruct(a.shape, a.dtype))
    scratch.append(pltpu.SemaphoreType.DMA((2, len(arrays))))

    def kernel(*refs):
        n = len(arrays)
        src, dst, sem = refs[:n], refs[n : 2 * n], refs[-1]
        bufs = list(refs[2 * n : -1])
        first, second = [], []
        for i in range(n):
            if i in thirds:
                flat, split = bufs.pop(0), bufs.pop(0)
                first.append((pltpu.make_async_copy(src[i], flat, sem.at[0, i]), flat, split, i))
            else:
                second.append(pltpu.make_async_copy(src[i], dst[i], sem.at[1, i]))
        for cp in [x[0] for x in first] + second:
            cp.start()
        for cp, flat, split, i in first:
            cp.wait()
            cols = split.shape[2]
            for j in range(split.shape[1]):
                split[:, j, :] = flat[:, j * cols : (j + 1) * cols]
            second.append(pltpu.make_async_copy(split, dst[i], sem.at[1, i]))
            second[-1].start()
        for cp in second:
            cp.wait()

    return pl.pallas_call(
        kernel,
        in_specs=[in_hbm()] * len(arrays),
        out_specs=[in_hbm()] * len(arrays),
        out_shape=out_shape,
        scratch_shapes=scratch,
        compiler_params=pltpu.CompilerParams(vmem_limit_bytes=VMEM_LIMIT),
        name="publish",
    )(*arrays)


SPAN = 128


def exchange(stats, landing, send, recv):
    dp, me = lax.axis_index("dp"), lax.axis_index("mp")
    core, chip = me % 2, me // 2
    others = [chip * 2 + 1 - core, (1 - chip) * 2 + core, (1 - chip) * 2 + 1 - core]
    return [
        pltpu.make_async_remote_copy(
            stats, landing.at[i], send.at[i], recv.at[i], device_id=(dp, to), device_id_type=MESH
        )
        for i, to in enumerate(others)
    ]


def group_targets():
    dp, me = lax.axis_index("dp"), lax.axis_index("mp")
    core, chip = me % 2, me // 2
    return [(dp, chip * 2 + 1 - core), (dp, (1 - chip) * 2 + core), (dp, (1 - chip) * 2 + 1 - core)]


def to_rows(first, second):
    lane = lax.broadcasted_iota(jnp.int32, (SPAN, SPAN), 1)
    both = jnp.where(lane == 0, first, jnp.where(lane == 1, second, 0.0))
    return both.T[:8]


def to_columns(rows8):
    return jnp.concatenate([rows8, jnp.zeros((SPAN - 8, SPAN), jnp.float32)], 0).T


def shifted(window, by):
    return window if by == 0 else pltpu.roll(window, window.shape[0] - by, 0)


def conv_mid(glu, w_depth, gain_depth, width, cid):
    frames, chans = glu.shape
    taps = w_depth.shape[0]
    reach = taps - 1
    edge = (reach + 7) // 8 * 8
    f32, bf = jnp.float32, jnp.bfloat16
    tiles, lanes = frames // SPAN, chans // 128

    def kernel(glu_h, w_h, g_h, act_h, slope_h, unit_h, stat_h, pad, w_v, g_v, act, slope, unit, stat, sendbuf, landing, lsem, ssem, send, recv):
        meet = greet(group_targets())
        loads = [
            pltpu.make_async_copy(glu_h, pad.at[pl.ds(edge, frames)], lsem.at[0]),
            pltpu.make_async_copy(w_h, w_v, lsem.at[1]),
            pltpu.make_async_copy(g_h, g_v, lsem.at[2]),
        ]
        for cp in loads:
            cp.start()
        pad[:edge, :] = jnp.zeros((edge, chans), f32)
        for cp in loads:
            cp.wait()

        def tile(i, c):
            at = pl.multiple_of(i * SPAN, SPAN)
            for lane in range(lanes):
                cols = slice(lane * 128, (lane + 1) * 128)
                window = pad[pl.ds(at, SPAN + edge), cols]
                total = jnp.zeros((SPAN, 128), f32)
                for by in range(8):
                    moved = shifted(window, by)
                    for base in range(0, edge + 1, 8):
                        tap = base + by - (edge - reach)
                        if 0 <= tap < taps:
                            total = total + w_v[tap : tap + 1, cols] * moved[base : base + SPAN]
                unit[pl.ds(at, SPAN), cols] = total
            depth = unit[pl.ds(at, SPAN), :]
            mean = jnp.mean(depth, -1, keepdims=True)
            centred = depth - mean
            sendbuf[:, pl.ds(at, SPAN)] = to_rows(mean, jnp.sum(centred * centred, -1, keepdims=True))
            return c

        lax.fori_loop(0, tiles, tile, 0)
        meet()
        copies = exchange(sendbuf, landing, send, recv)
        for cp in copies:
            cp.start()
        for cp in copies:
            cp.wait_recv()
        rows = [sendbuf[...]] + [landing[i] for i in range(3)]
        mean = sum(r[0:1] for r in rows) * 0.25
        spread = sum(r[1:2] + chans * (r[0:1] - mean) * (r[0:1] - mean) for r in rows) / width
        inverse = lax.rsqrt(spread + epsilon)
        row = lax.broadcasted_iota(jnp.int32, (8, frames), 0)
        stat[...] = jnp.where(row == 0, mean, jnp.where(row == 1, inverse, 0.0))
        outs = [(act, act_h), (slope, slope_h), (unit, unit_h)]

        def store(i, n):
            at = pl.ds(pl.multiple_of(i * SPAN, SPAN), SPAN)
            return pltpu.make_async_copy(outs[n][0].at[at], outs[n][1].at[at], ssem.at[n, i])

        def finish(i, c):
            at = pl.multiple_of(i * SPAN, SPAN)
            cols = to_columns(stat[:, pl.ds(at, SPAN)])
            u = (unit[pl.ds(at, SPAN), :] - cols[:, 0:1]) * cols[:, 1:2]
            a, s = silu_pair(u * g_v[...])
            unit[pl.ds(at, SPAN), :] = u
            act[pl.ds(at, SPAN), :] = a.astype(bf)
            slope[pl.ds(at, SPAN), :] = s.astype(bf)
            for n in range(3):
                store(i, n).start()
            return c

        lax.fori_loop(0, tiles, finish, 0)
        last = pltpu.make_async_copy(stat, stat_h, lsem.at[0])
        last.start()
        for cp in copies:
            cp.wait_send()
        for i in range(tiles):
            for n in range(3):
                store(i, n).wait()
        last.wait()

    S = jax.ShapeDtypeStruct
    out_shape = [S((frames, chans), bf), S((frames, chans), bf), S((frames, chans), f32), S((8, frames), f32)]
    vm = pltpu.VMEM
    return pl.pallas_call(
        kernel,
        in_specs=[in_hbm()] * 3,
        out_specs=[in_hbm()] * 4,
        out_shape=out_shape,
        scratch_shapes=[
            vm((frames + edge, chans), f32), vm(w_depth.shape, f32), vm((1, chans), f32),
            vm((frames, chans), bf), vm((frames, chans), bf), vm((frames, chans), f32), vm((8, frames), f32),
            vm((8, frames), f32), vm((3, 8, frames), f32),
            pltpu.SemaphoreType.DMA((3,)), pltpu.SemaphoreType.DMA((3, tiles)), pltpu.SemaphoreType.DMA((3,)), pltpu.SemaphoreType.DMA((3,)),
        ],
        compiler_params=pltpu.CompilerParams(collective_id=cid, has_side_effects=True, vmem_limit_bytes=VMEM_LIMIT),
        name="conv_mid",
    )(glu, w_depth, gain_depth)


def conv_mid_back(grad, slope, unit, stat, glu, sig, tail, w_depth, gain_depth, width, cid):
    frames, chans = glu.shape
    taps = w_depth.shape[0]
    reach = taps - 1
    edge = (reach + 7) // 8 * 8
    f32, bf = jnp.float32, jnp.bfloat16
    tiles, lanes = frames // SPAN, chans // 128
    ins = [grad, slope, unit, stat, w_depth, gain_depth, glu, sig, tail]

    def kernel(*refs):
        hbm, (pair_h, taps_h) = refs[:9], refs[9:11]
        (grad_v, slope_v, unit_v, stat_v, w_v, g_v, pad, sig_v, tail_v, back, pair, taps_v, acc, gacc, sendbuf, landing, lsem, ssem, send, recv) = refs[11:]
        meet = greet(group_targets())
        dst = [grad_v, slope_v, unit_v, stat_v, w_v, g_v, pad.at[pl.ds(edge, frames)], sig_v, tail_v]
        loads = [pltpu.make_async_copy(h, d, lsem.at[i]) for i, (h, d) in enumerate(zip(hbm, dst))]
        for cp in loads:
            cp.start()
        pad[:edge, :] = jnp.zeros((edge, chans), f32)
        back[frames:, :] = jnp.zeros((edge, chans), f32)
        acc[...] = jnp.zeros_like(acc)
        gacc[...] = jnp.zeros_like(gacc)
        for cp in loads[:6]:
            cp.wait()

        def first(i, c):
            at = pl.ds(pl.multiple_of(i * SPAN, SPAN), SPAN)
            u = unit_v[at, :]
            de = grad_v[at, :] * slope_v[at, :].astype(f32)
            gacc[...] += fold8(de * u)
            du = de * g_v[...]
            back[at, :] = du
            sendbuf[:, at] = to_rows(jnp.sum(du, -1, keepdims=True), jnp.sum(du * u, -1, keepdims=True))
            return c

        lax.fori_loop(0, tiles, first, 0)
        meet()
        copies = exchange(sendbuf, landing, send, recv)
        for cp in copies:
            cp.start()
        for cp in loads[6:]:
            cp.wait()
        for cp in copies:
            cp.wait_recv()
        means = (sendbuf[...] + landing[0] + landing[1] + landing[2]) / width
        row = lax.broadcasted_iota(jnp.int32, (8, frames), 0)
        stat_v[...] = jnp.where(row == 1, stat_v[...], jnp.where(row == 0, means[0:1], jnp.where(row == 2, means[1:2], 0.0)))

        def second(i, c):
            at = pl.ds(pl.multiple_of(i * SPAN, SPAN), SPAN)
            cols = to_columns(stat_v[:, at])
            back[at, :] = cols[:, 1:2] * (back[at, :] - cols[:, 0:1] - unit_v[at, :] * cols[:, 2:3])
            return c

        lax.fori_loop(0, tiles, second, 0)

        def store(i):
            at = pl.ds(pl.multiple_of(i * SPAN, SPAN), SPAN)
            return pltpu.make_async_copy(pair.at[at], pair_h.at[at], ssem.at[i])

        def third(i, c):
            at = pl.multiple_of(i * SPAN, SPAN)
            rows = pl.ds(at, SPAN)
            for lane in range(lanes):
                cols = slice(lane * 128, (lane + 1) * 128)
                ahead = back[pl.ds(at, SPAN + edge), cols]
                total = jnp.zeros((SPAN, 128), f32)
                for by in range(8):
                    moved = shifted(ahead, by)
                    for base in range(0, edge, 8):
                        tap = reach - (base + by)
                        if 0 <= tap < taps:
                            total = total + w_v[tap : tap + 1, cols] * moved[base : base + SPAN]
                pair[rows, cols] = (total * sig_v[rows, cols].astype(f32)).astype(bf)
                pair[rows, chans + lane * 128 : chans + (lane + 1) * 128] = (total * tail_v[rows, cols].astype(f32)).astype(bf)
            store(i).start()
            for lane in range(lanes):
                cols = slice(lane * 128, (lane + 1) * 128)
                here = back[rows, cols]
                window = pad[pl.ds(at, SPAN + edge), cols]
                for by in range(8):
                    moved = shifted(window, by)
                    for base in range(0, edge + 1, 8):
                        tap = base + by - (edge - reach)
                        if 0 <= tap < taps:
                            acc[tap * 8 : tap * 8 + 8, cols] += fold8(here * moved[base : base + SPAN])
            return c

        lax.fori_loop(0, tiles, third, 0)
        for tap in range(taps):
            taps_v[tap : tap + 1, :] = jnp.sum(acc[tap * 8 : tap * 8 + 8, :], 0, keepdims=True)
        taps_v[taps : taps + 1, :] = jnp.sum(gacc[...], 0, keepdims=True)
        last = pltpu.make_async_copy(taps_v, taps_h, lsem.at[0])
        last.start()
        for cp in copies:
            cp.wait_send()
        for i in range(tiles):
            store(i).wait()
        last.wait()

    S = jax.ShapeDtypeStruct
    vm = pltpu.VMEM
    return pl.pallas_call(
        kernel,
        in_specs=[in_hbm()] * 9,
        out_specs=[in_hbm()] * 2,
        out_shape=[S((frames, 2 * chans), bf), S((taps + 1, chans), f32)],
        scratch_shapes=[
            vm((frames, chans), f32), vm((frames, chans), bf), vm((frames, chans), f32), vm((8, frames), f32),
            vm(w_depth.shape, f32), vm((1, chans), f32), vm((frames + edge, chans), f32), vm((frames, chans), bf), vm((frames, chans), bf),
            vm((frames + edge, chans), f32), vm((frames, 2 * chans), bf), vm((taps + 1, chans), f32), vm((taps * 8, chans), f32), vm((8, chans), f32),
            vm((8, frames), f32), vm((3, 8, frames), f32),
            pltpu.SemaphoreType.DMA((9,)), pltpu.SemaphoreType.DMA((tiles,)), pltpu.SemaphoreType.DMA((3,)), pltpu.SemaphoreType.DMA((3,)),
        ],
        compiler_params=pltpu.CompilerParams(collective_id=cid, has_side_effects=True, vmem_limit_bytes=VMEM_LIMIT),
        name="conv_mid_back",
    )(*ins)


def split_pair(x):
    left = lax.broadcasted_iota(jnp.int32, x.shape, 1) < HEAD
    zero = jnp.zeros_like(x)
    return jnp.concatenate([jnp.where(left, x, zero), jnp.where(left, zero, x)], 0)

def join_pair(x):
    rows = x.shape[0] // 2
    left = lax.broadcasted_iota(jnp.int32, (rows, x.shape[1]), 1) < HEAD
    return jnp.where(left, x[:rows], x[rows:])

def fwd_kernel(q_ref, k_ref, v_ref, rel_ref, mixed_ref, probs_ref, bias_ref):
    ib = pl.program_id(1)
    qs = split_pair(q_ref[...] * 0.125)
    s = nt(qs, k_ref[...])
    b = nt(qs, rel_ref[...])
    rows = b.shape[0] // 2
    bias_ref[:, 0:BQ] = b[:, 3 * BQ : 4 * BQ]
    for h in range(2):
        r = pltpu.roll(b[h * rows : (h + 1) * rows, :WIN], 0, 1, stride=1, stride_axis=0)
        bias_ref[h * rows : (h + 1) * rows, BQ : 4 * BQ] = r[:, : 3 * BQ]
    bias_ref[:, 4 * BQ :] = b[:, 4 * BQ :]
    nkeys = s.shape[1] // BQ
    parts = []
    for jb in range(nkeys):
        at = pl.multiple_of(jnp.clip(jb - ib + 2, 0, 4) * BQ, BQ)
        parts.append(s[:, jb * BQ : (jb + 1) * BQ] + bias_ref[:, pl.ds(at, BQ)])
    top = functools.reduce(jnp.maximum, parts)
    m = jnp.max(top, -1, keepdims=True)
    es = [jnp.exp(p - m) for p in parts]
    tot = jnp.sum(functools.reduce(jnp.add, es), -1, keepdims=True)
    inv = 1.0 / tot
    for jb in range(nkeys):
        probs_ref[0, :, jb * BQ : (jb + 1) * BQ] = (es[jb] * inv).astype(jnp.bfloat16)
    mixed_ref[...] = join_pair(nn(probs_ref[0], v_ref[...])).astype(jnp.bfloat16)

def bwd_kernel(plan, *refs):
    n = len(plan)
    pairs_in, refs = refs[7 : 7 + n], refs[:7] + refs[7 + n :]
    q_ref, k_ref, v_ref, relb_ref, hot_ref, probs_ref, do_ref, dq_ref, dk_ref, dv_ref, dt_ref = refs[:11]
    grads_out, refs = refs[11 : 11 + n], refs[11 + n :]
    tot_ref, dkt, dvt, dta, dz_ref = refs[:5]
    landings, keeps, halves, sems = refs[5 : 5 + n], refs[5 + n : 5 + 2 * n], refs[5 + 2 * n : 5 + 3 * n], refs[5 + 3 * n :]
    pr, ib, nb = pl.program_id(0), pl.program_id(1), pl.num_programs(1)
    dp, mp = lax.axis_index("dp"), lax.axis_index("mp")
    hops, holds, slot = [], [], 0
    for i, ((pieces, bit, turned), src, landing, keep, half, out) in enumerate(zip(plan, pairs_in, landings, keeps, halves, grads_out)):
        holds.append(halving_keep(src, keep, bit, sems[2].at[i]))
        flip = turned and landing.shape[2] % 128 == 0
        for p in range(pieces):
            move = halving_copy(src, landing, p, bit, sems[0], sems[1], slot)
            store = pltpu.make_async_copy(region(half, p, PIECE, flip), region(out, p, PIECE, flip), sems[3].at[slot])
            hops.append((move, store, lambda q, j, keep=keep: keep[q, j], landing, half, p, turned))
            slot += 1

    if hops:

        @pl.when((ib == 0) & (pr == 0))
        def _():
            meet = greet([(place(dp, b)[1], mp) for b in sorted({x[1] for x in plan})])
            for hold in holds:
                hold.start()
            meet()
            for hop in hops:
                hop[0].start()

    @pl.when(ib == 0)
    def _():
        dkt[...] = jnp.zeros_like(dkt)
        dvt[...] = jnp.zeros_like(dvt)
    @pl.when((ib == 0) & (pr == 0))
    def _():
        dta[...] = jnp.zeros_like(dta)
    qs = split_pair(q_ref[...] * 0.125)
    dos = split_pair(do_ref[...])
    p = probs_ref[0]
    dp = nt(dos, v_ref[...])
    nkeys = dp.shape[1] // BQ
    dvt[...] += tn(dos, p)
    pf = p.astype(jnp.float32)
    acc = None
    for jb in range(nkeys):
        sl = slice(jb * BQ, (jb + 1) * BQ)
        t = pf[:, sl] * dp[:, sl]
        acc = t if acc is None else acc + t
    inner = jnp.sum(acc, -1, keepdims=True)
    tot_ref[...] = jnp.zeros_like(tot_ref)
    for jb in range(nkeys):
        sl = slice(jb * BQ, (jb + 1) * BQ)
        dz = (pf[:, sl] * (dp[:, sl] - inner)).astype(jnp.bfloat16)
        dz_ref[:, sl] = dz
        at = pl.multiple_of(jnp.clip(jb - ib + 2, 0, 4) * BQ, BQ)
        tot_ref[:, pl.ds(at, BQ)] += dz.astype(jnp.float32)
    rows = BQ
    r2 = lax.broadcasted_iota(jnp.int32, (2 * rows, 2 * rows), 0)
    c2 = lax.broadcasted_iota(jnp.int32, (2 * rows, 2 * rows), 1)
    mirror = (r2 + c2 == jnp.where(r2 < rows, rows - 1, 3 * rows - 1)).astype(jnp.bfloat16)
    w = jnp.concatenate([tot_ref[:, BQ : 4 * BQ].astype(jnp.bfloat16), jnp.zeros((2 * rows, BQ), jnp.bfloat16)], 1)
    w = nn(mirror, w)
    outs = [pltpu.roll(w[h * rows : (h + 1) * rows], WIN - rows + 1, 1, stride=1, stride_axis=0) for h in range(2)]
    d = nn(mirror, jnp.concatenate(outs, 0).astype(jnp.bfloat16)).astype(jnp.bfloat16)
    drel = nn(d, hot_ref[...])
    col = lax.broadcasted_iota(jnp.int32, drel.shape, 1)
    low = jnp.sum(tot_ref[:, :BQ], -1, keepdims=True)
    high = jnp.sum(tot_ref[:, 4 * BQ :], -1, keepdims=True)
    drel = drel + jnp.where(col == 0, low, 0.0) + jnp.where(col == REL_LEFT + REL_RIGHT, high, 0.0)
    drel = drel.astype(jnp.bfloat16)
    dz = dz_ref[...]
    dq = nn(dz, k_ref[...]) + nn(drel, relb_ref[...])
    dq_ref[...] = (join_pair(dq) * 0.125).astype(jnp.bfloat16)
    dkt[...] += tn(qs, dz)
    dta[...] += tn(drel, qs)
    @pl.when(ib == nb - 1)
    def _():
        dk_ref[...] = dkt[...].T.astype(jnp.bfloat16)
        dv_ref[...] = dvt[...].T.astype(jnp.bfloat16)
        dt_ref[...] = dta[...]

    if hops:

        @pl.when((ib == nb - 1) & (pr == pl.num_programs(0) - 1))
        def _():
            for hold in holds:
                hold.wait()
            for hop in hops:
                hop[0].wait_recv()
                halving_add(*hop[2:])
                hop[1].start()
            for hop in hops:
                hop[0].wait_send()
                hop[1].wait()

def rel_tables(rel_table):
    spots = jnp.arange(5 * BQ)
    idx = jnp.where(spots < 3 * BQ, jnp.clip(spots - REL_LEFT, 0, REL_LEFT + REL_RIGHT), jnp.where(spots < 4 * BQ, 0, REL_LEFT + REL_RIGHT))
    hot = (jnp.arange(BQ)[None, :] == idx[:, None]).astype(jnp.bfloat16)
    padded = jnp.pad(rel_table, ((0, BQ - rel_table.shape[0]), (0, 0)))
    padded = jnp.concatenate([padded, padded], 1)
    ext = jnp.dot(hot, padded, preferred_element_type=jnp.float32).astype(jnp.bfloat16)
    return ext, hot[:WIN], padded

def attn_fwd(qkv, ext):
    frames, cols = qkv.shape
    pairs = cols // 3 // 128
    nb = frames // BQ
    bf = jnp.bfloat16
    return pl.pallas_call(
        fwd_kernel,
        grid=(pairs, nb),
        in_specs=[
            pl.BlockSpec((BQ, 128), lambda p, i: (i, p)),
            pl.BlockSpec((frames, 128), lambda p, i: (0, pairs + p)),
            pl.BlockSpec((frames, 128), lambda p, i: (0, 2 * pairs + p)),
            pl.BlockSpec(ext.shape, lambda p, i: (0, 0)),
        ],
        out_specs=[
            pl.BlockSpec((BQ, 128), lambda p, i: (i, p)),
            pl.BlockSpec((1, 2 * BQ, frames), lambda p, i: (p, i, 0)),
        ],
        out_shape=[jax.ShapeDtypeStruct((frames, cols // 3), bf), jax.ShapeDtypeStruct((pairs, 2 * frames, frames), bf)],
        scratch_shapes=[pltpu.VMEM((2 * BQ, 5 * BQ), jnp.float32)],
        compiler_params=pltpu.CompilerParams(vmem_limit_bytes=VMEM_LIMIT),
        name="attn_fwd",
    )(qkv, qkv, qkv, ext)

def attn_bwd(qkv, padded, hot, probs, dmixed, grads, cid):
    frames, cols = qkv.shape
    pairs = cols // 3 // 128
    nb = frames // BQ
    bf = jnp.bfloat16
    blk = pl.BlockSpec((BQ, 128), lambda p, i: (i, p))
    full = pl.BlockSpec((frames, 128), lambda p, i: (0, p))
    plan = [(g.array.shape[0], g.bit, g.turned) for g in grads]
    after = [halved(g.array.shape, g.turned) for g in grads]
    slots = sum(x[0] for x in plan)
    outs = pl.pallas_call(
        functools.partial(bwd_kernel, plan),
        grid=(pairs, nb),
        in_specs=[
            blk,
            pl.BlockSpec((frames, 128), lambda p, i: (0, pairs + p)),
            pl.BlockSpec((frames, 128), lambda p, i: (0, 2 * pairs + p)),
            pl.BlockSpec(padded.shape, lambda p, i: (0, 0)),
            pl.BlockSpec(hot.shape, lambda p, i: (0, 0)),
            pl.BlockSpec((1, 2 * BQ, frames), lambda p, i: (p, i, 0)),
            blk,
        ]
        + [in_hbm()] * len(grads),
        out_specs=[blk, full, full, pl.BlockSpec((128, 128), lambda p, i: (0, 0))] + [in_hbm()] * len(after),
        out_shape=[jax.ShapeDtypeStruct((frames, cols // 3), bf)] * 3 + [jax.ShapeDtypeStruct((128, 128), jnp.float32)] + after,
        scratch_shapes=[pltpu.VMEM((2 * BQ, 5 * BQ), jnp.float32), pltpu.VMEM((128, frames), jnp.float32), pltpu.VMEM((128, frames), jnp.float32),
                        pltpu.VMEM((128, 128), jnp.float32), pltpu.VMEM((2 * BQ, frames), bf)]
        + [arriving(g.array.shape) for g in grads]
        + [arriving(g.array.shape) for g in grads]
        + [pltpu.VMEM(a.shape, a.dtype) for a in after]
        + ([pltpu.SemaphoreType.DMA((slots,))] * 2 + [pltpu.SemaphoreType.DMA((len(grads),)), pltpu.SemaphoreType.DMA((slots,))] if grads else []),
        compiler_params=pltpu.CompilerParams(
            vmem_limit_bytes=VMEM_LIMIT, collective_id=cid, has_side_effects=True
        ),
        cost_estimate=pl.CostEstimate(flops=20 * frames * frames * 128 * pairs, bytes_accessed=20_000_000, transcendentals=0),
        name="attn_bwd",
    )(qkv, qkv, qkv, padded, hot, probs, dmixed, *[g.array for g in grads])
    return list(outs[:4]) + [[Grad(a, b + 1, t) for a, (_, b, t) in zip(outs[4:], plan)]]


def body(
    features,
    w1_in,
    w1_out,
    gain_ffn1,
    w_qkv,
    w_attn_out,
    rel_table,
    gain_attn,
    w_conv_in,
    w_depth,
    gain_depth,
    w_conv_out,
    gain_conv,
    w2_in,
    w2_out,
    gain_ffn2,
    gain_final,
    cotangent,
):
    local_frames, clip_count, width = features.shape
    rows = local_frames * clip_count
    f32, bf = jnp.float32, jnp.bfloat16
    s0 = features.reshape(rows, width)
    seed = cotangent.reshape(rows, width)
    gains = jnp.stack([gain_ffn1, gain_attn, gain_conv, gain_ffn2, gain_final] + [gain_final] * 3).astype(f32)
    flat_qkv = w_qkv.reshape(width, -1)
    flat_conv = w_conv_in.reshape(width, -1)
    units = w1_in.shape[1]
    dp_count = lax.axis_size("dp")
    done = dp_count.bit_length() - 1
    pending = lambda items: [g for g in items if g.bit < done]
    chans = w_conv_out.shape[0]

    def swish_out(h, extra, outs):
        act, slope = silu_pair(h)
        outs[0][...] = act.astype(bf)
        outs[1][...] = slope.astype(bf)

    def plain_out(h, extra, outs):
        outs[0][...] = h.astype(outs[0].dtype)

    def glu_out(h, extra, outs):
        p0 = h[:, :chans]
        sig = jax.nn.sigmoid(h[:, chans:])
        glu = p0 * sig
        outs[0][...] = glu
        outs[1][...] = sig.astype(bf)
        outs[2][...] = (glu * (1.0 - sig)).astype(bf)

    def slope_out(h, extra, outs):
        outs[0][...] = (h * extra[0][...].astype(f32)).astype(bf)

    def first(branch, ins, gains, outs, sums):
        return (unit_norm(ins[0].astype(f32))[0] * gains[0:1, :]).astype(bf)

    def forward(scale, row):
        def run(branch, ins, gains, outs, sums):
            fresh = ins[0].astype(f32) + scale * branch
            outs[0][...] = fresh
            sums[0][...] += fold8(branch * branch)
            return (unit_norm(fresh)[0] * gains[row : row + 1, :]).astype(bf)
        return run

    def turn(branch, ins, gains, outs, sums):
        fresh = ins[0] + 0.5 * branch
        sums[0][...] += fold8(branch * branch)
        sums[1][...] += fold8(fresh * fresh)
        unit, inverse = unit_norm(fresh)
        outs[0][...] = unit * gains[4:5, :]
        grad = ins[1].astype(f32)
        scaled = grad * gains[4:5, :]
        mean_one = jnp.mean(scaled, -1, keepdims=True)
        mean_two = jnp.mean(scaled * unit, -1, keepdims=True)
        sums[2][...] += fold8(grad * unit)
        back = inverse * (scaled - mean_one - unit * mean_two)
        outs[1][...] = back
        return (0.5 * back).astype(bf)

    def backward(scale, row):
        def run(branch, ins, gains, outs, sums):
            pull, grad_gain = norm_pull(branch, ins[1].astype(f32), gains[row : row + 1, :])
            fresh = ins[0] + pull
            outs[0][...] = fresh
            sums[0][...] += grad_gain
            return (scale * fresh).astype(bf)
        return run

    a1, act1, slope1, _ = stage(
        "ffn1_in", 0, rows, width, dp_count, gains, enter=(w1_in, False, swish_out, (), ((units, bf), (units, bf))),
        junction=first, row_in=(s0,),
    )
    a2, qkv, s1, sq1, _ = stage(
        "ffn1_out", 1, rows, width, dp_count, gains, leave=(act1, w1_out, False),
        enter=(flat_qkv, False, plain_out, (), ((flat_qkv.shape[1], bf),)),
        junction=forward(0.5, 1), row_in=(s0,), row_out=(f32,), sums=1,
    )
    ext, hot, padded = rel_tables(rel_table)
    mixed, probs = attn_fwd(qkv, ext)
    a3, glu, sig, tail, s2, sq2, _ = stage(
        "attn_out", 2, rows, width, dp_count, gains, leave=(mixed, w_attn_out, False),
        enter=(flat_conv, False, glu_out, (), ((chans, f32), (chans, bf), (chans, bf))),
        junction=forward(1.0, 2), row_in=(s1,), row_out=(f32,), sums=1,
    )
    depth_taps = w_depth.astype(f32)
    depth_gain = gain_depth.astype(f32)[None]
    act3, slope3, depth_unit, depth_stat = conv_mid(glu, depth_taps, depth_gain, width, 10)
    a4, act2, slope2, s3, sq3, _ = stage(
        "conv_out", 3, rows, width, dp_count, gains, leave=(act3, w_conv_out, False),
        enter=(w2_in, False, swish_out, (), ((units, bf), (units, bf))),
        junction=forward(1.0, 3), row_in=(s2,), row_out=(f32,), sums=1,
    )
    db4, dh2, output, grad4, sq4, sq5, dgf, _ = stage(
        "ffn2_out", 4, rows, width, dp_count, gains, leave=(act2, w2_out, False),
        enter=(w2_out, True, slope_out, (slope2,), ((units, bf),)),
        junction=turn, row_in=(s3, seed), row_out=(f32, f32), sums=3,
    )
    db3, de3, grad3, dg2, (gw2_in, gw2_out) = stage(
        "ffn2_back", 5, rows, width, dp_count, gains, leave=(dh2, w2_in, True),
        enter=(w_conv_out, True, plain_out, (), ((chans, f32),)), dws=((a4, dh2, "join", False, 0), (db4, act2, "far", True, 1)),
        junction=backward(1.0, 3), row_in=(grad4, s3), row_out=(f32,), sums=1,
    )
    dpaired, tap_sums = conv_mid_back(de3, slope3, depth_unit, depth_stat, glu, sig, tail, depth_taps, depth_gain, width, 11)
    db2, dmixed, grad2, dgc, (gconv_in, gconv_out, gw2_in, gw2_out) = stage(
        "conv_back", 6, rows, width, dp_count, gains, leave=(dpaired, flat_conv, True),
        enter=(w_attn_out, True, plain_out, (), ((w_attn_out.shape[0], bf),)), dws=((a3, dpaired, "join", False, 0), (db3, act3, "join", True, 0)), grads=(gw2_in, gw2_out),
        junction=backward(1.0, 2), row_in=(grad3, s2), row_out=(f32,), sums=1,
    )
    dq, dk, dv, dt, (gconv_in, gconv_out, gw2_in, gw2_out) = attn_bwd(
        qkv, padded, hot, probs, dmixed, [gconv_in, gconv_out, gw2_in, gw2_out], 9
    )
    dqkv = jnp.concatenate([dq, dk, dv], 1)
    db1, dh1, grad1, dga, (gqkv, gattn, gconv_in, gconv_out, gw2_in) = stage(
        "attn_back", 7, rows, width, dp_count, gains, leave=(dqkv, flat_qkv, True),
        enter=(w1_out, True, slope_out, (slope1,), ((units, bf),)), dws=((a2, dqkv, "far", False, 1), (db2, mixed, "far", True, 1)), grads=(gconv_in, gconv_out, gw2_in),
        junction=backward(0.5, 1), row_in=(grad2, s1), row_out=(f32,), sums=1,
    )
    early = [gqkv, gattn, gconv_in, gconv_out, gw2_in, gw2_out]
    waiting = pending(early)
    grad0, dg1, ends, small_rows, table, taps_end = stage(
        "ffn1_back", 8, rows, width, dp_count, gains, leave=(dh1, w1_in, True),
        dws=((db1, act1, "far", True, 1), (a1, dh1, "near", False, 1)), grads=waiting,
        small=[dga, dgc, dg2, dgf, sq1, sq2, sq3, sq4, sq5, dt, tap_sums],
        junction=backward(1.0, 0), row_in=(grad1, s0), row_out=(f32,), sums=1,
    )
    gw1_out, gw1_in = ends[:2]
    for item, end in zip(waiting, ends[2:]):
        item.array = end.array

    def finish(item):
        flip = item.turned and item.array.shape[0] * dp_count == width and (width // dp_count) % 128 != 0
        return item.array.T if flip else item.array

    ends = [output, grad0] + [finish(g) for g in (gw1_in, gw1_out, gqkv, gattn, gconv_in, gconv_out, gw2_in, gw2_out)]
    ends = publish(ends + [small_rows, table, taps_end], {0: 1, 1: 1, 4: 3, 6: 2})
    small_rows, table, taps_end = ends[10:]
    rel = rel_table.shape[0]
    table_sum = table[:rel, :HEAD] + table[:rel, HEAD:]
    depth_sum, depth_gain_sum = taps_end[:-1], taps_end[-1]
    total_squares = jnp.sum(small_rows[5:10], -1)
    token_total = rows * lax.axis_size("mp") * lax.axis_size("dp")
    rms_stats = jnp.sqrt(total_squares / (token_total * width))
    whole = lambda x: x.reshape(local_frames, clip_count, width)
    return (
        whole(ends[0]),
        whole(ends[1]),
        ends[2],
        ends[3],
        small_rows[0],
        ends[4],
        ends[5],
        table_sum,
        small_rows[1],
        ends[6],
        depth_sum,
        depth_gain_sum,
        ends[7],
        small_rows[2],
        ends[8],
        ends[9],
        small_rows[3],
        small_rows[4],
        rms_stats,
    )


def solution(mesh):
    return jax.shard_map(
        body,
        mesh=mesh,
        in_specs=(
            P("mp", "dp", None),
            P(None, "mp"),
            P("mp", None),
            P(),
            P(None, None, "mp"),
            P("mp", None),
            P(),
            P(),
            P(None, None, "mp"),
            P(None, "mp"),
            P("mp"),
            P("mp", None),
            P(),
            P(None, "mp"),
            P("mp", None),
            P(),
            P(),
            P("mp", "dp", None),
        ),
        out_specs=(
            P("mp", "dp", None),
            P("mp", "dp", None),
            P("dp", "mp"),
            P("mp", "dp"),
            P(),
            P("dp", None, "mp"),
            P("mp", "dp"),
            P(),
            P(),
            P("dp", None, "mp"),
            P(None, "mp"),
            P("mp"),
            P("mp", "dp"),
            P(),
            P("dp", "mp"),
            P("mp", "dp"),
            P(),
            P(),
            P(),
        ),
        check_vma=False,
    )
```

```python
import functools

import jax
import jax.numpy as jnp
from jax import lax
from jax.experimental import pallas as pl
from jax.experimental.pallas import tpu as pltpu
from jax.sharding import PartitionSpec as P

HEAD = 64
REL_LEFT = 64
REL_RIGHT = 8
BQ = 128
WIN = 4 * BQ


epsilon = 1e-05


def nt(a, b):
    return lax.dot_general(a, b, (((1,), (1,)), ((), ())), preferred_element_type=jnp.float32)
def nn(a, b):
    return lax.dot_general(a, b, (((1,), (0,)), ((), ())), preferred_element_type=jnp.float32)
def tn(a, b):
    return lax.dot_general(a, b, (((0,), (0,)), ((), ())), preferred_element_type=jnp.float32)

MESH = pl.DeviceIdType.MESH
CHUNKS = 4
PIECE = 256
VMEM_LIMIT = 58 << 20


def silu_pair(h):
    sig = jax.nn.sigmoid(h)
    act = h * sig
    return act, sig + act * (1.0 - sig)


def unit_norm(s):
    centred = s - jnp.mean(s, -1, keepdims=True)
    inverse = lax.rsqrt(jnp.mean(centred * centred, -1, keepdims=True) + epsilon)
    return centred * inverse, inverse


def fold8(x):
    return jnp.sum(x.reshape(x.shape[0] // 8, 8, x.shape[1]), 0)


def norm_pull(grad, s, gain):
    unit, inverse = unit_norm(s)
    scaled = grad * gain
    first = jnp.mean(scaled, -1, keepdims=True)
    second = jnp.mean(scaled * unit, -1, keepdims=True)
    return inverse * (scaled - first - unit * second), fold8(grad * unit)


def in_hbm():
    return pl.BlockSpec(memory_space=pltpu.HBM)


class Grad:
    def __init__(self, array, bit, turned):
        self.array, self.bit, self.turned = array, bit, turned


def halved(shape, turned):
    pieces, pairs, _, block, cols = shape
    if pairs > 1:
        return jax.ShapeDtypeStruct((pieces, pairs // 2, 2, block, cols), jnp.bfloat16)
    if turned and block % 128 == 0:
        return jax.ShapeDtypeStruct((pieces * cols, block), jnp.float32)
    return jax.ShapeDtypeStruct((block, pieces * cols), jnp.float32)


def arriving(shape):
    return pltpu.VMEM((shape[0], shape[1]) + tuple(shape[3:]), jnp.bfloat16)


def place(dp, bit):
    own = (dp // 2**bit) % 2
    return own, dp + 2**bit * (1 - 2 * own)


def halving_copy(src, landing, piece, bit, send, recv, slot):
    dp, mp = lax.axis_index("dp"), lax.axis_index("mp")
    own, partner = place(dp, bit)
    return pltpu.make_async_remote_copy(
        src.at[piece, :, 1 - own], landing.at[piece], send.at[slot], recv.at[slot],
        device_id=(partner, mp), device_id_type=MESH,
    )


def halving_keep(src, kept, bit, sem):
    own, _ = place(lax.axis_index("dp"), bit)
    return pltpu.make_async_copy(src.at[:, :, own], kept, sem)


def region(ref, piece, cols, turned):
    if len(ref.shape) > 2:
        return ref.at[piece]
    at = pl.ds(piece * cols, cols)
    return ref.at[at, :] if turned else ref.at[:, at]


def halving_add(held, landing, out, piece, turned):
    pairs, block, cols = landing.shape[1:]
    f32 = jnp.float32
    if pairs == 1:
        total = held(piece, 0).astype(f32) + landing[piece, 0].astype(f32)
        turned = turned and block % 128 == 0
        region(out, piece, cols, turned)[...] = total.T if turned else total
        return

    def add(j, c):
        total = held(piece, j).astype(f32) + landing[piece, j].astype(f32)
        out[piece, j // 2, j % 2] = total.astype(jnp.bfloat16)
        return c

    lax.fori_loop(0, pairs, add, 0)


def weight(lhs, rhs, where, turned, deep=1, lo=0, pieces=None):
    cols = sum(r.shape[1] for r in rhs) if isinstance(rhs, tuple) else rhs.shape[1]
    return lhs, rhs, where, turned, deep, lo, cols // PIECE if pieces is None else pieces


class Riders:
    def __init__(self, grads):
        self.plan = [(g.array.shape[0], g.bit, g.turned) for g in grads]
        self.arrays = [g.array for g in grads]
        self.after = [halved(g.array.shape, g.turned) for g in grads]
        self.slots = sum(x[0] for x in self.plan)
        self.scratch = [arriving(g.array.shape) for g in grads] * 2 + [pltpu.VMEM(a.shape, a.dtype) for a in self.after]
        if grads:
            self.scratch += [pltpu.SemaphoreType.DMA((self.slots,))] * 3 + [pltpu.SemaphoreType.DMA((len(grads),))]

    def bind(self, srcs, outs, scratch):
        n = len(self.plan)
        sems = scratch[3 * n :]
        holds, hops, slot = [], [], 0
        for i, (pieces, bit, turned) in enumerate(self.plan):
            landing, keep, half = scratch[i], scratch[n + i], scratch[2 * n + i]
            holds.append(halving_keep(srcs[i], keep, bit, sems[3].at[i]))
            flip = turned and landing.shape[2] % 128 == 0
            for p in range(pieces):
                move = halving_copy(srcs[i], landing, p, bit, sems[0], sems[1], slot)
                store = pltpu.make_async_copy(region(half, p, PIECE, flip), region(outs[i], p, PIECE, flip), sems[2].at[slot])
                hops.append((move, store, lambda q, j, keep=keep: keep[q, j], landing, half, p, turned))
                slot += 1
        self.holds, self.hops = holds, hops

    def targets(self):
        dp, mp = lax.axis_index("dp"), lax.axis_index("mp")
        return [(place(dp, b)[1], mp) for b in sorted({x[1] for x in self.plan})]

    def start(self):
        for hold in self.holds:
            hold.start()
        for hop in self.hops:
            hop[0].start()

    def finish(self):
        for hold in self.holds:
            hold.wait()
        for hop in self.hops:
            hop[0].wait_recv()
            halving_add(*hop[2:])
            hop[1].start()
        for hop in self.hops:
            hop[0].wait_send()
            hop[1].wait()

    def results(self, outs):
        return [Grad(a, b + 1, t) for a, (_, b, t) in zip(outs, self.plan)]


def greet(targets):
    barrier = pltpu.get_barrier_semaphore()
    for to in targets:
        pl.semaphore_signal(barrier, inc=1, device_id=to, device_id_type=MESH)
    return lambda: pl.semaphore_wait(barrier, len(targets))


def stage(name, cid, rows, width, count, gains, *, leave=None, enter=None, dws=(), grads=(), small=None, junction, row_in=(), row_out=(), sums=0):
    chunk = rows // CHUNKS
    frames = rows * 4
    bits_all = count.bit_length() - 1
    last = small is not None
    f32, bf = jnp.float32, jnp.bfloat16
    ins, vm_ins, out_shape, scratch = [], [], [], []
    known = {}

    def add_in(array, direct=False):
        if direct:
            ins.append(array)
            return len(ins) - 1
        if id(array) not in known:
            group = array if isinstance(array, tuple) else (array,)
            known[id(array)] = len(vm_ins)
            vm_ins.append((len(ins), len(group), pltpu.VMEM((group[0].shape[0], sum(a.shape[1] for a in group)), group[0].dtype)))
            ins.extend(group)
        return known[id(array)]

    out_slots = [0]

    def add_out(shape, dtype, slots):
        out_shape.append(jax.ShapeDtypeStruct(shape, dtype))
        first = out_slots[0]
        out_slots[0] += slots
        return len(out_shape) - 1, first

    def add_scratch(item):
        scratch.append(item)
        return len(scratch) - 1

    if leave:
        x_i, wl_i = add_in(leave[0]), add_in(leave[1])
        leave_s = [add_scratch(pltpu.VMEM((rows, width), f32)) for _ in range(2)]
        leave_s += [add_scratch(pltpu.VMEM((rows, width), bf)) for _ in range(6)]
        wl_s = add_scratch(pltpu.VMEM(leave[1].shape[::-1], bf)) if leave[2] else None
    dw_in = [(add_in(d[0]), add_in(d[1])) for d in dws if d[2] != "join"]
    gains_i = add_in(gains)
    row_i = [add_in(r) for r in row_in]
    dw_join = [(add_in(d[0]), add_in(d[1])) for d in dws if d[2] == "join"]
    if enter:
        we_i = add_in(enter[0])
        extra_i = [add_in(e) for e in enter[3]]
        we_s = add_scratch(pltpu.VMEM(enter[0].shape[::-1], bf)) if enter[1] else None
        all_o = add_out((frames, width), bf, 4 * CHUNKS)
        e_o = [add_out((frames, c), d, 4 * CHUNKS) for c, d in enter[4]]
    r_o = [add_out((rows, width), d, CHUNKS) for d in row_out]
    s_o = [add_out((8, width), f32, 1) for _ in range(sums)]
    fixed_out = len(out_shape)
    plan, join_o = [], []
    for lhs, rhs, where, turned, deep, lo, pieces in dws:
        shape = (pieces, count // 2, 2, width // count, PIECE)
        if where == "join":
            join_o.append(add_out(shape, bf, shape[0]))
        else:
            plan.append((shape, 0, turned, bits_all if last else min(deep, bits_all), add_scratch(pltpu.VMEM(shape, bf)), None, None))
    first_grad = len(plan)
    for g in grads:
        shape = g.array.shape
        plan.append((shape, g.bit, g.turned, bits_all if last else g.bit + 1, None, add_in(g.array, True), add_scratch(arriving(shape))))
    chains = []
    slots = 0
    for shape, bit, turned, end, src_s, src_i, keep_s in plan:
        links = []
        pieces = shape[0]
        for b in range(bit, end):
            nxt = halved(shape, turned)
            final = b == end - 1
            land_s = add_scratch(arriving(shape))
            if final:
                links.append((b, slots, land_s, None, add_out(nxt.shape, nxt.dtype, pieces)))
            else:
                links.append((b, slots, land_s, add_scratch(pltpu.VMEM(nxt.shape, nxt.dtype)), None))
            slots += pieces
            shape = nxt.shape
        chains.append((pieces, turned, src_s, src_i, keep_s, links))
    if last:
        small_i = [add_in(s) for s in small]
        small_shapes = [(16, width), small[-2].shape, small[-1].shape]
        small_o = [add_out(s, f32, 1) for s in small_shapes]
        hops = bits_all + 2
        land_small = [add_scratch(pltpu.VMEM((hops,) + s, f32)) for s in small_shapes]
        small_sems = [add_scratch(pltpu.SemaphoreType.DMA((3, hops))) for _ in range(2)]
    if slots:
        grad_sems = [add_scratch(pltpu.SemaphoreType.DMA((slots,))) for _ in range(2)]
    ring_sems = [add_scratch(pltpu.SemaphoreType.DMA((6, CHUNKS))) for _ in range(2)]
    load_sem = add_scratch(pltpu.SemaphoreType.DMA((len(ins),)))
    store_sem = add_scratch(pltpu.SemaphoreType.DMA((out_slots[0],)))
    n_in, n_out, n_scratch = len(ins), len(out_shape), len(scratch)
    vm_at = [add_scratch(item[2]) for item in vm_ins]
    vo_at = [add_scratch(pltpu.VMEM(o.shape, o.dtype)) for o in out_shape]

    def kernel(*refs):
        hbm_in, hbm_out, t = refs[:n_in], refs[n_in : n_in + n_out], refs[n_in + n_out :]
        vin = lambda i: t[vm_at[i]]
        vout = lambda i: t[vo_at[i]]
        waited = set()

        def load(i):
            first, parts, _ = vm_ins[i]
            if parts == 1:
                return [pltpu.make_async_copy(hbm_in[first], vin(i), t[load_sem].at[first])]
            copies, at = [], 0
            for n in range(first, first + parts):
                cols = hbm_in[n].shape[1]
                copies.append(pltpu.make_async_copy(hbm_in[n], vin(i).at[:, pl.ds(at, cols)], t[load_sem].at[n]))
                at += cols
            return copies

        def need(*items):
            for i in items:
                if i not in waited:
                    waited.add(i)
                    for cp in load(i):
                        cp.wait()

        dp, me = lax.axis_index("dp"), lax.axis_index("mp")
        core, chip = me % 2, me // 2
        sib = chip * 2 + 1 - core
        far = (1 - chip) * 2 + core
        diag = (1 - chip) * 2 + 1 - core
        bits = sorted({link[0] for ch in chains for link in ch[5]})
        meet = greet([(dp, sib), (dp, far)] + [(place(dp, b)[1], me) for b in bits])
        for i in range(len(vm_ins)):
            for cp in load(i):
                cp.start()

        def part(ref, block, k):
            return ref.at[pl.ds(pl.multiple_of(block * rows + k * chunk, chunk), chunk)]

        def store_rows(o, block, k):
            i, first = o
            return pltpu.make_async_copy(part(vout(i), block, k), part(hbm_out[i], block, k), t[store_sem].at[first + block * CHUNKS + k])

        def store_whole(o):
            i, first = o
            return pltpu.make_async_copy(vout(i), hbm_out[i], t[store_sem].at[first])

        def store_piece(o, piece, cols, turned):
            i, first = o
            return pltpu.make_async_copy(
                region(vout(i), piece, cols, turned), region(hbm_out[i], piece, cols, turned), t[store_sem].at[first + piece]
            )

        def copy(kind, k, src, dst, to):
            return pltpu.make_async_remote_copy(
                src, dst, t[ring_sems[0]].at[kind, k], t[ring_sems[1]].at[kind, k], device_id=(dp, to), device_id_type=MESH
            )

        if leave:
            px, own, sb, sr, xs, xr, ob, orv = [t[s] for s in leave_s]
            x_ref = vin(x_i)
            wl_ref = t[wl_s] if leave[2] else vin(wl_i)
        if enter:
            all_ref = vout(all_o[0])
            we_ref = t[we_s] if enter[1] else vin(we_i)
        pair_send = lambda k: copy(0, k, part(sb, 0, k), part(sr, 0, k), sib)
        far_send = lambda k: copy(1, k, part(xs, 0, k), part(xr, 0, k), far)
        own_send = lambda k: copy(2, k, part(ob, 0, k), part(orv, 0, k), sib)
        all_far = lambda k: copy(3, k, part(all_ref, me, k), part(all_ref, me, k), far)
        all_sib = lambda k: copy(4, k, part(all_ref, me, k), part(all_ref, me, k), sib)
        all_fwd = lambda k: copy(5, k, part(all_ref, far, k), part(all_ref, far, k), sib)
        got_far = lambda k: copy(3, k, part(all_ref, far, k), part(all_ref, far, k), far)
        got_sib = lambda k: copy(4, k, part(all_ref, sib, k), part(all_ref, sib, k), sib)
        got_diag = lambda k: copy(5, k, part(all_ref, diag, k), part(all_ref, diag, k), sib)

        def source(c, step):
            pieces, turned, src_s, src_i, keep_s, links = chains[c]
            if step:
                return t[links[step - 1][3]]
            return t[src_s] if src_s is not None else hbm_in[src_i]

        def hop(c, step, piece):
            b, slot, land_s, _, _ = chains[c][5][step]
            return halving_copy(source(c, step), t[land_s], piece, b, t[grad_sems[0]], t[grad_sems[1]], slot + piece)

        def keep(c):
            return halving_keep(hbm_in[chains[c][3]], t[chains[c][4]], chains[c][5][0][0], t[load_sem].at[chains[c][3]])

        kept = set()

        def settle(c, step, piece):
            pieces, turned, src_s, src_i, keep_s, links = chains[c]
            b, slot, land_s, out_s, out_o = links[step]
            hop(c, step, piece).wait_recv()
            if step == 0 and src_s is None:
                if c not in kept:
                    kept.add(c)
                    keep(c).wait()
                held = lambda p, j: t[keep_s][p, j]
            else:
                own_bit, _ = place(dp, b)
                src = source(c, step)
                held = lambda p, j: src[p, j, own_bit]
            landing = t[land_s]
            out = t[out_s] if out_o is None else vout(out_o[0])
            halving_add(held, landing, out, piece, turned)
            if out_o is not None:
                store_piece(out_o, piece, PIECE, turned and landing.shape[2] % 128 == 0).start()

        for c in range(first_grad, len(chains)):
            keep(c).start()
        meet()
        for c in range(first_grad, len(chains)):
            for p in range(chains[c][0]):
                hop(c, 0, p).start()
        for o in s_o:
            vout(o[0])[...] = jnp.zeros((8, width), f32)

        def fill(k, where):
            n_far, n_join = 0, 0
            for lhs, rhs, at_loop, turned, deep, lo, pieces in dws:
                if at_loop == "join":
                    (a, b), o, c = dw_join[n_join], join_o[n_join], None
                    n_join += 1
                else:
                    (a, b), c = dw_in[n_far], n_far
                    n_far += 1
                if at_loop != where:
                    continue
                dw = vout(o[0]) if c is None else t[chains[c][2]]

                @pl.when(k < dw.shape[0])
                def _(a=a, b=b, dw=dw, c=c, o=o if c is None else None, lo=lo):
                    g = tn(vin(a)[...], vin(b)[:, pl.ds(pl.multiple_of((lo + k) * PIECE, PIECE), PIECE)])
                    dw[k] = g.astype(bf).reshape(dw.shape[1:])
                    if c is None:
                        store_piece(o, k, PIECE, False).start()
                    else:
                        hop(c, 0, k).start()

        if leave:
            need(x_i, wl_i)
            if leave[2]:
                wl_ref[...] = vin(wl_i)[...].T
            for a, b in dw_in:
                need(a, b)

            def two(k, block_a, block_b):
                lhs = jnp.concatenate([part(x_ref, block_a, k)[...], part(x_ref, block_b, k)[...]], 0)
                return nn(lhs, wl_ref[...])

            def push(k):
                pair_send(k).wait_recv()
                part(xs, 0, k)[...] = (part(px, 0, k)[...] + part(sr, 0, k)[...].astype(f32)).astype(bf)
                far_send(k).start()

            def out_far(k, c):
                p = two(k, far, diag)
                part(px, 0, k)[...] = p[:chunk]
                part(sb, 0, k)[...] = p[chunk:].astype(bf)
                pair_send(k).start()

                @pl.when(k > 0)
                def _():
                    push(k - 1)

                fill(k, "far")
                return c

            lax.fori_loop(0, CHUNKS, out_far, 0)

            def out_near(k, c):
                p = two(k, me, sib)
                part(own, 0, k)[...] = p[:chunk]
                part(ob, 0, k)[...] = p[chunk:].astype(bf)
                own_send(k).start()

                @pl.when(k == 0)
                def _():
                    push(CHUNKS - 1)

                fill(k, "near")
                return c

            lax.fori_loop(0, CHUNKS, out_near, 0)
        need(gains_i, *row_i)
        for a, b in dw_join:
            need(a, b)
        if enter and enter[1]:
            need(we_i)
            we_ref[...] = vin(we_i)[...].T

        def join(k, c):
            fill(k, "join")
            branch = None
            if leave:
                own_send(k).wait_recv()
                far_send(k).wait_recv()
                branch = part(own, 0, k)[...] + part(orv, 0, k)[...].astype(f32) + part(xr, 0, k)[...].astype(f32)
            fresh = junction(
                branch, [part(vin(r), 0, k)[...] for r in row_i], vin(gains_i), [part(vout(o[0]), 0, k) for o in r_o], [vout(o[0]) for o in s_o]
            )
            if enter:
                part(all_ref, me, k)[...] = fresh
                all_far(k).start()
                all_sib(k).start()
            for o in r_o:
                store_rows(o, 0, k).start()
            return c

        lax.fori_loop(0, CHUNKS, join, 0)
        for o in s_o:
            store_whole(o).start()

        lead = [c for c in range(first_grad) if len(chains[c][5]) == 2] if enter else []
        if enter:
            need(we_i, *extra_i)

            def work(k, block_a, block_b):
                lhs = jnp.concatenate([part(all_ref, block_a, k)[...], part(all_ref, block_b, k)[...]], 0)
                h = nn(lhs, we_ref[...])
                for i, block in enumerate((block_a, block_b)):
                    view = lambda ref: part(ref, block, k)
                    enter[2](h[i * chunk : (i + 1) * chunk], [view(vin(r))[...] for r in extra_i], [view(vout(o[0])) for o in e_o])
                    for o in [all_o] + e_o:
                        store_rows(o, block, k).start()

            def gather(k, c):
                got_sib(k).wait_recv()
                work(k, me, sib)
                got_far(k).wait_recv()
                all_fwd(k).start()
                got_diag(k).wait_recv()
                work(k, far, diag)
                if lead:

                    @pl.when(k == CHUNKS - 2)
                    def _():
                        for ch in lead:
                            for p in range(chains[ch][0]):
                                settle(ch, 0, p)
                                hop(ch, 1, p).start()

                return c

            lax.fori_loop(0, CHUNKS, gather, 0)

        if last:
            need(*small_i)
            *vectors, table, taps = [vin(i) for i in small_i]
            rows_ref, table_ref, taps_ref = [vout(o[0]) for o in small_o]
            rows_ref[...] = jnp.zeros(rows_ref.shape, f32)
            for i, v in enumerate([vout(s_o[0][0])] + vectors):
                rows_ref[i : i + 1, :] = jnp.sum(v[...], 0, keepdims=True)
            table_ref[...] = table[...]
            taps_ref[...] = taps[...]
            course = ["sib", "far"] + list(range(bits_all - 1, -1, -1))

            def double(n):
                at = course[n]
                to = (dp, sib) if at == "sib" else (dp, far) if at == "far" else (place(dp, at)[1], me)
                return [
                    (
                        pltpu.make_async_remote_copy(
                            r, t[l].at[n], t[small_sems[0]].at[i, n], t[small_sems[1]].at[i, n], device_id=to, device_id_type=MESH
                        ),
                        r,
                        t[l].at[n],
                    )
                    for i, (r, l) in enumerate(zip((rows_ref, table_ref, taps_ref), land_small))
                    if i < 2 or n > 1
                ]

            def finish_double(n):
                for cp, r, l in double(n):
                    cp.wait()
                    r[...] += l[...]

            for cp, _, _ in double(0):
                cp.start()

        pieces = [(c, p) for c in range(len(chains)) for p in range(chains[c][0])]
        order = [x for x in pieces if x[0] >= first_grad] + [x for x in pieces if x[0] < first_grad]
        depth = lambda c: len(chains[c][5])
        begin = lambda c: 1 if c in lead else 0
        deepest = max([depth(c) - begin(c) for c in range(len(chains))] + [0])
        total_slots = max(len(order) + deepest - 1, len(course) if last else 0)
        for slot in range(total_slots):
            if last:
                for n in range(len(course) - 1):
                    if slot == (n if n < 2 else min(3 * n - 3, total_slots - 1)):
                        finish_double(n)
                        for cp, _, _ in double(n + 1):
                            cp.start()
            for s in reversed(range(deepest)):
                if 0 <= slot - s < len(order):
                    c, p = order[slot - s]
                    step = s + begin(c)
                    if step < depth(c):
                        settle(c, step, p)
                        if step + 1 < depth(c):
                            hop(c, step + 1, p).start()
        if last:
            finish_double(len(course) - 1)
            for o in small_o:
                store_whole(o).start()
        for c in range(len(chains)):
            for s in range(depth(c)):
                for p in range(chains[c][0]):
                    hop(c, s, p).wait_send()
            out_o = chains[c][5][-1][4]
            block = chains[c][5][-1][2]
            for p in range(chains[c][0]):
                store_piece(out_o, p, PIECE, chains[c][1] and t[block].shape[2] % 128 == 0).wait()

        def drain(k, c):
            if leave:
                pair_send(k).wait_send()
                far_send(k).wait_send()
                own_send(k).wait_send()
            if enter:
                all_far(k).wait_send()
                all_sib(k).wait_send()
                all_fwd(k).wait_send()
                for block in range(4):
                    for o in [all_o] + e_o:
                        store_rows(o, block, k).wait()
            for o in r_o:
                store_rows(o, 0, k).wait()
            return c

        lax.fori_loop(0, CHUNKS, drain, 0)
        for o in s_o + (small_o if last else []):
            store_whole(o).wait()
        for o in join_o:
            for p in range(out_shape[o[0]].shape[0]):
                store_piece(o, p, PIECE, False).wait()

    flops = 0
    if leave:
        flops += 2 * frames * leave[1].shape[1 if leave[2] else 0] * width
    if enter:
        flops += 2 * frames * width * sum(c for c, _ in enter[4])
    flops += sum(2 * frames * width * PIECE * d[6] for d in dws)
    outs = pl.pallas_call(
        kernel,
        in_specs=[in_hbm()] * n_in,
        out_specs=[in_hbm()] * n_out,
        out_shape=out_shape,
        scratch_shapes=scratch,
        compiler_params=pltpu.CompilerParams(collective_id=cid, has_side_effects=True, vmem_limit_bytes=VMEM_LIMIT),
        cost_estimate=pl.CostEstimate(flops=flops, bytes_accessed=60_000_000, transcendentals=0),
        name=name,
    )(*ins)
    fixed, rest = list(outs[:fixed_out]), list(outs[fixed_out:])
    fresh = [Grad(rest.pop(0), 0, d[3]) for d in dws if d[2] == "join"]
    for item in plan:
        fresh.append(Grad(rest.pop(0), item[3], item[2]))
    return fixed + [fresh] + rest


def publish(ends, small, sizes, rel, total):
    flat, outs, where = [], [], []
    f32 = jnp.float32
    for arrays, parts in ends:
        rows = arrays[0].shape[0]
        joined = len(arrays) > 1 and sizes[len(outs)]
        shape = (rows, sum(a.shape[1] for a in arrays)) if not joined else (sum(a.shape[0] for a in arrays), arrays[0].shape[1])
        where.append((len(flat), arrays, joined))
        flat.extend(arrays)
        outs.append((shape, (shape[0], parts, shape[1] // parts) if parts else None))
    n, m = len(flat), len(ends)
    width = small[0].shape[1]
    taps = small[2].shape
    split_at = [i for i in range(m) if outs[i][1]]
    small_shapes = [(1, width)] * 5 + [(rel, HEAD), (taps[0] - 1, taps[1]), (1, taps[1]), (1, 128)]

    def kernel(*refs):
        src, small_in = refs[:n], refs[n : n + 3]
        dst, small_out = refs[n + 3 : n + 3 + m], refs[n + 3 + m : n + 12 + m]
        rest = refs[n + 12 + m :]
        held, split = rest[:m], dict(zip(split_at, rest[m:-1]))
        sem = rest[-1]
        loads, stores = [], []
        for i, (first, arrays, joined) in enumerate(where):
            at, copies = 0, []
            for k in range(len(arrays)):
                ref = src[first + k]
                size = ref.shape[0 if joined else 1]
                part = held[i].at[pl.ds(at, size)] if joined else held[i].at[:, pl.ds(at, size)]
                copies.append(pltpu.make_async_copy(ref, part, sem.at[first + k]))
                at += size
            loads.append(copies)
            stores.append(pltpu.make_async_copy(split.get(i, held[i]), dst[i], sem.at[n + i]))
        for copies in loads:
            for cp in copies:
                cp.start()
        rows, table, tap = [r[...] for r in small_in]
        for i in range(5):
            small_out[i][...] = rows[i : i + 1]
        small_out[5][...] = table[:rel, :HEAD] + table[:rel, HEAD:]
        small_out[6][...] = tap[:-1]
        small_out[7][...] = tap[-1:]
        square = jnp.sum(rows, -1, keepdims=True) / total
        lane = lax.broadcasted_iota(jnp.int32, (rows.shape[0], 128), 1)
        row = lax.broadcasted_iota(jnp.int32, (rows.shape[0], 128), 0)
        small_out[8][...] = jnp.sqrt(jnp.sum(jnp.where(row == lane + 5, square, 0.0), 0, keepdims=True))
        for i in range(m):
            for cp in loads[i]:
                cp.wait()
            if i in split:
                cols = split[i].shape[2]
                for j in range(split[i].shape[1]):
                    split[i][:, j, :] = held[i][:, j * cols : (j + 1) * cols]
            stores[i].start()
        for cp in stores:
            cp.wait()

    vm = pl.BlockSpec(memory_space=pltpu.VMEM)
    return pl.pallas_call(
        kernel,
        in_specs=[in_hbm()] * n + [vm] * 3,
        out_specs=[in_hbm()] * m + [vm] * 9,
        out_shape=[jax.ShapeDtypeStruct(o[1] or o[0], f32) for o in outs] + [jax.ShapeDtypeStruct(s, f32) for s in small_shapes],
        scratch_shapes=[pltpu.VMEM(o[0], f32) for o in outs]
        + [pltpu.VMEM(outs[i][1], f32) for i in split_at]
        + [pltpu.SemaphoreType.DMA((n + m,))],
        compiler_params=pltpu.CompilerParams(vmem_limit_bytes=VMEM_LIMIT),
        name="publish",
    )(*flat, *small)


SPAN = 128


def exchange(stats, landing, send, recv):
    dp, me = lax.axis_index("dp"), lax.axis_index("mp")
    core, chip = me % 2, me // 2
    others = [chip * 2 + 1 - core, (1 - chip) * 2 + core, (1 - chip) * 2 + 1 - core]
    return [
        pltpu.make_async_remote_copy(
            stats, landing.at[i], send.at[i], recv.at[i], device_id=(dp, to), device_id_type=MESH
        )
        for i, to in enumerate(others)
    ]


def group_targets():
    dp, me = lax.axis_index("dp"), lax.axis_index("mp")
    core, chip = me % 2, me // 2
    return [(dp, chip * 2 + 1 - core), (dp, (1 - chip) * 2 + core), (dp, (1 - chip) * 2 + 1 - core)]


def to_rows(first, second):
    lane = lax.broadcasted_iota(jnp.int32, (SPAN, SPAN), 1)
    both = jnp.where(lane == 0, first, jnp.where(lane == 1, second, 0.0))
    return both.T[:8]


def to_columns(rows8):
    return jnp.concatenate([rows8, jnp.zeros((SPAN - 8, SPAN), jnp.float32)], 0).T


def shifted(window, by):
    return window if by == 0 else pltpu.roll(window, window.shape[0] - by, 0)


def conv_mid(glu, w_depth, gain_depth, width, cid):
    frames, chans = glu.shape
    taps = w_depth.shape[0]
    reach = taps - 1
    edge = (reach + 7) // 8 * 8
    f32, bf = jnp.float32, jnp.bfloat16
    tiles, lanes = frames // SPAN, chans // 128

    def kernel(glu_h, w_h, g_h, act_h, slope_h, unit_h, stat_h, pad, w_v, g_v, act, slope, unit, stat, sendbuf, landing, lsem, ssem, send, recv):
        meet = greet(group_targets())
        loads = [
            pltpu.make_async_copy(glu_h, pad.at[pl.ds(edge, frames)], lsem.at[0]),
            pltpu.make_async_copy(w_h, w_v, lsem.at[1]),
            pltpu.make_async_copy(g_h, g_v, lsem.at[2]),
        ]
        for cp in loads:
            cp.start()
        pad[:edge, :] = jnp.zeros((edge, chans), f32)
        for cp in loads:
            cp.wait()

        def tile(i, c):
            at = pl.multiple_of(i * SPAN, SPAN)
            for lane in range(lanes):
                cols = slice(lane * 128, (lane + 1) * 128)
                window = pad[pl.ds(at, SPAN + edge), cols]
                total = jnp.zeros((SPAN, 128), f32)
                for by in range(8):
                    moved = shifted(window, by)
                    for base in range(0, edge + 1, 8):
                        tap = base + by - (edge - reach)
                        if 0 <= tap < taps:
                            total = total + w_v[tap : tap + 1, cols] * moved[base : base + SPAN]
                unit[pl.ds(at, SPAN), cols] = total
            depth = unit[pl.ds(at, SPAN), :]
            mean = jnp.mean(depth, -1, keepdims=True)
            centred = depth - mean
            sendbuf[:, pl.ds(at, SPAN)] = to_rows(mean, jnp.sum(centred * centred, -1, keepdims=True))
            return c

        lax.fori_loop(0, tiles, tile, 0)
        meet()
        copies = exchange(sendbuf, landing, send, recv)
        for cp in copies:
            cp.start()
        for cp in copies:
            cp.wait_recv()
        rows = [sendbuf[...]] + [landing[i] for i in range(3)]
        mean = sum(r[0:1] for r in rows) * 0.25
        spread = sum(r[1:2] + chans * (r[0:1] - mean) * (r[0:1] - mean) for r in rows) / width
        inverse = lax.rsqrt(spread + epsilon)
        row = lax.broadcasted_iota(jnp.int32, (8, frames), 0)
        stat[...] = jnp.where(row == 0, mean, jnp.where(row == 1, inverse, 0.0))
        outs = [(act, act_h), (slope, slope_h), (unit, unit_h)]

        def store(i, n):
            at = pl.ds(pl.multiple_of(i * SPAN, SPAN), SPAN)
            return pltpu.make_async_copy(outs[n][0].at[at], outs[n][1].at[at], ssem.at[n, i])

        def finish(i, c):
            at = pl.multiple_of(i * SPAN, SPAN)
            cols = to_columns(stat[:, pl.ds(at, SPAN)])
            u = (unit[pl.ds(at, SPAN), :] - cols[:, 0:1]) * cols[:, 1:2]
            a, s = silu_pair(u * g_v[...])
            unit[pl.ds(at, SPAN), :] = u
            act[pl.ds(at, SPAN), :] = a.astype(bf)
            slope[pl.ds(at, SPAN), :] = s.astype(bf)
            for n in range(3):
                store(i, n).start()
            return c

        lax.fori_loop(0, tiles, finish, 0)
        last = pltpu.make_async_copy(stat, stat_h, lsem.at[0])
        last.start()
        for cp in copies:
            cp.wait_send()
        for i in range(tiles):
            for n in range(3):
                store(i, n).wait()
        last.wait()

    S = jax.ShapeDtypeStruct
    out_shape = [S((frames, chans), bf), S((frames, chans), bf), S((frames, chans), f32), S((8, frames), f32)]
    vm = pltpu.VMEM
    return pl.pallas_call(
        kernel,
        in_specs=[in_hbm()] * 3,
        out_specs=[in_hbm()] * 4,
        out_shape=out_shape,
        scratch_shapes=[
            vm((frames + edge, chans), f32), vm(w_depth.shape, f32), vm((1, chans), f32),
            vm((frames, chans), bf), vm((frames, chans), bf), vm((frames, chans), f32), vm((8, frames), f32),
            vm((8, frames), f32), vm((3, 8, frames), f32),
            pltpu.SemaphoreType.DMA((3,)), pltpu.SemaphoreType.DMA((3, tiles)), pltpu.SemaphoreType.DMA((3,)), pltpu.SemaphoreType.DMA((3,)),
        ],
        compiler_params=pltpu.CompilerParams(collective_id=cid, has_side_effects=True, vmem_limit_bytes=VMEM_LIMIT),
        name="conv_mid",
    )(glu, w_depth, gain_depth)


def conv_mid_back(grad, slope, unit, stat, glu, sig, tail, w_depth, gain_depth, width, cid, grads):
    frames, chans = glu.shape
    taps = w_depth.shape[0]
    reach = taps - 1
    edge = (reach + 7) // 8 * 8
    f32, bf = jnp.float32, jnp.bfloat16
    tiles, lanes = frames // SPAN, chans // 128
    ins = [grad, slope, unit, stat, w_depth, gain_depth, glu, sig, tail]
    riders = Riders(grads)
    n = len(grads)

    def kernel(*refs):
        hbm, ride_in, (pair_h, taps_h), ride_out = refs[:9], refs[9 : 9 + n], refs[9 + n : 11 + n], refs[11 + n : 11 + 2 * n]
        refs = refs[2 * n :]
        (grad_v, slope_v, unit_v, stat_v, w_v, g_v, pad, sig_v, tail_v, back, pair, taps_v, acc, gacc, sendbuf, landing, lsem, ssem, send, recv) = refs[11:31]
        riders.bind(ride_in, ride_out, refs[31:])
        meet = greet(group_targets() + riders.targets())
        dst = [grad_v, slope_v, unit_v, stat_v, w_v, g_v, pad.at[pl.ds(edge, frames)], sig_v, tail_v]
        loads = [pltpu.make_async_copy(h, d, lsem.at[i]) for i, (h, d) in enumerate(zip(hbm, dst))]
        for cp in loads:
            cp.start()
        pad[:edge, :] = jnp.zeros((edge, chans), f32)
        back[frames:, :] = jnp.zeros((edge, chans), f32)
        acc[...] = jnp.zeros_like(acc)
        gacc[...] = jnp.zeros_like(gacc)
        for cp in loads[:6]:
            cp.wait()

        def first(i, c):
            at = pl.ds(pl.multiple_of(i * SPAN, SPAN), SPAN)
            u = unit_v[at, :]
            de = grad_v[at, :] * slope_v[at, :].astype(f32)
            gacc[...] += fold8(de * u)
            du = de * g_v[...]
            back[at, :] = du
            sendbuf[:, at] = to_rows(jnp.sum(du, -1, keepdims=True), jnp.sum(du * u, -1, keepdims=True))
            return c

        meet()
        riders.start()
        lax.fori_loop(0, tiles, first, 0)
        copies = exchange(sendbuf, landing, send, recv)
        for cp in copies:
            cp.start()
        for cp in loads[6:]:
            cp.wait()
        for cp in copies:
            cp.wait_recv()
        means = (sendbuf[...] + landing[0] + landing[1] + landing[2]) / width
        row = lax.broadcasted_iota(jnp.int32, (8, frames), 0)
        stat_v[...] = jnp.where(row == 1, stat_v[...], jnp.where(row == 0, means[0:1], jnp.where(row == 2, means[1:2], 0.0)))

        def second(i, c):
            at = pl.ds(pl.multiple_of(i * SPAN, SPAN), SPAN)
            cols = to_columns(stat_v[:, at])
            back[at, :] = cols[:, 1:2] * (back[at, :] - cols[:, 0:1] - unit_v[at, :] * cols[:, 2:3])
            return c

        lax.fori_loop(0, tiles, second, 0)

        def store(i):
            at = pl.ds(pl.multiple_of(i * SPAN, SPAN), SPAN)
            return pltpu.make_async_copy(pair.at[at], pair_h.at[at], ssem.at[i])

        def third(i, c):
            at = pl.multiple_of(i * SPAN, SPAN)
            rows = pl.ds(at, SPAN)
            for lane in range(lanes):
                cols = slice(lane * 128, (lane + 1) * 128)
                ahead = back[pl.ds(at, SPAN + edge), cols]
                total = jnp.zeros((SPAN, 128), f32)
                for by in range(8):
                    moved = shifted(ahead, by)
                    for base in range(0, edge, 8):
                        tap = reach - (base + by)
                        if 0 <= tap < taps:
                            total = total + w_v[tap : tap + 1, cols] * moved[base : base + SPAN]
                pair[rows, cols] = (total * sig_v[rows, cols].astype(f32)).astype(bf)
                pair[rows, chans + lane * 128 : chans + (lane + 1) * 128] = (total * tail_v[rows, cols].astype(f32)).astype(bf)
            store(i).start()
            for lane in range(lanes):
                cols = slice(lane * 128, (lane + 1) * 128)
                here = back[rows, cols]
                window = pad[pl.ds(at, SPAN + edge), cols]
                for by in range(8):
                    moved = shifted(window, by)
                    for base in range(0, edge + 1, 8):
                        tap = base + by - (edge - reach)
                        if 0 <= tap < taps:
                            acc[tap * 8 : tap * 8 + 8, cols] += fold8(here * moved[base : base + SPAN])
            return c

        lax.fori_loop(0, tiles, third, 0)
        for tap in range(taps):
            taps_v[tap : tap + 1, :] = jnp.sum(acc[tap * 8 : tap * 8 + 8, :], 0, keepdims=True)
        taps_v[taps : taps + 1, :] = jnp.sum(gacc[...], 0, keepdims=True)
        last = pltpu.make_async_copy(taps_v, taps_h, lsem.at[0])
        last.start()
        for cp in copies:
            cp.wait_send()
        riders.finish()
        for i in range(tiles):
            store(i).wait()
        last.wait()

    S = jax.ShapeDtypeStruct
    vm = pltpu.VMEM
    outs = pl.pallas_call(
        kernel,
        in_specs=[in_hbm()] * (9 + n),
        out_specs=[in_hbm()] * (2 + n),
        out_shape=[S((frames, 2 * chans), bf), S((taps + 1, chans), f32)] + riders.after,
        scratch_shapes=[
            vm((frames, chans), f32), vm((frames, chans), bf), vm((frames, chans), f32), vm((8, frames), f32),
            vm(w_depth.shape, f32), vm((1, chans), f32), vm((frames + edge, chans), f32), vm((frames, chans), bf), vm((frames, chans), bf),
            vm((frames + edge, chans), f32), vm((frames, 2 * chans), bf), vm((taps + 1, chans), f32), vm((taps * 8, chans), f32), vm((8, chans), f32),
            vm((8, frames), f32), vm((3, 8, frames), f32),
            pltpu.SemaphoreType.DMA((9,)), pltpu.SemaphoreType.DMA((tiles,)), pltpu.SemaphoreType.DMA((3,)), pltpu.SemaphoreType.DMA((3,)),
        ] + riders.scratch,
        compiler_params=pltpu.CompilerParams(collective_id=cid, has_side_effects=True, vmem_limit_bytes=VMEM_LIMIT),
        name="conv_mid_back",
    )(*ins, *riders.arrays)
    return outs[0], outs[1], riders.results(outs[2:])


def split_pair(x):
    left = lax.broadcasted_iota(jnp.int32, x.shape, 1) < HEAD
    zero = jnp.zeros_like(x)
    return jnp.concatenate([jnp.where(left, x, zero), jnp.where(left, zero, x)], 0)

def join_pair(x):
    rows = x.shape[0] // 2
    left = lax.broadcasted_iota(jnp.int32, (rows, x.shape[1]), 1) < HEAD
    return jnp.where(left, x[:rows], x[rows:])

def spot_table(spots):
    spot = lax.broadcasted_iota(jnp.int32, (spots, BQ), 0)
    inner = jnp.clip(spot - REL_LEFT, 0, REL_LEFT + REL_RIGHT)
    row = jnp.where(spot < 3 * BQ, inner, jnp.where(spot < 4 * BQ, 0, REL_LEFT + REL_RIGHT))
    return (lax.broadcasted_iota(jnp.int32, (spots, BQ), 1) == row).astype(jnp.bfloat16)


def fwd_kernel(q_ref, k_ref, v_ref, relb_ref, mixed_ref, probs_ref, bias_ref, rel_ref):
    ib = pl.program_id(1)

    @pl.when((ib == 0) & (pl.program_id(0) == 0))
    def _():
        rel_ref[...] = nn(spot_table(5 * BQ), relb_ref[...]).astype(jnp.bfloat16)

    qs = split_pair(q_ref[...] * 0.125)
    s = nt(qs, k_ref[...])
    b = nt(qs, rel_ref[...])
    rows = b.shape[0] // 2
    bias_ref[:, 0:BQ] = b[:, 3 * BQ : 4 * BQ]
    for h in range(2):
        r = pltpu.roll(b[h * rows : (h + 1) * rows, :WIN], 0, 1, stride=1, stride_axis=0)
        bias_ref[h * rows : (h + 1) * rows, BQ : 4 * BQ] = r[:, : 3 * BQ]
    bias_ref[:, 4 * BQ :] = b[:, 4 * BQ :]
    nkeys = s.shape[1] // BQ
    parts = []
    for jb in range(nkeys):
        at = pl.multiple_of(jnp.clip(jb - ib + 2, 0, 4) * BQ, BQ)
        parts.append(s[:, jb * BQ : (jb + 1) * BQ] + bias_ref[:, pl.ds(at, BQ)])
    top = functools.reduce(jnp.maximum, parts)
    m = jnp.max(top, -1, keepdims=True)
    es = [jnp.exp(p - m) for p in parts]
    tot = jnp.sum(functools.reduce(jnp.add, es), -1, keepdims=True)
    inv = 1.0 / tot
    for jb in range(nkeys):
        probs_ref[0, :, jb * BQ : (jb + 1) * BQ] = (es[jb] * inv).astype(jnp.bfloat16)
    mixed_ref[...] = join_pair(nn(probs_ref[0], v_ref[...])).astype(jnp.bfloat16)

def bwd_kernel(riders, *refs):
    n = len(riders.plan)
    q_ref, k_ref, v_ref, relb_ref, probs_ref, do_ref, db_h, mix_h = refs[:8]
    ride_in = refs[8 : 8 + n]
    dq_ref, dk_ref, dv_ref, dt_ref, dw_h = refs[8 + n : 13 + n]
    ride_out = refs[13 + n : 13 + 2 * n]
    tot_ref, dkt, dvt, dta, dz_ref, hot_ref, db_v, mix_v, dw_v, dw_land, dw_half, osem, psem = refs[13 + 2 * n : 26 + 2 * n]
    riders.bind(ride_in, ride_out, refs[26 + 2 * n :])
    pr, ib, nb = pl.program_id(0), pl.program_id(1), pl.num_programs(1)
    dp, mp = lax.axis_index("dp"), lax.axis_index("mp")
    loads = [pltpu.make_async_copy(db_h, db_v, osem.at[0]), pltpu.make_async_copy(mix_h, mix_v, osem.at[1])]
    pieces = dw_v.shape[0]
    hops = [halving_copy(dw_v, dw_land, p, 0, psem.at[0], psem.at[1], p) for p in range(pieces)]
    flip = dw_land.shape[2] % 128 == 0
    stores = [
        pltpu.make_async_copy(region(dw_half, p, PIECE, flip), region(dw_h, p, PIECE, flip), psem.at[2, p]) for p in range(pieces)
    ]

    @pl.when((ib == 0) & (pr == 0))
    def _():
        meet = greet(sorted_targets(riders, dp, mp))
        for cp in loads:
            cp.start()
        hot_ref[...] = spot_table(WIN)
        meet()
        riders.start()
        for cp in loads:
            cp.wait()
        for p in range(pieces):
            g = tn(db_v[...], mix_v[:, p * PIECE : (p + 1) * PIECE])
            dw_v[p] = g.astype(jnp.bfloat16).reshape(dw_v.shape[1:])
            hops[p].start()

    @pl.when(ib == 0)
    def _():
        dkt[...] = jnp.zeros_like(dkt)
        dvt[...] = jnp.zeros_like(dvt)
    @pl.when((ib == 0) & (pr == 0))
    def _():
        dta[...] = jnp.zeros_like(dta)
    qs = split_pair(q_ref[...] * 0.125)
    dos = split_pair(do_ref[...])
    p = probs_ref[0]
    dp = nt(dos, v_ref[...])
    nkeys = dp.shape[1] // BQ
    dvt[...] += tn(dos, p)
    pf = p.astype(jnp.float32)
    acc = None
    for jb in range(nkeys):
        sl = slice(jb * BQ, (jb + 1) * BQ)
        t = pf[:, sl] * dp[:, sl]
        acc = t if acc is None else acc + t
    inner = jnp.sum(acc, -1, keepdims=True)
    tot_ref[...] = jnp.zeros_like(tot_ref)
    for jb in range(nkeys):
        sl = slice(jb * BQ, (jb + 1) * BQ)
        dz = (pf[:, sl] * (dp[:, sl] - inner)).astype(jnp.bfloat16)
        dz_ref[:, sl] = dz
        at = pl.multiple_of(jnp.clip(jb - ib + 2, 0, 4) * BQ, BQ)
        tot_ref[:, pl.ds(at, BQ)] += dz.astype(jnp.float32)
    rows = BQ
    r2 = lax.broadcasted_iota(jnp.int32, (2 * rows, 2 * rows), 0)
    c2 = lax.broadcasted_iota(jnp.int32, (2 * rows, 2 * rows), 1)
    mirror = (r2 + c2 == jnp.where(r2 < rows, rows - 1, 3 * rows - 1)).astype(jnp.bfloat16)
    w = jnp.concatenate([tot_ref[:, BQ : 4 * BQ].astype(jnp.bfloat16), jnp.zeros((2 * rows, BQ), jnp.bfloat16)], 1)
    w = nn(mirror, w)
    outs = [pltpu.roll(w[h * rows : (h + 1) * rows], WIN - rows + 1, 1, stride=1, stride_axis=0) for h in range(2)]
    d = nn(mirror, jnp.concatenate(outs, 0).astype(jnp.bfloat16)).astype(jnp.bfloat16)
    drel = nn(d, hot_ref[...])
    col = lax.broadcasted_iota(jnp.int32, drel.shape, 1)
    low = jnp.sum(tot_ref[:, :BQ], -1, keepdims=True)
    high = jnp.sum(tot_ref[:, 4 * BQ :], -1, keepdims=True)
    drel = drel + jnp.where(col == 0, low, 0.0) + jnp.where(col == REL_LEFT + REL_RIGHT, high, 0.0)
    drel = drel.astype(jnp.bfloat16)
    dz = dz_ref[...]
    dq = nn(dz, k_ref[...]) + nn(drel, relb_ref[...])
    dq_ref[...] = (join_pair(dq) * 0.125).astype(jnp.bfloat16)
    dkt[...] += tn(qs, dz)
    dta[...] += tn(drel, qs)
    @pl.when(ib == nb - 1)
    def _():
        dk_ref[...] = dkt[...].T.astype(jnp.bfloat16)
        dv_ref[...] = dvt[...].T.astype(jnp.bfloat16)
        dt_ref[...] = dta[...]

    @pl.when((ib == nb - 1) & (pr == pl.num_programs(0) - 1))
    def _():
        own, _ = place(lax.axis_index("dp"), 0)
        for p in range(pieces):
            hops[p].wait_recv()
            halving_add(lambda q, j: dw_v[q, j, own], dw_land, dw_half, p, True)
            stores[p].start()
        riders.finish()
        for p in range(pieces):
            hops[p].wait_send()
            stores[p].wait()


def sorted_targets(riders, dp, mp):
    return [(place(dp, b)[1], mp) for b in sorted({0} | {x[1] for x in riders.plan})]


def wide_table(rel_table):
    padded = jnp.pad(rel_table, ((0, BQ - rel_table.shape[0]), (0, 0)))
    return jnp.concatenate([padded, padded], 1)


def attn_fwd(qkv, rel):
    frames, cols = qkv.shape
    pairs = cols // 3 // 128
    nb = frames // BQ
    bf = jnp.bfloat16
    return pl.pallas_call(
        fwd_kernel,
        grid=(pairs, nb),
        in_specs=[
            pl.BlockSpec((BQ, 128), lambda p, i: (i, p)),
            pl.BlockSpec((frames, 128), lambda p, i: (0, pairs + p)),
            pl.BlockSpec((frames, 128), lambda p, i: (0, 2 * pairs + p)),
            pl.BlockSpec(rel.shape, lambda p, i: (0, 0)),
        ],
        out_specs=[
            pl.BlockSpec((BQ, 128), lambda p, i: (i, p)),
            pl.BlockSpec((1, 2 * BQ, frames), lambda p, i: (p, i, 0)),
        ],
        out_shape=[jax.ShapeDtypeStruct((frames, cols // 3), bf), jax.ShapeDtypeStruct((pairs, 2 * frames, frames), bf)],
        scratch_shapes=[pltpu.VMEM((2 * BQ, 5 * BQ), jnp.float32), pltpu.VMEM((5 * BQ, 128), bf)],
        compiler_params=pltpu.CompilerParams(vmem_limit_bytes=VMEM_LIMIT),
        name="attn_fwd",
    )(qkv, qkv, qkv, rel)

def attn_bwd(qkv, rel, probs, dmixed, grad_rows, mixed, grads, cid):
    frames, cols = qkv.shape
    pairs = cols // 3 // 128
    nb = frames // BQ
    bf = jnp.bfloat16
    count = lax.axis_size("dp")
    blk = pl.BlockSpec((BQ, 128), lambda p, i: (i, p))
    full = pl.BlockSpec((frames, 128), lambda p, i: (0, p))
    riders = Riders(grads)
    width = grad_rows.shape[1]
    shape = (mixed.shape[1] // PIECE, count // 2, 2, width // count, PIECE)
    half = halved(shape, True)
    vm = pltpu.VMEM
    outs = pl.pallas_call(
        functools.partial(bwd_kernel, riders),
        grid=(pairs, nb),
        in_specs=[
            blk,
            pl.BlockSpec((frames, 128), lambda p, i: (0, pairs + p)),
            pl.BlockSpec((frames, 128), lambda p, i: (0, 2 * pairs + p)),
            pl.BlockSpec(rel.shape, lambda p, i: (0, 0)),
            pl.BlockSpec((1, 2 * BQ, frames), lambda p, i: (p, i, 0)),
            blk,
        ]
        + [in_hbm()] * (2 + len(grads)),
        out_specs=[blk, full, full, pl.BlockSpec((128, 128), lambda p, i: (0, 0))] + [in_hbm()] * (1 + len(grads)),
        out_shape=[jax.ShapeDtypeStruct((frames, cols // 3), bf)] * 3 + [jax.ShapeDtypeStruct((128, 128), jnp.float32), half] + riders.after,
        scratch_shapes=[
            vm((2 * BQ, 5 * BQ), jnp.float32), vm((128, frames), jnp.float32), vm((128, frames), jnp.float32),
            vm((128, 128), jnp.float32), vm((2 * BQ, frames), bf), vm((WIN, BQ), bf),
            vm(grad_rows.shape, bf), vm(mixed.shape, bf), vm(shape, bf), arriving(shape), vm(half.shape, half.dtype),
            pltpu.SemaphoreType.DMA((2,)), pltpu.SemaphoreType.DMA((3, shape[0])),
        ]
        + riders.scratch,
        compiler_params=pltpu.CompilerParams(vmem_limit_bytes=VMEM_LIMIT, collective_id=cid, has_side_effects=True),
        cost_estimate=pl.CostEstimate(flops=20 * frames * frames * 128 * pairs, bytes_accessed=20_000_000, transcendentals=0),
        name="attn_bwd",
    )(qkv, qkv, qkv, rel, probs, dmixed, grad_rows, mixed, *riders.arrays)
    return list(outs[:4]) + [[Grad(outs[4], 1, True)] + riders.results(outs[5:])]


def body(
    features,
    w1_in,
    w1_out,
    gain_ffn1,
    w_qkv,
    w_attn_out,
    rel_table,
    gain_attn,
    w_conv_in,
    w_depth,
    gain_depth,
    w_conv_out,
    gain_conv,
    w2_in,
    w2_out,
    gain_ffn2,
    gain_final,
    cotangent,
):
    local_frames, clip_count, width = features.shape
    rows = local_frames * clip_count
    f32, bf = jnp.float32, jnp.bfloat16
    s0 = features.reshape(rows, width)
    seed = cotangent.reshape(rows, width)
    row = jnp.arange(8)[:, None]
    gains = sum(
        jnp.where(row == i, g.astype(f32)[None], 0.0)
        for i, g in enumerate((gain_ffn1, gain_attn, gain_conv, gain_ffn2, gain_final))
    )
    flat_qkv = w_qkv.reshape(width, -1)
    flat_conv = w_conv_in.reshape(width, -1)
    units = w1_in.shape[1]
    half = units // PIECE // 2
    dp_count = lax.axis_size("dp")
    done = dp_count.bit_length() - 1
    pending = lambda items: [g for g in items if g.bit < done]
    chans = w_conv_out.shape[0]

    def swish_out(h, extra, outs):
        act, slope = silu_pair(h)
        outs[0][...] = act.astype(bf)
        outs[1][...] = slope.astype(bf)

    def plain_out(h, extra, outs):
        outs[0][...] = h.astype(outs[0].dtype)

    def glu_out(h, extra, outs):
        p0 = h[:, :chans]
        sig = jax.nn.sigmoid(h[:, chans:])
        glu = p0 * sig
        outs[0][...] = glu
        outs[1][...] = sig.astype(bf)
        outs[2][...] = (glu * (1.0 - sig)).astype(bf)

    def slope_out(h, extra, outs):
        outs[0][...] = (h * extra[0][...].astype(f32)).astype(bf)

    def first(branch, ins, gains, outs, sums):
        return (unit_norm(ins[0].astype(f32))[0] * gains[0:1, :]).astype(bf)

    def forward(scale, row):
        def run(branch, ins, gains, outs, sums):
            fresh = ins[0].astype(f32) + scale * branch
            outs[0][...] = fresh
            sums[0][...] += fold8(branch * branch)
            return (unit_norm(fresh)[0] * gains[row : row + 1, :]).astype(bf)
        return run

    def turn(branch, ins, gains, outs, sums):
        fresh = ins[0] + 0.5 * branch
        sums[0][...] += fold8(branch * branch)
        sums[1][...] += fold8(fresh * fresh)
        unit, inverse = unit_norm(fresh)
        outs[0][...] = unit * gains[4:5, :]
        grad = ins[1].astype(f32)
        scaled = grad * gains[4:5, :]
        mean_one = jnp.mean(scaled, -1, keepdims=True)
        mean_two = jnp.mean(scaled * unit, -1, keepdims=True)
        sums[2][...] += fold8(grad * unit)
        back = inverse * (scaled - mean_one - unit * mean_two)
        outs[1][...] = back
        return (0.5 * back).astype(bf)

    def backward(scale, row):
        def run(branch, ins, gains, outs, sums):
            pull, grad_gain = norm_pull(branch, ins[1].astype(f32), gains[row : row + 1, :])
            fresh = ins[0] + pull
            outs[0][...] = fresh
            sums[0][...] += grad_gain
            return (scale * fresh).astype(bf)
        return run

    a1, act1, slope1, _ = stage(
        "ffn1_in", 0, rows, width, dp_count, gains, enter=(w1_in, False, swish_out, (), ((units, bf), (units, bf))),
        junction=first, row_in=(s0,),
    )
    a2, qkv, s1, sq1, _ = stage(
        "ffn1_out", 1, rows, width, dp_count, gains, leave=(act1, w1_out, False),
        enter=(flat_qkv, False, plain_out, (), ((flat_qkv.shape[1], bf),)),
        junction=forward(0.5, 1), row_in=(s0,), row_out=(f32,), sums=1,
    )
    wide = wide_table(rel_table)
    mixed, probs = attn_fwd(qkv, wide)
    a3, glu, sig, tail, s2, sq2, _ = stage(
        "attn_out", 2, rows, width, dp_count, gains, leave=(mixed, w_attn_out, False),
        enter=(flat_conv, False, glu_out, (), ((chans, f32), (chans, bf), (chans, bf))),
        junction=forward(1.0, 2), row_in=(s1,), row_out=(f32,), sums=1,
    )
    depth_taps = w_depth.astype(f32)
    depth_gain = gain_depth.astype(f32)[None]
    act3, slope3, depth_unit, depth_stat = conv_mid(glu, depth_taps, depth_gain, width, 10)
    a4, act2, slope2, s3, sq3, _ = stage(
        "conv_out", 3, rows, width, dp_count, gains, leave=(act3, w_conv_out, False),
        enter=(w2_in, False, swish_out, (), ((units, bf), (units, bf))),
        junction=forward(1.0, 3), row_in=(s2,), row_out=(f32,), sums=1,
    )
    db4, dh2, output, grad4, sq4, sq5, dgf, _ = stage(
        "ffn2_out", 4, rows, width, dp_count, gains, leave=(act2, w2_out, False),
        enter=(w2_out, True, slope_out, (slope2,), ((units, bf),)),
        junction=turn, row_in=(s3, seed), row_out=(f32, f32), sums=3,
    )
    db3, de3, grad3, dg2, (ga_in, gb_in, gw2_out) = stage(
        "ffn2_back", 5, rows, width, dp_count, gains, leave=(dh2, w2_in, True),
        enter=(w_conv_out, True, plain_out, (), ((chans, f32),)), dws=(
            weight(a4, dh2, "join", False, 1, 0, half),
            weight(a4, dh2, "join", False, 1, half, units // PIECE - half),
            weight(db4, act2, "far", True),
        ),
        junction=backward(1.0, 3), row_in=(grad4, s3), row_out=(f32,), sums=1,
    )
    dpaired, tap_sums, (gw2_out, ga_in) = conv_mid_back(
        de3, slope3, depth_unit, depth_stat, glu, sig, tail, depth_taps, depth_gain, width, 11, [gw2_out, ga_in]
    )
    db2, dmixed, grad2, dgc, (gconv_in, gconv_out, gb_in, gw2_out, ga_in) = stage(
        "conv_back", 6, rows, width, dp_count, gains, leave=(dpaired, flat_conv, True),
        enter=(w_attn_out, True, plain_out, (), ((w_attn_out.shape[0], bf),)), dws=(weight(a3, dpaired, "far", False), weight(db3, act3, "far", True)), grads=(gb_in, gw2_out, ga_in),
        junction=backward(1.0, 2), row_in=(grad3, s2), row_out=(f32,), sums=1,
    )
    dq, dk, dv, dt, (gattn, gb_in, ga_in, gconv_in, gconv_out) = attn_bwd(
        qkv, wide, probs, dmixed, db2, mixed, [gb_in, ga_in, gconv_in, gconv_out], 9
    )
    dqkv = (dq, dk, dv)
    db1, dh1, grad1, dga, (gqkv, gconv_in, gconv_out, gb_in) = stage(
        "attn_back", 7, rows, width, dp_count, gains, leave=(dqkv, flat_qkv, True),
        enter=(w1_out, True, slope_out, (slope1,), ((units, bf),)), dws=(weight(a2, dqkv, "far", False, 2),), grads=(gconv_in, gconv_out, gb_in),
        junction=backward(0.5, 1), row_in=(grad2, s1), row_out=(f32,), sums=1,
    )
    early = [gqkv, gattn, gconv_in, gconv_out, ga_in, gb_in, gw2_out]
    waiting = pending(early)
    grad0, dg1, ends, small_rows, table, taps_end = stage(
        "ffn1_back", 8, rows, width, dp_count, gains, leave=(dh1, w1_in, True),
        dws=(weight(db1, act1, "far", True), weight(a1, dh1, "near", False)), grads=waiting,
        small=[dga, dgc, dg2, dgf, sq1, sq2, sq3, sq4, sq5, dt, tap_sums],
        junction=backward(1.0, 0), row_in=(grad1, s0), row_out=(f32,), sums=1,
    )
    gw1_out, gw1_in = ends[:2]
    for item, end in zip(waiting, ends[2:]):
        item.array = end.array

    def finish(item):
        flip = item.turned and item.array.shape[0] * dp_count == width and (width // dp_count) % 128 != 0
        return item.array.T if flip else item.array

    token_total = rows * lax.axis_size("mp") * dp_count
    ends = [
        ([output], 1),
        ([grad0], 1),
        ([finish(gw1_in)], 0),
        ([finish(gw1_out)], 0),
        ([finish(gqkv)], 3),
        ([finish(gattn)], 0),
        ([finish(gconv_in)], 2),
        ([finish(gconv_out)], 0),
        ([finish(ga_in), finish(gb_in)], 0),
        ([finish(gw2_out)], 0),
    ]
    done_ends = publish(ends, [small_rows, table, taps_end], {8: False}, rel_table.shape[0], float(token_total * width))
    (output, grad0, gw1_in, gw1_out, gqkv, gattn, gconv_in, gconv_out, gw2_in, gw2_out) = done_ends[:10]
    *gain_sums, table_sum, depth_sum, depth_gain_sum, rms_stats = done_ends[10:]
    gain_sums = [g[0] for g in gain_sums]
    return (
        output,
        grad0,
        gw1_in,
        gw1_out,
        gain_sums[0],
        gqkv,
        gattn,
        table_sum,
        gain_sums[1],
        gconv_in,
        depth_sum,
        depth_gain_sum[0],
        gconv_out,
        gain_sums[2],
        gw2_in,
        gw2_out,
        gain_sums[3],
        gain_sums[4],
        rms_stats[0, :5],
    )


def solution(mesh):
    return jax.shard_map(
        body,
        mesh=mesh,
        in_specs=(
            P("mp", "dp", None),
            P(None, "mp"),
            P("mp", None),
            P(),
            P(None, None, "mp"),
            P("mp", None),
            P(),
            P(),
            P(None, None, "mp"),
            P(None, "mp"),
            P("mp"),
            P("mp", None),
            P(),
            P(None, "mp"),
            P("mp", None),
            P(),
            P(),
            P("mp", "dp", None),
        ),
        out_specs=(
            P("mp", "dp", None),
            P("mp", "dp", None),
            P("dp", "mp"),
            P("mp", "dp"),
            P(),
            P("dp", None, "mp"),
            P("mp", "dp"),
            P(),
            P(),
            P("dp", None, "mp"),
            P(None, "mp"),
            P("mp"),
            P("mp", "dp"),
            P(),
            P("dp", "mp"),
            P("mp", "dp"),
            P(),
            P(),
            P(),
        ),
        check_vma=False,
    )
```

```python
import functools

import jax
import jax.numpy as jnp
from jax import lax
from jax.experimental import pallas as pl
from jax.experimental.pallas import tpu as pltpu
from jax.sharding import PartitionSpec as P

HEAD = 64
REL_LEFT = 64
REL_RIGHT = 8
BQ = 128
WIN = 4 * BQ


epsilon = 1e-05


def nt(a, b):
    return lax.dot_general(a, b, (((1,), (1,)), ((), ())), preferred_element_type=jnp.float32)
def nn(a, b):
    return lax.dot_general(a, b, (((1,), (0,)), ((), ())), preferred_element_type=jnp.float32)
def tn(a, b):
    return lax.dot_general(a, b, (((0,), (0,)), ((), ())), preferred_element_type=jnp.float32)

MESH = pl.DeviceIdType.MESH
CHUNKS = 4
TABLE_ROWS = 40
PIECE = 256
VMEM_LIMIT = 58 << 20


def silu_pair(h):
    sig = jax.nn.sigmoid(h)
    act = h * sig
    return act, sig + act * (1.0 - sig)


def unit_norm(s):
    centred = s - jnp.mean(s, -1, keepdims=True)
    inverse = lax.rsqrt(jnp.mean(centred * centred, -1, keepdims=True) + epsilon)
    return centred * inverse, inverse


def fold8(x):
    return jnp.sum(x.reshape(x.shape[0] // 8, 8, x.shape[1]), 0)


def norm_pull(grad, s, gain):
    unit, inverse = unit_norm(s)
    scaled = grad * gain
    first = jnp.mean(scaled, -1, keepdims=True)
    second = jnp.mean(scaled * unit, -1, keepdims=True)
    return inverse * (scaled - first - unit * second), fold8(grad * unit)


def in_hbm():
    return pl.BlockSpec(memory_space=pltpu.HBM)


class Grad:
    def __init__(self, array, bit, turned):
        self.array, self.bit, self.turned = array, bit, turned


def halved(shape, turned):
    pieces, pairs, _, block, cols = shape
    if pairs > 1:
        return jax.ShapeDtypeStruct((pieces, pairs // 2, 2, block, cols), jnp.bfloat16)
    if turned and block % 128 == 0:
        return jax.ShapeDtypeStruct((pieces * cols, block), jnp.float32)
    return jax.ShapeDtypeStruct((block, pieces * cols), jnp.float32)


def arriving(shape):
    return pltpu.VMEM((shape[0], shape[1]) + tuple(shape[3:]), jnp.bfloat16)


def place(dp, bit):
    own = (dp // 2**bit) % 2
    return own, dp + 2**bit * (1 - 2 * own)


def halving_copy(src, landing, piece, bit, send, recv, slot):
    dp, mp = lax.axis_index("dp"), lax.axis_index("mp")
    own, partner = place(dp, bit)
    return pltpu.make_async_remote_copy(
        src.at[piece, :, 1 - own], landing.at[piece], send.at[slot], recv.at[slot],
        device_id=(partner, mp), device_id_type=MESH,
    )


def halving_keep(src, kept, bit, sem):
    own, _ = place(lax.axis_index("dp"), bit)
    return pltpu.make_async_copy(src.at[:, :, own], kept, sem)


def region(ref, piece, cols, turned):
    if len(ref.shape) > 2:
        return ref.at[piece]
    at = pl.ds(piece * cols, cols)
    return ref.at[at, :] if turned else ref.at[:, at]


def halving_add(held, landing, out, piece, turned):
    pairs, block, cols = landing.shape[1:]
    f32 = jnp.float32
    if pairs == 1:
        total = held(piece, 0).astype(f32) + landing[piece, 0].astype(f32)
        turned = turned and block % 128 == 0
        region(out, piece, cols, turned)[...] = total.T if turned else total
        return

    def add(j, c):
        total = held(piece, j).astype(f32) + landing[piece, j].astype(f32)
        out[piece, j // 2, j % 2] = total.astype(jnp.bfloat16)
        return c

    lax.fori_loop(0, pairs, add, 0)


def weight(lhs, rhs, where, turned, deep=1, lo=0, pieces=None):
    cols = sum(r.shape[1] for r in rhs) if isinstance(rhs, tuple) else rhs.shape[1]
    return lhs, rhs, where, turned, deep, lo, cols // PIECE if pieces is None else pieces


def flat_shape(array):
    if isinstance(array, tuple):
        return array[0].shape[0], sum(a.shape[1] for a in array)
    if len(array.shape) == 3:
        return array.shape[1], array.shape[0] * array.shape[2]
    return array.shape


def gain_row(ref, i, width):
    first = i * width // 128
    return jnp.concatenate([ref[first + j : first + j + 1, :] for j in range(width // 128)], 1)


class Riders:
    def __init__(self, grads):
        self.plan = [(g.array.shape[0], g.bit, g.turned) for g in grads]
        self.arrays = [g.array for g in grads]
        self.after = [halved(g.array.shape, g.turned) for g in grads]
        self.slots = sum(x[0] for x in self.plan)
        self.scratch = [arriving(g.array.shape) for g in grads] * 2 + [pltpu.VMEM(a.shape, a.dtype) for a in self.after]
        if grads:
            self.scratch += [pltpu.SemaphoreType.DMA((self.slots,))] * 3 + [pltpu.SemaphoreType.DMA((len(grads),))]

    def bind(self, srcs, outs, scratch):
        n = len(self.plan)
        sems = scratch[3 * n :]
        holds, hops, slot = [], [], 0
        for i, (pieces, bit, turned) in enumerate(self.plan):
            landing, keep, half = scratch[i], scratch[n + i], scratch[2 * n + i]
            holds.append(halving_keep(srcs[i], keep, bit, sems[3].at[i]))
            flip = turned and landing.shape[2] % 128 == 0
            for p in range(pieces):
                move = halving_copy(srcs[i], landing, p, bit, sems[0], sems[1], slot)
                store = pltpu.make_async_copy(region(half, p, PIECE, flip), region(outs[i], p, PIECE, flip), sems[2].at[slot])
                hops.append((move, store, lambda q, j, keep=keep: keep[q, j], landing, half, p, turned))
                slot += 1
        self.holds, self.hops = holds, hops

    def targets(self):
        dp, mp = lax.axis_index("dp"), lax.axis_index("mp")
        return [(place(dp, b)[1], mp) for b in sorted({x[1] for x in self.plan})]

    def start(self):
        for hold in self.holds:
            hold.start()
        for hop in self.hops:
            hop[0].start()

    def finish(self):
        for hold in self.holds:
            hold.wait()
        for hop in self.hops:
            hop[0].wait_recv()
            halving_add(*hop[2:])
            hop[1].start()
        for hop in self.hops:
            hop[0].wait_send()
            hop[1].wait()

    def results(self, outs):
        return [Grad(a, b + 1, t) for a, (_, b, t) in zip(outs, self.plan)]


def greet(targets):
    barrier = pltpu.get_barrier_semaphore()
    for to in targets:
        pl.semaphore_signal(barrier, inc=1, device_id=to, device_id_type=MESH)
    return lambda: pl.semaphore_wait(barrier, len(targets))


def stage(name, cid, rows, width, count, gains, *, leave=None, enter=None, dws=(), grads=(), small=None, last=False, junction, row_in=(), row_out=(), sums=0):
    chunk = rows // CHUNKS
    frames = rows * 4
    bits_all = count.bit_length() - 1
    f32, bf = jnp.float32, jnp.bfloat16
    ins, vm_ins, out_shape, scratch = [], [], [], []
    known = {}

    def add_in(array, direct=False):
        if direct:
            ins.append(array)
            return len(ins) - 1
        if id(array) not in known:
            group = array if isinstance(array, tuple) else (array,)
            known[id(array)] = len(vm_ins)
            vm_ins.append((len(ins), len(group), pltpu.VMEM(flat_shape(array), group[0].dtype)))
            ins.extend(group)
        return known[id(array)]

    out_slots = [0]

    def add_out(shape, dtype, slots):
        out_shape.append(jax.ShapeDtypeStruct(shape, dtype))
        first = out_slots[0]
        out_slots[0] += slots
        return len(out_shape) - 1, first

    def add_scratch(item):
        scratch.append(item)
        return len(scratch) - 1

    if leave:
        front_in = [(add_in(d[0]), add_in(d[1])) for d in dws if d[2] == "front"]
        x_i, wl_i = add_in(leave[0]), add_in(leave[1])
        leave_s = [add_scratch(pltpu.VMEM((rows, width), f32)) for _ in range(2)]
        leave_s += [add_scratch(pltpu.VMEM((rows, width), bf)) for _ in range(6)]
        wl_s = add_scratch(pltpu.VMEM(flat_shape(leave[1])[::-1], bf)) if leave[2] else None
    dw_in = [(add_in(d[0]), add_in(d[1])) for d in dws if d[2] != "join"]
    gains_i = add_in(gains)
    gain_s = add_scratch(pltpu.VMEM((8, width), f32))
    row_i = [add_in(r) for r in row_in]
    dw_join = [(add_in(d[0]), add_in(d[1])) for d in dws if d[2] == "join"]
    if enter:
        we_i = add_in(enter[0])
        extra_i = [add_in(e) for e in enter[3]]
        we_s = add_scratch(pltpu.VMEM(flat_shape(enter[0])[::-1], bf)) if enter[1] else None
        all_o = add_out((frames, width), bf, 4 * CHUNKS)
        e_o = [add_out((frames, c), d, 4 * CHUNKS) for c, d in enter[4]]
    r_o = [add_out((rows, width), d, CHUNKS) for d in row_out]
    s_o = [add_out((8, width), f32, 1) for _ in range(sums)]
    fixed_out = len(out_shape)
    plan, join_o = [], []
    for lhs, rhs, where, turned, deep, lo, pieces in dws:
        shape = (pieces, count // 2, 2, width // count, PIECE)
        if where == "join":
            join_o.append(add_out(shape, bf, shape[0]))
        else:
            plan.append((shape, 0, turned, bits_all if last else min(deep, bits_all), add_scratch(pltpu.VMEM(shape, bf)), None, None))
    first_grad = len(plan)
    for g in grads:
        shape = g.array.shape
        plan.append((shape, g.bit, g.turned, bits_all if last else g.bit + 1, None, add_in(g.array, True), add_scratch(arriving(shape))))
    chains = []
    slots = 0
    for shape, bit, turned, end, src_s, src_i, keep_s in plan:
        links = []
        pieces = shape[0]
        for b in range(bit, end):
            nxt = halved(shape, turned)
            final = b == end - 1
            land_s = add_scratch(arriving(shape))
            if final:
                links.append((b, slots, land_s, None, add_out(nxt.shape, nxt.dtype, pieces)))
            else:
                links.append((b, slots, land_s, add_scratch(pltpu.VMEM(nxt.shape, nxt.dtype)), None))
            slots += pieces
            shape = nxt.shape
        chains.append((pieces, turned, src_s, src_i, keep_s, links))
    if small:
        vectors_in, table_in, taps_in = small
        vector_i = [add_in(v) for v in vectors_in]
        small_shapes = [(1 + len(vectors_in), width)]
        if table_in is not None:
            table_i, taps_i = add_in(table_in), add_in(taps_in)
            small_shapes += [(TABLE_ROWS, 128), taps_in.shape]
        small_o = [add_out(s, f32, 1) for s in small_shapes]
        if last:
            course = ["sib", "far"] + list(range(bits_all - 1, -1, -1))
        else:
            course = list(range(bits_all - 1, -1, -1)) + ["sib", "far"]
        land_small = [add_scratch(pltpu.VMEM((len(course),) + s, f32)) for s in small_shapes]
        small_sems = [add_scratch(pltpu.SemaphoreType.DMA((3, len(course)))) for _ in range(2)]
    if slots:
        grad_sems = [add_scratch(pltpu.SemaphoreType.DMA((slots,))) for _ in range(2)]
    ring_sems = [add_scratch(pltpu.SemaphoreType.DMA((6, CHUNKS))) for _ in range(2)]
    load_sem = add_scratch(pltpu.SemaphoreType.DMA((len(ins),)))
    store_sem = add_scratch(pltpu.SemaphoreType.DMA((out_slots[0],)))
    n_in, n_out, n_scratch = len(ins), len(out_shape), len(scratch)
    vm_at = [add_scratch(item[2]) for item in vm_ins]
    vo_at = [add_scratch(pltpu.VMEM(o.shape, o.dtype)) for o in out_shape]

    def kernel(*refs):
        hbm_in, hbm_out, t = refs[:n_in], refs[n_in : n_in + n_out], refs[n_in + n_out :]
        vin = lambda i: t[vm_at[i]]
        vout = lambda i: t[vo_at[i]]
        waited = set()

        def load(i):
            first, parts, _ = vm_ins[i]
            if len(hbm_in[first].shape) == 3:
                slabs, _, cols = hbm_in[first].shape
                return [
                    pltpu.make_async_copy(hbm_in[first].at[n], vin(i).at[:, pl.ds(n * cols, cols)], t[load_sem].at[first])
                    for n in range(slabs)
                ]
            if parts == 1:
                return [pltpu.make_async_copy(hbm_in[first], vin(i), t[load_sem].at[first])]
            copies, at = [], 0
            for n in range(first, first + parts):
                cols = hbm_in[n].shape[1]
                copies.append(pltpu.make_async_copy(hbm_in[n], vin(i).at[:, pl.ds(at, cols)], t[load_sem].at[n]))
                at += cols
            return copies

        def need(*items):
            for i in items:
                if i not in waited:
                    waited.add(i)
                    for cp in load(i):
                        cp.wait()

        dp, me = lax.axis_index("dp"), lax.axis_index("mp")
        core, chip = me % 2, me // 2
        sib = chip * 2 + 1 - core
        far = (1 - chip) * 2 + core
        diag = (1 - chip) * 2 + 1 - core
        bits = sorted({link[0] for ch in chains for link in ch[5]} | set(range(bits_all) if small else ()))
        meet = greet([(dp, sib), (dp, far)] + [(place(dp, b)[1], me) for b in bits])
        for i in range(len(vm_ins)):
            for cp in load(i):
                cp.start()

        def part(ref, block, k):
            return ref.at[pl.ds(pl.multiple_of(block * rows + k * chunk, chunk), chunk)]

        def store_rows(o, block, k):
            i, first = o
            return pltpu.make_async_copy(part(vout(i), block, k), part(hbm_out[i], block, k), t[store_sem].at[first + block * CHUNKS + k])

        def store_whole(o):
            i, first = o
            return pltpu.make_async_copy(vout(i), hbm_out[i], t[store_sem].at[first])

        def store_piece(o, piece, cols, turned):
            i, first = o
            return pltpu.make_async_copy(
                region(vout(i), piece, cols, turned), region(hbm_out[i], piece, cols, turned), t[store_sem].at[first + piece]
            )

        def copy(kind, k, src, dst, to):
            return pltpu.make_async_remote_copy(
                src, dst, t[ring_sems[0]].at[kind, k], t[ring_sems[1]].at[kind, k], device_id=(dp, to), device_id_type=MESH
            )

        if leave:
            px, own, sb, sr, xs, xr, ob, orv = [t[s] for s in leave_s]
            x_ref = vin(x_i)
            wl_ref = t[wl_s] if leave[2] else vin(wl_i)
        if enter:
            all_ref = vout(all_o[0])
            we_ref = t[we_s] if enter[1] else vin(we_i)
        pair_send = lambda k: copy(0, k, part(sb, 0, k), part(sr, 0, k), sib)
        far_send = lambda k: copy(1, k, part(xs, 0, k), part(xr, 0, k), far)
        own_send = lambda k: copy(2, k, part(ob, 0, k), part(orv, 0, k), sib)
        all_far = lambda k: copy(3, k, part(all_ref, me, k), part(all_ref, me, k), far)
        all_sib = lambda k: copy(4, k, part(all_ref, me, k), part(all_ref, me, k), sib)
        all_fwd = lambda k: copy(5, k, part(all_ref, far, k), part(all_ref, far, k), sib)
        got_far = lambda k: copy(3, k, part(all_ref, far, k), part(all_ref, far, k), far)
        got_sib = lambda k: copy(4, k, part(all_ref, sib, k), part(all_ref, sib, k), sib)
        got_diag = lambda k: copy(5, k, part(all_ref, diag, k), part(all_ref, diag, k), sib)

        def source(c, step):
            pieces, turned, src_s, src_i, keep_s, links = chains[c]
            if step:
                return t[links[step - 1][3]]
            return t[src_s] if src_s is not None else hbm_in[src_i]

        def hop(c, step, piece):
            b, slot, land_s, _, _ = chains[c][5][step]
            return halving_copy(source(c, step), t[land_s], piece, b, t[grad_sems[0]], t[grad_sems[1]], slot + piece)

        def keep(c):
            return halving_keep(hbm_in[chains[c][3]], t[chains[c][4]], chains[c][5][0][0], t[load_sem].at[chains[c][3]])

        kept = set()

        def settle(c, step, piece):
            pieces, turned, src_s, src_i, keep_s, links = chains[c]
            b, slot, land_s, out_s, out_o = links[step]
            hop(c, step, piece).wait_recv()
            if step == 0 and src_s is None:
                if c not in kept:
                    kept.add(c)
                    keep(c).wait()
                held = lambda p, j: t[keep_s][p, j]
            else:
                own_bit, _ = place(dp, b)
                src = source(c, step)
                held = lambda p, j: src[p, j, own_bit]
            landing = t[land_s]
            out = t[out_s] if out_o is None else vout(out_o[0])
            halving_add(held, landing, out, piece, turned)
            if out_o is not None:
                store_piece(out_o, piece, PIECE, turned and landing.shape[2] % 128 == 0).start()

        for c in range(first_grad, len(chains)):
            keep(c).start()
        meet()
        for c in range(first_grad, len(chains)):
            for p in range(chains[c][0]):
                hop(c, 0, p).start()
        for o in s_o:
            vout(o[0])[...] = jnp.zeros((8, width), f32)

        def fill(k, where):
            n_far, n_join = 0, 0
            for lhs, rhs, at_loop, turned, deep, lo, pieces in dws:
                if at_loop == "join":
                    (a, b), o, c = dw_join[n_join], join_o[n_join], None
                    n_join += 1
                else:
                    (a, b), c = dw_in[n_far], n_far
                    n_far += 1
                if at_loop != where:
                    continue
                dw = vout(o[0]) if c is None else t[chains[c][2]]

                @pl.when(k < dw.shape[0])
                def _(a=a, b=b, dw=dw, c=c, o=o if c is None else None, lo=lo):
                    g = tn(vin(a)[...], vin(b)[:, pl.ds(pl.multiple_of((lo + k) * PIECE, PIECE), PIECE)])
                    dw[k] = g.astype(bf).reshape(dw.shape[1:])
                    if c is None:
                        store_piece(o, k, PIECE, False).start()
                    else:
                        hop(c, 0, k).start()

        def need_for(where):
            for (a, b), d in zip(dw_in, [d for d in dws if d[2] != "join"]):
                if d[2] == where:
                    need(a, b)

        if leave:
            if front_in:
                need_for("front")

                def front(k, c):
                    fill(k, "front")
                    return c

                lax.fori_loop(0, CHUNKS, front, 0)
            need(x_i, wl_i)
            if leave[2]:
                wl_ref[...] = vin(wl_i)[...].T
            need_for("far")

            def two(k, block_a, block_b):
                lhs = jnp.concatenate([part(x_ref, block_a, k)[...], part(x_ref, block_b, k)[...]], 0)
                return nn(lhs, wl_ref[...])

            def push(k):
                pair_send(k).wait_recv()
                part(xs, 0, k)[...] = (part(px, 0, k)[...] + part(sr, 0, k)[...].astype(f32)).astype(bf)
                far_send(k).start()

            def out_far(k, c):
                p = two(k, far, diag)
                part(px, 0, k)[...] = p[:chunk]
                part(sb, 0, k)[...] = p[chunk:].astype(bf)
                pair_send(k).start()

                @pl.when(k > 0)
                def _():
                    push(k - 1)

                fill(k, "far")
                return c

            lax.fori_loop(0, CHUNKS, out_far, 0)
            need_for("near")

            def out_near(k, c):
                p = two(k, me, sib)
                part(own, 0, k)[...] = p[:chunk]
                part(ob, 0, k)[...] = p[chunk:].astype(bf)
                own_send(k).start()

                @pl.when(k == 0)
                def _():
                    push(CHUNKS - 1)

                fill(k, "near")
                return c

            lax.fori_loop(0, CHUNKS, out_near, 0)
        need(gains_i, *row_i)
        for i in range(5):
            t[gain_s][i : i + 1, :] = gain_row(vin(gains_i), i, width)
        for a, b in dw_join:
            need(a, b)
        if enter and enter[1]:
            need(we_i)
            we_ref[...] = vin(we_i)[...].T

        def join(k, c):
            fill(k, "join")
            branch = None
            if leave:
                own_send(k).wait_recv()
                far_send(k).wait_recv()
                branch = part(own, 0, k)[...] + part(orv, 0, k)[...].astype(f32) + part(xr, 0, k)[...].astype(f32)
            fresh = junction(
                branch, [part(vin(r), 0, k)[...] for r in row_i], t[gain_s], [part(vout(o[0]), 0, k) for o in r_o], [vout(o[0]) for o in s_o]
            )
            if enter:
                part(all_ref, me, k)[...] = fresh
                all_far(k).start()
                all_sib(k).start()
            for o in r_o:
                store_rows(o, 0, k).start()
            return c

        lax.fori_loop(0, CHUNKS, join, 0)
        for o in s_o:
            store_whole(o).start()

        if small:
            need(*vector_i)
            rows_ref = vout(small_o[0][0])
            for i, v in enumerate([vout(s_o[0][0])] + [vin(i) for i in vector_i]):
                rows_ref[i : i + 1, :] = jnp.sum(v[...], 0, keepdims=True)
            if table_in is not None:
                need(table_i, taps_i)
                both = vin(table_i)[...]
                both = both + pltpu.roll(both, 64, 1)
                left = lax.broadcasted_iota(jnp.int32, (TABLE_ROWS, 128), 1) < HEAD
                vout(small_o[1][0])[...] = jnp.where(left, both[:TABLE_ROWS], both[TABLE_ROWS : 2 * TABLE_ROWS])
                vout(small_o[2][0])[...] = vin(taps_i)[...]

            def double(n):
                at = course[n]
                to = (dp, sib) if at == "sib" else (dp, far) if at == "far" else (place(dp, at)[1], me)
                return [
                    (
                        pltpu.make_async_remote_copy(
                            vout(o[0]), t[l].at[n], t[small_sems[0]].at[i, n], t[small_sems[1]].at[i, n],
                            device_id=to, device_id_type=MESH,
                        ),
                        vout(o[0]),
                        t[l].at[n],
                    )
                    for i, (o, l) in enumerate(zip(small_o, land_small))
                    if i < 2 or not isinstance(at, str)
                ]

            def advance(n):
                for cp, r, l in double(n):
                    cp.wait()
                    r[...] += l[...]
                if n + 1 < len(course):
                    for cp, _, _ in double(n + 1):
                        cp.start()

            for cp, _, _ in double(0):
                cp.start()

        lead = [c for c in range(first_grad) if len(chains[c][5]) == 2] if enter else []
        if enter:
            need(we_i, *extra_i)

            def work(k, block_a, block_b):
                lhs = jnp.concatenate([part(all_ref, block_a, k)[...], part(all_ref, block_b, k)[...]], 0)
                h = nn(lhs, we_ref[...])
                for i, block in enumerate((block_a, block_b)):
                    view = lambda ref: part(ref, block, k)
                    enter[2](h[i * chunk : (i + 1) * chunk], [view(vin(r))[...] for r in extra_i], [view(vout(o[0])) for o in e_o])
                    for o in [all_o] + e_o:
                        store_rows(o, block, k).start()

            def gather(k, c):
                got_sib(k).wait_recv()
                work(k, me, sib)
                got_far(k).wait_recv()
                all_fwd(k).start()
                got_diag(k).wait_recv()
                work(k, far, diag)
                if small:
                    for n in range(min(CHUNKS, len(course))):

                        @pl.when(k == n)
                        def _(n=n):
                            advance(n)

                if lead:

                    @pl.when(k == CHUNKS - 2)
                    def _():
                        for ch in lead:
                            for p in range(chains[ch][0]):
                                settle(ch, 0, p)
                                hop(ch, 1, p).start()

                return c

            lax.fori_loop(0, CHUNKS, gather, 0)
            if small:
                for n in range(CHUNKS, len(course)):
                    advance(n)

        pieces = [(c, p) for c in range(len(chains)) for p in range(chains[c][0])]
        order = [x for x in pieces if x[0] >= first_grad] + [x for x in pieces if x[0] < first_grad]
        depth = lambda c: len(chains[c][5])
        begin = lambda c: 1 if c in lead else 0
        deepest = max([depth(c) - begin(c) for c in range(len(chains))] + [0])
        total_slots = max(len(order) + deepest - 1, len(course) if last else 0)
        for slot in range(total_slots):
            if last:
                for n in range(len(course) - 1):
                    if slot == (n if n < 2 else min(3 * n - 3, total_slots - 1)):
                        advance(n)
            for s in reversed(range(deepest)):
                if 0 <= slot - s < len(order):
                    c, p = order[slot - s]
                    step = s + begin(c)
                    if step < depth(c):
                        settle(c, step, p)
                        if step + 1 < depth(c):
                            hop(c, step + 1, p).start()
        if last:
            advance(len(course) - 1)
        if small:
            for o in small_o:
                store_whole(o).start()
        for c in range(len(chains)):
            for s in range(depth(c)):
                for p in range(chains[c][0]):
                    hop(c, s, p).wait_send()
            out_o = chains[c][5][-1][4]
            block = chains[c][5][-1][2]
            for p in range(chains[c][0]):
                store_piece(out_o, p, PIECE, chains[c][1] and t[block].shape[2] % 128 == 0).wait()

        def drain(k, c):
            if leave:
                pair_send(k).wait_send()
                far_send(k).wait_send()
                own_send(k).wait_send()
            if enter:
                all_far(k).wait_send()
                all_sib(k).wait_send()
                all_fwd(k).wait_send()
                for block in range(4):
                    for o in [all_o] + e_o:
                        store_rows(o, block, k).wait()
            for o in r_o:
                store_rows(o, 0, k).wait()
            return c

        lax.fori_loop(0, CHUNKS, drain, 0)
        for o in s_o + (small_o if small else []):
            store_whole(o).wait()
        for o in join_o:
            for p in range(out_shape[o[0]].shape[0]):
                store_piece(o, p, PIECE, False).wait()

    flops = 0
    if leave:
        flops += 2 * frames * flat_shape(leave[1])[1 if leave[2] else 0] * width
    if enter:
        flops += 2 * frames * width * sum(c for c, _ in enter[4])
    flops += sum(2 * frames * width * PIECE * d[6] for d in dws)
    outs = pl.pallas_call(
        kernel,
        in_specs=[in_hbm()] * n_in,
        out_specs=[in_hbm()] * n_out,
        out_shape=out_shape,
        scratch_shapes=scratch,
        compiler_params=pltpu.CompilerParams(collective_id=cid, has_side_effects=True, vmem_limit_bytes=VMEM_LIMIT),
        cost_estimate=pl.CostEstimate(flops=flops, bytes_accessed=60_000_000, transcendentals=0),
        name=name,
    )(*ins)
    fixed, rest = list(outs[:fixed_out]), list(outs[fixed_out:])
    fresh = [Grad(rest.pop(0), 0, d[3]) for d in dws if d[2] == "join"]
    for item in plan:
        fresh.append(Grad(rest.pop(0), item[3], item[2]))
    return fixed + [fresh] + rest


def publish(ends, small, sizes, rel, total):
    flat, outs, where = [], [], []
    f32 = jnp.float32
    for arrays, parts in ends:
        rows = arrays[0].shape[0]
        joined = len(arrays) > 1 and sizes[len(outs)]
        shape = (rows, sum(a.shape[1] for a in arrays)) if not joined else (sum(a.shape[0] for a in arrays), arrays[0].shape[1])
        where.append((len(flat), arrays, joined))
        flat.extend(arrays)
        if parts < 0:
            outs.append((shape, (-parts, shape[0], shape[1] // -parts)))
        else:
            outs.append((shape, (shape[0], parts, shape[1] // parts) if parts else None))
    n, m = len(flat), len(ends)
    width = small[0].shape[1]
    taps = small[3].shape
    split_at = [i for i in range(m) if ends[i][1] > 0]
    slab_at = [i for i in range(m) if ends[i][1] < 0]
    small_shapes = [(1, width)] * 5 + [(HEAD, rel), (taps[0] - 1, taps[1]), (1, taps[1]), (1, 5)]

    def kernel(*refs):
        src, small_in = refs[:n], refs[n : n + 4]
        dst, small_out = refs[n + 4 : n + 4 + m], refs[n + 4 + m : n + 13 + m]
        rest = refs[n + 13 + m :]
        held, split = rest[:m], dict(zip(split_at, rest[m:-1]))
        sem = rest[-1]
        loads, stores = [], []
        for i, (first, arrays, joined) in enumerate(where):
            at, copies = 0, []
            for k in range(len(arrays)):
                ref = src[first + k]
                size = ref.shape[0 if joined else 1]
                part = held[i].at[pl.ds(at, size)] if joined else held[i].at[:, pl.ds(at, size)]
                copies.append(pltpu.make_async_copy(ref, part, sem.at[first + k]))
                at += size
            loads.append(copies)
            if i in slab_at:
                slabs, _, cols = dst[i].shape
                stores.append(
                    [
                        pltpu.make_async_copy(held[i].at[:, pl.ds(k * cols, cols)], dst[i].at[k], sem.at[n + m + k])
                        for k in range(slabs)
                    ]
                )
            else:
                stores.append([pltpu.make_async_copy(split.get(i, held[i]), dst[i], sem.at[n + i])])
        for copies in loads:
            for cp in copies:
                cp.start()
        lead, rows, table, tap = [r[...] for r in small_in]
        small_out[0][...] = lead
        for i in range(4):
            small_out[1 + i][...] = rows[i : i + 1]
        turned = jnp.concatenate([table, jnp.zeros((128 - TABLE_ROWS, 128), f32)], 0).T
        small_out[5][:, :TABLE_ROWS] = turned[:HEAD, :TABLE_ROWS]
        small_out[5][:, TABLE_ROWS:] = turned[HEAD:, : rel - TABLE_ROWS]
        small_out[6][...] = tap[:-1]
        small_out[7][...] = tap[-1:]
        square = jnp.sum(rows, -1, keepdims=True) / total
        lane = lax.broadcasted_iota(jnp.int32, (rows.shape[0], 128), 1)
        row = lax.broadcasted_iota(jnp.int32, (rows.shape[0], 128), 0)
        root = jnp.sqrt(jnp.sum(jnp.where(row == lane + 4, square, 0.0), 0, keepdims=True))
        small_out[8][...] = root[:, :5]
        for i in range(m):
            for cp in loads[i]:
                cp.wait()
            if i in split:
                cols = split[i].shape[2]
                for j in range(split[i].shape[1]):
                    split[i][:, j, :] = held[i][:, j * cols : (j + 1) * cols]
            for cp in stores[i]:
                cp.start()
        for copies in stores:
            for cp in copies:
                cp.wait()

    vm = pl.BlockSpec(memory_space=pltpu.VMEM)
    return pl.pallas_call(
        kernel,
        in_specs=[in_hbm()] * n + [vm] * 4,
        out_specs=[in_hbm()] * m + [vm] * 9,
        out_shape=[jax.ShapeDtypeStruct(o[1] or o[0], f32) for o in outs] + [jax.ShapeDtypeStruct(s, f32) for s in small_shapes],
        scratch_shapes=[pltpu.VMEM(o[0], f32) for o in outs]
        + [pltpu.VMEM(outs[i][1], f32) for i in split_at]
        + [pltpu.SemaphoreType.DMA((n + m + 4,))],
        compiler_params=pltpu.CompilerParams(vmem_limit_bytes=VMEM_LIMIT),
        name="publish",
    )(*flat, *small)


SPAN = 128


def exchange(stats, landing, send, recv):
    dp, me = lax.axis_index("dp"), lax.axis_index("mp")
    core, chip = me % 2, me // 2
    others = [chip * 2 + 1 - core, (1 - chip) * 2 + core, (1 - chip) * 2 + 1 - core]
    return [
        pltpu.make_async_remote_copy(
            stats, landing.at[i], send.at[i], recv.at[i], device_id=(dp, to), device_id_type=MESH
        )
        for i, to in enumerate(others)
    ]


def group_targets():
    dp, me = lax.axis_index("dp"), lax.axis_index("mp")
    core, chip = me % 2, me // 2
    return [(dp, chip * 2 + 1 - core), (dp, (1 - chip) * 2 + core), (dp, (1 - chip) * 2 + 1 - core)]


def to_rows(first, second):
    lane = lax.broadcasted_iota(jnp.int32, (SPAN, SPAN), 1)
    both = jnp.where(lane == 0, first, jnp.where(lane == 1, second, 0.0))
    return both.T[:8]


def to_columns(rows8):
    return jnp.concatenate([rows8, jnp.zeros((SPAN - 8, SPAN), jnp.float32)], 0).T


def shifted(window, by):
    return window if by == 0 else pltpu.roll(window, window.shape[0] - by, 0)


def depth_gain_row(ref, width, chans):
    first = 5 * width // 128
    return jnp.concatenate([ref[first + j : first + j + 1, :] for j in range(chans // 128)], 1)


def conv_mid(glu, w_depth, gains, width, cid):
    frames, chans = glu.shape
    taps = w_depth.shape[0]
    reach = taps - 1
    edge = (reach + 7) // 8 * 8
    f32, bf = jnp.float32, jnp.bfloat16
    tiles, lanes = frames // SPAN, chans // 128

    def kernel(glu_h, w_h, g_h, act_h, slope_h, unit_h, stat_h, pad, w_raw, g_raw, w_v, g_v, act, slope, unit, stat, sendbuf, landing, lsem, ssem, send, recv):
        meet = greet(group_targets())
        loads = [
            pltpu.make_async_copy(glu_h, pad.at[pl.ds(edge, frames)], lsem.at[0]),
            pltpu.make_async_copy(w_h, w_raw, lsem.at[1]),
            pltpu.make_async_copy(g_h, g_raw, lsem.at[2]),
        ]
        for cp in loads:
            cp.start()
        pad[:edge, :] = jnp.zeros((edge, chans), f32)
        for cp in loads:
            cp.wait()
        w_v[...] = w_raw[...].astype(f32)
        g_v[...] = depth_gain_row(g_raw, width, chans)

        def tile(i, c):
            at = pl.multiple_of(i * SPAN, SPAN)
            for lane in range(lanes):
                cols = slice(lane * 128, (lane + 1) * 128)
                window = pad[pl.ds(at, SPAN + edge), cols]
                total = jnp.zeros((SPAN, 128), f32)
                for by in range(8):
                    moved = shifted(window, by)
                    for base in range(0, edge + 1, 8):
                        tap = base + by - (edge - reach)
                        if 0 <= tap < taps:
                            total = total + w_v[tap : tap + 1, cols] * moved[base : base + SPAN]
                unit[pl.ds(at, SPAN), cols] = total
            depth = unit[pl.ds(at, SPAN), :]
            mean = jnp.mean(depth, -1, keepdims=True)
            centred = depth - mean
            sendbuf[:, pl.ds(at, SPAN)] = to_rows(mean, jnp.sum(centred * centred, -1, keepdims=True))
            return c

        lax.fori_loop(0, tiles, tile, 0)
        meet()
        copies = exchange(sendbuf, landing, send, recv)
        for cp in copies:
            cp.start()
        for cp in copies:
            cp.wait_recv()
        rows = [sendbuf[...]] + [landing[i] for i in range(3)]
        mean = sum(r[0:1] for r in rows) * 0.25
        spread = sum(r[1:2] + chans * (r[0:1] - mean) * (r[0:1] - mean) for r in rows) / width
        inverse = lax.rsqrt(spread + epsilon)
        row = lax.broadcasted_iota(jnp.int32, (8, frames), 0)
        stat[...] = jnp.where(row == 0, mean, jnp.where(row == 1, inverse, 0.0))
        outs = [(act, act_h), (slope, slope_h), (unit, unit_h)]

        def store(i, n):
            at = pl.ds(pl.multiple_of(i * SPAN, SPAN), SPAN)
            return pltpu.make_async_copy(outs[n][0].at[at], outs[n][1].at[at], ssem.at[n, i])

        def finish(i, c):
            at = pl.multiple_of(i * SPAN, SPAN)
            cols = to_columns(stat[:, pl.ds(at, SPAN)])
            u = (unit[pl.ds(at, SPAN), :] - cols[:, 0:1]) * cols[:, 1:2]
            a, s = silu_pair(u * g_v[...])
            unit[pl.ds(at, SPAN), :] = u
            act[pl.ds(at, SPAN), :] = a.astype(bf)
            slope[pl.ds(at, SPAN), :] = s.astype(bf)
            for n in range(3):
                store(i, n).start()
            return c

        lax.fori_loop(0, tiles, finish, 0)
        last = pltpu.make_async_copy(stat, stat_h, lsem.at[0])
        last.start()
        for cp in copies:
            cp.wait_send()
        for i in range(tiles):
            for n in range(3):
                store(i, n).wait()
        last.wait()

    S = jax.ShapeDtypeStruct
    out_shape = [S((frames, chans), bf), S((frames, chans), bf), S((frames, chans), f32), S((8, frames), f32)]
    vm = pltpu.VMEM
    return pl.pallas_call(
        kernel,
        in_specs=[in_hbm()] * 3,
        out_specs=[in_hbm()] * 4,
        out_shape=out_shape,
        scratch_shapes=[
            vm((frames + edge, chans), f32), vm(w_depth.shape, bf), vm(gains.shape, f32), vm(w_depth.shape, f32), vm((1, chans), f32),
            vm((frames, chans), bf), vm((frames, chans), bf), vm((frames, chans), f32), vm((8, frames), f32),
            vm((8, frames), f32), vm((3, 8, frames), f32),
            pltpu.SemaphoreType.DMA((3,)), pltpu.SemaphoreType.DMA((3, tiles)), pltpu.SemaphoreType.DMA((3,)), pltpu.SemaphoreType.DMA((3,)),
        ],
        compiler_params=pltpu.CompilerParams(collective_id=cid, has_side_effects=True, vmem_limit_bytes=VMEM_LIMIT),
        name="conv_mid",
    )(glu, w_depth, gains)


def conv_mid_back(grad, slope, unit, stat, glu, sig, tail, w_depth, gains, width, cid, grads):
    frames, chans = glu.shape
    taps = w_depth.shape[0]
    reach = taps - 1
    edge = (reach + 7) // 8 * 8
    f32, bf = jnp.float32, jnp.bfloat16
    tiles, lanes = frames // SPAN, chans // 128
    ins = [grad, slope, unit, stat, w_depth, gains, glu, sig, tail]
    riders = Riders(grads)
    n = len(grads)

    def kernel(*refs):
        hbm, ride_in, (pair_h, taps_h), ride_out = refs[:9], refs[9 : 9 + n], refs[9 + n : 11 + n], refs[11 + n : 11 + 2 * n]
        refs = refs[2 * n :]
        (grad_v, slope_v, unit_v, stat_v, w_raw, g_raw, pad, sig_v, tail_v, w_v, g_v, back, pair, taps_v, acc, gacc, sendbuf, landing, lsem, ssem, send, recv) = refs[11:33]
        riders.bind(ride_in, ride_out, refs[33:])
        meet = greet(group_targets() + riders.targets())
        dst = [grad_v, slope_v, unit_v, stat_v, w_raw, g_raw, pad.at[pl.ds(edge, frames)], sig_v, tail_v]
        loads = [pltpu.make_async_copy(h, d, lsem.at[i]) for i, (h, d) in enumerate(zip(hbm, dst))]
        for cp in loads:
            cp.start()
        pad[:edge, :] = jnp.zeros((edge, chans), f32)
        back[frames:, :] = jnp.zeros((edge, chans), f32)
        acc[...] = jnp.zeros_like(acc)
        gacc[...] = jnp.zeros_like(gacc)
        for cp in loads[:6]:
            cp.wait()
        w_v[...] = w_raw[...].astype(f32)
        g_v[...] = depth_gain_row(g_raw, width, chans)

        def first(i, c):
            at = pl.ds(pl.multiple_of(i * SPAN, SPAN), SPAN)
            u = unit_v[at, :]
            de = grad_v[at, :] * slope_v[at, :].astype(f32)
            gacc[...] += fold8(de * u)
            du = de * g_v[...]
            back[at, :] = du
            sendbuf[:, at] = to_rows(jnp.sum(du, -1, keepdims=True), jnp.sum(du * u, -1, keepdims=True))
            return c

        meet()
        riders.start()
        lax.fori_loop(0, tiles, first, 0)
        copies = exchange(sendbuf, landing, send, recv)
        for cp in copies:
            cp.start()
        for cp in loads[6:]:
            cp.wait()
        for cp in copies:
            cp.wait_recv()
        means = (sendbuf[...] + landing[0] + landing[1] + landing[2]) / width
        row = lax.broadcasted_iota(jnp.int32, (8, frames), 0)
        stat_v[...] = jnp.where(row == 1, stat_v[...], jnp.where(row == 0, means[0:1], jnp.where(row == 2, means[1:2], 0.0)))

        def second(i, c):
            at = pl.ds(pl.multiple_of(i * SPAN, SPAN), SPAN)
            cols = to_columns(stat_v[:, at])
            back[at, :] = cols[:, 1:2] * (back[at, :] - cols[:, 0:1] - unit_v[at, :] * cols[:, 2:3])
            return c

        lax.fori_loop(0, tiles, second, 0)

        def store(i):
            at = pl.ds(pl.multiple_of(i * SPAN, SPAN), SPAN)
            return pltpu.make_async_copy(pair.at[at], pair_h.at[at], ssem.at[i])

        def third(i, c):
            at = pl.multiple_of(i * SPAN, SPAN)
            rows = pl.ds(at, SPAN)
            for lane in range(lanes):
                cols = slice(lane * 128, (lane + 1) * 128)
                ahead = back[pl.ds(at, SPAN + edge), cols]
                total = jnp.zeros((SPAN, 128), f32)
                for by in range(8):
                    moved = shifted(ahead, by)
                    for base in range(0, edge, 8):
                        tap = reach - (base + by)
                        if 0 <= tap < taps:
                            total = total + w_v[tap : tap + 1, cols] * moved[base : base + SPAN]
                pair[rows, cols] = (total * sig_v[rows, cols].astype(f32)).astype(bf)
                pair[rows, chans + lane * 128 : chans + (lane + 1) * 128] = (total * tail_v[rows, cols].astype(f32)).astype(bf)
            store(i).start()
            for lane in range(lanes):
                cols = slice(lane * 128, (lane + 1) * 128)
                here = back[rows, cols]
                window = pad[pl.ds(at, SPAN + edge), cols]
                for by in range(8):
                    moved = shifted(window, by)
                    for base in range(0, edge + 1, 8):
                        tap = base + by - (edge - reach)
                        if 0 <= tap < taps:
                            acc[tap * 8 : tap * 8 + 8, cols] += fold8(here * moved[base : base + SPAN])
            return c

        lax.fori_loop(0, tiles, third, 0)
        for tap in range(taps):
            taps_v[tap : tap + 1, :] = jnp.sum(acc[tap * 8 : tap * 8 + 8, :], 0, keepdims=True)
        taps_v[taps : taps + 1, :] = jnp.sum(gacc[...], 0, keepdims=True)
        last = pltpu.make_async_copy(taps_v, taps_h, lsem.at[0])
        last.start()
        for cp in copies:
            cp.wait_send()
        riders.finish()
        for i in range(tiles):
            store(i).wait()
        last.wait()

    S = jax.ShapeDtypeStruct
    vm = pltpu.VMEM
    outs = pl.pallas_call(
        kernel,
        in_specs=[in_hbm()] * (9 + n),
        out_specs=[in_hbm()] * (2 + n),
        out_shape=[S((frames, 2 * chans), bf), S((taps + 1, chans), f32)] + riders.after,
        scratch_shapes=[
            vm((frames, chans), f32), vm((frames, chans), bf), vm((frames, chans), f32), vm((8, frames), f32),
            vm(w_depth.shape, bf), vm(gains.shape, f32), vm((frames + edge, chans), f32), vm((frames, chans), bf), vm((frames, chans), bf),
            vm(w_depth.shape, f32), vm((1, chans), f32),
            vm((frames + edge, chans), f32), vm((frames, 2 * chans), bf), vm((taps + 1, chans), f32), vm((taps * 8, chans), f32), vm((8, chans), f32),
            vm((8, frames), f32), vm((3, 8, frames), f32),
            pltpu.SemaphoreType.DMA((9,)), pltpu.SemaphoreType.DMA((tiles,)), pltpu.SemaphoreType.DMA((3,)), pltpu.SemaphoreType.DMA((3,)),
        ] + riders.scratch,
        compiler_params=pltpu.CompilerParams(collective_id=cid, has_side_effects=True, vmem_limit_bytes=VMEM_LIMIT),
        name="conv_mid_back",
    )(*ins, *riders.arrays)
    return outs[0], outs[1], riders.results(outs[2:])


def split_pair(x):
    left = lax.broadcasted_iota(jnp.int32, x.shape, 1) < HEAD
    zero = jnp.zeros_like(x)
    return jnp.concatenate([jnp.where(left, x, zero), jnp.where(left, zero, x)], 0)

def join_pair(x):
    rows = x.shape[0] // 2
    left = lax.broadcasted_iota(jnp.int32, (rows, x.shape[1]), 1) < HEAD
    return jnp.where(left, x[:rows], x[rows:])

def spot_table(spots):
    spot = lax.broadcasted_iota(jnp.int32, (spots, BQ), 0)
    inner = jnp.clip(spot - REL_LEFT, 0, REL_LEFT + REL_RIGHT)
    row = jnp.where(spot < 3 * BQ, inner, jnp.where(spot < 4 * BQ, 0, REL_LEFT + REL_RIGHT))
    return (lax.broadcasted_iota(jnp.int32, (spots, BQ), 1) == row).astype(jnp.bfloat16)


def wide_table(rel_ref, wide_ref):
    wide_ref[...] = jnp.zeros_like(wide_ref)
    turned = rel_ref[...].astype(jnp.float32)
    cols = turned.shape[1]
    wide_ref[0:HEAD, :cols] = turned
    wide_ref[HEAD : 2 * HEAD, :cols] = turned
    return wide_ref[...].T.astype(jnp.bfloat16)


def fwd_kernel(q_ref, k_ref, v_ref, relt_ref, mixed_ref, probs_ref, bias_ref, rel_ref, wide_ref):
    ib = pl.program_id(1)

    @pl.when((ib == 0) & (pl.program_id(0) == 0))
    def _():
        rel_ref[...] = nn(spot_table(5 * BQ), wide_table(relt_ref, wide_ref)).astype(jnp.bfloat16)

    qs = split_pair(q_ref[...] * 0.125)
    s = nt(qs, k_ref[...])
    b = nt(qs, rel_ref[...])
    rows = b.shape[0] // 2
    bias_ref[:, 0:BQ] = b[:, 3 * BQ : 4 * BQ]
    for h in range(2):
        r = pltpu.roll(b[h * rows : (h + 1) * rows, :WIN], 0, 1, stride=1, stride_axis=0)
        bias_ref[h * rows : (h + 1) * rows, BQ : 4 * BQ] = r[:, : 3 * BQ]
    bias_ref[:, 4 * BQ :] = b[:, 4 * BQ :]
    nkeys = s.shape[1] // BQ
    parts = []
    for jb in range(nkeys):
        at = pl.multiple_of(jnp.clip(jb - ib + 2, 0, 4) * BQ, BQ)
        parts.append(s[:, jb * BQ : (jb + 1) * BQ] + bias_ref[:, pl.ds(at, BQ)])
    top = functools.reduce(jnp.maximum, parts)
    m = jnp.max(top, -1, keepdims=True)
    es = [jnp.exp(p - m) for p in parts]
    tot = jnp.sum(functools.reduce(jnp.add, es), -1, keepdims=True)
    inv = 1.0 / tot
    for jb in range(nkeys):
        probs_ref[0, :, jb * BQ : (jb + 1) * BQ] = (es[jb] * inv).astype(jnp.bfloat16)
    mixed_ref[...] = join_pair(nn(probs_ref[0], v_ref[...])).astype(jnp.bfloat16)

def bwd_kernel(riders, *refs):
    n = len(riders.plan)
    q_ref, k_ref, v_ref, relt_ref, probs_ref, do_ref, db_h, mix_h = refs[:8]
    ride_in = refs[8 : 8 + n]
    dq_ref, dk_ref, dv_ref, dt_ref, dw_h = refs[8 + n : 13 + n]
    ride_out = refs[13 + n : 13 + 2 * n]
    tot_ref, dkt, dvt, dta, dz_ref, hot_ref, db_v, mix_v, dw_v, dw_land, dw_half, relb_ref, wide_ref, osem, psem = refs[13 + 2 * n : 28 + 2 * n]
    riders.bind(ride_in, ride_out, refs[28 + 2 * n :])
    pr, ib, nb = pl.program_id(0), pl.program_id(1), pl.num_programs(1)
    dp, mp = lax.axis_index("dp"), lax.axis_index("mp")
    loads = [pltpu.make_async_copy(db_h, db_v, osem.at[0]), pltpu.make_async_copy(mix_h, mix_v, osem.at[1])]
    pieces = dw_v.shape[0]
    hops = [halving_copy(dw_v, dw_land, p, 0, psem.at[0], psem.at[1], p) for p in range(pieces)]
    flip = dw_land.shape[2] % 128 == 0
    stores = [
        pltpu.make_async_copy(region(dw_half, p, PIECE, flip), region(dw_h, p, PIECE, flip), psem.at[2, p]) for p in range(pieces)
    ]

    @pl.when((ib == 0) & (pr == 0))
    def _():
        meet = greet(sorted_targets(riders, dp, mp))
        for cp in loads:
            cp.start()
        hot_ref[...] = spot_table(WIN)
        relb_ref[...] = wide_table(relt_ref, wide_ref)
        meet()
        riders.start()
        for cp in loads:
            cp.wait()
        for p in range(pieces):
            g = tn(db_v[...], mix_v[:, p * PIECE : (p + 1) * PIECE])
            dw_v[p] = g.astype(jnp.bfloat16).reshape(dw_v.shape[1:])
            hops[p].start()

    @pl.when(ib == 0)
    def _():
        dkt[...] = jnp.zeros_like(dkt)
        dvt[...] = jnp.zeros_like(dvt)
    @pl.when((ib == 0) & (pr == 0))
    def _():
        dta[...] = jnp.zeros_like(dta)
    qs = split_pair(q_ref[...] * 0.125)
    dos = split_pair(do_ref[...])
    p = probs_ref[0]
    dp = nt(dos, v_ref[...])
    nkeys = dp.shape[1] // BQ
    dvt[...] += tn(dos, p)
    pf = p.astype(jnp.float32)
    acc = None
    for jb in range(nkeys):
        sl = slice(jb * BQ, (jb + 1) * BQ)
        t = pf[:, sl] * dp[:, sl]
        acc = t if acc is None else acc + t
    inner = jnp.sum(acc, -1, keepdims=True)
    tot_ref[...] = jnp.zeros_like(tot_ref)
    for jb in range(nkeys):
        sl = slice(jb * BQ, (jb + 1) * BQ)
        dz = (pf[:, sl] * (dp[:, sl] - inner)).astype(jnp.bfloat16)
        dz_ref[:, sl] = dz
        at = pl.multiple_of(jnp.clip(jb - ib + 2, 0, 4) * BQ, BQ)
        tot_ref[:, pl.ds(at, BQ)] += dz.astype(jnp.float32)
    rows = BQ
    r2 = lax.broadcasted_iota(jnp.int32, (2 * rows, 2 * rows), 0)
    c2 = lax.broadcasted_iota(jnp.int32, (2 * rows, 2 * rows), 1)
    mirror = (r2 + c2 == jnp.where(r2 < rows, rows - 1, 3 * rows - 1)).astype(jnp.bfloat16)
    w = jnp.concatenate([tot_ref[:, BQ : 4 * BQ].astype(jnp.bfloat16), jnp.zeros((2 * rows, BQ), jnp.bfloat16)], 1)
    w = nn(mirror, w)
    outs = [pltpu.roll(w[h * rows : (h + 1) * rows], WIN - rows + 1, 1, stride=1, stride_axis=0) for h in range(2)]
    d = nn(mirror, jnp.concatenate(outs, 0).astype(jnp.bfloat16)).astype(jnp.bfloat16)
    drel = nn(d, hot_ref[...])
    col = lax.broadcasted_iota(jnp.int32, drel.shape, 1)
    low = jnp.sum(tot_ref[:, :BQ], -1, keepdims=True)
    high = jnp.sum(tot_ref[:, 4 * BQ :], -1, keepdims=True)
    drel = drel + jnp.where(col == 0, low, 0.0) + jnp.where(col == REL_LEFT + REL_RIGHT, high, 0.0)
    drel = drel.astype(jnp.bfloat16)
    dz = dz_ref[...]
    dq = nn(dz, k_ref[...]) + nn(drel, relb_ref[...])
    dq_ref[...] = (join_pair(dq) * 0.125).astype(jnp.bfloat16)
    dkt[...] += tn(qs, dz)
    dta[...] += tn(drel, qs)
    @pl.when(ib == nb - 1)
    def _():
        dk_ref[...] = dkt[...].T.astype(jnp.bfloat16)
        dv_ref[...] = dvt[...].T.astype(jnp.bfloat16)
        dt_ref[...] = dta[...]

    @pl.when((ib == nb - 1) & (pr == pl.num_programs(0) - 1))
    def _():
        own, _ = place(lax.axis_index("dp"), 0)
        for p in range(pieces):
            hops[p].wait_recv()
            halving_add(lambda q, j: dw_v[q, j, own], dw_land, dw_half, p, True)
            stores[p].start()
        riders.finish()
        for p in range(pieces):
            hops[p].wait_send()
            stores[p].wait()


def sorted_targets(riders, dp, mp):
    return [(place(dp, b)[1], mp) for b in sorted({0} | {x[1] for x in riders.plan})]


def attn_fwd(qkv, rel):
    frames, cols = qkv.shape
    pairs = cols // 3 // 128
    nb = frames // BQ
    bf = jnp.bfloat16
    return pl.pallas_call(
        fwd_kernel,
        grid=(pairs, nb),
        in_specs=[
            pl.BlockSpec((BQ, 128), lambda p, i: (i, p)),
            pl.BlockSpec((frames, 128), lambda p, i: (0, pairs + p)),
            pl.BlockSpec((frames, 128), lambda p, i: (0, 2 * pairs + p)),
            pl.BlockSpec(rel.shape, lambda p, i: (0, 0)),
        ],
        out_specs=[
            pl.BlockSpec((BQ, 128), lambda p, i: (i, p)),
            pl.BlockSpec((1, 2 * BQ, frames), lambda p, i: (p, i, 0)),
        ],
        out_shape=[jax.ShapeDtypeStruct((frames, cols // 3), bf), jax.ShapeDtypeStruct((pairs, 2 * frames, frames), bf)],
        scratch_shapes=[pltpu.VMEM((2 * BQ, 5 * BQ), jnp.float32), pltpu.VMEM((5 * BQ, 128), bf), pltpu.VMEM((128, 128), jnp.float32)],
        compiler_params=pltpu.CompilerParams(vmem_limit_bytes=VMEM_LIMIT),
        name="attn_fwd",
    )(qkv, qkv, qkv, rel)

def attn_bwd(qkv, rel, probs, dmixed, grad_rows, mixed, grads, cid):
    frames, cols = qkv.shape
    pairs = cols // 3 // 128
    nb = frames // BQ
    bf = jnp.bfloat16
    count = lax.axis_size("dp")
    blk = pl.BlockSpec((BQ, 128), lambda p, i: (i, p))
    full = pl.BlockSpec((frames, 128), lambda p, i: (0, p))
    riders = Riders(grads)
    width = grad_rows.shape[1]
    shape = (mixed.shape[1] // PIECE, count // 2, 2, width // count, PIECE)
    half = halved(shape, True)
    vm = pltpu.VMEM
    outs = pl.pallas_call(
        functools.partial(bwd_kernel, riders),
        grid=(pairs, nb),
        in_specs=[
            blk,
            pl.BlockSpec((frames, 128), lambda p, i: (0, pairs + p)),
            pl.BlockSpec((frames, 128), lambda p, i: (0, 2 * pairs + p)),
            pl.BlockSpec(rel.shape, lambda p, i: (0, 0)),
            pl.BlockSpec((1, 2 * BQ, frames), lambda p, i: (p, i, 0)),
            blk,
        ]
        + [in_hbm()] * (2 + len(grads)),
        out_specs=[blk, full, full, pl.BlockSpec((128, 128), lambda p, i: (0, 0))] + [in_hbm()] * (1 + len(grads)),
        out_shape=[jax.ShapeDtypeStruct((frames, cols // 3), bf)] * 3 + [jax.ShapeDtypeStruct((128, 128), jnp.float32), half] + riders.after,
        scratch_shapes=[
            vm((2 * BQ, 5 * BQ), jnp.float32), vm((128, frames), jnp.float32), vm((128, frames), jnp.float32),
            vm((128, 128), jnp.float32), vm((2 * BQ, frames), bf), vm((WIN, BQ), bf),
            vm(grad_rows.shape, bf), vm(mixed.shape, bf), vm(shape, bf), arriving(shape), vm(half.shape, half.dtype),
            vm((128, 128), bf), vm((128, 128), jnp.float32),
            pltpu.SemaphoreType.DMA((2,)), pltpu.SemaphoreType.DMA((3, shape[0])),
        ]
        + riders.scratch,
        compiler_params=pltpu.CompilerParams(vmem_limit_bytes=VMEM_LIMIT, collective_id=cid, has_side_effects=True),
        cost_estimate=pl.CostEstimate(flops=20 * frames * frames * 128 * pairs, bytes_accessed=20_000_000, transcendentals=0),
        name="attn_bwd",
    )(qkv, qkv, qkv, rel, probs, dmixed, grad_rows, mixed, *riders.arrays)
    return list(outs[:4]) + [[Grad(outs[4], 1, True)] + riders.results(outs[5:])]


def body(
    features,
    w1_in,
    w1_out,
    gain_ffn1,
    w_qkv,
    w_attn_out,
    rel_table,
    gain_attn,
    w_conv_in,
    w_depth,
    gain_depth,
    w_conv_out,
    gain_conv,
    w2_in,
    w2_out,
    gain_ffn2,
    gain_final,
    cotangent,
):
    local_frames, clip_count, width = features.shape
    rows = local_frames * clip_count
    f32, bf = jnp.float32, jnp.bfloat16
    s0 = features.reshape(rows, width)
    seed = cotangent.reshape(rows, width)
    spare = jnp.zeros((width - gain_depth.shape[0],), bf)
    gains = jnp.concatenate([gain_ffn1, gain_attn, gain_conv, gain_ffn2, gain_final, gain_depth, spare])
    gains = gains.astype(f32).reshape(-1, 128)
    flat_qkv = w_qkv.transpose(1, 0, 2)
    flat_conv = w_conv_in.reshape(width, -1)
    units = w1_in.shape[1]
    half = units // PIECE // 2
    dp_count = lax.axis_size("dp")
    done = dp_count.bit_length() - 1
    pending = lambda items: [g for g in items if g.bit < done]
    chans = w_conv_out.shape[0]

    def swish_out(h, extra, outs):
        act, slope = silu_pair(h)
        outs[0][...] = act.astype(bf)
        outs[1][...] = slope.astype(bf)

    def plain_out(h, extra, outs):
        outs[0][...] = h.astype(outs[0].dtype)

    def glu_out(h, extra, outs):
        p0 = h[:, :chans]
        sig = jax.nn.sigmoid(h[:, chans:])
        glu = p0 * sig
        outs[0][...] = glu
        outs[1][...] = sig.astype(bf)
        outs[2][...] = (glu * (1.0 - sig)).astype(bf)

    def slope_out(h, extra, outs):
        outs[0][...] = (h * extra[0][...].astype(f32)).astype(bf)

    def first(branch, ins, gains, outs, sums):
        return (unit_norm(ins[0].astype(f32))[0] * gains[0:1, :]).astype(bf)

    def forward(scale, row):
        def run(branch, ins, gains, outs, sums):
            fresh = ins[0].astype(f32) + scale * branch
            outs[0][...] = fresh
            sums[0][...] += fold8(branch * branch)
            return (unit_norm(fresh)[0] * gains[row : row + 1, :]).astype(bf)
        return run

    def turn(branch, ins, gains, outs, sums):
        fresh = ins[0] + 0.5 * branch
        sums[0][...] += fold8(branch * branch)
        sums[1][...] += fold8(fresh * fresh)
        unit, inverse = unit_norm(fresh)
        outs[0][...] = unit * gains[4:5, :]
        grad = ins[1].astype(f32)
        scaled = grad * gains[4:5, :]
        mean_one = jnp.mean(scaled, -1, keepdims=True)
        mean_two = jnp.mean(scaled * unit, -1, keepdims=True)
        sums[2][...] += fold8(grad * unit)
        back = inverse * (scaled - mean_one - unit * mean_two)
        outs[1][...] = back
        return (0.5 * back).astype(bf)

    def backward(scale, row):
        def run(branch, ins, gains, outs, sums):
            pull, grad_gain = norm_pull(branch, ins[1].astype(f32), gains[row : row + 1, :])
            fresh = ins[0] + pull
            outs[0][...] = fresh
            sums[0][...] += grad_gain
            return (scale * fresh).astype(bf)
        return run

    a1, act1, slope1, _ = stage(
        "ffn1_in", 0, rows, width, dp_count, gains, enter=(w1_in, False, swish_out, (), ((units, bf), (units, bf))),
        junction=first, row_in=(s0,),
    )
    a2, qkv, s1, sq1, _ = stage(
        "ffn1_out", 1, rows, width, dp_count, gains, leave=(act1, w1_out, False),
        enter=(flat_qkv, False, plain_out, (), ((3 * w_qkv.shape[2], bf),)),
        junction=forward(0.5, 1), row_in=(s0,), row_out=(f32,), sums=1,
    )
    turned_table = rel_table.T
    mixed, probs = attn_fwd(qkv, turned_table)
    a3, glu, sig, tail, s2, sq2, _ = stage(
        "attn_out", 2, rows, width, dp_count, gains, leave=(mixed, w_attn_out, False),
        enter=(flat_conv, False, glu_out, (), ((chans, f32), (chans, bf), (chans, bf))),
        junction=forward(1.0, 2), row_in=(s1,), row_out=(f32,), sums=1,
    )
    act3, slope3, depth_unit, depth_stat = conv_mid(glu, w_depth, gains, width, 10)
    a4, act2, slope2, s3, sq3, _ = stage(
        "conv_out", 3, rows, width, dp_count, gains, leave=(act3, w_conv_out, False),
        enter=(w2_in, False, swish_out, (), ((units, bf), (units, bf))),
        junction=forward(1.0, 3), row_in=(s2,), row_out=(f32,), sums=1,
    )
    db4, dh2, output, grad4, sq4, sq5, dgf, _ = stage(
        "ffn2_out", 4, rows, width, dp_count, gains, leave=(act2, w2_out, False),
        enter=(w2_out, True, slope_out, (slope2,), ((units, bf),)),
        junction=turn, row_in=(s3, seed), row_out=(f32, f32), sums=3,
    )
    db3, de3, grad3, dg2, (ga_in, gb_in, gw2_out) = stage(
        "ffn2_back", 5, rows, width, dp_count, gains, leave=(dh2, w2_in, True),
        enter=(w_conv_out, True, plain_out, (), ((chans, f32),)), dws=(
            weight(a4, dh2, "join", False, 1, 0, half),
            weight(a4, dh2, "join", False, 1, half, units // PIECE - half),
            weight(db4, act2, "far", True),
        ),
        junction=backward(1.0, 3), row_in=(grad4, s3), row_out=(f32,), sums=1,
    )
    dpaired, tap_sums, (gw2_out, ga_in) = conv_mid_back(
        de3, slope3, depth_unit, depth_stat, glu, sig, tail, w_depth, gains, width, 11, [gw2_out, ga_in]
    )
    db2, dmixed, grad2, dgc, (gconv_in, gconv_out, gb_in, gw2_out, ga_in) = stage(
        "conv_back", 6, rows, width, dp_count, gains, leave=(dpaired, flat_conv, True),
        enter=(w_attn_out, True, plain_out, (), ((w_attn_out.shape[0], bf),)), dws=(weight(a3, dpaired, "far", False), weight(db3, act3, "far", True)), grads=(gb_in, gw2_out, ga_in),
        junction=backward(1.0, 2), row_in=(grad3, s2), row_out=(f32,), sums=1,
    )
    dq, dk, dv, dt, (gattn, gb_in, ga_in, gconv_in, gconv_out) = attn_bwd(
        qkv, turned_table, probs, dmixed, db2, mixed, [gb_in, ga_in, gconv_in, gconv_out], 9
    )
    dqkv = (dq, dk, dv)
    db1, dh1, grad1, dga, (gqkv, gconv_in, gconv_out, gb_in), other_rows, table_end, taps_end = stage(
        "attn_back", 7, rows, width, dp_count, gains, leave=(dqkv, flat_qkv, True),
        enter=(w1_out, True, slope_out, (slope1,), ((units, bf),)), dws=(weight(a2, dqkv, "far", False),), grads=(gconv_in, gconv_out, gb_in),
        small=((dgc, dg2, dgf, sq1, sq2, sq3, sq4, sq5), dt, tap_sums),
        junction=backward(0.5, 1), row_in=(grad2, s1), row_out=(f32,), sums=1,
    )
    early = [gqkv, gattn, gconv_in, gconv_out, ga_in, gb_in, gw2_out]
    waiting = pending(early)
    grad0, dg1, ends, lead_row = stage(
        "ffn1_back", 8, rows, width, dp_count, gains, leave=(dh1, w1_in, True),
        dws=(weight(db1, act1, "front", True), weight(a1, dh1, "near", False)), grads=waiting,
        small=((), None, None), last=True,
        junction=backward(1.0, 0), row_in=(grad1, s0), row_out=(f32,), sums=1,
    )
    gw1_out, gw1_in = ends[:2]
    for item, end in zip(waiting, ends[2:]):
        item.array = end.array

    def finish(item):
        flip = item.turned and item.array.shape[0] * dp_count == width and (width // dp_count) % 128 != 0
        return item.array.T if flip else item.array

    token_total = rows * lax.axis_size("mp") * dp_count
    ends = [
        ([output], 1),
        ([grad0], 1),
        ([finish(gw1_in)], 0),
        ([finish(gw1_out)], 0),
        ([finish(gqkv)], -3),
        ([finish(gattn)], 0),
        ([finish(gconv_in)], 2),
        ([finish(gconv_out)], 0),
        ([finish(ga_in), finish(gb_in)], 0),
        ([finish(gw2_out)], 0),
    ]
    done_ends = publish(ends, [lead_row, other_rows, table_end, taps_end], {8: False}, rel_table.shape[0], float(token_total * width))
    (output, grad0, gw1_in, gw1_out, gqkv, gattn, gconv_in, gconv_out, gw2_in, gw2_out) = done_ends[:10]
    *gain_sums, table_sum, depth_sum, depth_gain_sum, rms_stats = done_ends[10:]
    gain_sums = [g[0] for g in gain_sums]
    return (
        output,
        grad0,
        gw1_in,
        gw1_out,
        gain_sums[0],
        gqkv.transpose(1, 0, 2),
        gattn,
        table_sum.T,
        gain_sums[1],
        gconv_in,
        depth_sum,
        depth_gain_sum[0],
        gconv_out,
        gain_sums[2],
        gw2_in,
        gw2_out,
        gain_sums[3],
        gain_sums[4],
        rms_stats[0],
    )


def solution(mesh):
    return jax.shard_map(
        body,
        mesh=mesh,
        in_specs=(
            P("mp", "dp", None),
            P(None, "mp"),
            P("mp", None),
            P(),
            P(None, None, "mp"),
            P("mp", None),
            P(),
            P(),
            P(None, None, "mp"),
            P(None, "mp"),
            P("mp"),
            P("mp", None),
            P(),
            P(None, "mp"),
            P("mp", None),
            P(),
            P(),
            P("mp", "dp", None),
        ),
        out_specs=(
            P("mp", "dp", None),
            P("mp", "dp", None),
            P("dp", "mp"),
            P("mp", "dp"),
            P(),
            P("dp", None, "mp"),
            P("mp", "dp"),
            P(),
            P(),
            P("dp", None, "mp"),
            P(None, "mp"),
            P("mp"),
            P("mp", "dp"),
            P(),
            P("dp", "mp"),
            P("mp", "dp"),
            P(),
            P(),
            P(),
        ),
        check_vma=False,
    )
```

```python
import functools

import jax
import jax.numpy as jnp
from jax import lax
from jax.experimental import pallas as pl
from jax.experimental.pallas import tpu as pltpu
from jax.sharding import PartitionSpec as P

HEAD = 64
REL_LEFT = 64
REL_RIGHT = 8
BQ = 128
WIN = 4 * BQ


epsilon = 1e-05


def nt(a, b):
    return lax.dot_general(a, b, (((1,), (1,)), ((), ())), preferred_element_type=jnp.float32)
def nn(a, b):
    return lax.dot_general(a, b, (((1,), (0,)), ((), ())), preferred_element_type=jnp.float32)
def tn(a, b):
    return lax.dot_general(a, b, (((0,), (0,)), ((), ())), preferred_element_type=jnp.float32)

MESH = pl.DeviceIdType.MESH
CHUNKS = 4
TABLE_ROWS = 40
PIECE = 256
VMEM_LIMIT = 58 << 20


def silu_pair(h):
    sig = jax.nn.sigmoid(h)
    act = h * sig
    return act, sig + act * (1.0 - sig)


def unit_norm(s):
    centred = s - jnp.mean(s, -1, keepdims=True)
    inverse = lax.rsqrt(jnp.mean(centred * centred, -1, keepdims=True) + epsilon)
    return centred * inverse, inverse


def fold8(x):
    return jnp.sum(x.reshape(x.shape[0] // 8, 8, x.shape[1]), 0)


def norm_pull(grad, s, gain):
    unit, inverse = unit_norm(s)
    scaled = grad * gain
    first = jnp.mean(scaled, -1, keepdims=True)
    second = jnp.mean(scaled * unit, -1, keepdims=True)
    return inverse * (scaled - first - unit * second), fold8(grad * unit)


def in_hbm():
    return pl.BlockSpec(memory_space=pltpu.HBM)


class Grad:
    def __init__(self, array, bit, turned):
        self.array, self.bit, self.turned = array, bit, turned


def halved(shape, turned):
    pieces, pairs, _, block, cols = shape
    if pairs > 1:
        return jax.ShapeDtypeStruct((pieces, pairs // 2, 2, block, cols), jnp.bfloat16)
    if turned and block % 128 == 0:
        return jax.ShapeDtypeStruct((pieces * cols, block), jnp.float32)
    return jax.ShapeDtypeStruct((block, pieces * cols), jnp.float32)


def arriving(shape):
    return pltpu.VMEM((shape[0], shape[1]) + tuple(shape[3:]), jnp.bfloat16)


def place(dp, bit):
    own = (dp // 2**bit) % 2
    return own, dp + 2**bit * (1 - 2 * own)


def halving_copy(src, landing, piece, bit, send, recv, slot):
    dp, mp = lax.axis_index("dp"), lax.axis_index("mp")
    own, partner = place(dp, bit)
    return pltpu.make_async_remote_copy(
        src.at[piece, :, 1 - own], landing.at[piece], send.at[slot], recv.at[slot],
        device_id=(partner, mp), device_id_type=MESH,
    )


def halving_keep(src, kept, bit, sem):
    own, _ = place(lax.axis_index("dp"), bit)
    return pltpu.make_async_copy(src.at[:, :, own], kept, sem)


def region(ref, piece, cols, turned):
    if len(ref.shape) > 2:
        return ref.at[piece]
    at = pl.ds(piece * cols, cols)
    return ref.at[at, :] if turned else ref.at[:, at]


def halving_add(held, landing, out, piece, turned):
    pairs, block, cols = landing.shape[1:]
    f32 = jnp.float32
    if pairs == 1:
        total = held(piece, 0).astype(f32) + landing[piece, 0].astype(f32)
        turned = turned and block % 128 == 0
        region(out, piece, cols, turned)[...] = total.T if turned else total
        return

    def add(j, c):
        total = held(piece, j).astype(f32) + landing[piece, j].astype(f32)
        out[piece, j // 2, j % 2] = total.astype(jnp.bfloat16)
        return c

    lax.fori_loop(0, pairs, add, 0)


def weight(lhs, rhs, where, turned, deep=1, lo=0, pieces=None):
    if pieces is None:
        pieces = (sum(r.shape[1] for r in rhs) if isinstance(rhs, tuple) else rhs.shape[1]) // PIECE
    return lhs, rhs, where, turned, deep, lo, pieces


def flat_shape(array):
    if isinstance(array, tuple):
        return array[0].shape[0], sum(a.shape[1] for a in array)
    if len(array.shape) == 3:
        return array.shape[1], array.shape[0] * array.shape[2]
    return array.shape


def gain_row(ref, i, width):
    first = i * width // 128
    return jnp.concatenate([ref[first + j : first + j + 1, :] for j in range(width // 128)], 1)


class Riders:
    def __init__(self, grads):
        self.plan = [(g.array.shape[0], g.bit, g.turned) for g in grads]
        self.arrays = [g.array for g in grads]
        self.after = [halved(g.array.shape, g.turned) for g in grads]
        self.slots = sum(x[0] for x in self.plan)
        self.scratch = [arriving(g.array.shape) for g in grads] * 2 + [pltpu.VMEM(a.shape, a.dtype) for a in self.after]
        if grads:
            self.scratch += [pltpu.SemaphoreType.DMA((self.slots,))] * 3 + [pltpu.SemaphoreType.DMA((len(grads),))]

    def bind(self, srcs, outs, scratch):
        n = len(self.plan)
        sems = scratch[3 * n :]
        holds, hops, slot = [], [], 0
        for i, (pieces, bit, turned) in enumerate(self.plan):
            landing, keep, half = scratch[i], scratch[n + i], scratch[2 * n + i]
            holds.append(halving_keep(srcs[i], keep, bit, sems[3].at[i]))
            flip = turned and landing.shape[2] % 128 == 0
            for p in range(pieces):
                move = halving_copy(srcs[i], landing, p, bit, sems[0], sems[1], slot)
                store = pltpu.make_async_copy(region(half, p, PIECE, flip), region(outs[i], p, PIECE, flip), sems[2].at[slot])
                hops.append((move, store, lambda q, j, keep=keep: keep[q, j], landing, half, p, turned))
                slot += 1
        self.holds, self.hops = holds, hops

    def targets(self):
        dp, mp = lax.axis_index("dp"), lax.axis_index("mp")
        return [(place(dp, b)[1], mp) for b in sorted({x[1] for x in self.plan})]

    def start(self):
        for hold in self.holds:
            hold.start()
        for hop in self.hops:
            hop[0].start()

    def finish(self):
        for hold in self.holds:
            hold.wait()
        for hop in self.hops:
            hop[0].wait_recv()
            halving_add(*hop[2:])
            hop[1].start()
        for hop in self.hops:
            hop[0].wait_send()
            hop[1].wait()

    def results(self, outs):
        return [Grad(a, b + 1, t) for a, (_, b, t) in zip(outs, self.plan)]


def greet(targets):
    barrier = pltpu.get_barrier_semaphore()
    for to in targets:
        pl.semaphore_signal(barrier, inc=1, device_id=to, device_id_type=MESH)
    return lambda: pl.semaphore_wait(barrier, len(targets))


class Doubling:
    def __init__(self, course, refs, lands, sems, partner):
        self.course, self.items, self.sems, self.partner = course, list(zip(refs, lands)), sems, partner
        self.done = 0

    def copies(self, n):
        at = self.course[n]
        return [
            (
                pltpu.make_async_remote_copy(
                    r, l.at[n], self.sems[0].at[i, n], self.sems[1].at[i, n], device_id=self.partner(at), device_id_type=MESH
                ),
                r,
                l.at[n],
            )
            for i, (r, l) in enumerate(self.items)
            if i < 2 or not isinstance(at, str)
        ]

    def start(self, n=0):
        for cp, _, _ in self.copies(n):
            cp.start()

    def advance(self, n):
        for cp, r, l in self.copies(n):
            cp.wait()
            r[...] += l[...]
        if n + 1 < len(self.course):
            self.start(n + 1)

    def step(self):
        if self.done < len(self.course):
            self.advance(self.done)
            self.done += 1


def stage(name, cid, rows, width, count, gains, *, leave=None, enter=None, dws=(), grads=(), small=None, tail=None, junction, row_in=(), row_out=(), sums=0):
    chunk = rows // CHUNKS
    frames = rows * 4
    bits_all = count.bit_length() - 1
    f32, bf = jnp.float32, jnp.bfloat16
    ins, vm_ins, out_shape, scratch = [], [], [], []
    known = {}

    def add_in(array, direct=False):
        if isinstance(array, str):
            return array
        if direct:
            ins.append(array)
            return len(ins) - 1
        if id(array) not in known:
            group = array if isinstance(array, tuple) else (array,)
            known[id(array)] = len(vm_ins)
            vm_ins.append((len(ins), len(group), pltpu.VMEM(flat_shape(array), group[0].dtype)))
            ins.extend(group)
        return known[id(array)]

    out_slots = [0]

    def add_scratch(item):
        scratch.append(item)
        return len(scratch) - 1

    def add_out(shape, dtype, slots, kept=True):
        if not kept:
            return -1 - add_scratch(pltpu.VMEM(shape, dtype)), None
        out_shape.append(jax.ShapeDtypeStruct(shape, dtype))
        first = out_slots[0]
        out_slots[0] += slots
        return len(out_shape) - 1, first

    add_dw = lambda where: [(add_in(d[0]), add_in(d[1])) if d[2] in where else None for d in dws]
    groups = []
    if leave:
        x_i, wl_i = add_in(leave[0]), add_in(leave[1])
        leave_s = [add_scratch(pltpu.VMEM((rows, width), f32)) for _ in range(2)]
        leave_s += [add_scratch(pltpu.VMEM((rows, width), bf)) for _ in range(6)]
        wl_s = add_scratch(pltpu.VMEM(flat_shape(leave[1])[::-1], bf)) if leave[2] else None
        groups.append(len(vm_ins))
        add_dw(("far",))
    gains_i = add_in(gains)
    gain_s = add_scratch(pltpu.VMEM((8, width), f32))
    row_i = [add_in(r) for r in row_in]
    if not leave:
        groups.append(len(vm_ins))
    add_dw(("near", "join"))
    kept = not tail
    if enter:
        we_i = add_in(enter[0])
        extra_i = [add_in(e) for e in enter[3]]
        we_s = add_scratch(pltpu.VMEM(flat_shape(enter[0])[::-1], bf)) if enter[1] else None
        all_o = add_out((frames, width), bf, 4 * CHUNKS, kept)
        e_o = [add_out((frames, c), d, 4 * CHUNKS, kept) for c, d in enter[4]]
    r_o = [add_out((rows, width), d, CHUNKS, kept) for d in row_out]
    s_o = [add_out((8, width), f32, 1, kept) for _ in range(sums)]
    if small:
        vectors_in, table_in, taps_in = small
        vector_i = [add_in(v) for v in vectors_in]
        table_i, taps_i = add_in(table_in), add_in(taps_in)
    groups.append(len(vm_ins))
    if tail:
        add_dw(("front",))
        tw_i = add_in(tail[0])
        tw_s = add_scratch(pltpu.VMEM(flat_shape(tail[0])[::-1], bf))
        tail_i = [add_in(r) for r in tail[2]]
        add_dw(("close",))
        tail_o = [add_out((rows, width), f32, CHUNKS)]
        tail_sum = add_out((8, width), f32, 1, False)
    groups.append(len(vm_ins))
    fixed_out = len(out_shape)
    plan, dw_o = [], []
    for d in dws:
        shape = (d[6], count // 2, 2, width // count, PIECE)
        if d[2] == "join":
            dw_o.append(add_out(shape, bf, shape[0]))
        else:
            plan.append((shape, 0, d[3], bits_all if tail else 1, add_scratch(pltpu.VMEM(shape, bf)), None, None))
            dw_o.append(len(plan) - 1)
    dw_in = [(add_in(d[0]), add_in(d[1])) for d in dws]
    first_grad = len(plan)
    for g in grads:
        shape = g.array.shape
        plan.append((shape, g.bit, g.turned, bits_all if tail else g.bit + 1, None, add_in(g.array, True), add_scratch(arriving(shape))))
    chains = []
    slots = 0
    for shape, bit, turned, end, src_s, src_i, keep_s in plan:
        links = []
        pieces = shape[0]
        for b in range(bit, end):
            nxt = halved(shape, turned)
            land_s = add_scratch(arriving(shape))
            if b == end - 1:
                links.append((b, slots, land_s, None, add_out(nxt.shape, nxt.dtype, pieces)))
            else:
                links.append((b, slots, land_s, add_scratch(pltpu.VMEM(nxt.shape, nxt.dtype)), None))
            slots += pieces
            shape = nxt.shape
        chains.append((pieces, turned, src_s, src_i, keep_s, links))
    if small:
        small_shapes = [(8, width), (TABLE_ROWS, 128), taps_in.shape]
        small_o = [add_out(s, f32, 1) for s in small_shapes]
        lead_o = add_out((1, width), f32, 1)
        downward = list(range(bits_all - 1, -1, -1))
        courses = [downward + ["sib", "far"], ["sib", "far"] + downward]
        small_l = [add_scratch(pltpu.VMEM((bits_all + 2,) + s, f32)) for s in small_shapes]
        lead_l = [add_scratch(pltpu.VMEM((bits_all + 2, 1, width), f32))]
        small_sems = [add_scratch(pltpu.SemaphoreType.DMA((3, bits_all + 2))) for _ in range(4)]
    if slots:
        grad_sems = [add_scratch(pltpu.SemaphoreType.DMA((slots,))) for _ in range(2)]
    ring_sems = [add_scratch(pltpu.SemaphoreType.DMA((6, CHUNKS))) for _ in range(2)]
    load_sem = add_scratch(pltpu.SemaphoreType.DMA((len(ins),)))
    store_sem = add_scratch(pltpu.SemaphoreType.DMA((out_slots[0],)))
    n_in, n_out = len(ins), len(out_shape)
    vm_at = [add_scratch(item[2]) for item in vm_ins]
    vo_at = [add_scratch(pltpu.VMEM(o.shape, o.dtype)) for o in out_shape]

    def kernel(*refs):
        hbm_in, hbm_out, t = refs[:n_in], refs[n_in : n_in + n_out], refs[n_in + n_out :]
        vout = lambda o: t[-1 - o[0]] if o[0] < 0 else t[vo_at[o[0]]]

        def vin(i):
            if i == "all":
                return vout(all_o)
            if i == "out":
                return vout(e_o[0])
            return t[vm_at[i]]

        waited = set()

        def load(i):
            first, parts, _ = vm_ins[i]
            if len(hbm_in[first].shape) == 3:
                slabs, _, cols = hbm_in[first].shape
                return [
                    pltpu.make_async_copy(hbm_in[first].at[n], vin(i).at[:, pl.ds(n * cols, cols)], t[load_sem].at[first])
                    for n in range(slabs)
                ]
            if parts == 1:
                return [pltpu.make_async_copy(hbm_in[first], vin(i), t[load_sem].at[first])]
            copies, at = [], 0
            for n in range(first, first + parts):
                cols = hbm_in[n].shape[1]
                copies.append(pltpu.make_async_copy(hbm_in[n], vin(i).at[:, pl.ds(at, cols)], t[load_sem].at[n]))
                at += cols
            return copies

        begun = [0]

        def begin_loads(group):
            for i in range(begun[0], groups[group]):
                for cp in load(i):
                    cp.start()
            begun[0] = max(begun[0], groups[group])

        def need(*items):
            for i in items:
                if not isinstance(i, str) and i not in waited:
                    waited.add(i)
                    for cp in load(i):
                        cp.wait()

        dp, me = lax.axis_index("dp"), lax.axis_index("mp")
        core, chip = me % 2, me // 2
        sib = chip * 2 + 1 - core
        far = (1 - chip) * 2 + core
        diag = (1 - chip) * 2 + 1 - core
        bits = sorted({link[0] for ch in chains for link in ch[5]} | set(range(bits_all) if small else ()))
        meet = greet([(dp, sib), (dp, far)] + [(place(dp, b)[1], me) for b in bits])
        begin_loads(0)

        def part(ref, block, k):
            return ref.at[pl.ds(pl.multiple_of(block * rows + k * chunk, chunk), chunk)]

        def store_rows(o, block, k):
            return pltpu.make_async_copy(
                part(vout(o), block, k), part(hbm_out[o[0]], block, k), t[store_sem].at[o[1] + block * CHUNKS + k]
            )

        def store_whole(o):
            return pltpu.make_async_copy(vout(o), hbm_out[o[0]], t[store_sem].at[o[1]])

        def store_piece(o, piece, cols, turned):
            return pltpu.make_async_copy(
                region(vout(o), piece, cols, turned), region(hbm_out[o[0]], piece, cols, turned), t[store_sem].at[o[1] + piece]
            )

        def copy(kind, k, src, dst, to):
            return pltpu.make_async_remote_copy(
                src, dst, t[ring_sems[0]].at[kind, k], t[ring_sems[1]].at[kind, k], device_id=(dp, to), device_id_type=MESH
            )

        if leave:
            px, own, sb, sr, xs, xr, ob, orv = [t[s] for s in leave_s]
        if enter:
            all_ref = vout(all_o)
            we_ref = t[we_s] if enter[1] else vin(we_i)
        pair_send = lambda k: copy(0, k, part(sb, 0, k), part(sr, 0, k), sib)
        far_send = lambda k: copy(1, k, part(xs, 0, k), part(xr, 0, k), far)
        own_send = lambda k: copy(2, k, part(ob, 0, k), part(orv, 0, k), sib)
        all_far = lambda k: copy(3, k, part(all_ref, me, k), part(all_ref, me, k), far)
        all_sib = lambda k: copy(4, k, part(all_ref, me, k), part(all_ref, me, k), sib)
        all_fwd = lambda k: copy(5, k, part(all_ref, far, k), part(all_ref, far, k), sib)
        got_far = lambda k: copy(3, k, part(all_ref, far, k), part(all_ref, far, k), far)
        got_sib = lambda k: copy(4, k, part(all_ref, sib, k), part(all_ref, sib, k), sib)
        got_diag = lambda k: copy(5, k, part(all_ref, diag, k), part(all_ref, diag, k), sib)

        def source(c, step):
            pieces, turned, src_s, src_i, keep_s, links = chains[c]
            if step:
                return t[links[step - 1][3]]
            return t[src_s] if src_s is not None else hbm_in[src_i]

        def hop(c, step, piece):
            b, slot, land_s, _, _ = chains[c][5][step]
            return halving_copy(source(c, step), t[land_s], piece, b, t[grad_sems[0]], t[grad_sems[1]], slot + piece)

        def keep(c):
            return halving_keep(hbm_in[chains[c][3]], t[chains[c][4]], chains[c][5][0][0], t[load_sem].at[chains[c][3]])

        held_back = set()

        def settle(c, step, piece):
            pieces, turned, src_s, src_i, keep_s, links = chains[c]
            b, slot, land_s, out_s, out_o = links[step]
            hop(c, step, piece).wait_recv()
            if step == 0 and src_s is None:
                if c not in held_back:
                    held_back.add(c)
                    keep(c).wait()
                held = lambda p, j: t[keep_s][p, j]
            else:
                own_bit, _ = place(dp, b)
                src = source(c, step)
                held = lambda p, j: src[p, j, own_bit]
            landing = t[land_s]
            out = t[out_s] if out_o is None else vout(out_o)
            halving_add(held, landing, out, piece, turned)
            if out_o is not None:
                store_piece(out_o, piece, PIECE, turned and landing.shape[2] % 128 == 0).start()

        def fill(k, where):
            for d, (a, b), o in zip(dws, dw_in, dw_o):
                if d[2] != where:
                    continue
                chain = None if where == "join" else o
                dw = vout(o) if chain is None else t[chains[o][2]]

                @pl.when(k < dw.shape[0])
                def _(a=a, b=b, dw=dw, chain=chain, o=o, lo=d[5]):
                    g = tn(vin(a)[...], vin(b)[:, pl.ds(pl.multiple_of((lo + k) * PIECE, PIECE), PIECE)])
                    dw[k] = g.astype(bf).reshape(dw.shape[1:])
                    if chain is None:
                        store_piece(o, k, PIECE, False).start()
                    else:
                        hop(chain, 0, k).start()

        def need_for(where):
            for d, (a, b) in zip(dws, dw_in):
                if d[2] == where:
                    need(a, b)

        def leave_phase(x_ref, wl_ref, far_fill, near_fill):
            def two(k, block_a, block_b):
                lhs = jnp.concatenate([part(x_ref, block_a, k)[...], part(x_ref, block_b, k)[...]], 0)
                return nn(lhs, wl_ref[...])

            def push(k):
                pair_send(k).wait_recv()
                part(xs, 0, k)[...] = (part(px, 0, k)[...] + part(sr, 0, k)[...].astype(f32)).astype(bf)
                far_send(k).start()

            def out_far(k, c):
                p = two(k, far, diag)
                part(px, 0, k)[...] = p[:chunk]
                part(sb, 0, k)[...] = p[chunk:].astype(bf)
                pair_send(k).start()

                @pl.when(k > 0)
                def _():
                    push(k - 1)

                fill(k, far_fill)
                return c

            lax.fori_loop(0, CHUNKS, out_far, 0)
            need_for(near_fill)

            def out_near(k, c):
                p = two(k, me, sib)
                part(own, 0, k)[...] = p[:chunk]
                part(ob, 0, k)[...] = p[chunk:].astype(bf)
                own_send(k).start()

                @pl.when(k == 0)
                def _():
                    push(CHUNKS - 1)

                fill(k, near_fill)
                return c

            lax.fori_loop(0, CHUNKS, out_near, 0)

        def leave_drain():
            def drain(k, c):
                pair_send(k).wait_send()
                far_send(k).wait_send()
                own_send(k).wait_send()
                return c

            lax.fori_loop(0, CHUNKS, drain, 0)

        def join_phase(rule, has_leave, in_refs, outs, totals, gathers):
            def join(k, c):
                fill(k, "join")
                branch = None
                if has_leave:
                    own_send(k).wait_recv()
                    far_send(k).wait_recv()
                    branch = part(own, 0, k)[...] + part(orv, 0, k)[...].astype(f32) + part(xr, 0, k)[...].astype(f32)
                fresh = rule(
                    branch, [part(r, 0, k)[...] for r in in_refs], t[gain_s], [part(vout(o), 0, k) for o in outs], [vout(o) for o in totals]
                )
                if gathers:
                    part(all_ref, me, k)[...] = fresh
                    all_far(k).start()
                    all_sib(k).start()
                for o in outs:
                    if o[0] >= 0:
                        store_rows(o, 0, k).start()
                return c

            lax.fori_loop(0, CHUNKS, join, 0)
            for o in totals:
                if o[0] >= 0:
                    store_whole(o).start()

        for o in s_o + ([tail_sum] if tail else []):
            vout(o)[...] = jnp.zeros((8, width), f32)
        meet()
        if leave:
            need(x_i, wl_i)
        begin_loads(1)
        for c in range(first_grad, len(chains)):
            for p in range(chains[c][0]):
                hop(c, 0, p).start()
        if leave:
            if leave[2]:
                t[wl_s][...] = vin(wl_i)[...].T
            need_for("far")
            leave_phase(vin(x_i), t[wl_s] if leave[2] else vin(wl_i), "far", "near")
        for c in range(first_grad, len(chains)):
            keep(c).start()
        need(gains_i, *row_i)
        for i in range(5):
            t[gain_s][i : i + 1, :] = gain_row(vin(gains_i), i, width)
        need_for("join")
        if enter and enter[1]:
            need(we_i)
            we_ref[...] = vin(we_i)[...].T
        join_phase(junction, bool(leave), [vin(r) for r in row_i], r_o, s_o, bool(enter))

        lead = [c for c in range(first_grad) if tail and dws[[i for i, o in enumerate(dw_o) if o == c][0]][2] == "far"]
        if small:
            partner = lambda at: (dp, sib) if at == "sib" else (dp, far) if at == "far" else (place(dp, at)[1], me)
            need(*vector_i, table_i, taps_i)
            rows_ref = vout(small_o[0])
            rows_ref[...] = jnp.zeros((8, width), f32)
            vectors = [vout(s_o[0])] + [vin(i) for i in vector_i]
            for i, v in enumerate(vectors[:4]):
                rows_ref[i : i + 1, :] = jnp.sum(v[...], 0, keepdims=True)
            for i, v in enumerate(vectors[4:]):
                line = jnp.sum(v[...], 0, keepdims=True)
                rows_ref[4:5, i * 128 : (i + 1) * 128] = functools.reduce(
                    jnp.add, [line[:, j * 128 : (j + 1) * 128] for j in range(width // 128)]
                )
            both = vin(table_i)[...]
            both = both + pltpu.roll(both, 64, 1)
            left = lax.broadcasted_iota(jnp.int32, (TABLE_ROWS, 128), 1) < HEAD
            vout(small_o[1])[...] = jnp.where(left, both[:TABLE_ROWS], both[TABLE_ROWS : 2 * TABLE_ROWS])
            vout(small_o[2])[...] = vin(taps_i)[...]
            wide = Doubling(courses[0], [vout(o) for o in small_o], [t[l] for l in small_l], [t[s] for s in small_sems[:2]], partner)
            wide.start()

        if enter:
            begin_loads(len(groups) - 1)
            need(we_i, *extra_i)

            def work(k, block_a, block_b):
                lhs = jnp.concatenate([part(all_ref, block_a, k)[...], part(all_ref, block_b, k)[...]], 0)
                h = nn(lhs, we_ref[...])
                for i, block in enumerate((block_a, block_b)):
                    view = lambda ref: part(ref, block, k)
                    enter[2](h[i * chunk : (i + 1) * chunk], [view(vin(r))[...] for r in extra_i], [view(vout(o)) for o in e_o])
                    for o in [all_o] + e_o:
                        if o[0] >= 0:
                            store_rows(o, block, k).start()

            def gather(k, c):
                got_sib(k).wait_recv()
                work(k, me, sib)
                got_far(k).wait_recv()
                all_fwd(k).start()
                got_diag(k).wait_recv()
                work(k, far, diag)
                if small:

                    @pl.when(k == 1)
                    def _():
                        wide.advance(0)

                if lead:

                    @pl.when(k == CHUNKS - 2)
                    def _():
                        for ch in lead:
                            for p in range(chains[ch][0]):
                                settle(ch, 0, p)
                                hop(ch, 1, p).start()

                return c

            lax.fori_loop(0, CHUNKS, gather, 0)
            if small:
                wide.done = 1

        early = 0
        if tail:
            need_for("front")

            def front(k, c):
                fill(k, "front")
                return c

            lax.fori_loop(0, CHUNKS, front, 0)
            wide.step()
            early = 1
            if lead and bits_all > 2:
                early = 2
                for ch in lead:
                    for p in range(chains[ch][0]):
                        settle(ch, 1, p)
                        hop(ch, 2, p).start()
            leave_drain()
            need(tw_i, *tail_i)
            t[tw_s][...] = vin(tw_i)[...].T
            wide.step()
            leave_phase(vin("out"), t[tw_s], None, "close")
            wide.step()
            join_phase(tail[1], True, [vout(r_o[0])] + [vin(r) for r in tail_i], tail_o, [tail_sum], False)
            vout(lead_o)[...] = jnp.sum(vout(tail_sum)[...], 0, keepdims=True)
            final = Doubling(courses[1], [vout(lead_o)], [t[l] for l in lead_l], [t[s] for s in small_sems[2:]], partner)
            final.start()
            while wide.done < len(courses[0]):
                wide.step()

        pieces = [(c, p) for c in range(len(chains)) for p in range(chains[c][0])]
        order = [x for x in pieces if x[0] >= first_grad] + [x for x in pieces if x[0] in lead]
        order += [x for x in pieces if x not in order]
        depth = lambda c: len(chains[c][5])
        begin = lambda c: early if c in lead else 0
        deepest = max([depth(c) - begin(c) for c in range(len(chains))] + [0])
        total_slots = len(order) + deepest - 1
        for slot in range(total_slots):
            if tail and (slot < 2 or slot % 3 == 0) and final.done < len(courses[1]) - 1:
                final.step()
            for s in reversed(range(deepest)):
                if 0 <= slot - s < len(order):
                    c, p = order[slot - s]
                    step = s + begin(c)
                    if step < depth(c):
                        settle(c, step, p)
                        if step + 1 < depth(c):
                            hop(c, step + 1, p).start()
        if tail:
            while final.done < len(courses[1]):
                final.step()
            for o in small_o + [lead_o]:
                store_whole(o).start()
        for c in range(len(chains)):
            for s in range(depth(c)):
                for p in range(chains[c][0]):
                    hop(c, s, p).wait_send()
            out_o = chains[c][5][-1][4]
            block = chains[c][5][-1][2]
            for p in range(chains[c][0]):
                store_piece(out_o, p, PIECE, chains[c][1] and t[block].shape[2] % 128 == 0).wait()
        if leave:
            leave_drain()

        def drain(k, c):
            if enter:
                all_far(k).wait_send()
                all_sib(k).wait_send()
                all_fwd(k).wait_send()
                for block in range(4):
                    for o in [all_o] + e_o:
                        if o[0] >= 0:
                            store_rows(o, block, k).wait()
            for o in r_o + (tail_o if tail else []):
                if o[0] >= 0:
                    store_rows(o, 0, k).wait()
            return c

        lax.fori_loop(0, CHUNKS, drain, 0)
        for o in s_o + (small_o + [lead_o] if tail else []):
            if o[0] >= 0:
                store_whole(o).wait()
        for d, o in zip(dws, dw_o):
            if d[2] == "join":
                for p in range(d[6]):
                    store_piece(o, p, PIECE, False).wait()

    flops = 0
    if leave:
        flops += 2 * frames * flat_shape(leave[1])[1 if leave[2] else 0] * width
    if enter:
        flops += 2 * frames * width * sum(c for c, _ in enter[4])
    flops += sum(2 * frames * width * PIECE * d[6] for d in dws)
    outs = pl.pallas_call(
        kernel,
        in_specs=[in_hbm()] * n_in,
        out_specs=[in_hbm()] * n_out,
        out_shape=out_shape,
        scratch_shapes=scratch,
        compiler_params=pltpu.CompilerParams(collective_id=cid, has_side_effects=True, vmem_limit_bytes=VMEM_LIMIT),
        cost_estimate=pl.CostEstimate(flops=flops, bytes_accessed=60_000_000, transcendentals=0),
        name=name,
    )(*ins)
    fixed, rest = list(outs[:fixed_out]), list(outs[fixed_out:])
    fresh = [Grad(rest.pop(0), 0, d[3]) for d in dws if d[2] == "join"]
    for item in plan:
        fresh.append(Grad(rest.pop(0), item[3], item[2]))
    return fixed + [fresh] + rest


def publish(ends, small, sizes, rel, total):
    flat, outs, where = [], [], []
    f32 = jnp.float32
    for arrays, parts in ends:
        rows = arrays[0].shape[0]
        joined = len(arrays) > 1 and sizes[len(outs)]
        shape = (rows, sum(a.shape[1] for a in arrays)) if not joined else (sum(a.shape[0] for a in arrays), arrays[0].shape[1])
        where.append((len(flat), arrays, joined))
        flat.extend(arrays)
        if parts < 0:
            outs.append((shape, (-parts, shape[0], shape[1] // -parts)))
        else:
            outs.append((shape, (shape[0], parts, shape[1] // parts) if parts else None))
    n, m = len(flat), len(ends)
    width = small[0].shape[1]
    taps = small[3].shape
    split_at = [i for i in range(m) if ends[i][1] > 0]
    slab_at = [i for i in range(m) if ends[i][1] < 0]
    small_shapes = [(1, width)] * 5 + [(HEAD, rel), (taps[0] - 1, taps[1]), (1, taps[1]), (1, 5)]

    def kernel(*refs):
        src, small_in = refs[:n], refs[n : n + 4]
        dst, small_out = refs[n + 4 : n + 4 + m], refs[n + 4 + m : n + 13 + m]
        rest = refs[n + 13 + m :]
        held, split = rest[:m], dict(zip(split_at, rest[m:-1]))
        sem = rest[-1]
        loads, stores = [], []
        for i, (first, arrays, joined) in enumerate(where):
            at, copies = 0, []
            for k in range(len(arrays)):
                ref = src[first + k]
                size = ref.shape[0 if joined else 1]
                part = held[i].at[pl.ds(at, size)] if joined else held[i].at[:, pl.ds(at, size)]
                copies.append(pltpu.make_async_copy(ref, part, sem.at[first + k]))
                at += size
            loads.append(copies)
            if i in slab_at:
                slabs, _, cols = dst[i].shape
                stores.append(
                    [
                        pltpu.make_async_copy(held[i].at[:, pl.ds(k * cols, cols)], dst[i].at[k], sem.at[n + m + k])
                        for k in range(slabs)
                    ]
                )
            else:
                stores.append([pltpu.make_async_copy(split.get(i, held[i]), dst[i], sem.at[n + i])])
        for copies in loads:
            for cp in copies:
                cp.start()
        lead, rows, table, tap = [r[...] for r in small_in]
        small_out[0][...] = lead
        for i in range(4):
            small_out[1 + i][...] = rows[i : i + 1]
        turned = jnp.concatenate([table, jnp.zeros((128 - TABLE_ROWS, 128), f32)], 0).T
        small_out[5][:, :TABLE_ROWS] = turned[:HEAD, :TABLE_ROWS]
        small_out[5][:, TABLE_ROWS:] = turned[HEAD:, : rel - TABLE_ROWS]
        small_out[6][...] = tap[:-1]
        small_out[7][...] = tap[-1:]
        lane = lax.broadcasted_iota(jnp.int32, (1, 128), 1)
        mean = jnp.zeros((1, 128), f32)
        for i in range(5):
            mean = jnp.where(lane == i, jnp.sum(rows[4:5, i * 128 : (i + 1) * 128], -1, keepdims=True) / total, mean)
        root = jnp.sqrt(mean)
        small_out[8][...] = root[:, :5]
        for i in range(m):
            for cp in loads[i]:
                cp.wait()
            if i in split:
                cols = split[i].shape[2]
                for j in range(split[i].shape[1]):
                    split[i][:, j, :] = held[i][:, j * cols : (j + 1) * cols]
            for cp in stores[i]:
                cp.start()
        for copies in stores:
            for cp in copies:
                cp.wait()

    vm = pl.BlockSpec(memory_space=pltpu.VMEM)
    return pl.pallas_call(
        kernel,
        in_specs=[in_hbm()] * n + [vm] * 4,
        out_specs=[in_hbm()] * m + [vm] * 9,
        out_shape=[jax.ShapeDtypeStruct(o[1] or o[0], f32) for o in outs] + [jax.ShapeDtypeStruct(s, f32) for s in small_shapes],
        scratch_shapes=[pltpu.VMEM(o[0], f32) for o in outs]
        + [pltpu.VMEM(outs[i][1], f32) for i in split_at]
        + [pltpu.SemaphoreType.DMA((n + m + 4,))],
        compiler_params=pltpu.CompilerParams(vmem_limit_bytes=VMEM_LIMIT),
        name="publish",
    )(*flat, *small)


SPAN = 128


def exchange(stats, landing, send, recv):
    dp, me = lax.axis_index("dp"), lax.axis_index("mp")
    core, chip = me % 2, me // 2
    others = [chip * 2 + 1 - core, (1 - chip) * 2 + core, (1 - chip) * 2 + 1 - core]
    return [
        pltpu.make_async_remote_copy(
            stats, landing.at[i], send.at[i], recv.at[i], device_id=(dp, to), device_id_type=MESH
        )
        for i, to in enumerate(others)
    ]


def group_targets():
    dp, me = lax.axis_index("dp"), lax.axis_index("mp")
    core, chip = me % 2, me // 2
    return [(dp, chip * 2 + 1 - core), (dp, (1 - chip) * 2 + core), (dp, (1 - chip) * 2 + 1 - core)]


def to_rows(first, second):
    lane = lax.broadcasted_iota(jnp.int32, (SPAN, SPAN), 1)
    both = jnp.where(lane == 0, first, jnp.where(lane == 1, second, 0.0))
    return both.T[:8]


def to_columns(rows8):
    return jnp.concatenate([rows8, jnp.zeros((SPAN - 8, SPAN), jnp.float32)], 0).T


def shifted(window, by):
    return window if by == 0 else pltpu.roll(window, window.shape[0] - by, 0)


def depth_gain_row(ref, width, chans):
    first = 5 * width // 128
    return jnp.concatenate([ref[first + j : first + j + 1, :] for j in range(chans // 128)], 1)


def conv_mid(glu, w_depth, gains, width, cid):
    frames, chans = glu.shape
    taps = w_depth.shape[0]
    reach = taps - 1
    edge = (reach + 7) // 8 * 8
    f32, bf = jnp.float32, jnp.bfloat16
    tiles, lanes = frames // SPAN, chans // 128

    def kernel(glu_h, w_h, g_h, act_h, slope_h, unit_h, stat_h, pad, w_raw, g_raw, w_v, g_v, act, slope, unit, stat, sendbuf, landing, lsem, ssem, send, recv):
        meet = greet(group_targets())
        loads = [
            pltpu.make_async_copy(glu_h, pad.at[pl.ds(edge, frames)], lsem.at[0]),
            pltpu.make_async_copy(w_h, w_raw, lsem.at[1]),
            pltpu.make_async_copy(g_h, g_raw, lsem.at[2]),
        ]
        for cp in loads:
            cp.start()
        pad[:edge, :] = jnp.zeros((edge, chans), f32)
        for cp in loads:
            cp.wait()
        w_v[...] = w_raw[...].astype(f32)
        g_v[...] = depth_gain_row(g_raw, width, chans)

        def tile(i, c):
            at = pl.multiple_of(i * SPAN, SPAN)
            for lane in range(lanes):
                cols = slice(lane * 128, (lane + 1) * 128)
                window = pad[pl.ds(at, SPAN + edge), cols]
                total = jnp.zeros((SPAN, 128), f32)
                for by in range(8):
                    moved = shifted(window, by)
                    for base in range(0, edge + 1, 8):
                        tap = base + by - (edge - reach)
                        if 0 <= tap < taps:
                            total = total + w_v[tap : tap + 1, cols] * moved[base : base + SPAN]
                unit[pl.ds(at, SPAN), cols] = total
            depth = unit[pl.ds(at, SPAN), :]
            mean = jnp.mean(depth, -1, keepdims=True)
            centred = depth - mean
            sendbuf[:, pl.ds(at, SPAN)] = to_rows(mean, jnp.sum(centred * centred, -1, keepdims=True))
            return c

        lax.fori_loop(0, tiles, tile, 0)
        meet()
        copies = exchange(sendbuf, landing, send, recv)
        for cp in copies:
            cp.start()
        for cp in copies:
            cp.wait_recv()
        rows = [sendbuf[...]] + [landing[i] for i in range(3)]
        mean = sum(r[0:1] for r in rows) * 0.25
        spread = sum(r[1:2] + chans * (r[0:1] - mean) * (r[0:1] - mean) for r in rows) / width
        inverse = lax.rsqrt(spread + epsilon)
        row = lax.broadcasted_iota(jnp.int32, (8, frames), 0)
        stat[...] = jnp.where(row == 0, mean, jnp.where(row == 1, inverse, 0.0))
        outs = [(act, act_h), (slope, slope_h), (unit, unit_h)]

        def store(i, n):
            at = pl.ds(pl.multiple_of(i * SPAN, SPAN), SPAN)
            return pltpu.make_async_copy(outs[n][0].at[at], outs[n][1].at[at], ssem.at[n, i])

        def finish(i, c):
            at = pl.multiple_of(i * SPAN, SPAN)
            cols = to_columns(stat[:, pl.ds(at, SPAN)])
            u = (unit[pl.ds(at, SPAN), :] - cols[:, 0:1]) * cols[:, 1:2]
            a, s = silu_pair(u * g_v[...])
            unit[pl.ds(at, SPAN), :] = u
            act[pl.ds(at, SPAN), :] = a.astype(bf)
            slope[pl.ds(at, SPAN), :] = s.astype(bf)
            for n in range(3):
                store(i, n).start()
            return c

        lax.fori_loop(0, tiles, finish, 0)
        last = pltpu.make_async_copy(stat, stat_h, lsem.at[0])
        last.start()
        for cp in copies:
            cp.wait_send()
        for i in range(tiles):
            for n in range(3):
                store(i, n).wait()
        last.wait()

    S = jax.ShapeDtypeStruct
    out_shape = [S((frames, chans), bf), S((frames, chans), bf), S((frames, chans), f32), S((8, frames), f32)]
    vm = pltpu.VMEM
    return pl.pallas_call(
        kernel,
        in_specs=[in_hbm()] * 3,
        out_specs=[in_hbm()] * 4,
        out_shape=out_shape,
        scratch_shapes=[
            vm((frames + edge, chans), f32), vm(w_depth.shape, bf), vm(gains.shape, f32), vm(w_depth.shape, f32), vm((1, chans), f32),
            vm((frames, chans), bf), vm((frames, chans), bf), vm((frames, chans), f32), vm((8, frames), f32),
            vm((8, frames), f32), vm((3, 8, frames), f32),
            pltpu.SemaphoreType.DMA((3,)), pltpu.SemaphoreType.DMA((3, tiles)), pltpu.SemaphoreType.DMA((3,)), pltpu.SemaphoreType.DMA((3,)),
        ],
        compiler_params=pltpu.CompilerParams(collective_id=cid, has_side_effects=True, vmem_limit_bytes=VMEM_LIMIT),
        name="conv_mid",
    )(glu, w_depth, gains)


def conv_mid_back(grad, slope, unit, stat, glu, sig, tail, w_depth, gains, width, cid, grads):
    frames, chans = glu.shape
    taps = w_depth.shape[0]
    reach = taps - 1
    edge = (reach + 7) // 8 * 8
    f32, bf = jnp.float32, jnp.bfloat16
    tiles, lanes = frames // SPAN, chans // 128
    ins = [grad, slope, unit, stat, w_depth, gains, glu, sig, tail]
    riders = Riders(grads)
    n = len(grads)

    def kernel(*refs):
        hbm, ride_in, (pair_h, taps_h), ride_out = refs[:9], refs[9 : 9 + n], refs[9 + n : 11 + n], refs[11 + n : 11 + 2 * n]
        refs = refs[2 * n :]
        (grad_v, slope_v, unit_v, stat_v, w_raw, g_raw, pad, sig_v, tail_v, w_v, g_v, back, pair, taps_v, acc, gacc, sendbuf, landing, lsem, ssem, send, recv) = refs[11:33]
        riders.bind(ride_in, ride_out, refs[33:])
        meet = greet(group_targets() + riders.targets())
        dst = [grad_v, slope_v, unit_v, stat_v, w_raw, g_raw, pad.at[pl.ds(edge, frames)], sig_v, tail_v]
        loads = [pltpu.make_async_copy(h, d, lsem.at[i]) for i, (h, d) in enumerate(zip(hbm, dst))]
        for cp in loads:
            cp.start()
        pad[:edge, :] = jnp.zeros((edge, chans), f32)
        back[frames:, :] = jnp.zeros((edge, chans), f32)
        acc[...] = jnp.zeros_like(acc)
        gacc[...] = jnp.zeros_like(gacc)
        for cp in loads[:6]:
            cp.wait()
        w_v[...] = w_raw[...].astype(f32)
        g_v[...] = depth_gain_row(g_raw, width, chans)

        def first(i, c):
            at = pl.ds(pl.multiple_of(i * SPAN, SPAN), SPAN)
            u = unit_v[at, :]
            de = grad_v[at, :] * slope_v[at, :].astype(f32)
            gacc[...] += fold8(de * u)
            du = de * g_v[...]
            back[at, :] = du
            sendbuf[:, at] = to_rows(jnp.sum(du, -1, keepdims=True), jnp.sum(du * u, -1, keepdims=True))
            return c

        meet()
        riders.start()
        lax.fori_loop(0, tiles, first, 0)
        copies = exchange(sendbuf, landing, send, recv)
        for cp in copies:
            cp.start()
        for cp in loads[6:]:
            cp.wait()
        for cp in copies:
            cp.wait_recv()
        means = (sendbuf[...] + landing[0] + landing[1] + landing[2]) / width
        row = lax.broadcasted_iota(jnp.int32, (8, frames), 0)
        stat_v[...] = jnp.where(row == 1, stat_v[...], jnp.where(row == 0, means[0:1], jnp.where(row == 2, means[1:2], 0.0)))

        def second(i, c):
            at = pl.ds(pl.multiple_of(i * SPAN, SPAN), SPAN)
            cols = to_columns(stat_v[:, at])
            back[at, :] = cols[:, 1:2] * (back[at, :] - cols[:, 0:1] - unit_v[at, :] * cols[:, 2:3])
            return c

        lax.fori_loop(0, tiles, second, 0)

        def store(i):
            at = pl.ds(pl.multiple_of(i * SPAN, SPAN), SPAN)
            return pltpu.make_async_copy(pair.at[at], pair_h.at[at], ssem.at[i])

        def third(i, c):
            at = pl.multiple_of(i * SPAN, SPAN)
            rows = pl.ds(at, SPAN)
            for lane in range(lanes):
                cols = slice(lane * 128, (lane + 1) * 128)
                ahead = back[pl.ds(at, SPAN + edge), cols]
                total = jnp.zeros((SPAN, 128), f32)
                for by in range(8):
                    moved = shifted(ahead, by)
                    for base in range(0, edge, 8):
                        tap = reach - (base + by)
                        if 0 <= tap < taps:
                            total = total + w_v[tap : tap + 1, cols] * moved[base : base + SPAN]
                pair[rows, cols] = (total * sig_v[rows, cols].astype(f32)).astype(bf)
                pair[rows, chans + lane * 128 : chans + (lane + 1) * 128] = (total * tail_v[rows, cols].astype(f32)).astype(bf)
            store(i).start()
            for lane in range(lanes):
                cols = slice(lane * 128, (lane + 1) * 128)
                here = back[rows, cols]
                window = pad[pl.ds(at, SPAN + edge), cols]
                for by in range(8):
                    moved = shifted(window, by)
                    for base in range(0, edge + 1, 8):
                        tap = base + by - (edge - reach)
                        if 0 <= tap < taps:
                            acc[tap * 8 : tap * 8 + 8, cols] += fold8(here * moved[base : base + SPAN])
            return c

        lax.fori_loop(0, tiles, third, 0)
        for tap in range(taps):
            taps_v[tap : tap + 1, :] = jnp.sum(acc[tap * 8 : tap * 8 + 8, :], 0, keepdims=True)
        taps_v[taps : taps + 1, :] = jnp.sum(gacc[...], 0, keepdims=True)
        last = pltpu.make_async_copy(taps_v, taps_h, lsem.at[0])
        last.start()
        for cp in copies:
            cp.wait_send()
        riders.finish()
        for i in range(tiles):
            store(i).wait()
        last.wait()

    S = jax.ShapeDtypeStruct
    vm = pltpu.VMEM
    outs = pl.pallas_call(
        kernel,
        in_specs=[in_hbm()] * (9 + n),
        out_specs=[in_hbm()] * (2 + n),
        out_shape=[S((frames, 2 * chans), bf), S((taps + 1, chans), f32)] + riders.after,
        scratch_shapes=[
            vm((frames, chans), f32), vm((frames, chans), bf), vm((frames, chans), f32), vm((8, frames), f32),
            vm(w_depth.shape, bf), vm(gains.shape, f32), vm((frames + edge, chans), f32), vm((frames, chans), bf), vm((frames, chans), bf),
            vm(w_depth.shape, f32), vm((1, chans), f32),
            vm((frames + edge, chans), f32), vm((frames, 2 * chans), bf), vm((taps + 1, chans), f32), vm((taps * 8, chans), f32), vm((8, chans), f32),
            vm((8, frames), f32), vm((3, 8, frames), f32),
            pltpu.SemaphoreType.DMA((9,)), pltpu.SemaphoreType.DMA((tiles,)), pltpu.SemaphoreType.DMA((3,)), pltpu.SemaphoreType.DMA((3,)),
        ] + riders.scratch,
        compiler_params=pltpu.CompilerParams(collective_id=cid, has_side_effects=True, vmem_limit_bytes=VMEM_LIMIT),
        name="conv_mid_back",
    )(*ins, *riders.arrays)
    return outs[0], outs[1], riders.results(outs[2:])


def split_pair(x):
    left = lax.broadcasted_iota(jnp.int32, x.shape, 1) < HEAD
    zero = jnp.zeros_like(x)
    return jnp.concatenate([jnp.where(left, x, zero), jnp.where(left, zero, x)], 0)

def join_pair(x):
    rows = x.shape[0] // 2
    left = lax.broadcasted_iota(jnp.int32, (rows, x.shape[1]), 1) < HEAD
    return jnp.where(left, x[:rows], x[rows:])

def spot_table(spots):
    spot = lax.broadcasted_iota(jnp.int32, (spots, BQ), 0)
    inner = jnp.clip(spot - REL_LEFT, 0, REL_LEFT + REL_RIGHT)
    row = jnp.where(spot < 3 * BQ, inner, jnp.where(spot < 4 * BQ, 0, REL_LEFT + REL_RIGHT))
    return (lax.broadcasted_iota(jnp.int32, (spots, BQ), 1) == row).astype(jnp.bfloat16)


def wide_table(rel_ref, wide_ref):
    wide_ref[...] = jnp.zeros_like(wide_ref)
    turned = rel_ref[...].astype(jnp.float32)
    cols = turned.shape[1]
    wide_ref[0:HEAD, :cols] = turned
    wide_ref[HEAD : 2 * HEAD, :cols] = turned
    return wide_ref[...].T.astype(jnp.bfloat16)


def fwd_kernel(q_ref, k_ref, v_ref, relt_ref, mixed_ref, probs_ref, bias_ref, rel_ref, wide_ref):
    ib = pl.program_id(1)

    @pl.when((ib == 0) & (pl.program_id(0) == 0))
    def _():
        rel_ref[...] = nn(spot_table(5 * BQ), wide_table(relt_ref, wide_ref)).astype(jnp.bfloat16)

    qs = split_pair(q_ref[...] * 0.125)
    s = nt(qs, k_ref[...])
    b = nt(qs, rel_ref[...])
    rows = b.shape[0] // 2
    bias_ref[:, 0:BQ] = b[:, 3 * BQ : 4 * BQ]
    for h in range(2):
        r = pltpu.roll(b[h * rows : (h + 1) * rows, :WIN], 0, 1, stride=1, stride_axis=0)
        bias_ref[h * rows : (h + 1) * rows, BQ : 4 * BQ] = r[:, : 3 * BQ]
    bias_ref[:, 4 * BQ :] = b[:, 4 * BQ :]
    nkeys = s.shape[1] // BQ
    parts = []
    for jb in range(nkeys):
        at = pl.multiple_of(jnp.clip(jb - ib + 2, 0, 4) * BQ, BQ)
        parts.append(s[:, jb * BQ : (jb + 1) * BQ] + bias_ref[:, pl.ds(at, BQ)])
    top = functools.reduce(jnp.maximum, parts)
    m = jnp.max(top, -1, keepdims=True)
    es = [jnp.exp(p - m) for p in parts]
    tot = jnp.sum(functools.reduce(jnp.add, es), -1, keepdims=True)
    inv = 1.0 / tot
    for jb in range(nkeys):
        probs_ref[0, :, jb * BQ : (jb + 1) * BQ] = (es[jb] * inv).astype(jnp.bfloat16)
    mixed_ref[...] = join_pair(nn(probs_ref[0], v_ref[...])).astype(jnp.bfloat16)

def bwd_kernel(riders, *refs):
    n = len(riders.plan)
    q_ref, k_ref, v_ref, relt_ref, probs_ref, do_ref, db_h, mix_h = refs[:8]
    ride_in = refs[8 : 8 + n]
    dq_ref, dk_ref, dv_ref, dt_ref, dw_h = refs[8 + n : 13 + n]
    ride_out = refs[13 + n : 13 + 2 * n]
    tot_ref, dkt, dvt, dta, dz_ref, hot_ref, db_v, mix_v, dw_v, dw_land, dw_half, relb_ref, wide_ref, osem, psem = refs[13 + 2 * n : 28 + 2 * n]
    riders.bind(ride_in, ride_out, refs[28 + 2 * n :])
    pr, ib, nb = pl.program_id(0), pl.program_id(1), pl.num_programs(1)
    dp, mp = lax.axis_index("dp"), lax.axis_index("mp")
    loads = [pltpu.make_async_copy(db_h, db_v, osem.at[0]), pltpu.make_async_copy(mix_h, mix_v, osem.at[1])]
    pieces = dw_v.shape[0]
    hops = [halving_copy(dw_v, dw_land, p, 0, psem.at[0], psem.at[1], p) for p in range(pieces)]
    flip = dw_land.shape[2] % 128 == 0
    stores = [
        pltpu.make_async_copy(region(dw_half, p, PIECE, flip), region(dw_h, p, PIECE, flip), psem.at[2, p]) for p in range(pieces)
    ]

    @pl.when((ib == 0) & (pr == 0))
    def _():
        meet = greet(sorted_targets(riders, dp, mp))
        for cp in loads:
            cp.start()
        hot_ref[...] = spot_table(WIN)
        relb_ref[...] = wide_table(relt_ref, wide_ref)
        meet()
        riders.start()
        for cp in loads:
            cp.wait()
        for p in range(pieces):
            g = tn(db_v[...], mix_v[:, p * PIECE : (p + 1) * PIECE])
            dw_v[p] = g.astype(jnp.bfloat16).reshape(dw_v.shape[1:])
            hops[p].start()

    @pl.when(ib == 0)
    def _():
        dkt[...] = jnp.zeros_like(dkt)
        dvt[...] = jnp.zeros_like(dvt)
    @pl.when((ib == 0) & (pr == 0))
    def _():
        dta[...] = jnp.zeros_like(dta)
    qs = split_pair(q_ref[...] * 0.125)
    dos = split_pair(do_ref[...])
    p = probs_ref[0]
    dp = nt(dos, v_ref[...])
    nkeys = dp.shape[1] // BQ
    dvt[...] += tn(dos, p)
    pf = p.astype(jnp.float32)
    acc = None
    for jb in range(nkeys):
        sl = slice(jb * BQ, (jb + 1) * BQ)
        t = pf[:, sl] * dp[:, sl]
        acc = t if acc is None else acc + t
    inner = jnp.sum(acc, -1, keepdims=True)
    tot_ref[...] = jnp.zeros_like(tot_ref)
    for jb in range(nkeys):
        sl = slice(jb * BQ, (jb + 1) * BQ)
        dz = (pf[:, sl] * (dp[:, sl] - inner)).astype(jnp.bfloat16)
        dz_ref[:, sl] = dz
        at = pl.multiple_of(jnp.clip(jb - ib + 2, 0, 4) * BQ, BQ)
        tot_ref[:, pl.ds(at, BQ)] += dz.astype(jnp.float32)
    rows = BQ
    r2 = lax.broadcasted_iota(jnp.int32, (2 * rows, 2 * rows), 0)
    c2 = lax.broadcasted_iota(jnp.int32, (2 * rows, 2 * rows), 1)
    mirror = (r2 + c2 == jnp.where(r2 < rows, rows - 1, 3 * rows - 1)).astype(jnp.bfloat16)
    w = jnp.concatenate([tot_ref[:, BQ : 4 * BQ].astype(jnp.bfloat16), jnp.zeros((2 * rows, BQ), jnp.bfloat16)], 1)
    w = nn(mirror, w)
    outs = [pltpu.roll(w[h * rows : (h + 1) * rows], WIN - rows + 1, 1, stride=1, stride_axis=0) for h in range(2)]
    d = nn(mirror, jnp.concatenate(outs, 0).astype(jnp.bfloat16)).astype(jnp.bfloat16)
    drel = nn(d, hot_ref[...])
    col = lax.broadcasted_iota(jnp.int32, drel.shape, 1)
    low = jnp.sum(tot_ref[:, :BQ], -1, keepdims=True)
    high = jnp.sum(tot_ref[:, 4 * BQ :], -1, keepdims=True)
    drel = drel + jnp.where(col == 0, low, 0.0) + jnp.where(col == REL_LEFT + REL_RIGHT, high, 0.0)
    drel = drel.astype(jnp.bfloat16)
    dz = dz_ref[...]
    dq = nn(dz, k_ref[...]) + nn(drel, relb_ref[...])
    dq_ref[...] = (join_pair(dq) * 0.125).astype(jnp.bfloat16)
    dkt[...] += tn(qs, dz)
    dta[...] += tn(drel, qs)
    @pl.when(ib == nb - 1)
    def _():
        dk_ref[...] = dkt[...].T.astype(jnp.bfloat16)
        dv_ref[...] = dvt[...].T.astype(jnp.bfloat16)
        dt_ref[...] = dta[...]

    @pl.when((ib == nb - 1) & (pr == pl.num_programs(0) - 1))
    def _():
        own, _ = place(lax.axis_index("dp"), 0)
        for p in range(pieces):
            hops[p].wait_recv()
            halving_add(lambda q, j: dw_v[q, j, own], dw_land, dw_half, p, True)
            stores[p].start()
        riders.finish()
        for p in range(pieces):
            hops[p].wait_send()
            stores[p].wait()


def sorted_targets(riders, dp, mp):
    return [(place(dp, b)[1], mp) for b in sorted({0} | {x[1] for x in riders.plan})]


def attn_fwd(qkv, rel):
    frames, cols = qkv.shape
    pairs = cols // 3 // 128
    nb = frames // BQ
    bf = jnp.bfloat16
    return pl.pallas_call(
        fwd_kernel,
        grid=(pairs, nb),
        in_specs=[
            pl.BlockSpec((BQ, 128), lambda p, i: (i, p)),
            pl.BlockSpec((frames, 128), lambda p, i: (0, pairs + p)),
            pl.BlockSpec((frames, 128), lambda p, i: (0, 2 * pairs + p)),
            pl.BlockSpec(rel.shape, lambda p, i: (0, 0)),
        ],
        out_specs=[
            pl.BlockSpec((BQ, 128), lambda p, i: (i, p)),
            pl.BlockSpec((1, 2 * BQ, frames), lambda p, i: (p, i, 0)),
        ],
        out_shape=[jax.ShapeDtypeStruct((frames, cols // 3), bf), jax.ShapeDtypeStruct((pairs, 2 * frames, frames), bf)],
        scratch_shapes=[pltpu.VMEM((2 * BQ, 5 * BQ), jnp.float32), pltpu.VMEM((5 * BQ, 128), bf), pltpu.VMEM((128, 128), jnp.float32)],
        compiler_params=pltpu.CompilerParams(vmem_limit_bytes=VMEM_LIMIT),
        name="attn_fwd",
    )(qkv, qkv, qkv, rel)

def attn_bwd(qkv, rel, probs, dmixed, grad_rows, mixed, grads, cid):
    frames, cols = qkv.shape
    pairs = cols // 3 // 128
    nb = frames // BQ
    bf = jnp.bfloat16
    count = lax.axis_size("dp")
    blk = pl.BlockSpec((BQ, 128), lambda p, i: (i, p))
    full = pl.BlockSpec((frames, 128), lambda p, i: (0, p))
    riders = Riders(grads)
    width = grad_rows.shape[1]
    shape = (mixed.shape[1] // PIECE, count // 2, 2, width // count, PIECE)
    half = halved(shape, True)
    vm = pltpu.VMEM
    outs = pl.pallas_call(
        functools.partial(bwd_kernel, riders),
        grid=(pairs, nb),
        in_specs=[
            blk,
            pl.BlockSpec((frames, 128), lambda p, i: (0, pairs + p)),
            pl.BlockSpec((frames, 128), lambda p, i: (0, 2 * pairs + p)),
            pl.BlockSpec(rel.shape, lambda p, i: (0, 0)),
            pl.BlockSpec((1, 2 * BQ, frames), lambda p, i: (p, i, 0)),
            blk,
        ]
        + [in_hbm()] * (2 + len(grads)),
        out_specs=[blk, full, full, pl.BlockSpec((128, 128), lambda p, i: (0, 0))] + [in_hbm()] * (1 + len(grads)),
        out_shape=[jax.ShapeDtypeStruct((frames, cols // 3), bf)] * 3 + [jax.ShapeDtypeStruct((128, 128), jnp.float32), half] + riders.after,
        scratch_shapes=[
            vm((2 * BQ, 5 * BQ), jnp.float32), vm((128, frames), jnp.float32), vm((128, frames), jnp.float32),
            vm((128, 128), jnp.float32), vm((2 * BQ, frames), bf), vm((WIN, BQ), bf),
            vm(grad_rows.shape, bf), vm(mixed.shape, bf), vm(shape, bf), arriving(shape), vm(half.shape, half.dtype),
            vm((128, 128), bf), vm((128, 128), jnp.float32),
            pltpu.SemaphoreType.DMA((2,)), pltpu.SemaphoreType.DMA((3, shape[0])),
        ]
        + riders.scratch,
        compiler_params=pltpu.CompilerParams(vmem_limit_bytes=VMEM_LIMIT, collective_id=cid, has_side_effects=True),
        cost_estimate=pl.CostEstimate(flops=20 * frames * frames * 128 * pairs, bytes_accessed=20_000_000, transcendentals=0),
        name="attn_bwd",
    )(qkv, qkv, qkv, rel, probs, dmixed, grad_rows, mixed, *riders.arrays)
    return list(outs[:4]) + [[Grad(outs[4], 1, True)] + riders.results(outs[5:])]


def body(
    features,
    w1_in,
    w1_out,
    gain_ffn1,
    w_qkv,
    w_attn_out,
    rel_table,
    gain_attn,
    w_conv_in,
    w_depth,
    gain_depth,
    w_conv_out,
    gain_conv,
    w2_in,
    w2_out,
    gain_ffn2,
    gain_final,
    cotangent,
):
    local_frames, clip_count, width = features.shape
    rows = local_frames * clip_count
    f32, bf = jnp.float32, jnp.bfloat16
    s0 = features.reshape(rows, width)
    seed = cotangent.reshape(rows, width)
    spare = jnp.zeros((width - gain_depth.shape[0],), bf)
    gains = jnp.concatenate([gain_ffn1, gain_attn, gain_conv, gain_ffn2, gain_final, gain_depth, spare])
    gains = gains.astype(f32).reshape(-1, 128)
    flat_qkv = w_qkv.transpose(1, 0, 2)
    flat_conv = w_conv_in.reshape(width, -1)
    units = w1_in.shape[1]
    half = units // PIECE // 2
    dp_count = lax.axis_size("dp")
    done = dp_count.bit_length() - 1
    pending = lambda items: [g for g in items if g.bit < done]
    chans = w_conv_out.shape[0]

    def swish_out(h, extra, outs):
        act, slope = silu_pair(h)
        outs[0][...] = act.astype(bf)
        outs[1][...] = slope.astype(bf)

    def plain_out(h, extra, outs):
        outs[0][...] = h.astype(outs[0].dtype)

    def glu_out(h, extra, outs):
        p0 = h[:, :chans]
        sig = jax.nn.sigmoid(h[:, chans:])
        glu = p0 * sig
        outs[0][...] = glu
        outs[1][...] = sig.astype(bf)
        outs[2][...] = (glu * (1.0 - sig)).astype(bf)

    def slope_out(h, extra, outs):
        outs[0][...] = (h * extra[0][...].astype(f32)).astype(bf)

    def first(branch, ins, gains, outs, sums):
        return (unit_norm(ins[0].astype(f32))[0] * gains[0:1, :]).astype(bf)

    def forward(scale, row):
        def run(branch, ins, gains, outs, sums):
            fresh = ins[0].astype(f32) + scale * branch
            outs[0][...] = fresh
            sums[0][...] += fold8(branch * branch)
            return (unit_norm(fresh)[0] * gains[row : row + 1, :]).astype(bf)
        return run

    def turn(branch, ins, gains, outs, sums):
        fresh = ins[0] + 0.5 * branch
        sums[0][...] += fold8(branch * branch)
        sums[1][...] += fold8(fresh * fresh)
        unit, inverse = unit_norm(fresh)
        outs[0][...] = unit * gains[4:5, :]
        grad = ins[1].astype(f32)
        scaled = grad * gains[4:5, :]
        mean_one = jnp.mean(scaled, -1, keepdims=True)
        mean_two = jnp.mean(scaled * unit, -1, keepdims=True)
        sums[2][...] += fold8(grad * unit)
        back = inverse * (scaled - mean_one - unit * mean_two)
        outs[1][...] = back
        return (0.5 * back).astype(bf)

    def backward(scale, row):
        def run(branch, ins, gains, outs, sums):
            pull, grad_gain = norm_pull(branch, ins[1].astype(f32), gains[row : row + 1, :])
            fresh = ins[0] + pull
            outs[0][...] = fresh
            sums[0][...] += grad_gain
            return (scale * fresh).astype(bf)
        return run

    a1, act1, slope1, _ = stage(
        "ffn1_in", 0, rows, width, dp_count, gains, enter=(w1_in, False, swish_out, (), ((units, bf), (units, bf))),
        junction=first, row_in=(s0,),
    )
    a2, qkv, s1, sq1, _ = stage(
        "ffn1_out", 1, rows, width, dp_count, gains, leave=(act1, w1_out, False),
        enter=(flat_qkv, False, plain_out, (), ((3 * w_qkv.shape[2], bf),)),
        junction=forward(0.5, 1), row_in=(s0,), row_out=(f32,), sums=1,
    )
    turned_table = rel_table.T
    mixed, probs = attn_fwd(qkv, turned_table)
    a3, glu, sig, tail, s2, sq2, _ = stage(
        "attn_out", 2, rows, width, dp_count, gains, leave=(mixed, w_attn_out, False),
        enter=(flat_conv, False, glu_out, (), ((chans, f32), (chans, bf), (chans, bf))),
        junction=forward(1.0, 2), row_in=(s1,), row_out=(f32,), sums=1,
    )
    act3, slope3, depth_unit, depth_stat = conv_mid(glu, w_depth, gains, width, 10)
    a4, act2, slope2, s3, sq3, _ = stage(
        "conv_out", 3, rows, width, dp_count, gains, leave=(act3, w_conv_out, False),
        enter=(w2_in, False, swish_out, (), ((units, bf), (units, bf))),
        junction=forward(1.0, 3), row_in=(s2,), row_out=(f32,), sums=1,
    )
    db4, dh2, output, grad4, sq4, sq5, dgf, _ = stage(
        "ffn2_out", 4, rows, width, dp_count, gains, leave=(act2, w2_out, False),
        enter=(w2_out, True, slope_out, (slope2,), ((units, bf),)),
        junction=turn, row_in=(s3, seed), row_out=(f32, f32), sums=3,
    )
    db3, de3, grad3, dg2, (ga_in, gb_in, gw2_out) = stage(
        "ffn2_back", 5, rows, width, dp_count, gains, leave=(dh2, w2_in, True),
        enter=(w_conv_out, True, plain_out, (), ((chans, f32),)), dws=(
            weight(a4, dh2, "join", False, 1, 0, half),
            weight(a4, dh2, "join", False, 1, half, units // PIECE - half),
            weight(db4, act2, "far", True),
        ),
        junction=backward(1.0, 3), row_in=(grad4, s3), row_out=(f32,), sums=1,
    )
    dpaired, tap_sums, (gw2_out, ga_in) = conv_mid_back(
        de3, slope3, depth_unit, depth_stat, glu, sig, tail, w_depth, gains, width, 11, [gw2_out, ga_in]
    )
    db2, dmixed, grad2, dgc, (gconv_in, gconv_out, gb_in, gw2_out, ga_in) = stage(
        "conv_back", 6, rows, width, dp_count, gains, leave=(dpaired, flat_conv, True),
        enter=(w_attn_out, True, plain_out, (), ((w_attn_out.shape[0], bf),)), dws=(weight(a3, dpaired, "far", False), weight(db3, act3, "far", True)), grads=(gb_in, gw2_out, ga_in),
        junction=backward(1.0, 2), row_in=(grad3, s2), row_out=(f32,), sums=1,
    )
    dq, dk, dv, dt, (gattn, gb_in, ga_in, gconv_in, gconv_out) = attn_bwd(
        qkv, turned_table, probs, dmixed, db2, mixed, [gb_in, ga_in, gconv_in, gconv_out], 9
    )
    dqkv = (dq, dk, dv)
    waiting = pending([gattn, gconv_in, gconv_out, ga_in, gb_in, gw2_out])
    grad0, ends, other_rows, table_end, taps_end, lead_row = stage(
        "attn_back", 7, rows, width, dp_count, gains, leave=(dqkv, flat_qkv, True),
        enter=(w1_out, True, slope_out, (slope1,), ((units, bf),)),
        dws=(
            weight(a2, dqkv, "far", False),
            weight("all", act1, "front", True),
            weight(a1, "out", "close", False, pieces=units // PIECE),
        ),
        grads=waiting, small=((dgc, dg2, dgf, sq1, sq2, sq3, sq4, sq5), dt, tap_sums),
        tail=(w1_in, backward(1.0, 0), (s0,)),
        junction=backward(0.5, 1), row_in=(grad2, s1), row_out=(f32,), sums=1,
    )
    gqkv, gw1_out, gw1_in = ends[:3]
    for item, end in zip(waiting, ends[3:]):
        item.array = end.array

    def finish(item):
        flip = item.turned and item.array.shape[0] * dp_count == width and (width // dp_count) % 128 != 0
        return item.array.T if flip else item.array

    token_total = rows * lax.axis_size("mp") * dp_count
    ends = [
        ([output], 1),
        ([grad0], 1),
        ([finish(gw1_in)], 0),
        ([finish(gw1_out)], 0),
        ([finish(gqkv)], -3),
        ([finish(gattn)], 0),
        ([finish(gconv_in)], 2),
        ([finish(gconv_out)], 0),
        ([finish(ga_in), finish(gb_in)], 0),
        ([finish(gw2_out)], 0),
    ]
    done_ends = publish(ends, [lead_row, other_rows, table_end, taps_end], {8: False}, rel_table.shape[0], float(token_total * width))
    (output, grad0, gw1_in, gw1_out, gqkv, gattn, gconv_in, gconv_out, gw2_in, gw2_out) = done_ends[:10]
    *gain_sums, table_sum, depth_sum, depth_gain_sum, rms_stats = done_ends[10:]
    gain_sums = [g[0] for g in gain_sums]
    return (
        output,
        grad0,
        gw1_in,
        gw1_out,
        gain_sums[0],
        gqkv.transpose(1, 0, 2),
        gattn,
        table_sum.T,
        gain_sums[1],
        gconv_in,
        depth_sum,
        depth_gain_sum[0],
        gconv_out,
        gain_sums[2],
        gw2_in,
        gw2_out,
        gain_sums[3],
        gain_sums[4],
        rms_stats[0],
    )


def solution(mesh):
    return jax.shard_map(
        body,
        mesh=mesh,
        in_specs=(
            P("mp", "dp", None),
            P(None, "mp"),
            P("mp", None),
            P(),
            P(None, None, "mp"),
            P("mp", None),
            P(),
            P(),
            P(None, None, "mp"),
            P(None, "mp"),
            P("mp"),
            P("mp", None),
            P(),
            P(None, "mp"),
            P("mp", None),
            P(),
            P(),
            P("mp", "dp", None),
        ),
        out_specs=(
            P("mp", "dp", None),
            P("mp", "dp", None),
            P("dp", "mp"),
            P("mp", "dp"),
            P(),
            P("dp", None, "mp"),
            P("mp", "dp"),
            P(),
            P(),
            P("dp", None, "mp"),
            P(None, "mp"),
            P("mp"),
            P("mp", "dp"),
            P(),
            P("dp", "mp"),
            P("mp", "dp"),
            P(),
            P(),
            P(),
        ),
        check_vma=False,
    )
```

```python
import functools

import jax
import jax.numpy as jnp
from jax import lax
from jax.experimental import pallas as pl
from jax.experimental.pallas import tpu as pltpu
from jax.sharding import PartitionSpec as P

HEAD = 64
REL_LEFT = 64
REL_RIGHT = 8
BQ = 128
WIN = 4 * BQ


epsilon = 1e-05


def nt(a, b):
    return lax.dot_general(a, b, (((1,), (1,)), ((), ())), preferred_element_type=jnp.float32)
def nn(a, b):
    return lax.dot_general(a, b, (((1,), (0,)), ((), ())), preferred_element_type=jnp.float32)
def tn(a, b):
    return lax.dot_general(a, b, (((0,), (0,)), ((), ())), preferred_element_type=jnp.float32)

MESH = pl.DeviceIdType.MESH
CHUNKS = 4
TABLE_ROWS = 40
LAG = 2
JOIN_SLOT = 3
PIECE = 256
VMEM_LIMIT = 58 << 20


def silu_pair(h):
    sig = jax.nn.sigmoid(h)
    act = h * sig
    return act, sig + act * (1.0 - sig)


def unit_norm(s):
    centred = s - jnp.mean(s, -1, keepdims=True)
    inverse = lax.rsqrt(jnp.mean(centred * centred, -1, keepdims=True) + epsilon)
    return centred * inverse, inverse


def fold8(x):
    return jnp.sum(x.reshape(x.shape[0] // 8, 8, x.shape[1]), 0)


def norm_pull(grad, s, gain):
    unit, inverse = unit_norm(s)
    scaled = grad * gain
    first = jnp.mean(scaled, -1, keepdims=True)
    second = jnp.mean(scaled * unit, -1, keepdims=True)
    return inverse * (scaled - first - unit * second), fold8(grad * unit)


def in_hbm():
    return pl.BlockSpec(memory_space=pltpu.HBM)


class Grad:
    def __init__(self, array, bit, turned):
        self.array, self.bit, self.turned = array, bit, turned


def halved(shape, turned):
    pieces, pairs, _, block, cols = shape
    if pairs > 1:
        return jax.ShapeDtypeStruct((pieces, pairs // 2, 2, block, cols), jnp.bfloat16)
    if turned and block % 128 == 0:
        return jax.ShapeDtypeStruct((pieces * cols, block), jnp.float32)
    return jax.ShapeDtypeStruct((block, pieces * cols), jnp.float32)


def arriving(shape):
    return pltpu.VMEM((shape[0], shape[1]) + tuple(shape[3:]), jnp.bfloat16)


def place(dp, bit):
    own = (dp // 2**bit) % 2
    return own, dp + 2**bit * (1 - 2 * own)


def halving_copy(src, landing, piece, bit, send, recv, slot):
    dp, mp = lax.axis_index("dp"), lax.axis_index("mp")
    own, partner = place(dp, bit)
    return pltpu.make_async_remote_copy(
        src.at[piece, :, 1 - own], landing.at[piece], send.at[slot], recv.at[slot],
        device_id=(partner, mp), device_id_type=MESH,
    )


def halving_keep(src, kept, bit, sem):
    own, _ = place(lax.axis_index("dp"), bit)
    return pltpu.make_async_copy(src.at[:, :, own], kept, sem)


def region(ref, piece, cols, turned):
    if len(ref.shape) > 2:
        return ref.at[piece]
    at = pl.ds(piece * cols, cols)
    return ref.at[at, :] if turned else ref.at[:, at]


def halving_add(held, landing, out, piece, turned):
    pairs, block, cols = landing.shape[1:]
    f32 = jnp.float32
    if pairs == 1:
        total = held(piece, 0).astype(f32) + landing[piece, 0].astype(f32)
        turned = turned and block % 128 == 0
        region(out, piece, cols, turned)[...] = total.T if turned else total
        return

    def add(j, c):
        total = held(piece, j).astype(f32) + landing[piece, j].astype(f32)
        out[piece, j // 2, j % 2] = total.astype(jnp.bfloat16)
        return c

    lax.fori_loop(0, pairs, add, 0)


def weight(lhs, rhs, where, turned, deep=1, lo=0, pieces=None):
    if pieces is None:
        pieces = (sum(r.shape[1] for r in rhs) if isinstance(rhs, tuple) else rhs.shape[1]) // PIECE
    return lhs, rhs, where, turned, deep, lo, pieces


def flat_shape(array):
    if isinstance(array, tuple):
        return array[0].shape[0], sum(a.shape[1] for a in array)
    if len(array.shape) == 3:
        return array.shape[1], array.shape[0] * array.shape[2]
    return array.shape


def gain_row(ref, i, width):
    first = i * width // 128
    return jnp.concatenate([ref[first + j : first + j + 1, :] for j in range(width // 128)], 1)


class Riders:
    def __init__(self, grads):
        self.plan = [(g.array.shape[0], g.bit, g.turned) for g in grads]
        self.arrays = [g.array for g in grads]
        self.after = [halved(g.array.shape, g.turned) for g in grads]
        self.slots = sum(x[0] for x in self.plan)
        self.scratch = [arriving(g.array.shape) for g in grads] * 2 + [pltpu.VMEM(a.shape, a.dtype) for a in self.after]
        if grads:
            self.scratch += [pltpu.SemaphoreType.DMA((self.slots,))] * 3 + [pltpu.SemaphoreType.DMA((len(grads),))]

    def bind(self, srcs, outs, scratch):
        n = len(self.plan)
        sems = scratch[3 * n :]
        holds, hops, slot = [], [], 0
        for i, (pieces, bit, turned) in enumerate(self.plan):
            landing, keep, half = scratch[i], scratch[n + i], scratch[2 * n + i]
            holds.append(halving_keep(srcs[i], keep, bit, sems[3].at[i]))
            flip = turned and landing.shape[2] % 128 == 0
            for p in range(pieces):
                move = halving_copy(srcs[i], landing, p, bit, sems[0], sems[1], slot)
                store = pltpu.make_async_copy(region(half, p, PIECE, flip), region(outs[i], p, PIECE, flip), sems[2].at[slot])
                hops.append((move, store, lambda q, j, keep=keep: keep[q, j], landing, half, p, turned))
                slot += 1
        self.holds, self.hops = holds, hops

    def targets(self):
        dp, mp = lax.axis_index("dp"), lax.axis_index("mp")
        return [(place(dp, b)[1], mp) for b in sorted({x[1] for x in self.plan})]

    def start(self):
        for hold in self.holds:
            hold.start()
        for hop in self.hops:
            hop[0].start()

    def finish(self):
        for hold in self.holds:
            hold.wait()
        for hop in self.hops:
            hop[0].wait_recv()
            halving_add(*hop[2:])
            hop[1].start()
        for hop in self.hops:
            hop[0].wait_send()
            hop[1].wait()

    def results(self, outs):
        return [Grad(a, b + 1, t) for a, (_, b, t) in zip(outs, self.plan)]


def greet(targets):
    barrier = pltpu.get_barrier_semaphore()
    for to in targets:
        pl.semaphore_signal(barrier, inc=1, device_id=to, device_id_type=MESH)
    return lambda: pl.semaphore_wait(barrier, len(targets))


class Doubling:
    def __init__(self, course, refs, lands, sems, partner):
        self.course, self.items, self.sems, self.partner = course, list(zip(refs, lands)), sems, partner
        self.done = 0

    def copies(self, n):
        at = self.course[n]
        return [
            (
                pltpu.make_async_remote_copy(
                    r, l.at[n], self.sems[0].at[i, n], self.sems[1].at[i, n], device_id=self.partner(at), device_id_type=MESH
                ),
                r,
                l.at[n],
            )
            for i, (r, l) in enumerate(self.items)
            if i < 2 or not isinstance(at, str)
        ]

    def start(self, n=0):
        for cp, _, _ in self.copies(n):
            cp.start()

    def advance(self, n):
        for cp, r, l in self.copies(n):
            cp.wait()
            r[...] += l[...]
        if n + 1 < len(self.course):
            self.start(n + 1)

    def step(self):
        if self.done < len(self.course):
            self.advance(self.done)
            self.done += 1


def stage(name, cid, rows, width, count, gains, *, leave=None, enter=None, dws=(), grads=(), small=None, tail=None, junction, row_in=(), row_out=(), sums=0):
    chunk = rows // CHUNKS
    frames = rows * 4
    bits_all = count.bit_length() - 1
    f32, bf = jnp.float32, jnp.bfloat16
    ins, vm_ins, out_shape, scratch = [], [], [], []
    known = {}

    def add_in(array, direct=False):
        if isinstance(array, str):
            return array
        if direct:
            ins.append(array)
            return len(ins) - 1
        if id(array) not in known:
            group = array if isinstance(array, tuple) else (array,)
            known[id(array)] = len(vm_ins)
            vm_ins.append((len(ins), len(group), pltpu.VMEM(flat_shape(array), group[0].dtype)))
            ins.extend(group)
        return known[id(array)]

    out_slots = [0]

    def add_scratch(item):
        scratch.append(item)
        return len(scratch) - 1

    def add_out(shape, dtype, slots, kept=True):
        if not kept:
            return -1 - add_scratch(pltpu.VMEM(shape, dtype)), None
        out_shape.append(jax.ShapeDtypeStruct(shape, dtype))
        first = out_slots[0]
        out_slots[0] += slots
        return len(out_shape) - 1, first

    add_dw = lambda where: [(add_in(d[0]), add_in(d[1])) if d[2] in where else None for d in dws]
    groups = []
    if leave:
        x_i, wl_i = add_in(leave[0]), add_in(leave[1])
        leave_s = [add_scratch(pltpu.VMEM((rows, width), f32)) for _ in range(2)]
        leave_s += [add_scratch(pltpu.VMEM((rows, width), bf)) for _ in range(6)]
        wl_s = add_scratch(pltpu.VMEM(flat_shape(leave[1])[::-1], bf)) if leave[2] else None
        groups.append(len(vm_ins))
        add_dw(("far",))
    gains_i = add_in(gains)
    gain_s = add_scratch(pltpu.VMEM((8, width), f32))
    row_i = [add_in(r) for r in row_in]
    if not leave:
        groups.append(len(vm_ins))
    add_dw(("near", "join"))
    kept = not tail
    if enter:
        we_i = add_in(enter[0])
        extra_i = [add_in(e) for e in enter[3]]
        we_s = add_scratch(pltpu.VMEM(flat_shape(enter[0])[::-1], bf)) if enter[1] else None
        all_o = add_out((frames, width), bf, 4 * CHUNKS, kept)
        e_o = [add_out((frames, c), d, 4 * CHUNKS, kept) for c, d in enter[4]]
    r_o = [add_out((rows, width), d, CHUNKS, kept) for d in row_out]
    s_o = [add_out((8, width), f32, 1, kept) for _ in range(sums)]
    if small:
        vectors_in, table_in, taps_in = small
        vector_i = [add_in(v) for v in vectors_in]
        table_i, taps_i = add_in(table_in), add_in(taps_in)
    groups.append(len(vm_ins))
    if tail:
        add_dw(("front",))
        tw_i = add_in(tail[0])
        tw_s = add_scratch(pltpu.VMEM(flat_shape(tail[0])[::-1], bf))
        tail_i = [add_in(r) for r in tail[2]]
        add_dw(("close",))
        tail_o = [add_out((rows, width), f32, CHUNKS)]
        tail_sum = add_out((8, width), f32, 1, False)
    groups.append(len(vm_ins))
    fixed_out = len(out_shape)
    plan, dw_o = [], []
    for d in dws:
        shape = (d[6], count // 2, 2, width // count, PIECE)
        if d[2] == "join":
            dw_o.append(add_out(shape, bf, shape[0]))
        else:
            plan.append((shape, 0, d[3], bits_all if tail else 1, add_scratch(pltpu.VMEM(shape, bf)), None, None))
            dw_o.append(len(plan) - 1)
    dw_in = [(add_in(d[0]), add_in(d[1])) for d in dws]
    first_grad = len(plan)
    for g in grads:
        shape = g.array.shape
        plan.append((shape, g.bit, g.turned, bits_all if tail else g.bit + 1, None, add_in(g.array, True), add_scratch(arriving(shape))))
    chains = []
    slots = 0
    for shape, bit, turned, end, src_s, src_i, keep_s in plan:
        links = []
        pieces = shape[0]
        for b in range(bit, end):
            nxt = halved(shape, turned)
            land_s = add_scratch(arriving(shape))
            if b == end - 1:
                links.append((b, slots, land_s, None, add_out(nxt.shape, nxt.dtype, pieces)))
            else:
                links.append((b, slots, land_s, add_scratch(pltpu.VMEM(nxt.shape, nxt.dtype)), None))
            slots += pieces
            shape = nxt.shape
        chains.append((pieces, turned, src_s, src_i, keep_s, links))
    if small:
        small_shapes = [(8, width), (TABLE_ROWS, 128), taps_in.shape]
        small_o = [add_out(s, f32, 1) for s in small_shapes]
        lead_o = add_out((1, width), f32, 1)
        downward = list(range(bits_all - 1, -1, -1))
        courses = [downward[-1:] + downward[:-1] + ["sib", "far"], ["sib", "far"] + downward]
        small_l = [add_scratch(pltpu.VMEM((bits_all + 2,) + s, f32)) for s in small_shapes]
        lead_l = [add_scratch(pltpu.VMEM((bits_all + 2, 1, width), f32))]
        small_sems = [add_scratch(pltpu.SemaphoreType.DMA((3, bits_all + 2))) for _ in range(4)]
    if slots:
        grad_sems = [add_scratch(pltpu.SemaphoreType.DMA((slots,))) for _ in range(2)]
    ring_sems = [add_scratch(pltpu.SemaphoreType.DMA((6, CHUNKS))) for _ in range(2)]
    load_sem = add_scratch(pltpu.SemaphoreType.DMA((len(ins),)))
    store_sem = add_scratch(pltpu.SemaphoreType.DMA((out_slots[0],)))
    n_in, n_out = len(ins), len(out_shape)
    vm_at = [add_scratch(item[2]) for item in vm_ins]
    vo_at = [add_scratch(pltpu.VMEM(o.shape, o.dtype)) for o in out_shape]

    def kernel(*refs):
        hbm_in, hbm_out, t = refs[:n_in], refs[n_in : n_in + n_out], refs[n_in + n_out :]
        vout = lambda o: t[-1 - o[0]] if o[0] < 0 else t[vo_at[o[0]]]

        def vin(i):
            if i == "all":
                return vout(all_o)
            if i == "out":
                return vout(e_o[0])
            return t[vm_at[i]]

        waited = set()

        def load(i):
            first, parts, _ = vm_ins[i]
            if len(hbm_in[first].shape) == 3:
                slabs, _, cols = hbm_in[first].shape
                return [
                    pltpu.make_async_copy(hbm_in[first].at[n], vin(i).at[:, pl.ds(n * cols, cols)], t[load_sem].at[first])
                    for n in range(slabs)
                ]
            if parts == 1:
                return [pltpu.make_async_copy(hbm_in[first], vin(i), t[load_sem].at[first])]
            copies, at = [], 0
            for n in range(first, first + parts):
                cols = hbm_in[n].shape[1]
                copies.append(pltpu.make_async_copy(hbm_in[n], vin(i).at[:, pl.ds(at, cols)], t[load_sem].at[n]))
                at += cols
            return copies

        begun = [0]

        def begin_loads(group):
            for i in range(begun[0], groups[group]):
                for cp in load(i):
                    cp.start()
            begun[0] = max(begun[0], groups[group])

        def need(*items):
            for i in items:
                if not isinstance(i, str) and i not in waited:
                    waited.add(i)
                    for cp in load(i):
                        cp.wait()

        dp, me = lax.axis_index("dp"), lax.axis_index("mp")
        core, chip = me % 2, me // 2
        sib = chip * 2 + 1 - core
        far = (1 - chip) * 2 + core
        diag = (1 - chip) * 2 + 1 - core
        bits = sorted({link[0] for ch in chains for link in ch[5]} | set(range(bits_all) if small else ()))
        meet = greet([(dp, sib), (dp, far)] + [(place(dp, b)[1], me) for b in bits])
        begin_loads(0)

        def part(ref, block, k):
            return ref.at[pl.ds(pl.multiple_of(block * rows + k * chunk, chunk), chunk)]

        def store_rows(o, block, k):
            return pltpu.make_async_copy(
                part(vout(o), block, k), part(hbm_out[o[0]], block, k), t[store_sem].at[o[1] + block * CHUNKS + k]
            )

        def store_whole(o):
            return pltpu.make_async_copy(vout(o), hbm_out[o[0]], t[store_sem].at[o[1]])

        def store_piece(o, piece, cols, turned):
            return pltpu.make_async_copy(
                region(vout(o), piece, cols, turned), region(hbm_out[o[0]], piece, cols, turned), t[store_sem].at[o[1] + piece]
            )

        def copy(kind, k, src, dst, to):
            return pltpu.make_async_remote_copy(
                src, dst, t[ring_sems[0]].at[kind, k], t[ring_sems[1]].at[kind, k], device_id=(dp, to), device_id_type=MESH
            )

        if leave:
            px, own, sb, sr, xs, xr, ob, orv = [t[s] for s in leave_s]
        if enter:
            all_ref = vout(all_o)
            we_ref = t[we_s] if enter[1] else vin(we_i)
        pair_send = lambda k: copy(0, k, part(sb, 0, k), part(sr, 0, k), sib)
        far_send = lambda k: copy(1, k, part(xs, 0, k), part(xr, 0, k), far)
        own_send = lambda k: copy(2, k, part(ob, 0, k), part(orv, 0, k), sib)
        all_far = lambda k: copy(3, k, part(all_ref, me, k), part(all_ref, me, k), far)
        all_sib = lambda k: copy(4, k, part(all_ref, me, k), part(all_ref, me, k), sib)
        all_fwd = lambda k: copy(5, k, part(all_ref, far, k), part(all_ref, far, k), sib)
        got_far = lambda k: copy(3, k, part(all_ref, far, k), part(all_ref, far, k), far)
        got_sib = lambda k: copy(4, k, part(all_ref, sib, k), part(all_ref, sib, k), sib)
        got_diag = lambda k: copy(5, k, part(all_ref, diag, k), part(all_ref, diag, k), sib)

        def source(c, step):
            pieces, turned, src_s, src_i, keep_s, links = chains[c]
            if step:
                return t[links[step - 1][3]]
            return t[src_s] if src_s is not None else hbm_in[src_i]

        def hop(c, step, piece):
            b, slot, land_s, _, _ = chains[c][5][step]
            return halving_copy(source(c, step), t[land_s], piece, b, t[grad_sems[0]], t[grad_sems[1]], slot + piece)

        def keep(c):
            return halving_keep(hbm_in[chains[c][3]], t[chains[c][4]], chains[c][5][0][0], t[load_sem].at[chains[c][3]])

        held_back = set()

        def settle(c, step, piece):
            pieces, turned, src_s, src_i, keep_s, links = chains[c]
            b, slot, land_s, out_s, out_o = links[step]
            hop(c, step, piece).wait_recv()
            if step == 0 and src_s is None:
                if c not in held_back:
                    held_back.add(c)
                    keep(c).wait()
                held = lambda p, j: t[keep_s][p, j]
            else:
                own_bit, _ = place(dp, b)
                src = source(c, step)
                held = lambda p, j: src[p, j, own_bit]
            landing = t[land_s]
            out = t[out_s] if out_o is None else vout(out_o)
            halving_add(held, landing, out, piece, turned)
            if out_o is not None:
                store_piece(out_o, piece, PIECE, turned and landing.shape[2] % 128 == 0).start()

        def fill(k, where):
            for d, (a, b), o in zip(dws, dw_in, dw_o):
                if d[2] != where:
                    continue
                chain = None if where == "join" else o
                dw = vout(o) if chain is None else t[chains[o][2]]

                @pl.when(k < dw.shape[0])
                def _(a=a, b=b, dw=dw, chain=chain, o=o, lo=d[5]):
                    g = tn(vin(a)[...], vin(b)[:, pl.ds(pl.multiple_of((lo + k) * PIECE, PIECE), PIECE)])
                    dw[k] = g.astype(bf).reshape(dw.shape[1:])
                    if chain is None:
                        store_piece(o, k, PIECE, False).start()
                    else:
                        hop(chain, 0, k).start()

        def need_for(where):
            for d, (a, b) in zip(dws, dw_in):
                if d[2] == where:
                    need(a, b)

        def leave_phase(x_ref, wl_ref, far_fill, near_fill):
            def two(k, block_a, block_b):
                lhs = jnp.concatenate([part(x_ref, block_a, k)[...], part(x_ref, block_b, k)[...]], 0)
                return nn(lhs, wl_ref[...])

            def push(k):
                pair_send(k).wait_recv()
                part(xs, 0, k)[...] = (part(px, 0, k)[...] + part(sr, 0, k)[...].astype(f32)).astype(bf)
                far_send(k).start()

            def out_far(k, c):
                p = two(k, far, diag)
                part(px, 0, k)[...] = p[:chunk]
                part(sb, 0, k)[...] = p[chunk:].astype(bf)
                pair_send(k).start()

                @pl.when(k > 0)
                def _():
                    push(k - 1)

                fill(k, far_fill)
                return c

            lax.fori_loop(0, CHUNKS, out_far, 0)
            need_for(near_fill)

            def out_near(k, c):
                p = two(k, me, sib)
                part(own, 0, k)[...] = p[:chunk]
                part(ob, 0, k)[...] = p[chunk:].astype(bf)
                own_send(k).start()

                @pl.when(k == 0)
                def _():
                    push(CHUNKS - 1)

                fill(k, near_fill)
                return c

            lax.fori_loop(0, CHUNKS, out_near, 0)

        def leave_drain():
            def drain(k, c):
                pair_send(k).wait_send()
                far_send(k).wait_send()
                own_send(k).wait_send()
                return c

            lax.fori_loop(0, CHUNKS, drain, 0)

        def join_phase(rule, has_leave, in_refs, outs, totals, gathers):
            def join(k, c):
                fill(k, "join")
                branch = None
                if has_leave:
                    own_send(k).wait_recv()
                    far_send(k).wait_recv()
                    branch = part(own, 0, k)[...] + part(orv, 0, k)[...].astype(f32) + part(xr, 0, k)[...].astype(f32)
                fresh = rule(
                    branch, [part(r, 0, k)[...] for r in in_refs], t[gain_s], [part(vout(o), 0, k) for o in outs], [vout(o) for o in totals]
                )
                if gathers:
                    part(all_ref, me, k)[...] = fresh
                    all_far(k).start()
                    all_sib(k).start()
                for o in outs:
                    if o[0] >= 0:
                        store_rows(o, 0, k).start()
                return c

            lax.fori_loop(0, CHUNKS, join, 0)
            for o in totals:
                if o[0] >= 0:
                    store_whole(o).start()

        for o in s_o + ([tail_sum] if tail else []):
            vout(o)[...] = jnp.zeros((8, width), f32)
        meet()
        if leave:
            need(x_i, wl_i)
        begin_loads(1)
        for c in range(first_grad, len(chains)):
            for p in range(chains[c][0]):
                hop(c, 0, p).start()
        if leave:
            if leave[2]:
                t[wl_s][...] = vin(wl_i)[...].T
            need_for("far")
            leave_phase(vin(x_i), t[wl_s] if leave[2] else vin(wl_i), "far", "near")
        for c in range(first_grad, len(chains)):
            keep(c).start()
        need(gains_i, *row_i)
        for i in range(5):
            t[gain_s][i : i + 1, :] = gain_row(vin(gains_i), i, width)
        need_for("join")
        if enter and enter[1]:
            need(we_i)
            we_ref[...] = vin(we_i)[...].T
        join_phase(junction, bool(leave), [vin(r) for r in row_i], r_o, s_o, bool(enter))

        lead = [c for c in range(first_grad) if tail and dws[[i for i, o in enumerate(dw_o) if o == c][0]][2] == "far"]
        if small:
            partner = lambda at: (dp, sib) if at == "sib" else (dp, far) if at == "far" else (place(dp, at)[1], me)
            need(*vector_i, table_i, taps_i)
            rows_ref = vout(small_o[0])
            rows_ref[...] = jnp.zeros((8, width), f32)
            vectors = [vout(s_o[0])] + [vin(i) for i in vector_i]
            for i, v in enumerate(vectors[:4]):
                rows_ref[i : i + 1, :] = jnp.sum(v[...], 0, keepdims=True)
            for i, v in enumerate(vectors[4:]):
                line = jnp.sum(v[...], 0, keepdims=True)
                rows_ref[4:5, i * 128 : (i + 1) * 128] = functools.reduce(
                    jnp.add, [line[:, j * 128 : (j + 1) * 128] for j in range(width // 128)]
                )
            both = vin(table_i)[...]
            both = both + pltpu.roll(both, 64, 1)
            left = lax.broadcasted_iota(jnp.int32, (TABLE_ROWS, 128), 1) < HEAD
            vout(small_o[1])[...] = jnp.where(left, both[:TABLE_ROWS], both[TABLE_ROWS : 2 * TABLE_ROWS])
            vout(small_o[2])[...] = vin(taps_i)[...]
            wide = Doubling(courses[0], [vout(o) for o in small_o], [t[l] for l in small_l], [t[s] for s in small_sems[:2]], partner)
            wide.start()

        if enter:
            begin_loads(len(groups) - 1)
            need(we_i, *extra_i)

            def work(k, block_a, block_b):
                lhs = jnp.concatenate([part(all_ref, block_a, k)[...], part(all_ref, block_b, k)[...]], 0)
                h = nn(lhs, we_ref[...])
                for i, block in enumerate((block_a, block_b)):
                    view = lambda ref: part(ref, block, k)
                    enter[2](h[i * chunk : (i + 1) * chunk], [view(vin(r))[...] for r in extra_i], [view(vout(o)) for o in e_o])
                    for o in [all_o] + e_o:
                        if o[0] >= 0:
                            store_rows(o, block, k).start()

            def gather(k, c):
                got_sib(k).wait_recv()
                work(k, me, sib)
                got_far(k).wait_recv()
                all_fwd(k).start()
                got_diag(k).wait_recv()
                work(k, far, diag)
                if small:

                    for n, at in enumerate((1, CHUNKS - 1)):

                        @pl.when(k == at)
                        def _(n=n):
                            wide.advance(n)

                if lead:

                    @pl.when(k == CHUNKS - 2)
                    def _():
                        for ch in lead:
                            for p in range(chains[ch][0]):
                                settle(ch, 0, p)
                                hop(ch, 1, p).start()

                return c

            lax.fori_loop(0, CHUNKS, gather, 0)
            if small:
                wide.done = 2

        early = 0
        if tail:
            need_for("front")

            def front(k, c):
                fill(k, "front")
                return c

            lax.fori_loop(0, CHUNKS, front, 0)
            early = 1
            if lead and bits_all > 2:
                early = 2
                for ch in lead:
                    for p in range(chains[ch][0]):
                        settle(ch, 1, p)
                        hop(ch, 2, p).start()
            leave_drain()
            need(tw_i, *tail_i)
            t[tw_s][...] = vin(tw_i)[...].T
            leave_phase(vin("out"), t[tw_s], None, "close")
            wide.step()

        def close_rows():
            join_phase(tail[1], True, [vout(r_o[0])] + [vin(r) for r in tail_i], tail_o, [tail_sum], False)
            vout(lead_o)[...] = jnp.sum(vout(tail_sum)[...], 0, keepdims=True)
            final = Doubling(courses[1], [vout(lead_o)], [t[l] for l in lead_l], [t[s] for s in small_sems[2:]], partner)
            final.start()
            return final

        depth = lambda c: len(chains[c][5])
        begin = lambda c: early if c in lead else 0
        agenda, fresh_slot = {}, 1
        for c in range(len(chains)):
            new = tail and c < first_grad and c not in lead
            for p in range(chains[c][0]):
                slot = fresh_slot if new else 0
                fresh_slot += 1 if new else 0
                for step in range(begin(c), depth(c)):
                    agenda.setdefault(slot, []).append((step, c, p))
                    slot += LAG
        final = None
        for slot in range(max(list(agenda) + [0]) + 1):
            if tail and slot == JOIN_SLOT:
                final = close_rows()
            for step, c, p in sorted(agenda.get(slot, []), key=lambda x: -x[0]):
                settle(c, step, p)
                if step + 1 < depth(c):
                    hop(c, step + 1, p).start()
            if tail and wide.done < len(courses[0]):
                wide.step()
            elif final is not None and slot > JOIN_SLOT and final.done < len(courses[1]) - 1:
                final.step()
        if tail:
            while final.done < len(courses[1]):
                final.step()
            for o in small_o + [lead_o]:
                store_whole(o).start()
        for c in range(len(chains)):
            for s in range(depth(c)):
                for p in range(chains[c][0]):
                    hop(c, s, p).wait_send()
            out_o = chains[c][5][-1][4]
            block = chains[c][5][-1][2]
            for p in range(chains[c][0]):
                store_piece(out_o, p, PIECE, chains[c][1] and t[block].shape[2] % 128 == 0).wait()
        if leave:
            leave_drain()

        def drain(k, c):
            if enter:
                all_far(k).wait_send()
                all_sib(k).wait_send()
                all_fwd(k).wait_send()
                for block in range(4):
                    for o in [all_o] + e_o:
                        if o[0] >= 0:
                            store_rows(o, block, k).wait()
            for o in r_o + (tail_o if tail else []):
                if o[0] >= 0:
                    store_rows(o, 0, k).wait()
            return c

        lax.fori_loop(0, CHUNKS, drain, 0)
        for o in s_o + (small_o + [lead_o] if tail else []):
            if o[0] >= 0:
                store_whole(o).wait()
        for d, o in zip(dws, dw_o):
            if d[2] == "join":
                for p in range(d[6]):
                    store_piece(o, p, PIECE, False).wait()

    flops = 0
    if leave:
        flops += 2 * frames * flat_shape(leave[1])[1 if leave[2] else 0] * width
    if enter:
        flops += 2 * frames * width * sum(c for c, _ in enter[4])
    flops += sum(2 * frames * width * PIECE * d[6] for d in dws)
    outs = pl.pallas_call(
        kernel,
        in_specs=[in_hbm()] * n_in,
        out_specs=[in_hbm()] * n_out,
        out_shape=out_shape,
        scratch_shapes=scratch,
        compiler_params=pltpu.CompilerParams(collective_id=cid, has_side_effects=True, vmem_limit_bytes=VMEM_LIMIT),
        cost_estimate=pl.CostEstimate(flops=flops, bytes_accessed=60_000_000, transcendentals=0),
        name=name,
    )(*ins)
    fixed, rest = list(outs[:fixed_out]), list(outs[fixed_out:])
    fresh = [Grad(rest.pop(0), 0, d[3]) for d in dws if d[2] == "join"]
    for item in plan:
        fresh.append(Grad(rest.pop(0), item[3], item[2]))
    return fixed + [fresh] + rest


def publish(ends, small, sizes, rel, total):
    flat, outs, where = [], [], []
    f32 = jnp.float32
    for arrays, parts in ends:
        rows = arrays[0].shape[0]
        joined = len(arrays) > 1 and sizes[len(outs)]
        shape = (rows, sum(a.shape[1] for a in arrays)) if not joined else (sum(a.shape[0] for a in arrays), arrays[0].shape[1])
        where.append((len(flat), arrays, joined))
        flat.extend(arrays)
        if parts < 0:
            outs.append((shape, (-parts, shape[0], shape[1] // -parts)))
        else:
            outs.append((shape, (shape[0], parts, shape[1] // parts) if parts else None))
    n, m = len(flat), len(ends)
    width = small[0].shape[1]
    taps = small[3].shape
    split_at = [i for i in range(m) if ends[i][1] > 0]
    slab_at = [i for i in range(m) if ends[i][1] < 0]
    small_shapes = [(1, width)] * 5 + [(HEAD, rel), (taps[0] - 1, taps[1]), (1, taps[1]), (1, 5)]

    def kernel(*refs):
        src, small_in = refs[:n], refs[n : n + 4]
        dst, small_out = refs[n + 4 : n + 4 + m], refs[n + 4 + m : n + 13 + m]
        rest = refs[n + 13 + m :]
        held, split = rest[:m], dict(zip(split_at, rest[m:-1]))
        sem = rest[-1]
        loads, stores = [], []
        for i, (first, arrays, joined) in enumerate(where):
            at, copies = 0, []
            for k in range(len(arrays)):
                ref = src[first + k]
                size = ref.shape[0 if joined else 1]
                part = held[i].at[pl.ds(at, size)] if joined else held[i].at[:, pl.ds(at, size)]
                copies.append(pltpu.make_async_copy(ref, part, sem.at[first + k]))
                at += size
            loads.append(copies)
            if i in slab_at:
                slabs, _, cols = dst[i].shape
                stores.append(
                    [
                        pltpu.make_async_copy(held[i].at[:, pl.ds(k * cols, cols)], dst[i].at[k], sem.at[n + m + k])
                        for k in range(slabs)
                    ]
                )
            else:
                stores.append([pltpu.make_async_copy(split.get(i, held[i]), dst[i], sem.at[n + i])])
        for copies in loads:
            for cp in copies:
                cp.start()
        lead, rows, table, tap = [r[...] for r in small_in]
        small_out[0][...] = lead
        for i in range(4):
            small_out[1 + i][...] = rows[i : i + 1]
        turned = jnp.concatenate([table, jnp.zeros((128 - TABLE_ROWS, 128), f32)], 0).T
        small_out[5][:, :TABLE_ROWS] = turned[:HEAD, :TABLE_ROWS]
        small_out[5][:, TABLE_ROWS:] = turned[HEAD:, : rel - TABLE_ROWS]
        small_out[6][...] = tap[:-1]
        small_out[7][...] = tap[-1:]
        lane = lax.broadcasted_iota(jnp.int32, (1, 128), 1)
        mean = jnp.zeros((1, 128), f32)
        for i in range(5):
            mean = jnp.where(lane == i, jnp.sum(rows[4:5, i * 128 : (i + 1) * 128], -1, keepdims=True) / total, mean)
        root = jnp.sqrt(mean)
        small_out[8][...] = root[:, :5]
        for i in range(m):
            for cp in loads[i]:
                cp.wait()
            if i in split:
                cols = split[i].shape[2]
                for j in range(split[i].shape[1]):
                    split[i][:, j, :] = held[i][:, j * cols : (j + 1) * cols]
            for cp in stores[i]:
                cp.start()
        for copies in stores:
            for cp in copies:
                cp.wait()

    vm = pl.BlockSpec(memory_space=pltpu.VMEM)
    return pl.pallas_call(
        kernel,
        in_specs=[in_hbm()] * n + [vm] * 4,
        out_specs=[in_hbm()] * m + [vm] * 9,
        out_shape=[jax.ShapeDtypeStruct(o[1] or o[0], f32) for o in outs] + [jax.ShapeDtypeStruct(s, f32) for s in small_shapes],
        scratch_shapes=[pltpu.VMEM(o[0], f32) for o in outs]
        + [pltpu.VMEM(outs[i][1], f32) for i in split_at]
        + [pltpu.SemaphoreType.DMA((n + m + 4,))],
        compiler_params=pltpu.CompilerParams(vmem_limit_bytes=VMEM_LIMIT),
        name="publish",
    )(*flat, *small)


SPAN = 128


def exchange(stats, landing, send, recv):
    dp, me = lax.axis_index("dp"), lax.axis_index("mp")
    core, chip = me % 2, me // 2
    others = [chip * 2 + 1 - core, (1 - chip) * 2 + core, (1 - chip) * 2 + 1 - core]
    return [
        pltpu.make_async_remote_copy(
            stats, landing.at[i], send.at[i], recv.at[i], device_id=(dp, to), device_id_type=MESH
        )
        for i, to in enumerate(others)
    ]


def group_targets():
    dp, me = lax.axis_index("dp"), lax.axis_index("mp")
    core, chip = me % 2, me // 2
    return [(dp, chip * 2 + 1 - core), (dp, (1 - chip) * 2 + core), (dp, (1 - chip) * 2 + 1 - core)]


def to_rows(first, second):
    lane = lax.broadcasted_iota(jnp.int32, (SPAN, SPAN), 1)
    both = jnp.where(lane == 0, first, jnp.where(lane == 1, second, 0.0))
    return both.T[:8]


def to_columns(rows8):
    return jnp.concatenate([rows8, jnp.zeros((SPAN - 8, SPAN), jnp.float32)], 0).T


def shifted(window, by):
    return window if by == 0 else pltpu.roll(window, window.shape[0] - by, 0)


def depth_gain_row(ref, width, chans):
    first = 5 * width // 128
    return jnp.concatenate([ref[first + j : first + j + 1, :] for j in range(chans // 128)], 1)


def conv_mid(glu, w_depth, gains, width, cid):
    frames, chans = glu.shape
    taps = w_depth.shape[0]
    reach = taps - 1
    edge = (reach + 7) // 8 * 8
    f32, bf = jnp.float32, jnp.bfloat16
    tiles, lanes = frames // SPAN, chans // 128

    def kernel(glu_h, w_h, g_h, act_h, slope_h, unit_h, stat_h, pad, w_raw, g_raw, w_v, g_v, act, slope, unit, stat, sendbuf, landing, lsem, ssem, send, recv):
        meet = greet(group_targets())
        loads = [
            pltpu.make_async_copy(glu_h, pad.at[pl.ds(edge, frames)], lsem.at[0]),
            pltpu.make_async_copy(w_h, w_raw, lsem.at[1]),
            pltpu.make_async_copy(g_h, g_raw, lsem.at[2]),
        ]
        for cp in loads:
            cp.start()
        pad[:edge, :] = jnp.zeros((edge, chans), f32)
        for cp in loads:
            cp.wait()
        w_v[...] = w_raw[...].astype(f32)
        g_v[...] = depth_gain_row(g_raw, width, chans)

        def tile(i, c):
            at = pl.multiple_of(i * SPAN, SPAN)
            for lane in range(lanes):
                cols = slice(lane * 128, (lane + 1) * 128)
                window = pad[pl.ds(at, SPAN + edge), cols]
                total = jnp.zeros((SPAN, 128), f32)
                for by in range(8):
                    moved = shifted(window, by)
                    for base in range(0, edge + 1, 8):
                        tap = base + by - (edge - reach)
                        if 0 <= tap < taps:
                            total = total + w_v[tap : tap + 1, cols] * moved[base : base + SPAN]
                unit[pl.ds(at, SPAN), cols] = total
            depth = unit[pl.ds(at, SPAN), :]
            mean = jnp.mean(depth, -1, keepdims=True)
            centred = depth - mean
            sendbuf[:, pl.ds(at, SPAN)] = to_rows(mean, jnp.sum(centred * centred, -1, keepdims=True))
            return c

        lax.fori_loop(0, tiles, tile, 0)
        meet()
        copies = exchange(sendbuf, landing, send, recv)
        for cp in copies:
            cp.start()
        for cp in copies:
            cp.wait_recv()
        rows = [sendbuf[...]] + [landing[i] for i in range(3)]
        mean = sum(r[0:1] for r in rows) * 0.25
        spread = sum(r[1:2] + chans * (r[0:1] - mean) * (r[0:1] - mean) for r in rows) / width
        inverse = lax.rsqrt(spread + epsilon)
        row = lax.broadcasted_iota(jnp.int32, (8, frames), 0)
        stat[...] = jnp.where(row == 0, mean, jnp.where(row == 1, inverse, 0.0))
        outs = [(act, act_h), (slope, slope_h), (unit, unit_h)]

        def store(i, n):
            at = pl.ds(pl.multiple_of(i * SPAN, SPAN), SPAN)
            return pltpu.make_async_copy(outs[n][0].at[at], outs[n][1].at[at], ssem.at[n, i])

        def finish(i, c):
            at = pl.multiple_of(i * SPAN, SPAN)
            cols = to_columns(stat[:, pl.ds(at, SPAN)])
            u = (unit[pl.ds(at, SPAN), :] - cols[:, 0:1]) * cols[:, 1:2]
            a, s = silu_pair(u * g_v[...])
            unit[pl.ds(at, SPAN), :] = u
            act[pl.ds(at, SPAN), :] = a.astype(bf)
            slope[pl.ds(at, SPAN), :] = s.astype(bf)
            for n in range(3):
                store(i, n).start()
            return c

        lax.fori_loop(0, tiles, finish, 0)
        last = pltpu.make_async_copy(stat, stat_h, lsem.at[0])
        last.start()
        for cp in copies:
            cp.wait_send()
        for i in range(tiles):
            for n in range(3):
                store(i, n).wait()
        last.wait()

    S = jax.ShapeDtypeStruct
    out_shape = [S((frames, chans), bf), S((frames, chans), bf), S((frames, chans), f32), S((8, frames), f32)]
    vm = pltpu.VMEM
    return pl.pallas_call(
        kernel,
        in_specs=[in_hbm()] * 3,
        out_specs=[in_hbm()] * 4,
        out_shape=out_shape,
        scratch_shapes=[
            vm((frames + edge, chans), f32), vm(w_depth.shape, bf), vm(gains.shape, f32), vm(w_depth.shape, f32), vm((1, chans), f32),
            vm((frames, chans), bf), vm((frames, chans), bf), vm((frames, chans), f32), vm((8, frames), f32),
            vm((8, frames), f32), vm((3, 8, frames), f32),
            pltpu.SemaphoreType.DMA((3,)), pltpu.SemaphoreType.DMA((3, tiles)), pltpu.SemaphoreType.DMA((3,)), pltpu.SemaphoreType.DMA((3,)),
        ],
        compiler_params=pltpu.CompilerParams(collective_id=cid, has_side_effects=True, vmem_limit_bytes=VMEM_LIMIT),
        name="conv_mid",
    )(glu, w_depth, gains)


def conv_mid_back(grad, slope, unit, stat, glu, sig, tail, w_depth, gains, width, cid, grads):
    frames, chans = glu.shape
    taps = w_depth.shape[0]
    reach = taps - 1
    edge = (reach + 7) // 8 * 8
    f32, bf = jnp.float32, jnp.bfloat16
    tiles, lanes = frames // SPAN, chans // 128
    ins = [grad, slope, unit, stat, w_depth, gains, glu, sig, tail]
    riders = Riders(grads)
    n = len(grads)

    def kernel(*refs):
        hbm, ride_in, (pair_h, taps_h), ride_out = refs[:9], refs[9 : 9 + n], refs[9 + n : 11 + n], refs[11 + n : 11 + 2 * n]
        refs = refs[2 * n :]
        (grad_v, slope_v, unit_v, stat_v, w_raw, g_raw, pad, sig_v, tail_v, w_v, g_v, back, pair, taps_v, acc, gacc, sendbuf, landing, lsem, ssem, send, recv) = refs[11:33]
        riders.bind(ride_in, ride_out, refs[33:])
        meet = greet(group_targets() + riders.targets())
        dst = [grad_v, slope_v, unit_v, stat_v, w_raw, g_raw, pad.at[pl.ds(edge, frames)], sig_v, tail_v]
        loads = [pltpu.make_async_copy(h, d, lsem.at[i]) for i, (h, d) in enumerate(zip(hbm, dst))]
        for cp in loads:
            cp.start()
        pad[:edge, :] = jnp.zeros((edge, chans), f32)
        back[frames:, :] = jnp.zeros((edge, chans), f32)
        acc[...] = jnp.zeros_like(acc)
        gacc[...] = jnp.zeros_like(gacc)
        for cp in loads[:6]:
            cp.wait()
        w_v[...] = w_raw[...].astype(f32)
        g_v[...] = depth_gain_row(g_raw, width, chans)

        def first(i, c):
            at = pl.ds(pl.multiple_of(i * SPAN, SPAN), SPAN)
            u = unit_v[at, :]
            de = grad_v[at, :] * slope_v[at, :].astype(f32)
            gacc[...] += fold8(de * u)
            du = de * g_v[...]
            back[at, :] = du
            sendbuf[:, at] = to_rows(jnp.sum(du, -1, keepdims=True), jnp.sum(du * u, -1, keepdims=True))
            return c

        meet()
        riders.start()
        lax.fori_loop(0, tiles, first, 0)
        copies = exchange(sendbuf, landing, send, recv)
        for cp in copies:
            cp.start()
        for cp in loads[6:]:
            cp.wait()
        for cp in copies:
            cp.wait_recv()
        means = (sendbuf[...] + landing[0] + landing[1] + landing[2]) / width
        row = lax.broadcasted_iota(jnp.int32, (8, frames), 0)
        stat_v[...] = jnp.where(row == 1, stat_v[...], jnp.where(row == 0, means[0:1], jnp.where(row == 2, means[1:2], 0.0)))

        def second(i, c):
            at = pl.ds(pl.multiple_of(i * SPAN, SPAN), SPAN)
            cols = to_columns(stat_v[:, at])
            back[at, :] = cols[:, 1:2] * (back[at, :] - cols[:, 0:1] - unit_v[at, :] * cols[:, 2:3])
            return c

        lax.fori_loop(0, tiles, second, 0)

        def store(i):
            at = pl.ds(pl.multiple_of(i * SPAN, SPAN), SPAN)
            return pltpu.make_async_copy(pair.at[at], pair_h.at[at], ssem.at[i])

        def third(i, c):
            at = pl.multiple_of(i * SPAN, SPAN)
            rows = pl.ds(at, SPAN)
            for lane in range(lanes):
                cols = slice(lane * 128, (lane + 1) * 128)
                ahead = back[pl.ds(at, SPAN + edge), cols]
                total = jnp.zeros((SPAN, 128), f32)
                for by in range(8):
                    moved = shifted(ahead, by)
                    for base in range(0, edge, 8):
                        tap = reach - (base + by)
                        if 0 <= tap < taps:
                            total = total + w_v[tap : tap + 1, cols] * moved[base : base + SPAN]
                pair[rows, cols] = (total * sig_v[rows, cols].astype(f32)).astype(bf)
                pair[rows, chans + lane * 128 : chans + (lane + 1) * 128] = (total * tail_v[rows, cols].astype(f32)).astype(bf)
            store(i).start()
            for lane in range(lanes):
                cols = slice(lane * 128, (lane + 1) * 128)
                here = back[rows, cols]
                window = pad[pl.ds(at, SPAN + edge), cols]
                for by in range(8):
                    moved = shifted(window, by)
                    for base in range(0, edge + 1, 8):
                        tap = base + by - (edge - reach)
                        if 0 <= tap < taps:
                            acc[tap * 8 : tap * 8 + 8, cols] += fold8(here * moved[base : base + SPAN])
            return c

        lax.fori_loop(0, tiles, third, 0)
        for tap in range(taps):
            taps_v[tap : tap + 1, :] = jnp.sum(acc[tap * 8 : tap * 8 + 8, :], 0, keepdims=True)
        taps_v[taps : taps + 1, :] = jnp.sum(gacc[...], 0, keepdims=True)
        last = pltpu.make_async_copy(taps_v, taps_h, lsem.at[0])
        last.start()
        for cp in copies:
            cp.wait_send()
        riders.finish()
        for i in range(tiles):
            store(i).wait()
        last.wait()

    S = jax.ShapeDtypeStruct
    vm = pltpu.VMEM
    outs = pl.pallas_call(
        kernel,
        in_specs=[in_hbm()] * (9 + n),
        out_specs=[in_hbm()] * (2 + n),
        out_shape=[S((frames, 2 * chans), bf), S((taps + 1, chans), f32)] + riders.after,
        scratch_shapes=[
            vm((frames, chans), f32), vm((frames, chans), bf), vm((frames, chans), f32), vm((8, frames), f32),
            vm(w_depth.shape, bf), vm(gains.shape, f32), vm((frames + edge, chans), f32), vm((frames, chans), bf), vm((frames, chans), bf),
            vm(w_depth.shape, f32), vm((1, chans), f32),
            vm((frames + edge, chans), f32), vm((frames, 2 * chans), bf), vm((taps + 1, chans), f32), vm((taps * 8, chans), f32), vm((8, chans), f32),
            vm((8, frames), f32), vm((3, 8, frames), f32),
            pltpu.SemaphoreType.DMA((9,)), pltpu.SemaphoreType.DMA((tiles,)), pltpu.SemaphoreType.DMA((3,)), pltpu.SemaphoreType.DMA((3,)),
        ] + riders.scratch,
        compiler_params=pltpu.CompilerParams(collective_id=cid, has_side_effects=True, vmem_limit_bytes=VMEM_LIMIT),
        name="conv_mid_back",
    )(*ins, *riders.arrays)
    return outs[0], outs[1], riders.results(outs[2:])


def split_pair(x):
    left = lax.broadcasted_iota(jnp.int32, x.shape, 1) < HEAD
    zero = jnp.zeros_like(x)
    return jnp.concatenate([jnp.where(left, x, zero), jnp.where(left, zero, x)], 0)

def join_pair(x):
    rows = x.shape[0] // 2
    left = lax.broadcasted_iota(jnp.int32, (rows, x.shape[1]), 1) < HEAD
    return jnp.where(left, x[:rows], x[rows:])

def spot_table(spots):
    spot = lax.broadcasted_iota(jnp.int32, (spots, BQ), 0)
    inner = jnp.clip(spot - REL_LEFT, 0, REL_LEFT + REL_RIGHT)
    row = jnp.where(spot < 3 * BQ, inner, jnp.where(spot < 4 * BQ, 0, REL_LEFT + REL_RIGHT))
    return (lax.broadcasted_iota(jnp.int32, (spots, BQ), 1) == row).astype(jnp.bfloat16)


def wide_table(rel_ref, wide_ref):
    wide_ref[...] = jnp.zeros_like(wide_ref)
    turned = rel_ref[...].astype(jnp.float32)
    cols = turned.shape[1]
    wide_ref[0:HEAD, :cols] = turned
    wide_ref[HEAD : 2 * HEAD, :cols] = turned
    return wide_ref[...].T.astype(jnp.bfloat16)


def fwd_kernel(q_ref, k_ref, v_ref, relt_ref, mixed_ref, probs_ref, bias_ref, rel_ref, wide_ref):
    ib = pl.program_id(1)

    @pl.when((ib == 0) & (pl.program_id(0) == 0))
    def _():
        rel_ref[...] = nn(spot_table(5 * BQ), wide_table(relt_ref, wide_ref)).astype(jnp.bfloat16)

    qs = split_pair(q_ref[...] * 0.125)
    s = nt(qs, k_ref[...])
    b = nt(qs, rel_ref[...])
    rows = b.shape[0] // 2
    bias_ref[:, 0:BQ] = b[:, 3 * BQ : 4 * BQ]
    for h in range(2):
        r = pltpu.roll(b[h * rows : (h + 1) * rows, :WIN], 0, 1, stride=1, stride_axis=0)
        bias_ref[h * rows : (h + 1) * rows, BQ : 4 * BQ] = r[:, : 3 * BQ]
    bias_ref[:, 4 * BQ :] = b[:, 4 * BQ :]
    nkeys = s.shape[1] // BQ
    parts = []
    for jb in range(nkeys):
        at = pl.multiple_of(jnp.clip(jb - ib + 2, 0, 4) * BQ, BQ)
        parts.append(s[:, jb * BQ : (jb + 1) * BQ] + bias_ref[:, pl.ds(at, BQ)])
    top = functools.reduce(jnp.maximum, parts)
    m = jnp.max(top, -1, keepdims=True)
    es = [jnp.exp(p - m) for p in parts]
    tot = jnp.sum(functools.reduce(jnp.add, es), -1, keepdims=True)
    inv = 1.0 / tot
    for jb in range(nkeys):
        probs_ref[0, :, jb * BQ : (jb + 1) * BQ] = (es[jb] * inv).astype(jnp.bfloat16)
    mixed_ref[...] = join_pair(nn(probs_ref[0], v_ref[...])).astype(jnp.bfloat16)

def bwd_kernel(riders, *refs):
    n = len(riders.plan)
    q_ref, k_ref, v_ref, relt_ref, probs_ref, do_ref, db_h, mix_h = refs[:8]
    ride_in = refs[8 : 8 + n]
    dq_ref, dk_ref, dv_ref, dt_ref, dw_h = refs[8 + n : 13 + n]
    ride_out = refs[13 + n : 13 + 2 * n]
    tot_ref, dkt, dvt, dta, dz_ref, hot_ref, db_v, mix_v, dw_v, dw_land, dw_half, relb_ref, wide_ref, osem, psem = refs[13 + 2 * n : 28 + 2 * n]
    riders.bind(ride_in, ride_out, refs[28 + 2 * n :])
    pr, ib, nb = pl.program_id(0), pl.program_id(1), pl.num_programs(1)
    dp, mp = lax.axis_index("dp"), lax.axis_index("mp")
    loads = [pltpu.make_async_copy(db_h, db_v, osem.at[0]), pltpu.make_async_copy(mix_h, mix_v, osem.at[1])]
    pieces = dw_v.shape[0]
    hops = [halving_copy(dw_v, dw_land, p, 0, psem.at[0], psem.at[1], p) for p in range(pieces)]
    flip = dw_land.shape[2] % 128 == 0
    stores = [
        pltpu.make_async_copy(region(dw_half, p, PIECE, flip), region(dw_h, p, PIECE, flip), psem.at[2, p]) for p in range(pieces)
    ]

    @pl.when((ib == 0) & (pr == 0))
    def _():
        meet = greet(sorted_targets(riders, dp, mp))
        for cp in loads:
            cp.start()
        hot_ref[...] = spot_table(WIN)
        relb_ref[...] = wide_table(relt_ref, wide_ref)
        meet()
        riders.start()
        for cp in loads:
            cp.wait()
        for p in range(pieces):
            g = tn(db_v[...], mix_v[:, p * PIECE : (p + 1) * PIECE])
            dw_v[p] = g.astype(jnp.bfloat16).reshape(dw_v.shape[1:])
            hops[p].start()

    @pl.when(ib == 0)
    def _():
        dkt[...] = jnp.zeros_like(dkt)
        dvt[...] = jnp.zeros_like(dvt)
    @pl.when((ib == 0) & (pr == 0))
    def _():
        dta[...] = jnp.zeros_like(dta)
    qs = split_pair(q_ref[...] * 0.125)
    dos = split_pair(do_ref[...])
    p = probs_ref[0]
    dp = nt(dos, v_ref[...])
    nkeys = dp.shape[1] // BQ
    dvt[...] += tn(dos, p)
    pf = p.astype(jnp.float32)
    acc = None
    for jb in range(nkeys):
        sl = slice(jb * BQ, (jb + 1) * BQ)
        t = pf[:, sl] * dp[:, sl]
        acc = t if acc is None else acc + t
    inner = jnp.sum(acc, -1, keepdims=True)
    tot_ref[...] = jnp.zeros_like(tot_ref)
    for jb in range(nkeys):
        sl = slice(jb * BQ, (jb + 1) * BQ)
        dz = (pf[:, sl] * (dp[:, sl] - inner)).astype(jnp.bfloat16)
        dz_ref[:, sl] = dz
        at = pl.multiple_of(jnp.clip(jb - ib + 2, 0, 4) * BQ, BQ)
        tot_ref[:, pl.ds(at, BQ)] += dz.astype(jnp.float32)
    rows = BQ
    r2 = lax.broadcasted_iota(jnp.int32, (2 * rows, 2 * rows), 0)
    c2 = lax.broadcasted_iota(jnp.int32, (2 * rows, 2 * rows), 1)
    mirror = (r2 + c2 == jnp.where(r2 < rows, rows - 1, 3 * rows - 1)).astype(jnp.bfloat16)
    w = jnp.concatenate([tot_ref[:, BQ : 4 * BQ].astype(jnp.bfloat16), jnp.zeros((2 * rows, BQ), jnp.bfloat16)], 1)
    w = nn(mirror, w)
    outs = [pltpu.roll(w[h * rows : (h + 1) * rows], WIN - rows + 1, 1, stride=1, stride_axis=0) for h in range(2)]
    d = nn(mirror, jnp.concatenate(outs, 0).astype(jnp.bfloat16)).astype(jnp.bfloat16)
    drel = nn(d, hot_ref[...])
    col = lax.broadcasted_iota(jnp.int32, drel.shape, 1)
    low = jnp.sum(tot_ref[:, :BQ], -1, keepdims=True)
    high = jnp.sum(tot_ref[:, 4 * BQ :], -1, keepdims=True)
    drel = drel + jnp.where(col == 0, low, 0.0) + jnp.where(col == REL_LEFT + REL_RIGHT, high, 0.0)
    drel = drel.astype(jnp.bfloat16)
    dz = dz_ref[...]
    dq = nn(dz, k_ref[...]) + nn(drel, relb_ref[...])
    dq_ref[...] = (join_pair(dq) * 0.125).astype(jnp.bfloat16)
    dkt[...] += tn(qs, dz)
    dta[...] += tn(drel, qs)
    @pl.when(ib == nb - 1)
    def _():
        dk_ref[...] = dkt[...].T.astype(jnp.bfloat16)
        dv_ref[...] = dvt[...].T.astype(jnp.bfloat16)
        dt_ref[...] = dta[...]

    @pl.when((ib == nb - 1) & (pr == pl.num_programs(0) - 1))
    def _():
        own, _ = place(lax.axis_index("dp"), 0)
        for p in range(pieces):
            hops[p].wait_recv()
            halving_add(lambda q, j: dw_v[q, j, own], dw_land, dw_half, p, True)
            stores[p].start()
        riders.finish()
        for p in range(pieces):
            hops[p].wait_send()
            stores[p].wait()


def sorted_targets(riders, dp, mp):
    return [(place(dp, b)[1], mp) for b in sorted({0} | {x[1] for x in riders.plan})]


def attn_fwd(qkv, rel):
    frames, cols = qkv.shape
    pairs = cols // 3 // 128
    nb = frames // BQ
    bf = jnp.bfloat16
    return pl.pallas_call(
        fwd_kernel,
        grid=(pairs, nb),
        in_specs=[
            pl.BlockSpec((BQ, 128), lambda p, i: (i, p)),
            pl.BlockSpec((frames, 128), lambda p, i: (0, pairs + p)),
            pl.BlockSpec((frames, 128), lambda p, i: (0, 2 * pairs + p)),
            pl.BlockSpec(rel.shape, lambda p, i: (0, 0)),
        ],
        out_specs=[
            pl.BlockSpec((BQ, 128), lambda p, i: (i, p)),
            pl.BlockSpec((1, 2 * BQ, frames), lambda p, i: (p, i, 0)),
        ],
        out_shape=[jax.ShapeDtypeStruct((frames, cols // 3), bf), jax.ShapeDtypeStruct((pairs, 2 * frames, frames), bf)],
        scratch_shapes=[pltpu.VMEM((2 * BQ, 5 * BQ), jnp.float32), pltpu.VMEM((5 * BQ, 128), bf), pltpu.VMEM((128, 128), jnp.float32)],
        compiler_params=pltpu.CompilerParams(vmem_limit_bytes=VMEM_LIMIT),
        name="attn_fwd",
    )(qkv, qkv, qkv, rel)

def attn_bwd(qkv, rel, probs, dmixed, grad_rows, mixed, grads, cid):
    frames, cols = qkv.shape
    pairs = cols // 3 // 128
    nb = frames // BQ
    bf = jnp.bfloat16
    count = lax.axis_size("dp")
    blk = pl.BlockSpec((BQ, 128), lambda p, i: (i, p))
    full = pl.BlockSpec((frames, 128), lambda p, i: (0, p))
    riders = Riders(grads)
    width = grad_rows.shape[1]
    shape = (mixed.shape[1] // PIECE, count // 2, 2, width // count, PIECE)
    half = halved(shape, True)
    vm = pltpu.VMEM
    outs = pl.pallas_call(
        functools.partial(bwd_kernel, riders),
        grid=(pairs, nb),
        in_specs=[
            blk,
            pl.BlockSpec((frames, 128), lambda p, i: (0, pairs + p)),
            pl.BlockSpec((frames, 128), lambda p, i: (0, 2 * pairs + p)),
            pl.BlockSpec(rel.shape, lambda p, i: (0, 0)),
            pl.BlockSpec((1, 2 * BQ, frames), lambda p, i: (p, i, 0)),
            blk,
        ]
        + [in_hbm()] * (2 + len(grads)),
        out_specs=[blk, full, full, pl.BlockSpec((128, 128), lambda p, i: (0, 0))] + [in_hbm()] * (1 + len(grads)),
        out_shape=[jax.ShapeDtypeStruct((frames, cols // 3), bf)] * 3 + [jax.ShapeDtypeStruct((128, 128), jnp.float32), half] + riders.after,
        scratch_shapes=[
            vm((2 * BQ, 5 * BQ), jnp.float32), vm((128, frames), jnp.float32), vm((128, frames), jnp.float32),
            vm((128, 128), jnp.float32), vm((2 * BQ, frames), bf), vm((WIN, BQ), bf),
            vm(grad_rows.shape, bf), vm(mixed.shape, bf), vm(shape, bf), arriving(shape), vm(half.shape, half.dtype),
            vm((128, 128), bf), vm((128, 128), jnp.float32),
            pltpu.SemaphoreType.DMA((2,)), pltpu.SemaphoreType.DMA((3, shape[0])),
        ]
        + riders.scratch,
        compiler_params=pltpu.CompilerParams(vmem_limit_bytes=VMEM_LIMIT, collective_id=cid, has_side_effects=True),
        cost_estimate=pl.CostEstimate(flops=20 * frames * frames * 128 * pairs, bytes_accessed=20_000_000, transcendentals=0),
        name="attn_bwd",
    )(qkv, qkv, qkv, rel, probs, dmixed, grad_rows, mixed, *riders.arrays)
    return list(outs[:4]) + [[Grad(outs[4], 1, True)] + riders.results(outs[5:])]


def body(
    features,
    w1_in,
    w1_out,
    gain_ffn1,
    w_qkv,
    w_attn_out,
    rel_table,
    gain_attn,
    w_conv_in,
    w_depth,
    gain_depth,
    w_conv_out,
    gain_conv,
    w2_in,
    w2_out,
    gain_ffn2,
    gain_final,
    cotangent,
):
    local_frames, clip_count, width = features.shape
    rows = local_frames * clip_count
    f32, bf = jnp.float32, jnp.bfloat16
    s0 = features.reshape(rows, width)
    seed = cotangent.reshape(rows, width)
    spare = jnp.zeros((width - gain_depth.shape[0],), bf)
    gains = jnp.concatenate([gain_ffn1, gain_attn, gain_conv, gain_ffn2, gain_final, gain_depth, spare])
    gains = gains.astype(f32).reshape(-1, 128)
    flat_qkv = w_qkv.transpose(1, 0, 2)
    flat_conv = w_conv_in.reshape(width, -1)
    units = w1_in.shape[1]
    half = units // PIECE // 2
    dp_count = lax.axis_size("dp")
    done = dp_count.bit_length() - 1
    pending = lambda items: [g for g in items if g.bit < done]
    chans = w_conv_out.shape[0]

    def swish_out(h, extra, outs):
        act, slope = silu_pair(h)
        outs[0][...] = act.astype(bf)
        outs[1][...] = slope.astype(bf)

    def plain_out(h, extra, outs):
        outs[0][...] = h.astype(outs[0].dtype)

    def glu_out(h, extra, outs):
        p0 = h[:, :chans]
        sig = jax.nn.sigmoid(h[:, chans:])
        glu = p0 * sig
        outs[0][...] = glu
        outs[1][...] = sig.astype(bf)
        outs[2][...] = (glu * (1.0 - sig)).astype(bf)

    def slope_out(h, extra, outs):
        outs[0][...] = (h * extra[0][...].astype(f32)).astype(bf)

    def first(branch, ins, gains, outs, sums):
        return (unit_norm(ins[0].astype(f32))[0] * gains[0:1, :]).astype(bf)

    def forward(scale, row):
        def run(branch, ins, gains, outs, sums):
            fresh = ins[0].astype(f32) + scale * branch
            outs[0][...] = fresh
            sums[0][...] += fold8(branch * branch)
            return (unit_norm(fresh)[0] * gains[row : row + 1, :]).astype(bf)
        return run

    def turn(branch, ins, gains, outs, sums):
        fresh = ins[0] + 0.5 * branch
        sums[0][...] += fold8(branch * branch)
        sums[1][...] += fold8(fresh * fresh)
        unit, inverse = unit_norm(fresh)
        outs[0][...] = unit * gains[4:5, :]
        grad = ins[1].astype(f32)
        scaled = grad * gains[4:5, :]
        mean_one = jnp.mean(scaled, -1, keepdims=True)
        mean_two = jnp.mean(scaled * unit, -1, keepdims=True)
        sums[2][...] += fold8(grad * unit)
        back = inverse * (scaled - mean_one - unit * mean_two)
        outs[1][...] = back
        return (0.5 * back).astype(bf)

    def backward(scale, row):
        def run(branch, ins, gains, outs, sums):
            pull, grad_gain = norm_pull(branch, ins[1].astype(f32), gains[row : row + 1, :])
            fresh = ins[0] + pull
            outs[0][...] = fresh
            sums[0][...] += grad_gain
            return (scale * fresh).astype(bf)
        return run

    a1, act1, slope1, _ = stage(
        "ffn1_in", 0, rows, width, dp_count, gains, enter=(w1_in, False, swish_out, (), ((units, bf), (units, bf))),
        junction=first, row_in=(s0,),
    )
    a2, qkv, s1, sq1, _ = stage(
        "ffn1_out", 1, rows, width, dp_count, gains, leave=(act1, w1_out, False),
        enter=(flat_qkv, False, plain_out, (), ((3 * w_qkv.shape[2], bf),)),
        junction=forward(0.5, 1), row_in=(s0,), row_out=(f32,), sums=1,
    )
    turned_table = rel_table.T
    mixed, probs = attn_fwd(qkv, turned_table)
    a3, glu, sig, tail, s2, sq2, _ = stage(
        "attn_out", 2, rows, width, dp_count, gains, leave=(mixed, w_attn_out, False),
        enter=(flat_conv, False, glu_out, (), ((chans, f32), (chans, bf), (chans, bf))),
        junction=forward(1.0, 2), row_in=(s1,), row_out=(f32,), sums=1,
    )
    act3, slope3, depth_unit, depth_stat = conv_mid(glu, w_depth, gains, width, 10)
    a4, act2, slope2, s3, sq3, _ = stage(
        "conv_out", 3, rows, width, dp_count, gains, leave=(act3, w_conv_out, False),
        enter=(w2_in, False, swish_out, (), ((units, bf), (units, bf))),
        junction=forward(1.0, 3), row_in=(s2,), row_out=(f32,), sums=1,
    )
    db4, dh2, output, grad4, sq4, sq5, dgf, _ = stage(
        "ffn2_out", 4, rows, width, dp_count, gains, leave=(act2, w2_out, False),
        enter=(w2_out, True, slope_out, (slope2,), ((units, bf),)),
        junction=turn, row_in=(s3, seed), row_out=(f32, f32), sums=3,
    )
    db3, de3, grad3, dg2, (ga_in, gb_in, gw2_out) = stage(
        "ffn2_back", 5, rows, width, dp_count, gains, leave=(dh2, w2_in, True),
        enter=(w_conv_out, True, plain_out, (), ((chans, f32),)), dws=(
            weight(a4, dh2, "join", False, 1, 0, half),
            weight(a4, dh2, "join", False, 1, half, units // PIECE - half),
            weight(db4, act2, "far", True),
        ),
        junction=backward(1.0, 3), row_in=(grad4, s3), row_out=(f32,), sums=1,
    )
    dpaired, tap_sums, (gw2_out, ga_in) = conv_mid_back(
        de3, slope3, depth_unit, depth_stat, glu, sig, tail, w_depth, gains, width, 11, [gw2_out, ga_in]
    )
    db2, dmixed, grad2, dgc, (gconv_in, gconv_out, gb_in, gw2_out, ga_in) = stage(
        "conv_back", 6, rows, width, dp_count, gains, leave=(dpaired, flat_conv, True),
        enter=(w_attn_out, True, plain_out, (), ((w_attn_out.shape[0], bf),)), dws=(weight(a3, dpaired, "far", False), weight(db3, act3, "far", True)), grads=(gb_in, gw2_out, ga_in),
        junction=backward(1.0, 2), row_in=(grad3, s2), row_out=(f32,), sums=1,
    )
    dq, dk, dv, dt, (gattn, gb_in, ga_in, gconv_in, gconv_out) = attn_bwd(
        qkv, turned_table, probs, dmixed, db2, mixed, [gb_in, ga_in, gconv_in, gconv_out], 9
    )
    dqkv = (dq, dk, dv)
    waiting = pending([gattn, gconv_in, gconv_out, ga_in, gb_in, gw2_out])
    grad0, ends, other_rows, table_end, taps_end, lead_row = stage(
        "attn_back", 7, rows, width, dp_count, gains, leave=(dqkv, flat_qkv, True),
        enter=(w1_out, True, slope_out, (slope1,), ((units, bf),)),
        dws=(
            weight(a2, dqkv, "far", False),
            weight("all", act1, "front", True),
            weight(a1, "out", "close", False, pieces=units // PIECE),
        ),
        grads=waiting, small=((dgc, dg2, dgf, sq1, sq2, sq3, sq4, sq5), dt, tap_sums),
        tail=(w1_in, backward(1.0, 0), (s0,)),
        junction=backward(0.5, 1), row_in=(grad2, s1), row_out=(f32,), sums=1,
    )
    gqkv, gw1_out, gw1_in = ends[:3]
    for item, end in zip(waiting, ends[3:]):
        item.array = end.array

    def finish(item):
        flip = item.turned and item.array.shape[0] * dp_count == width and (width // dp_count) % 128 != 0
        return item.array.T if flip else item.array

    token_total = rows * lax.axis_size("mp") * dp_count
    ends = [
        ([output], 1),
        ([grad0], 1),
        ([finish(gw1_in)], 0),
        ([finish(gw1_out)], 0),
        ([finish(gqkv)], -3),
        ([finish(gattn)], 0),
        ([finish(gconv_in)], 2),
        ([finish(gconv_out)], 0),
        ([finish(ga_in), finish(gb_in)], 0),
        ([finish(gw2_out)], 0),
    ]
    done_ends = publish(ends, [lead_row, other_rows, table_end, taps_end], {8: False}, rel_table.shape[0], float(token_total * width))
    (output, grad0, gw1_in, gw1_out, gqkv, gattn, gconv_in, gconv_out, gw2_in, gw2_out) = done_ends[:10]
    *gain_sums, table_sum, depth_sum, depth_gain_sum, rms_stats = done_ends[10:]
    gain_sums = [g[0] for g in gain_sums]
    return (
        output,
        grad0,
        gw1_in,
        gw1_out,
        gain_sums[0],
        gqkv.transpose(1, 0, 2),
        gattn,
        table_sum.T,
        gain_sums[1],
        gconv_in,
        depth_sum,
        depth_gain_sum[0],
        gconv_out,
        gain_sums[2],
        gw2_in,
        gw2_out,
        gain_sums[3],
        gain_sums[4],
        rms_stats[0],
    )


def solution(mesh):
    return jax.shard_map(
        body,
        mesh=mesh,
        in_specs=(
            P("mp", "dp", None),
            P(None, "mp"),
            P("mp", None),
            P(),
            P(None, None, "mp"),
            P("mp", None),
            P(),
            P(),
            P(None, None, "mp"),
            P(None, "mp"),
            P("mp"),
            P("mp", None),
            P(),
            P(None, "mp"),
            P("mp", None),
            P(),
            P(),
            P("mp", "dp", None),
        ),
        out_specs=(
            P("mp", "dp", None),
            P("mp", "dp", None),
            P("dp", "mp"),
            P("mp", "dp"),
            P(),
            P("dp", None, "mp"),
            P("mp", "dp"),
            P(),
            P(),
            P("dp", None, "mp"),
            P(None, "mp"),
            P("mp"),
            P("mp", "dp"),
            P(),
            P("dp", "mp"),
            P("mp", "dp"),
            P(),
            P(),
            P(),
        ),
        check_vma=False,
    )
```

```python
import functools

import jax
import jax.numpy as jnp
from jax import lax
from jax.experimental import pallas as pl
from jax.experimental.pallas import tpu as pltpu
from jax.sharding import PartitionSpec as P

HEAD = 64
REL_LEFT = 64
REL_RIGHT = 8
BQ = 128
WIN = 4 * BQ


epsilon = 1e-05


def nt(a, b):
    return lax.dot_general(a, b, (((1,), (1,)), ((), ())), preferred_element_type=jnp.float32)
def nn(a, b):
    return lax.dot_general(a, b, (((1,), (0,)), ((), ())), preferred_element_type=jnp.float32)
def tn(a, b):
    return lax.dot_general(a, b, (((0,), (0,)), ((), ())), preferred_element_type=jnp.float32)

MESH = pl.DeviceIdType.MESH
CHUNKS = 4
TABLE_ROWS = 40
LAG = 2
JOIN_SLOT = 3
PIECE = 256
VMEM_LIMIT = 58 << 20


def silu_pair(h):
    sig = jax.nn.sigmoid(h)
    act = h * sig
    return act, sig + act * (1.0 - sig)


def unit_norm(s):
    centred = s - jnp.mean(s, -1, keepdims=True)
    inverse = lax.rsqrt(jnp.mean(centred * centred, -1, keepdims=True) + epsilon)
    return centred * inverse, inverse


def fold8(x):
    return jnp.sum(x.reshape(x.shape[0] // 8, 8, x.shape[1]), 0)


def norm_pull(grad, s, gain):
    unit, inverse = unit_norm(s)
    scaled = grad * gain
    first = jnp.mean(scaled, -1, keepdims=True)
    second = jnp.mean(scaled * unit, -1, keepdims=True)
    return inverse * (scaled - first - unit * second), fold8(grad * unit)


def in_hbm():
    return pl.BlockSpec(memory_space=pltpu.HBM)


class Grad:
    def __init__(self, array, bit, turned):
        self.array, self.bit, self.turned = array, bit, turned


def halved(shape, turned):
    pieces, pairs, _, block, cols = shape
    if pairs > 1:
        return jax.ShapeDtypeStruct((pieces, pairs // 2, 2, block, cols), jnp.bfloat16)
    if turned and block % 128 == 0:
        return jax.ShapeDtypeStruct((pieces * cols, block), jnp.float32)
    return jax.ShapeDtypeStruct((block, pieces * cols), jnp.float32)


def arriving(shape):
    return pltpu.VMEM((shape[0], shape[1]) + tuple(shape[3:]), jnp.bfloat16)


def place(dp, bit):
    own = (dp // 2**bit) % 2
    return own, dp + 2**bit * (1 - 2 * own)


def halving_copy(src, landing, piece, bit, send, recv, slot):
    dp, mp = lax.axis_index("dp"), lax.axis_index("mp")
    own, partner = place(dp, bit)
    return pltpu.make_async_remote_copy(
        src.at[piece, :, 1 - own], landing.at[piece], send.at[slot], recv.at[slot],
        device_id=(partner, mp), device_id_type=MESH,
    )


def halving_keep(src, kept, bit, sem):
    own, _ = place(lax.axis_index("dp"), bit)
    return pltpu.make_async_copy(src.at[:, :, own], kept, sem)


def region(ref, piece, cols, turned):
    if len(ref.shape) > 2:
        return ref.at[piece]
    at = pl.ds(piece * cols, cols)
    return ref.at[at, :] if turned else ref.at[:, at]


def halving_add(held, landing, out, piece, turned):
    pairs, block, cols = landing.shape[1:]
    f32 = jnp.float32
    if pairs == 1:
        total = held(piece, 0).astype(f32) + landing[piece, 0].astype(f32)
        turned = turned and block % 128 == 0
        region(out, piece, cols, turned)[...] = total.T if turned else total
        return

    def add(j, c):
        total = held(piece, j).astype(f32) + landing[piece, j].astype(f32)
        out[piece, j // 2, j % 2] = total.astype(jnp.bfloat16)
        return c

    lax.fori_loop(0, pairs, add, 0)


def weight(lhs, rhs, where, turned, deep=1, lo=0, pieces=None):
    if pieces is None:
        pieces = (sum(r.shape[1] for r in rhs) if isinstance(rhs, tuple) else rhs.shape[1]) // PIECE
    return lhs, rhs, where, turned, deep, lo, pieces


def flat_shape(array):
    if isinstance(array, tuple):
        return array[0].shape[0], sum(a.shape[1] for a in array)
    if len(array.shape) == 3:
        return array.shape[1], array.shape[0] * array.shape[2]
    return array.shape


def gain_row(ref, i, width):
    first = i * width // 128
    return jnp.concatenate([ref[first + j : first + j + 1, :] for j in range(width // 128)], 1)


class Riders:
    def __init__(self, grads):
        self.plan = [(g.array.shape[0], g.bit, g.turned) for g in grads]
        self.arrays = [g.array for g in grads]
        self.after = [halved(g.array.shape, g.turned) for g in grads]
        self.slots = sum(x[0] for x in self.plan)
        self.scratch = [arriving(g.array.shape) for g in grads] * 2 + [pltpu.VMEM(a.shape, a.dtype) for a in self.after]
        if grads:
            self.scratch += [pltpu.SemaphoreType.DMA((self.slots,))] * 3 + [pltpu.SemaphoreType.DMA((len(grads),))]

    def bind(self, srcs, outs, scratch):
        n = len(self.plan)
        sems = scratch[3 * n :]
        holds, hops, slot = [], [], 0
        for i, (pieces, bit, turned) in enumerate(self.plan):
            landing, keep, half = scratch[i], scratch[n + i], scratch[2 * n + i]
            holds.append(halving_keep(srcs[i], keep, bit, sems[3].at[i]))
            flip = turned and landing.shape[2] % 128 == 0
            for p in range(pieces):
                move = halving_copy(srcs[i], landing, p, bit, sems[0], sems[1], slot)
                store = pltpu.make_async_copy(region(half, p, PIECE, flip), region(outs[i], p, PIECE, flip), sems[2].at[slot])
                hops.append((move, store, lambda q, j, keep=keep: keep[q, j], landing, half, p, turned))
                slot += 1
        self.holds, self.hops = holds, hops

    def targets(self):
        dp, mp = lax.axis_index("dp"), lax.axis_index("mp")
        return [(place(dp, b)[1], mp) for b in sorted({x[1] for x in self.plan})]

    def start(self):
        for hold in self.holds:
            hold.start()
        for hop in self.hops:
            hop[0].start()

    def finish(self):
        for hold in self.holds:
            hold.wait()
        for hop in self.hops:
            hop[0].wait_recv()
            halving_add(*hop[2:])
            hop[1].start()
        for hop in self.hops:
            hop[0].wait_send()
            hop[1].wait()

    def results(self, outs):
        return [Grad(a, b + 1, t) for a, (_, b, t) in zip(outs, self.plan)]


def greet(targets):
    barrier = pltpu.get_barrier_semaphore()
    for to in targets:
        pl.semaphore_signal(barrier, inc=1, device_id=to, device_id_type=MESH)
    return lambda: pl.semaphore_wait(barrier, len(targets))


def split_pair(x):
    left = lax.broadcasted_iota(jnp.int32, x.shape, 1) < HEAD
    zero = jnp.zeros_like(x)
    return jnp.concatenate([jnp.where(left, x, zero), jnp.where(left, zero, x)], 0)

def join_pair(x):
    rows = x.shape[0] // 2
    left = lax.broadcasted_iota(jnp.int32, (rows, x.shape[1]), 1) < HEAD
    return jnp.where(left, x[:rows], x[rows:])

def spot_table(spots):
    spot = lax.broadcasted_iota(jnp.int32, (spots, BQ), 0)
    inner = jnp.clip(spot - REL_LEFT, 0, REL_LEFT + REL_RIGHT)
    row = jnp.where(spot < 3 * BQ, inner, jnp.where(spot < 4 * BQ, 0, REL_LEFT + REL_RIGHT))
    return (lax.broadcasted_iota(jnp.int32, (spots, BQ), 1) == row).astype(jnp.bfloat16)


def wide_table(rel_ref, wide_ref):
    wide_ref[...] = jnp.zeros_like(wide_ref)
    turned = rel_ref[...].astype(jnp.float32)
    cols = turned.shape[1]
    wide_ref[0:HEAD, :cols] = turned
    wide_ref[HEAD : 2 * HEAD, :cols] = turned
    return wide_ref[...].T.astype(jnp.bfloat16)


def fwd_kernel(q_ref, k_ref, v_ref, relt_ref, mixed_ref, probs_ref, bias_ref, rel_ref, wide_ref):
    ib = pl.program_id(0)

    @pl.when(ib == 0)
    def _():
        rel_ref[...] = nn(spot_table(5 * BQ), wide_table(relt_ref, wide_ref)).astype(jnp.bfloat16)

    pairs = q_ref.shape[1] // 128
    nkeys = k_ref.shape[0] // BQ
    places = [pl.multiple_of(jnp.clip(jb - ib + 2, 0, 4) * BQ, BQ) for jb in range(nkeys)]
    for pr in range(pairs):
        cols = slice(pr * 128, (pr + 1) * 128)
        qs = split_pair(q_ref[:, cols] * 0.125)
        s = nt(qs, k_ref[:, cols])
        b = nt(qs, rel_ref[...])
        rows = b.shape[0] // 2
        bias_ref[pr, :, 0:BQ] = b[:, 3 * BQ : 4 * BQ]
        for h in range(2):
            r = pltpu.roll(b[h * rows : (h + 1) * rows, :WIN], 0, 1, stride=1, stride_axis=0)
            bias_ref[pr, h * rows : (h + 1) * rows, BQ : 4 * BQ] = r[:, : 3 * BQ]
        bias_ref[pr, :, 4 * BQ :] = b[:, 4 * BQ :]
        parts = [s[:, jb * BQ : (jb + 1) * BQ] + bias_ref[pr, :, pl.ds(places[jb], BQ)] for jb in range(nkeys)]
        top = functools.reduce(jnp.maximum, parts)
        m = jnp.max(top, -1, keepdims=True)
        es = [jnp.exp(p - m) for p in parts]
        tot = jnp.sum(functools.reduce(jnp.add, es), -1, keepdims=True)
        inv = 1.0 / tot
        for jb in range(nkeys):
            probs_ref[pr, :, jb * BQ : (jb + 1) * BQ] = (es[jb] * inv).astype(jnp.bfloat16)
        mixed_ref[:, cols] = join_pair(nn(probs_ref[pr], v_ref[:, cols])).astype(jnp.bfloat16)


def attend_back_block(ib, qkv_ref, probs_ref, do_ref, dq_ref, tot_ref, dkt, dvt, dta, dz_ref, hot_ref, relb_ref):
    frames, heads = qkv_ref.shape[0], qkv_ref.shape[1] // 3
    at = pl.ds(pl.multiple_of(ib * BQ, BQ), BQ)
    pairs = heads // 128
    nkeys = frames // BQ
    rows = BQ
    r2 = lax.broadcasted_iota(jnp.int32, (2 * rows, 2 * rows), 0)
    c2 = lax.broadcasted_iota(jnp.int32, (2 * rows, 2 * rows), 1)
    mirror = (r2 + c2 == jnp.where(r2 < rows, rows - 1, 3 * rows - 1)).astype(jnp.bfloat16)
    places = [pl.multiple_of(jnp.clip(jb - ib + 2, 0, 4) * BQ, BQ) for jb in range(nkeys)]
    for pr in range(pairs):
        cols = slice(pr * 128, (pr + 1) * 128)
        keys = qkv_ref[:, heads + pr * 128 : heads + (pr + 1) * 128]
        values = qkv_ref[:, 2 * heads + pr * 128 : 2 * heads + (pr + 1) * 128]
        qs = split_pair(qkv_ref[at, cols] * 0.125)
        dos = split_pair(do_ref[at, cols])
        p = probs_ref[pr]
        dprob = nt(dos, values)
        dvt[pr] += tn(dos, p)
        pf = p.astype(jnp.float32)
        acc = functools.reduce(
            jnp.add, [pf[:, jb * BQ : (jb + 1) * BQ] * dprob[:, jb * BQ : (jb + 1) * BQ] for jb in range(nkeys)]
        )
        inner = jnp.sum(acc, -1, keepdims=True)
        tot_ref[pr] = jnp.zeros(tot_ref.shape[1:], jnp.float32)
        for jb in range(nkeys):
            sl = slice(jb * BQ, (jb + 1) * BQ)
            dz = (pf[:, sl] * (dprob[:, sl] - inner)).astype(jnp.bfloat16)
            dz_ref[pr, :, sl] = dz
            tot_ref[pr, :, pl.ds(places[jb], BQ)] += dz.astype(jnp.float32)
        w = jnp.concatenate([tot_ref[pr, :, BQ : 4 * BQ].astype(jnp.bfloat16), jnp.zeros((2 * rows, BQ), jnp.bfloat16)], 1)
        w = nn(mirror, w)
        outs = [pltpu.roll(w[h * rows : (h + 1) * rows], WIN - rows + 1, 1, stride=1, stride_axis=0) for h in range(2)]
        d = nn(mirror, jnp.concatenate(outs, 0).astype(jnp.bfloat16)).astype(jnp.bfloat16)
        drel = nn(d, hot_ref[...])
        col = lax.broadcasted_iota(jnp.int32, drel.shape, 1)
        low = jnp.sum(tot_ref[pr, :, :BQ], -1, keepdims=True)
        high = jnp.sum(tot_ref[pr, :, 4 * BQ :], -1, keepdims=True)
        drel = drel + jnp.where(col == 0, low, 0.0) + jnp.where(col == REL_LEFT + REL_RIGHT, high, 0.0)
        drel = drel.astype(jnp.bfloat16)
        dz = dz_ref[pr]
        dq = nn(dz, keys) + nn(drel, relb_ref[...])
        dq_ref[at, cols] = (join_pair(dq) * 0.125).astype(jnp.bfloat16)
        dkt[pr] += tn(qs, dz)
        dta[...] += tn(drel, qs)


class Doubling:
    def __init__(self, course, refs, lands, sems, partner):
        self.course, self.items, self.sems, self.partner = course, list(zip(refs, lands)), sems, partner
        self.done = 0

    def copies(self, n):
        at = self.course[n]
        return [
            (
                pltpu.make_async_remote_copy(
                    r, l.at[n], self.sems[0].at[i, n], self.sems[1].at[i, n], device_id=self.partner(at), device_id_type=MESH
                ),
                r,
                l.at[n],
            )
            for i, (r, l) in enumerate(self.items)
            if i < 2 or not isinstance(at, str)
        ]

    def start(self, n=0):
        for cp, _, _ in self.copies(n):
            cp.start()

    def advance(self, n):
        for cp, r, l in self.copies(n):
            cp.wait()
            r[...] += l[...]
        if n + 1 < len(self.course):
            self.start(n + 1)

    def step(self):
        if self.done < len(self.course):
            self.advance(self.done)
            self.done += 1


def stage(name, cid, rows, width, count, gains, *, leave=None, enter=None, dws=(), grads=(), small=None, tail=None, attend=None, junction, row_in=(), row_out=(), sums=0):
    chunk = rows // CHUNKS
    frames = rows * 4
    bits_all = count.bit_length() - 1
    f32, bf = jnp.float32, jnp.bfloat16
    ins, vm_ins, out_shape, scratch = [], [], [], []
    known = {}

    def add_in(array, direct=False):
        if isinstance(array, str):
            return array
        if direct:
            ins.append(array)
            return len(ins) - 1
        if id(array) not in known:
            group = array if isinstance(array, tuple) else (array,)
            known[id(array)] = len(vm_ins)
            vm_ins.append((len(ins), len(group), pltpu.VMEM(flat_shape(array), group[0].dtype)))
            ins.extend(group)
        return known[id(array)]

    out_slots = [0]

    def add_scratch(item):
        scratch.append(item)
        return len(scratch) - 1

    def add_out(shape, dtype, slots, kept=True):
        if not kept:
            return -1 - add_scratch(pltpu.VMEM(shape, dtype)), None
        out_shape.append(jax.ShapeDtypeStruct(shape, dtype))
        first = out_slots[0]
        out_slots[0] += slots
        return len(out_shape) - 1, first

    add_dw = lambda where: [(add_in(d[0]), add_in(d[1])) if d[2] in where else None for d in dws]
    groups = []
    if leave:
        x_i, wl_i = add_in(leave[0]), add_in(leave[1])
        leave_s = [add_scratch(pltpu.VMEM((rows, width), f32)) for _ in range(2)]
        leave_s += [add_scratch(pltpu.VMEM((rows, width), bf)) for _ in range(6)]
        wl_s = add_scratch(pltpu.VMEM(flat_shape(leave[1])[::-1], bf)) if leave[2] else None
        groups.append(len(vm_ins))
        add_dw(("far",))
    gains_i = add_in(gains)
    gain_s = add_scratch(pltpu.VMEM((8, width), f32))
    row_i = [add_in(r) for r in row_in]
    if not leave:
        groups.append(len(vm_ins))
    add_dw(("near", "join"))
    kept = not (tail or attend)
    kept_rows = not tail
    if enter:
        we_i = add_in(enter[0])
        extra_i = [add_in(e) for e in enter[3]]
        we_s = add_scratch(pltpu.VMEM(flat_shape(enter[0])[::-1], bf)) if enter[1] else None
        all_o = add_out((frames, width), bf, 4 * CHUNKS, kept)
        e_o = [add_out((frames, c), d, 4 * CHUNKS, kept) for c, d in enter[4]]
    r_o = [add_out((rows, width), d, CHUNKS, kept_rows) for d in row_out]
    s_o = [add_out((8, width), f32, 1, kept_rows) for _ in range(sums)]
    if attend:
        qkv_i, probs_i, table_i = add_in(attend[0]), add_in(attend[1], True), add_in(attend[2])
        add_dw(("post",))
        heads = attend[0].shape[1] // 3
        pairs = heads // 128
        d_o = [add_out((frames, heads), bf, 4 * CHUNKS) for _ in range(3)] + [add_out((128, 128), f32, 1)]
        attend_s = [
            add_scratch(item)
            for item in (
                pltpu.VMEM((pairs, 2 * BQ, 5 * BQ), f32), pltpu.VMEM((pairs, 128, frames), f32), pltpu.VMEM((pairs, 128, frames), f32),
                pltpu.VMEM((128, 128), f32), pltpu.VMEM((pairs, 2 * BQ, frames), bf), pltpu.VMEM((WIN, BQ), bf), pltpu.VMEM((128, 128), bf),
            )
        ]
        wide_s = add_scratch(pltpu.VMEM((128, 128), f32))
        probs_s = add_scratch(pltpu.VMEM((2, pairs, 2 * BQ, frames), bf))
        probs_sem = add_scratch(pltpu.SemaphoreType.DMA((2,)))
    if small:
        vectors_in, table_in, taps_in = small
        vector_i = [add_in(v) for v in vectors_in]
        table_i, taps_i = add_in(table_in), add_in(taps_in)
    groups.append(len(vm_ins))
    if tail:
        add_dw(("front",))
        tw_i = add_in(tail[0])
        tw_s = add_scratch(pltpu.VMEM(flat_shape(tail[0])[::-1], bf))
        tail_i = [add_in(r) for r in tail[2]]
        add_dw(("close",))
        tail_o = [add_out((rows, width), f32, CHUNKS)]
        tail_sum = add_out((8, width), f32, 1, False)
    groups.append(len(vm_ins))
    fixed_out = len(out_shape)
    plan, dw_o = [], []
    for d in dws:
        shape = (d[6], count // 2, 2, width // count, PIECE)
        if d[2] == "join":
            dw_o.append(add_out(shape, bf, shape[0]))
        else:
            plan.append((shape, 0, d[3], bits_all if tail else min(d[4], bits_all), add_scratch(pltpu.VMEM(shape, bf)), None, None))
            dw_o.append(len(plan) - 1)
    dw_in = [(add_in(d[0]), add_in(d[1])) for d in dws]
    first_grad = len(plan)
    for g in grads:
        g, ahead = g if isinstance(g, tuple) else (g, 1)
        shape = g.array.shape
        plan.append((shape, g.bit, g.turned, bits_all if tail else min(g.bit + ahead, bits_all), None, add_in(g.array, True), add_scratch(arriving(shape))))
    chains = []
    slots = 0
    for shape, bit, turned, end, src_s, src_i, keep_s in plan:
        links = []
        pieces = shape[0]
        for b in range(bit, end):
            nxt = halved(shape, turned)
            land_s = add_scratch(arriving(shape))
            if b == end - 1:
                links.append((b, slots, land_s, None, add_out(nxt.shape, nxt.dtype, pieces)))
            else:
                links.append((b, slots, land_s, add_scratch(pltpu.VMEM(nxt.shape, nxt.dtype)), None))
            slots += pieces
            shape = nxt.shape
        chains.append((pieces, turned, src_s, src_i, keep_s, links))
    if small:
        small_shapes = [(8, width), (TABLE_ROWS, 128), taps_in.shape]
        small_o = [add_out(s, f32, 1) for s in small_shapes]
        lead_o = add_out((1, width), f32, 1)
        downward = list(range(bits_all - 1, -1, -1))
        courses = [downward[-1:] + downward[:-1] + ["sib", "far"], ["sib", "far"] + downward]
        small_l = [add_scratch(pltpu.VMEM((bits_all + 2,) + s, f32)) for s in small_shapes]
        lead_l = [add_scratch(pltpu.VMEM((bits_all + 2, 1, width), f32))]
        small_sems = [add_scratch(pltpu.SemaphoreType.DMA((3, bits_all + 2))) for _ in range(4)]
    if slots:
        grad_sems = [add_scratch(pltpu.SemaphoreType.DMA((slots,))) for _ in range(2)]
    ring_sems = [add_scratch(pltpu.SemaphoreType.DMA((6, CHUNKS))) for _ in range(2)]
    load_sem = add_scratch(pltpu.SemaphoreType.DMA((len(ins),)))
    store_sem = add_scratch(pltpu.SemaphoreType.DMA((out_slots[0],)))
    n_in, n_out = len(ins), len(out_shape)
    vm_at = [add_scratch(item[2]) for item in vm_ins]
    vo_at = [add_scratch(pltpu.VMEM(o.shape, o.dtype)) for o in out_shape]

    def kernel(*refs):
        hbm_in, hbm_out, t = refs[:n_in], refs[n_in : n_in + n_out], refs[n_in + n_out :]
        vout = lambda o: t[-1 - o[0]] if o[0] < 0 else t[vo_at[o[0]]]

        def vin(i):
            if i == "all":
                return vout(all_o)
            if i == "out":
                return vout(e_o[0])
            return t[vm_at[i]]

        waited = set()

        def load(i):
            first, parts, _ = vm_ins[i]
            if len(hbm_in[first].shape) == 3:
                slabs, _, cols = hbm_in[first].shape
                return [
                    pltpu.make_async_copy(hbm_in[first].at[n], vin(i).at[:, pl.ds(n * cols, cols)], t[load_sem].at[first])
                    for n in range(slabs)
                ]
            if parts == 1:
                return [pltpu.make_async_copy(hbm_in[first], vin(i), t[load_sem].at[first])]
            copies, at = [], 0
            for n in range(first, first + parts):
                cols = hbm_in[n].shape[1]
                copies.append(pltpu.make_async_copy(hbm_in[n], vin(i).at[:, pl.ds(at, cols)], t[load_sem].at[n]))
                at += cols
            return copies

        begun = [0]

        def begin_loads(group):
            for i in range(begun[0], groups[group]):
                for cp in load(i):
                    cp.start()
            begun[0] = max(begun[0], groups[group])

        def need(*items):
            for i in items:
                if not isinstance(i, str) and i not in waited:
                    waited.add(i)
                    for cp in load(i):
                        cp.wait()

        dp, me = lax.axis_index("dp"), lax.axis_index("mp")
        core, chip = me % 2, me // 2
        sib = chip * 2 + 1 - core
        far = (1 - chip) * 2 + core
        diag = (1 - chip) * 2 + 1 - core
        bits = sorted({link[0] for ch in chains for link in ch[5]} | set(range(bits_all) if small else ()))
        meet = greet([(dp, sib), (dp, far)] + [(place(dp, b)[1], me) for b in bits])
        begin_loads(0)

        def part(ref, block, k):
            return ref.at[pl.ds(pl.multiple_of(block * rows + k * chunk, chunk), chunk)]

        def store_rows(o, block, k):
            return pltpu.make_async_copy(
                part(vout(o), block, k), part(hbm_out[o[0]], block, k), t[store_sem].at[o[1] + block * CHUNKS + k]
            )

        def store_whole(o):
            return pltpu.make_async_copy(vout(o), hbm_out[o[0]], t[store_sem].at[o[1]])

        def store_piece(o, piece, cols, turned):
            return pltpu.make_async_copy(
                region(vout(o), piece, cols, turned), region(hbm_out[o[0]], piece, cols, turned), t[store_sem].at[o[1] + piece]
            )

        def copy(kind, k, src, dst, to):
            return pltpu.make_async_remote_copy(
                src, dst, t[ring_sems[0]].at[kind, k], t[ring_sems[1]].at[kind, k], device_id=(dp, to), device_id_type=MESH
            )

        if leave:
            px, own, sb, sr, xs, xr, ob, orv = [t[s] for s in leave_s]
        if enter:
            all_ref = vout(all_o)
            we_ref = t[we_s] if enter[1] else vin(we_i)
        pair_send = lambda k: copy(0, k, part(sb, 0, k), part(sr, 0, k), sib)
        far_send = lambda k: copy(1, k, part(xs, 0, k), part(xr, 0, k), far)
        own_send = lambda k: copy(2, k, part(ob, 0, k), part(orv, 0, k), sib)
        all_far = lambda k: copy(3, k, part(all_ref, me, k), part(all_ref, me, k), far)
        all_sib = lambda k: copy(4, k, part(all_ref, me, k), part(all_ref, me, k), sib)
        all_fwd = lambda k: copy(5, k, part(all_ref, far, k), part(all_ref, far, k), sib)
        got_far = lambda k: copy(3, k, part(all_ref, far, k), part(all_ref, far, k), far)
        got_sib = lambda k: copy(4, k, part(all_ref, sib, k), part(all_ref, sib, k), sib)
        got_diag = lambda k: copy(5, k, part(all_ref, diag, k), part(all_ref, diag, k), sib)

        def source(c, step):
            pieces, turned, src_s, src_i, keep_s, links = chains[c]
            if step:
                return t[links[step - 1][3]]
            return t[src_s] if src_s is not None else hbm_in[src_i]

        def hop(c, step, piece):
            b, slot, land_s, _, _ = chains[c][5][step]
            return halving_copy(source(c, step), t[land_s], piece, b, t[grad_sems[0]], t[grad_sems[1]], slot + piece)

        def keep(c):
            return halving_keep(hbm_in[chains[c][3]], t[chains[c][4]], chains[c][5][0][0], t[load_sem].at[chains[c][3]])

        held_back = set()

        def settle(c, step, piece):
            pieces, turned, src_s, src_i, keep_s, links = chains[c]
            b, slot, land_s, out_s, out_o = links[step]
            hop(c, step, piece).wait_recv()
            if step == 0 and src_s is None:
                if c not in held_back:
                    held_back.add(c)
                    keep(c).wait()
                held = lambda p, j: t[keep_s][p, j]
            else:
                own_bit, _ = place(dp, b)
                src = source(c, step)
                held = lambda p, j: src[p, j, own_bit]
            landing = t[land_s]
            out = t[out_s] if out_o is None else vout(out_o)
            halving_add(held, landing, out, piece, turned)
            if out_o is not None:
                store_piece(out_o, piece, PIECE, turned and landing.shape[2] % 128 == 0).start()

        def fill(k, where):
            for d, (a, b), o in zip(dws, dw_in, dw_o):
                if d[2] != where:
                    continue
                chain = None if where == "join" else o
                dw = vout(o) if chain is None else t[chains[o][2]]

                @pl.when(k < dw.shape[0])
                def _(a=a, b=b, dw=dw, chain=chain, o=o, lo=d[5]):
                    g = tn(vin(a)[...], vin(b)[:, pl.ds(pl.multiple_of((lo + k) * PIECE, PIECE), PIECE)])
                    dw[k] = g.astype(bf).reshape(dw.shape[1:])
                    if chain is None:
                        store_piece(o, k, PIECE, False).start()
                    else:
                        hop(chain, 0, k).start()

        def need_for(where):
            for d, (a, b) in zip(dws, dw_in):
                if d[2] == where:
                    need(a, b)

        def leave_phase(x_ref, wl_ref, far_fill, near_fill):
            def two(k, block_a, block_b):
                lhs = jnp.concatenate([part(x_ref, block_a, k)[...], part(x_ref, block_b, k)[...]], 0)
                return nn(lhs, wl_ref[...])

            def push(k):
                pair_send(k).wait_recv()
                part(xs, 0, k)[...] = (part(px, 0, k)[...] + part(sr, 0, k)[...].astype(f32)).astype(bf)
                far_send(k).start()

            def out_far(k, c):
                p = two(k, far, diag)
                part(px, 0, k)[...] = p[:chunk]
                part(sb, 0, k)[...] = p[chunk:].astype(bf)
                pair_send(k).start()

                @pl.when(k > 0)
                def _():
                    push(k - 1)

                fill(k, far_fill)
                return c

            lax.fori_loop(0, CHUNKS, out_far, 0)
            need_for(near_fill)

            def out_near(k, c):
                p = two(k, me, sib)
                part(own, 0, k)[...] = p[:chunk]
                part(ob, 0, k)[...] = p[chunk:].astype(bf)
                own_send(k).start()

                @pl.when(k == 0)
                def _():
                    push(CHUNKS - 1)

                fill(k, near_fill)
                return c

            lax.fori_loop(0, CHUNKS, out_near, 0)

        def leave_drain():
            def drain(k, c):
                pair_send(k).wait_send()
                far_send(k).wait_send()
                own_send(k).wait_send()
                return c

            lax.fori_loop(0, CHUNKS, drain, 0)

        def join_phase(rule, has_leave, in_refs, outs, totals, gathers):
            def join(k, c):
                fill(k, "join")
                branch = None
                if has_leave:
                    own_send(k).wait_recv()
                    far_send(k).wait_recv()
                    branch = part(own, 0, k)[...] + part(orv, 0, k)[...].astype(f32) + part(xr, 0, k)[...].astype(f32)
                fresh = rule(
                    branch, [part(r, 0, k)[...] for r in in_refs], t[gain_s], [part(vout(o), 0, k) for o in outs], [vout(o) for o in totals]
                )
                if gathers:
                    part(all_ref, me, k)[...] = fresh
                    all_far(k).start()
                    all_sib(k).start()
                for o in outs:
                    if o[0] >= 0:
                        store_rows(o, 0, k).start()
                return c

            lax.fori_loop(0, CHUNKS, join, 0)
            for o in totals:
                if o[0] >= 0:
                    store_whole(o).start()

        for o in s_o + ([tail_sum] if tail else []):
            vout(o)[...] = jnp.zeros((8, width), f32)
        meet()
        if leave:
            need(x_i, wl_i)
        begin_loads(1)
        for c in range(first_grad, len(chains)):
            for p in range(chains[c][0]):
                hop(c, 0, p).start()
        if leave:
            if leave[2]:
                t[wl_s][...] = vin(wl_i)[...].T
            need_for("far")
            leave_phase(vin(x_i), t[wl_s] if leave[2] else vin(wl_i), "far", "near")
        for c in range(first_grad, len(chains)):
            keep(c).start()
        need(gains_i, *row_i)
        for i in range(5):
            t[gain_s][i : i + 1, :] = gain_row(vin(gains_i), i, width)
        need_for("join")
        if enter and enter[1]:
            need(we_i)
            we_ref[...] = vin(we_i)[...].T
        join_phase(junction, bool(leave), [vin(r) for r in row_i], r_o, s_o, bool(enter))

        lead = [c for c in range(first_grad) if tail and dws[[i for i, o in enumerate(dw_o) if o == c][0]][2] == "far"]
        if small:
            partner = lambda at: (dp, sib) if at == "sib" else (dp, far) if at == "far" else (place(dp, at)[1], me)
            need(*vector_i, table_i, taps_i)
            rows_ref = vout(small_o[0])
            rows_ref[...] = jnp.zeros((8, width), f32)
            vectors = [vout(s_o[0])] + [vin(i) for i in vector_i]
            for i, v in enumerate(vectors[:4]):
                rows_ref[i : i + 1, :] = jnp.sum(v[...], 0, keepdims=True)
            for i, v in enumerate(vectors[4:]):
                line = jnp.sum(v[...], 0, keepdims=True)
                rows_ref[4:5, i * 128 : (i + 1) * 128] = functools.reduce(
                    jnp.add, [line[:, j * 128 : (j + 1) * 128] for j in range(width // 128)]
                )
            both = vin(table_i)[...]
            both = both + pltpu.roll(both, 64, 1)
            left = lax.broadcasted_iota(jnp.int32, (TABLE_ROWS, 128), 1) < HEAD
            vout(small_o[1])[...] = jnp.where(left, both[:TABLE_ROWS], both[TABLE_ROWS : 2 * TABLE_ROWS])
            vout(small_o[2])[...] = vin(taps_i)[...]
            wide = Doubling(courses[0], [vout(o) for o in small_o], [t[l] for l in small_l], [t[s] for s in small_sems[:2]], partner)
            wide.start()

        mid = set()

        def hasten(which):
            for c in which:
                if len(chains[c][5]) > 1:
                    mid.add(c)
                    for p in range(chains[c][0]):
                        settle(c, 0, p)
                        hop(c, 1, p).start()

        if enter:
            begin_loads(len(groups) - 1)
            need(we_i, *extra_i)

            def work(k, block_a, block_b):
                lhs = jnp.concatenate([part(all_ref, block_a, k)[...], part(all_ref, block_b, k)[...]], 0)
                h = nn(lhs, we_ref[...])
                for i, block in enumerate((block_a, block_b)):
                    view = lambda ref: part(ref, block, k)
                    enter[2](h[i * chunk : (i + 1) * chunk], [view(vin(r))[...] for r in extra_i], [view(vout(o)) for o in e_o])
                    for o in [all_o] + e_o:
                        if o[0] >= 0:
                            store_rows(o, block, k).start()

        if attend:
            tot_ref, dkt, dvt, dta, dz_ref, hot_ref, relb_ref = [t[s] for s in attend_s]
            dq, dk, dv = [vout(o) for o in d_o[:3]]
            need(qkv_i, table_i)
            need_for("post")
            for ref in (dkt, dvt, dta):
                ref[...] = jnp.zeros(ref.shape, f32)
            hot_ref[...] = spot_table(WIN)
            relb_ref[...] = wide_table(vin(table_i), t[wide_s])

            def block_of(j):
                chip_j = chip + (j // 4) * (1 - 2 * chip)
                core_j = core + (j % 2) * (1 - 2 * core)
                return (chip_j * 2 + core_j) * 2 + (j // 2) % 2

            def fetch(j):
                at = pl.ds(pl.multiple_of(block_of(j) * 2 * BQ, 2 * BQ), 2 * BQ)
                return pltpu.make_async_copy(hbm_in[probs_i].at[:, at, :], t[probs_s].at[j % 2], t[probs_sem].at[j % 2])

            fetch(0).start()

            def pass_on(*ks):
                for k in ks:
                    got_far(k).wait_recv()
                    all_fwd(k).start()

            def near(*ks):
                for k in ks:
                    got_sib(k).wait_recv()
                    work(k, me, sib)

            def distant(*ks):
                for k in ks:
                    got_diag(k).wait_recv()
                    work(k, far, diag)

            def before(n):
                if n == 0:
                    near(0, 1)
                elif n == 1:
                    pass_on(0)
                elif n == 2:
                    near(2, 3)
                    pass_on(1)
                elif n == 3:
                    pass_on(2)
                    hasten(range(first_grad, len(chains)))
                elif n == 4:
                    pass_on(3)
                    distant(0, 1)
                elif n == 5:
                    hasten(range(first_grad))
                elif n == 6:
                    distant(2, 3)
                    for k in range(CHUNKS):
                        if any(d[2] == "post" and k < d[6] for d in dws):
                            fill(k, "post")

            def query_block(j, c):
                for n in range(7):

                    @pl.when(j == n)
                    def _(n=n):
                        before(n)

                @pl.when(j < 7)
                def _():
                    fetch(j + 1).start()

                fetch(j).wait()
                attend_back_block(
                    block_of(j), vin(qkv_i), t[probs_s].at[j % 2], vout(e_o[0]), dq, tot_ref, dkt, dvt, dta, dz_ref, hot_ref, relb_ref
                )
                return c

            lax.fori_loop(0, 8, query_block, 0)
            for pr in range(pairs):
                dk[:, pr * 128 : (pr + 1) * 128] = dkt[pr].T.astype(bf)
                dv[:, pr * 128 : (pr + 1) * 128] = dvt[pr].T.astype(bf)
            vout(d_o[3])[...] = dta[...]
            for o in d_o:
                store_whole(o).start()
        elif enter:
            got_sib(0).wait_recv()
            work(0, me, sib)

            def gather(k, c):
                got_far(k).wait_recv()
                all_fwd(k).start()

                @pl.when(k + 1 < CHUNKS)
                def _():
                    got_sib(k + 1).wait_recv()
                    work(k + 1, me, sib)

                got_diag(k).wait_recv()
                work(k, far, diag)
                if small:

                    for n, at in enumerate((1, CHUNKS - 1)):

                        @pl.when(k == at)
                        def _(n=n):
                            wide.advance(n)

                if lead:

                    @pl.when(k == CHUNKS - 2)
                    def _():
                        for ch in lead:
                            for p in range(chains[ch][0]):
                                settle(ch, 0, p)
                                hop(ch, 1, p).start()

                return c

            lax.fori_loop(0, CHUNKS, gather, 0)
            if small:
                wide.done = 2

        early = 0
        if tail:
            need_for("front")

            def front(k, c):
                fill(k, "front")
                return c

            lax.fori_loop(0, CHUNKS, front, 0)
            early = 1
            if lead and bits_all > 2:
                early = 2
                for ch in lead:
                    for p in range(chains[ch][0]):
                        settle(ch, 1, p)
                        hop(ch, 2, p).start()
            leave_drain()
            need(tw_i, *tail_i)
            t[tw_s][...] = vin(tw_i)[...].T
            leave_phase(vin("out"), t[tw_s], None, "close")
            wide.step()

        def close_rows():
            join_phase(tail[1], True, [vout(r_o[0])] + [vin(r) for r in tail_i], tail_o, [tail_sum], False)
            vout(lead_o)[...] = jnp.sum(vout(tail_sum)[...], 0, keepdims=True)
            final = Doubling(courses[1], [vout(lead_o)], [t[l] for l in lead_l], [t[s] for s in small_sems[2:]], partner)
            final.start()
            return final

        depth = lambda c: len(chains[c][5])
        begin = lambda c: early if c in lead else 1 if c in mid else 0
        agenda, fresh_slot = {}, 1
        for c in range(len(chains)):
            new = tail and c < first_grad and c not in lead
            for p in range(chains[c][0]):
                slot = fresh_slot if new else 0
                fresh_slot += 1 if new else 0
                for step in range(begin(c), depth(c)):
                    agenda.setdefault(slot, []).append((step, c, p))
                    slot += LAG
        final = None
        for slot in range(max(list(agenda) + [0]) + 1):
            if tail and slot == JOIN_SLOT:
                final = close_rows()
            for step, c, p in sorted(agenda.get(slot, []), key=lambda x: -x[0]):
                settle(c, step, p)
                if step + 1 < depth(c):
                    hop(c, step + 1, p).start()
            if tail and wide.done < len(courses[0]):
                wide.step()
            elif final is not None and slot > JOIN_SLOT and final.done < len(courses[1]) - 1:
                final.step()
        if tail:
            while final.done < len(courses[1]):
                final.step()
            for o in small_o + [lead_o]:
                store_whole(o).start()
        for c in range(len(chains)):
            for s in range(depth(c)):
                for p in range(chains[c][0]):
                    hop(c, s, p).wait_send()
            out_o = chains[c][5][-1][4]
            block = chains[c][5][-1][2]
            for p in range(chains[c][0]):
                store_piece(out_o, p, PIECE, chains[c][1] and t[block].shape[2] % 128 == 0).wait()
        if leave:
            leave_drain()

        def drain(k, c):
            if enter:
                all_far(k).wait_send()
                all_sib(k).wait_send()
                all_fwd(k).wait_send()
                for block in range(4):
                    for o in [all_o] + e_o:
                        if o[0] >= 0:
                            store_rows(o, block, k).wait()
            for o in r_o + (tail_o if tail else []):
                if o[0] >= 0:
                    store_rows(o, 0, k).wait()
            return c

        lax.fori_loop(0, CHUNKS, drain, 0)
        for o in s_o + (small_o + [lead_o] if tail else []) + (d_o if attend else []):
            if o[0] >= 0:
                store_whole(o).wait()
        for d, o in zip(dws, dw_o):
            if d[2] == "join":
                for p in range(d[6]):
                    store_piece(o, p, PIECE, False).wait()

    flops = 0
    if leave:
        flops += 2 * frames * flat_shape(leave[1])[1 if leave[2] else 0] * width
    if enter:
        flops += 2 * frames * width * sum(c for c, _ in enter[4])
    flops += sum(2 * frames * width * PIECE * d[6] for d in dws)
    outs = pl.pallas_call(
        kernel,
        in_specs=[in_hbm()] * n_in,
        out_specs=[in_hbm()] * n_out,
        out_shape=out_shape,
        scratch_shapes=scratch,
        compiler_params=pltpu.CompilerParams(collective_id=cid, has_side_effects=True, vmem_limit_bytes=VMEM_LIMIT),
        cost_estimate=pl.CostEstimate(flops=flops, bytes_accessed=60_000_000, transcendentals=0),
        name=name,
    )(*ins)
    fixed, rest = list(outs[:fixed_out]), list(outs[fixed_out:])
    fresh = [Grad(rest.pop(0), 0, d[3]) for d in dws if d[2] == "join"]
    for item in plan:
        fresh.append(Grad(rest.pop(0), item[3], item[2]))
    return fixed + [fresh] + rest


def publish(ends, small, sizes, rel, total):
    flat, outs, where = [], [], []
    f32 = jnp.float32
    for arrays, parts in ends:
        rows = arrays[0].shape[0]
        joined = len(arrays) > 1 and sizes[len(outs)]
        shape = (rows, sum(a.shape[1] for a in arrays)) if not joined else (sum(a.shape[0] for a in arrays), arrays[0].shape[1])
        where.append((len(flat), arrays, joined))
        flat.extend(arrays)
        if parts < 0:
            outs.append((shape, (-parts, shape[0], shape[1] // -parts)))
        else:
            outs.append((shape, (shape[0], parts, shape[1] // parts) if parts else None))
    n, m = len(flat), len(ends)
    width = small[0].shape[1]
    taps = small[3].shape
    split_at = [i for i in range(m) if ends[i][1] > 0]
    slab_at = [i for i in range(m) if ends[i][1] < 0]
    small_shapes = [(1, width)] * 5 + [(HEAD, rel), (taps[0] - 1, taps[1]), (1, taps[1]), (1, 5)]

    def kernel(*refs):
        src, small_in = refs[:n], refs[n : n + 4]
        dst, small_out = refs[n + 4 : n + 4 + m], refs[n + 4 + m : n + 13 + m]
        rest = refs[n + 13 + m :]
        held, split = rest[:m], dict(zip(split_at, rest[m:-1]))
        sem = rest[-1]
        loads, stores = [], []
        for i, (first, arrays, joined) in enumerate(where):
            at, copies = 0, []
            for k in range(len(arrays)):
                ref = src[first + k]
                size = ref.shape[0 if joined else 1]
                part = held[i].at[pl.ds(at, size)] if joined else held[i].at[:, pl.ds(at, size)]
                copies.append(pltpu.make_async_copy(ref, part, sem.at[first + k]))
                at += size
            loads.append(copies)
            if i in slab_at:
                slabs, _, cols = dst[i].shape
                stores.append(
                    [
                        pltpu.make_async_copy(held[i].at[:, pl.ds(k * cols, cols)], dst[i].at[k], sem.at[n + m + k])
                        for k in range(slabs)
                    ]
                )
            else:
                stores.append([pltpu.make_async_copy(split.get(i, held[i]), dst[i], sem.at[n + i])])
        for copies in loads:
            for cp in copies:
                cp.start()
        lead, rows, table, tap = [r[...] for r in small_in]
        small_out[0][...] = lead
        for i in range(4):
            small_out[1 + i][...] = rows[i : i + 1]
        turned = jnp.concatenate([table, jnp.zeros((128 - TABLE_ROWS, 128), f32)], 0).T
        small_out[5][:, :TABLE_ROWS] = turned[:HEAD, :TABLE_ROWS]
        small_out[5][:, TABLE_ROWS:] = turned[HEAD:, : rel - TABLE_ROWS]
        small_out[6][...] = tap[:-1]
        small_out[7][...] = tap[-1:]
        lane = lax.broadcasted_iota(jnp.int32, (1, 128), 1)
        mean = jnp.zeros((1, 128), f32)
        for i in range(5):
            mean = jnp.where(lane == i, jnp.sum(rows[4:5, i * 128 : (i + 1) * 128], -1, keepdims=True) / total, mean)
        root = jnp.sqrt(mean)
        small_out[8][...] = root[:, :5]
        for i in range(m):
            for cp in loads[i]:
                cp.wait()
            if i in split:
                cols = split[i].shape[2]
                for j in range(split[i].shape[1]):
                    split[i][:, j, :] = held[i][:, j * cols : (j + 1) * cols]
            for cp in stores[i]:
                cp.start()
        for copies in stores:
            for cp in copies:
                cp.wait()

    vm = pl.BlockSpec(memory_space=pltpu.VMEM)
    return pl.pallas_call(
        kernel,
        in_specs=[in_hbm()] * n + [vm] * 4,
        out_specs=[in_hbm()] * m + [vm] * 9,
        out_shape=[jax.ShapeDtypeStruct(o[1] or o[0], f32) for o in outs] + [jax.ShapeDtypeStruct(s, f32) for s in small_shapes],
        scratch_shapes=[pltpu.VMEM(o[0], f32) for o in outs]
        + [pltpu.VMEM(outs[i][1], f32) for i in split_at]
        + [pltpu.SemaphoreType.DMA((n + m + 4,))],
        compiler_params=pltpu.CompilerParams(vmem_limit_bytes=VMEM_LIMIT),
        name="publish",
    )(*flat, *small)


SPAN = 128


def exchange(stats, landing, send, recv):
    dp, me = lax.axis_index("dp"), lax.axis_index("mp")
    core, chip = me % 2, me // 2
    others = [chip * 2 + 1 - core, (1 - chip) * 2 + core, (1 - chip) * 2 + 1 - core]
    return [
        pltpu.make_async_remote_copy(
            stats, landing.at[i], send.at[i], recv.at[i], device_id=(dp, to), device_id_type=MESH
        )
        for i, to in enumerate(others)
    ]


def group_targets():
    dp, me = lax.axis_index("dp"), lax.axis_index("mp")
    core, chip = me % 2, me // 2
    return [(dp, chip * 2 + 1 - core), (dp, (1 - chip) * 2 + core), (dp, (1 - chip) * 2 + 1 - core)]


def to_rows(first, second):
    lane = lax.broadcasted_iota(jnp.int32, (SPAN, SPAN), 1)
    both = jnp.where(lane == 0, first, jnp.where(lane == 1, second, 0.0))
    return both.T[:8]


def to_columns(rows8):
    return jnp.concatenate([rows8, jnp.zeros((SPAN - 8, SPAN), jnp.float32)], 0).T


def shifted(window, by):
    return window if by == 0 else pltpu.roll(window, window.shape[0] - by, 0)


def depth_gain_row(ref, width, chans):
    first = 5 * width // 128
    return jnp.concatenate([ref[first + j : first + j + 1, :] for j in range(chans // 128)], 1)


def conv_mid(glu, w_depth, gains, width, cid):
    frames, chans = glu.shape
    taps = w_depth.shape[0]
    reach = taps - 1
    edge = (reach + 7) // 8 * 8
    f32, bf = jnp.float32, jnp.bfloat16
    tiles, lanes = frames // SPAN, chans // 128

    def kernel(glu_h, w_h, g_h, act_h, slope_h, unit_h, stat_h, pad, w_raw, g_raw, w_v, g_v, act, slope, unit, stat, sendbuf, landing, lsem, ssem, send, recv):
        meet = greet(group_targets())
        loads = [
            pltpu.make_async_copy(glu_h, pad.at[pl.ds(edge, frames)], lsem.at[0]),
            pltpu.make_async_copy(w_h, w_raw, lsem.at[1]),
            pltpu.make_async_copy(g_h, g_raw, lsem.at[2]),
        ]
        for cp in loads:
            cp.start()
        pad[:edge, :] = jnp.zeros((edge, chans), f32)
        for cp in loads:
            cp.wait()
        w_v[...] = w_raw[...].astype(f32)
        g_v[...] = depth_gain_row(g_raw, width, chans)

        def tile(i, c):
            at = pl.multiple_of(i * SPAN, SPAN)
            for lane in range(lanes):
                cols = slice(lane * 128, (lane + 1) * 128)
                window = pad[pl.ds(at, SPAN + edge), cols]
                total = jnp.zeros((SPAN, 128), f32)
                for by in range(8):
                    moved = shifted(window, by)
                    for base in range(0, edge + 1, 8):
                        tap = base + by - (edge - reach)
                        if 0 <= tap < taps:
                            total = total + w_v[tap : tap + 1, cols] * moved[base : base + SPAN]
                unit[pl.ds(at, SPAN), cols] = total
            depth = unit[pl.ds(at, SPAN), :]
            mean = jnp.mean(depth, -1, keepdims=True)
            centred = depth - mean
            sendbuf[:, pl.ds(at, SPAN)] = to_rows(mean, jnp.sum(centred * centred, -1, keepdims=True))
            return c

        lax.fori_loop(0, tiles, tile, 0)
        meet()
        copies = exchange(sendbuf, landing, send, recv)
        for cp in copies:
            cp.start()
        for cp in copies:
            cp.wait_recv()
        rows = [sendbuf[...]] + [landing[i] for i in range(3)]
        mean = sum(r[0:1] for r in rows) * 0.25
        spread = sum(r[1:2] + chans * (r[0:1] - mean) * (r[0:1] - mean) for r in rows) / width
        inverse = lax.rsqrt(spread + epsilon)
        row = lax.broadcasted_iota(jnp.int32, (8, frames), 0)
        stat[...] = jnp.where(row == 0, mean, jnp.where(row == 1, inverse, 0.0))
        outs = [(act, act_h), (slope, slope_h), (unit, unit_h)]

        def store(i, n):
            at = pl.ds(pl.multiple_of(i * SPAN, SPAN), SPAN)
            return pltpu.make_async_copy(outs[n][0].at[at], outs[n][1].at[at], ssem.at[n, i])

        def finish(i, c):
            at = pl.multiple_of(i * SPAN, SPAN)
            cols = to_columns(stat[:, pl.ds(at, SPAN)])
            u = (unit[pl.ds(at, SPAN), :] - cols[:, 0:1]) * cols[:, 1:2]
            a, s = silu_pair(u * g_v[...])
            unit[pl.ds(at, SPAN), :] = u
            act[pl.ds(at, SPAN), :] = a.astype(bf)
            slope[pl.ds(at, SPAN), :] = s.astype(bf)
            for n in range(3):
                store(i, n).start()
            return c

        lax.fori_loop(0, tiles, finish, 0)
        last = pltpu.make_async_copy(stat, stat_h, lsem.at[0])
        last.start()
        for cp in copies:
            cp.wait_send()
        for i in range(tiles):
            for n in range(3):
                store(i, n).wait()
        last.wait()

    S = jax.ShapeDtypeStruct
    out_shape = [S((frames, chans), bf), S((frames, chans), bf), S((frames, chans), f32), S((8, frames), f32)]
    vm = pltpu.VMEM
    return pl.pallas_call(
        kernel,
        in_specs=[in_hbm()] * 3,
        out_specs=[in_hbm()] * 4,
        out_shape=out_shape,
        scratch_shapes=[
            vm((frames + edge, chans), f32), vm(w_depth.shape, bf), vm(gains.shape, f32), vm(w_depth.shape, f32), vm((1, chans), f32),
            vm((frames, chans), bf), vm((frames, chans), bf), vm((frames, chans), f32), vm((8, frames), f32),
            vm((8, frames), f32), vm((3, 8, frames), f32),
            pltpu.SemaphoreType.DMA((3,)), pltpu.SemaphoreType.DMA((3, tiles)), pltpu.SemaphoreType.DMA((3,)), pltpu.SemaphoreType.DMA((3,)),
        ],
        compiler_params=pltpu.CompilerParams(collective_id=cid, has_side_effects=True, vmem_limit_bytes=VMEM_LIMIT),
        name="conv_mid",
    )(glu, w_depth, gains)


def conv_mid_back(grad, slope, unit, stat, glu, sig, tail, w_depth, gains, width, cid, grads):
    frames, chans = glu.shape
    taps = w_depth.shape[0]
    reach = taps - 1
    edge = (reach + 7) // 8 * 8
    f32, bf = jnp.float32, jnp.bfloat16
    tiles, lanes = frames // SPAN, chans // 128
    ins = [grad, slope, unit, stat, w_depth, gains, glu, sig, tail]
    riders = Riders(grads)
    n = len(grads)

    def kernel(*refs):
        hbm, ride_in, (pair_h, taps_h), ride_out = refs[:9], refs[9 : 9 + n], refs[9 + n : 11 + n], refs[11 + n : 11 + 2 * n]
        refs = refs[2 * n :]
        (grad_v, slope_v, unit_v, stat_v, w_raw, g_raw, pad, sig_v, tail_v, w_v, g_v, back, pair, taps_v, acc, gacc, sendbuf, landing, lsem, ssem, send, recv) = refs[11:33]
        riders.bind(ride_in, ride_out, refs[33:])
        meet = greet(group_targets() + riders.targets())
        dst = [grad_v, slope_v, unit_v, stat_v, w_raw, g_raw, pad.at[pl.ds(edge, frames)], sig_v, tail_v]
        loads = [pltpu.make_async_copy(h, d, lsem.at[i]) for i, (h, d) in enumerate(zip(hbm, dst))]
        for cp in loads:
            cp.start()
        pad[:edge, :] = jnp.zeros((edge, chans), f32)
        back[frames:, :] = jnp.zeros((edge, chans), f32)
        acc[...] = jnp.zeros_like(acc)
        gacc[...] = jnp.zeros_like(gacc)
        for cp in loads[:6]:
            cp.wait()
        w_v[...] = w_raw[...].astype(f32)
        g_v[...] = depth_gain_row(g_raw, width, chans)

        def first(i, c):
            at = pl.ds(pl.multiple_of(i * SPAN, SPAN), SPAN)
            u = unit_v[at, :]
            de = grad_v[at, :] * slope_v[at, :].astype(f32)
            gacc[...] += fold8(de * u)
            du = de * g_v[...]
            back[at, :] = du
            sendbuf[:, at] = to_rows(jnp.sum(du, -1, keepdims=True), jnp.sum(du * u, -1, keepdims=True))
            return c

        meet()
        riders.start()
        lax.fori_loop(0, tiles, first, 0)
        copies = exchange(sendbuf, landing, send, recv)
        for cp in copies:
            cp.start()
        for cp in loads[6:]:
            cp.wait()
        for cp in copies:
            cp.wait_recv()
        means = (sendbuf[...] + landing[0] + landing[1] + landing[2]) / width
        row = lax.broadcasted_iota(jnp.int32, (8, frames), 0)
        stat_v[...] = jnp.where(row == 1, stat_v[...], jnp.where(row == 0, means[0:1], jnp.where(row == 2, means[1:2], 0.0)))

        def second(i, c):
            at = pl.ds(pl.multiple_of(i * SPAN, SPAN), SPAN)
            cols = to_columns(stat_v[:, at])
            back[at, :] = cols[:, 1:2] * (back[at, :] - cols[:, 0:1] - unit_v[at, :] * cols[:, 2:3])
            return c

        lax.fori_loop(0, tiles, second, 0)

        def store(i):
            at = pl.ds(pl.multiple_of(i * SPAN, SPAN), SPAN)
            return pltpu.make_async_copy(pair.at[at], pair_h.at[at], ssem.at[i])

        def third(i, c):
            at = pl.multiple_of(i * SPAN, SPAN)
            rows = pl.ds(at, SPAN)
            for lane in range(lanes):
                cols = slice(lane * 128, (lane + 1) * 128)
                ahead = back[pl.ds(at, SPAN + edge), cols]
                total = jnp.zeros((SPAN, 128), f32)
                for by in range(8):
                    moved = shifted(ahead, by)
                    for base in range(0, edge, 8):
                        tap = reach - (base + by)
                        if 0 <= tap < taps:
                            total = total + w_v[tap : tap + 1, cols] * moved[base : base + SPAN]
                pair[rows, cols] = (total * sig_v[rows, cols].astype(f32)).astype(bf)
                pair[rows, chans + lane * 128 : chans + (lane + 1) * 128] = (total * tail_v[rows, cols].astype(f32)).astype(bf)
            store(i).start()
            for lane in range(lanes):
                cols = slice(lane * 128, (lane + 1) * 128)
                here = back[rows, cols]
                window = pad[pl.ds(at, SPAN + edge), cols]
                for by in range(8):
                    moved = shifted(window, by)
                    for base in range(0, edge + 1, 8):
                        tap = base + by - (edge - reach)
                        if 0 <= tap < taps:
                            acc[tap * 8 : tap * 8 + 8, cols] += fold8(here * moved[base : base + SPAN])
            return c

        lax.fori_loop(0, tiles, third, 0)
        for tap in range(taps):
            taps_v[tap : tap + 1, :] = jnp.sum(acc[tap * 8 : tap * 8 + 8, :], 0, keepdims=True)
        taps_v[taps : taps + 1, :] = jnp.sum(gacc[...], 0, keepdims=True)
        last = pltpu.make_async_copy(taps_v, taps_h, lsem.at[0])
        last.start()
        for cp in copies:
            cp.wait_send()
        riders.finish()
        for i in range(tiles):
            store(i).wait()
        last.wait()

    S = jax.ShapeDtypeStruct
    vm = pltpu.VMEM
    outs = pl.pallas_call(
        kernel,
        in_specs=[in_hbm()] * (9 + n),
        out_specs=[in_hbm()] * (2 + n),
        out_shape=[S((frames, 2 * chans), bf), S((taps + 1, chans), f32)] + riders.after,
        scratch_shapes=[
            vm((frames, chans), f32), vm((frames, chans), bf), vm((frames, chans), f32), vm((8, frames), f32),
            vm(w_depth.shape, bf), vm(gains.shape, f32), vm((frames + edge, chans), f32), vm((frames, chans), bf), vm((frames, chans), bf),
            vm(w_depth.shape, f32), vm((1, chans), f32),
            vm((frames + edge, chans), f32), vm((frames, 2 * chans), bf), vm((taps + 1, chans), f32), vm((taps * 8, chans), f32), vm((8, chans), f32),
            vm((8, frames), f32), vm((3, 8, frames), f32),
            pltpu.SemaphoreType.DMA((9,)), pltpu.SemaphoreType.DMA((tiles,)), pltpu.SemaphoreType.DMA((3,)), pltpu.SemaphoreType.DMA((3,)),
        ] + riders.scratch,
        compiler_params=pltpu.CompilerParams(collective_id=cid, has_side_effects=True, vmem_limit_bytes=VMEM_LIMIT),
        name="conv_mid_back",
    )(*ins, *riders.arrays)
    return outs[0], outs[1], riders.results(outs[2:])


def attn_fwd(qkv, rel):
    frames, cols = qkv.shape
    heads = cols // 3
    pairs = heads // 128
    nb = frames // BQ
    bf = jnp.bfloat16
    return pl.pallas_call(
        fwd_kernel,
        grid=(nb,),
        in_specs=[
            pl.BlockSpec((BQ, heads), lambda i: (i, 0)),
            pl.BlockSpec((frames, heads), lambda i: (0, 1)),
            pl.BlockSpec((frames, heads), lambda i: (0, 2)),
            pl.BlockSpec(rel.shape, lambda i: (0, 0)),
        ],
        out_specs=[
            pl.BlockSpec((BQ, heads), lambda i: (i, 0)),
            pl.BlockSpec((pairs, 2 * BQ, frames), lambda i: (0, i, 0)),
        ],
        out_shape=[jax.ShapeDtypeStruct((frames, heads), bf), jax.ShapeDtypeStruct((pairs, 2 * frames, frames), bf)],
        scratch_shapes=[
            pltpu.VMEM((pairs, 2 * BQ, 5 * BQ), jnp.float32), pltpu.VMEM((5 * BQ, 128), bf), pltpu.VMEM((128, 128), jnp.float32)
        ],
        compiler_params=pltpu.CompilerParams(vmem_limit_bytes=VMEM_LIMIT),
        name="attn_fwd",
    )(qkv, qkv, qkv, rel)


def body(
    features,
    w1_in,
    w1_out,
    gain_ffn1,
    w_qkv,
    w_attn_out,
    rel_table,
    gain_attn,
    w_conv_in,
    w_depth,
    gain_depth,
    w_conv_out,
    gain_conv,
    w2_in,
    w2_out,
    gain_ffn2,
    gain_final,
    cotangent,
):
    local_frames, clip_count, width = features.shape
    rows = local_frames * clip_count
    f32, bf = jnp.float32, jnp.bfloat16
    s0 = features.reshape(rows, width)
    seed = cotangent.reshape(rows, width)
    spare = jnp.zeros((width - gain_depth.shape[0],), bf)
    gains = jnp.concatenate([gain_ffn1, gain_attn, gain_conv, gain_ffn2, gain_final, gain_depth, spare])
    gains = gains.astype(f32).reshape(-1, 128)
    flat_qkv = w_qkv.transpose(1, 0, 2)
    flat_conv = w_conv_in.reshape(width, -1)
    units = w1_in.shape[1]
    half = units // PIECE // 2
    dp_count = lax.axis_size("dp")
    done = dp_count.bit_length() - 1
    pending = lambda items: [g for g in items if g.bit < done]
    chans = w_conv_out.shape[0]

    def swish_out(h, extra, outs):
        act, slope = silu_pair(h)
        outs[0][...] = act.astype(bf)
        outs[1][...] = slope.astype(bf)

    def plain_out(h, extra, outs):
        outs[0][...] = h.astype(outs[0].dtype)

    def glu_out(h, extra, outs):
        p0 = h[:, :chans]
        sig = jax.nn.sigmoid(h[:, chans:])
        glu = p0 * sig
        outs[0][...] = glu
        outs[1][...] = sig.astype(bf)
        outs[2][...] = (glu * (1.0 - sig)).astype(bf)

    def slope_out(h, extra, outs):
        outs[0][...] = (h * extra[0][...].astype(f32)).astype(bf)

    def first(branch, ins, gains, outs, sums):
        return (unit_norm(ins[0].astype(f32))[0] * gains[0:1, :]).astype(bf)

    def forward(scale, row):
        def run(branch, ins, gains, outs, sums):
            fresh = ins[0].astype(f32) + scale * branch
            outs[0][...] = fresh
            sums[0][...] += fold8(branch * branch)
            return (unit_norm(fresh)[0] * gains[row : row + 1, :]).astype(bf)
        return run

    def turn(branch, ins, gains, outs, sums):
        fresh = ins[0] + 0.5 * branch
        sums[0][...] += fold8(branch * branch)
        sums[1][...] += fold8(fresh * fresh)
        unit, inverse = unit_norm(fresh)
        outs[0][...] = unit * gains[4:5, :]
        grad = ins[1].astype(f32)
        scaled = grad * gains[4:5, :]
        mean_one = jnp.mean(scaled, -1, keepdims=True)
        mean_two = jnp.mean(scaled * unit, -1, keepdims=True)
        sums[2][...] += fold8(grad * unit)
        back = inverse * (scaled - mean_one - unit * mean_two)
        outs[1][...] = back
        return (0.5 * back).astype(bf)

    def backward(scale, row):
        def run(branch, ins, gains, outs, sums):
            pull, grad_gain = norm_pull(branch, ins[1].astype(f32), gains[row : row + 1, :])
            fresh = ins[0] + pull
            outs[0][...] = fresh
            sums[0][...] += grad_gain
            return (scale * fresh).astype(bf)
        return run

    a1, act1, slope1, _ = stage(
        "ffn1_in", 0, rows, width, dp_count, gains, enter=(w1_in, False, swish_out, (), ((units, bf), (units, bf))),
        junction=first, row_in=(s0,),
    )
    a2, qkv, s1, sq1, _ = stage(
        "ffn1_out", 1, rows, width, dp_count, gains, leave=(act1, w1_out, False),
        enter=(flat_qkv, False, plain_out, (), ((3 * w_qkv.shape[2], bf),)),
        junction=forward(0.5, 1), row_in=(s0,), row_out=(f32,), sums=1,
    )
    turned_table = rel_table.T
    mixed, probs = attn_fwd(qkv, turned_table)
    a3, glu, sig, tail, s2, sq2, _ = stage(
        "attn_out", 2, rows, width, dp_count, gains, leave=(mixed, w_attn_out, False),
        enter=(flat_conv, False, glu_out, (), ((chans, f32), (chans, bf), (chans, bf))),
        junction=forward(1.0, 2), row_in=(s1,), row_out=(f32,), sums=1,
    )
    act3, slope3, depth_unit, depth_stat = conv_mid(glu, w_depth, gains, width, 10)
    a4, act2, slope2, s3, sq3, _ = stage(
        "conv_out", 3, rows, width, dp_count, gains, leave=(act3, w_conv_out, False),
        enter=(w2_in, False, swish_out, (), ((units, bf), (units, bf))),
        junction=forward(1.0, 3), row_in=(s2,), row_out=(f32,), sums=1,
    )
    db4, dh2, output, grad4, sq4, sq5, dgf, _ = stage(
        "ffn2_out", 4, rows, width, dp_count, gains, leave=(act2, w2_out, False),
        enter=(w2_out, True, slope_out, (slope2,), ((units, bf),)),
        junction=turn, row_in=(s3, seed), row_out=(f32, f32), sums=3,
    )
    db3, de3, grad3, dg2, (ga_in, gb_in, gw2_out) = stage(
        "ffn2_back", 5, rows, width, dp_count, gains, leave=(dh2, w2_in, True),
        enter=(w_conv_out, True, plain_out, (), ((chans, f32),)), dws=(
            weight(a4, dh2, "join", False, 1, 0, half),
            weight(a4, dh2, "join", False, 1, half, units // PIECE - half),
            weight(db4, act2, "far", True),
        ),
        junction=backward(1.0, 3), row_in=(grad4, s3), row_out=(f32,), sums=1,
    )
    dpaired, tap_sums, (gw2_out, ga_in) = conv_mid_back(
        de3, slope3, depth_unit, depth_stat, glu, sig, tail, w_depth, gains, width, 11, [gw2_out, ga_in]
    )
    grad2, dgc, dq, dk, dv, dt, (gconv_in, gconv_out, gattn, gb_in, gw2_out, ga_in) = stage(
        "conv_back", 6, rows, width, dp_count, gains, leave=(dpaired, flat_conv, True),
        enter=(w_attn_out, True, plain_out, (), ((w_attn_out.shape[0], bf),)),
        dws=(
            weight(a3, dpaired, "far", False, 2),
            weight(db3, act3, "far", True, 2),
            weight("all", mixed, "post", True),
        ),
        grads=((gb_in, 2), gw2_out, (ga_in, 2)), attend=(qkv, probs, turned_table),
        junction=backward(1.0, 2), row_in=(grad3, s2), row_out=(f32,), sums=1,
    )
    dqkv = (dq, dk, dv)
    waiting = pending([gattn, gconv_in, gconv_out, ga_in, gb_in, gw2_out])
    grad0, ends, other_rows, table_end, taps_end, lead_row = stage(
        "attn_back", 7, rows, width, dp_count, gains, leave=(dqkv, flat_qkv, True),
        enter=(w1_out, True, slope_out, (slope1,), ((units, bf),)),
        dws=(
            weight(a2, dqkv, "far", False),
            weight("all", act1, "front", True),
            weight(a1, "out", "close", False, pieces=units // PIECE),
        ),
        grads=waiting, small=((dgc, dg2, dgf, sq1, sq2, sq3, sq4, sq5), dt, tap_sums),
        tail=(w1_in, backward(1.0, 0), (s0,)),
        junction=backward(0.5, 1), row_in=(grad2, s1), row_out=(f32,), sums=1,
    )
    gqkv, gw1_out, gw1_in = ends[:3]
    for item, end in zip(waiting, ends[3:]):
        item.array = end.array

    def finish(item):
        flip = item.turned and item.array.shape[0] * dp_count == width and (width // dp_count) % 128 != 0
        return item.array.T if flip else item.array

    token_total = rows * lax.axis_size("mp") * dp_count
    ends = [
        ([output], 1),
        ([grad0], 1),
        ([finish(gw1_in)], 0),
        ([finish(gw1_out)], 0),
        ([finish(gqkv)], -3),
        ([finish(gattn)], 0),
        ([finish(gconv_in)], 2),
        ([finish(gconv_out)], 0),
        ([finish(ga_in), finish(gb_in)], 0),
        ([finish(gw2_out)], 0),
    ]
    done_ends = publish(ends, [lead_row, other_rows, table_end, taps_end], {8: False}, rel_table.shape[0], float(token_total * width))
    (output, grad0, gw1_in, gw1_out, gqkv, gattn, gconv_in, gconv_out, gw2_in, gw2_out) = done_ends[:10]
    *gain_sums, table_sum, depth_sum, depth_gain_sum, rms_stats = done_ends[10:]
    gain_sums = [g[0] for g in gain_sums]
    return (
        output,
        grad0,
        gw1_in,
        gw1_out,
        gain_sums[0],
        gqkv.transpose(1, 0, 2),
        gattn,
        table_sum.T,
        gain_sums[1],
        gconv_in,
        depth_sum,
        depth_gain_sum[0],
        gconv_out,
        gain_sums[2],
        gw2_in,
        gw2_out,
        gain_sums[3],
        gain_sums[4],
        rms_stats[0],
    )


def solution(mesh):
    return jax.shard_map(
        body,
        mesh=mesh,
        in_specs=(
            P("mp", "dp", None),
            P(None, "mp"),
            P("mp", None),
            P(),
            P(None, None, "mp"),
            P("mp", None),
            P(),
            P(),
            P(None, None, "mp"),
            P(None, "mp"),
            P("mp"),
            P("mp", None),
            P(),
            P(None, "mp"),
            P("mp", None),
            P(),
            P(),
            P("mp", "dp", None),
        ),
        out_specs=(
            P("mp", "dp", None),
            P("mp", "dp", None),
            P("dp", "mp"),
            P("mp", "dp"),
            P(),
            P("dp", None, "mp"),
            P("mp", "dp"),
            P(),
            P(),
            P("dp", None, "mp"),
            P(None, "mp"),
            P("mp"),
            P("mp", "dp"),
            P(),
            P("dp", "mp"),
            P("mp", "dp"),
            P(),
            P(),
            P(),
        ),
        check_vma=False,
    )
```

```python
import functools

import jax
import jax.numpy as jnp
from jax import lax
from jax.experimental import pallas as pl
from jax.experimental.pallas import tpu as pltpu
from jax.sharding import PartitionSpec as P

HEAD = 64
REL_LEFT = 64
REL_RIGHT = 8
BQ = 128
WIN = 4 * BQ


epsilon = 1e-05


def nt(a, b):
    return lax.dot_general(a, b, (((1,), (1,)), ((), ())), preferred_element_type=jnp.float32)
def nn(a, b):
    return lax.dot_general(a, b, (((1,), (0,)), ((), ())), preferred_element_type=jnp.float32)
def tn(a, b):
    return lax.dot_general(a, b, (((0,), (0,)), ((), ())), preferred_element_type=jnp.float32)

MESH = pl.DeviceIdType.MESH
CHUNKS = 4
TABLE_ROWS = 40
LAG = 2
JOIN_SLOT = 3
PIECE = 256
VMEM_LIMIT = 58 << 20


def silu_pair(h):
    sig = jax.nn.sigmoid(h)
    act = h * sig
    return act, sig + act * (1.0 - sig)


def unit_norm(s):
    centred = s - jnp.mean(s, -1, keepdims=True)
    inverse = lax.rsqrt(jnp.mean(centred * centred, -1, keepdims=True) + epsilon)
    return centred * inverse, inverse


def fold8(x):
    return jnp.sum(x.reshape(x.shape[0] // 8, 8, x.shape[1]), 0)


def norm_pull(grad, s, gain):
    unit, inverse = unit_norm(s)
    scaled = grad * gain
    first = jnp.mean(scaled, -1, keepdims=True)
    second = jnp.mean(scaled * unit, -1, keepdims=True)
    return inverse * (scaled - first - unit * second), fold8(grad * unit)


def in_hbm():
    return pl.BlockSpec(memory_space=pltpu.HBM)


class Grad:
    def __init__(self, array, bit, turned):
        self.array, self.bit, self.turned = array, bit, turned


def halved(shape, turned):
    pieces, pairs, _, block, cols = shape
    if pairs > 1:
        return jax.ShapeDtypeStruct((pieces, pairs // 2, 2, block, cols), jnp.bfloat16)
    if turned and block % 128 == 0:
        return jax.ShapeDtypeStruct((pieces * cols, block), jnp.float32)
    return jax.ShapeDtypeStruct((block, pieces * cols), jnp.float32)


def arriving(shape):
    return pltpu.VMEM((shape[0], shape[1]) + tuple(shape[3:]), jnp.bfloat16)


def place(dp, bit):
    own = (dp // 2**bit) % 2
    return own, dp + 2**bit * (1 - 2 * own)


def halving_copy(src, landing, piece, bit, send, recv, slot):
    dp, mp = lax.axis_index("dp"), lax.axis_index("mp")
    own, partner = place(dp, bit)
    return pltpu.make_async_remote_copy(
        src.at[piece, :, 1 - own], landing.at[piece], send.at[slot], recv.at[slot],
        device_id=(partner, mp), device_id_type=MESH,
    )


def halving_keep(src, kept, bit, sem):
    own, _ = place(lax.axis_index("dp"), bit)
    return pltpu.make_async_copy(src.at[:, :, own], kept, sem)


def region(ref, piece, cols, turned):
    if len(ref.shape) > 2:
        return ref.at[piece]
    at = pl.ds(piece * cols, cols)
    return ref.at[at, :] if turned else ref.at[:, at]


def halving_add(held, landing, out, piece, turned):
    pairs, block, cols = landing.shape[1:]
    f32 = jnp.float32
    if pairs == 1:
        total = held(piece, 0).astype(f32) + landing[piece, 0].astype(f32)
        turned = turned and block % 128 == 0
        region(out, piece, cols, turned)[...] = total.T if turned else total
        return

    def add(j, c):
        total = held(piece, j).astype(f32) + landing[piece, j].astype(f32)
        out[piece, j // 2, j % 2] = total.astype(jnp.bfloat16)
        return c

    lax.fori_loop(0, pairs, add, 0)


def weight(lhs, rhs, where, turned, deep=1, lo=0, pieces=None):
    if pieces is None:
        pieces = (sum(r.shape[1] for r in rhs) if isinstance(rhs, tuple) else rhs.shape[1]) // PIECE
    return lhs, rhs, where, turned, deep, lo, pieces


def flat_shape(array):
    if isinstance(array, tuple):
        return array[0].shape[0], sum(a.shape[1] for a in array)
    if len(array.shape) == 3:
        return array.shape[1], array.shape[0] * array.shape[2]
    return array.shape


def gain_row(ref, i, width):
    first = i * width // 128
    return jnp.concatenate([ref[first + j : first + j + 1, :] for j in range(width // 128)], 1)


class Riders:
    def __init__(self, grads):
        self.plan = [(g.array.shape[0], g.bit, g.turned) for g in grads]
        self.arrays = [g.array for g in grads]
        self.after = [halved(g.array.shape, g.turned) for g in grads]
        self.slots = sum(x[0] for x in self.plan)
        self.scratch = [arriving(g.array.shape) for g in grads] * 2 + [pltpu.VMEM(a.shape, a.dtype) for a in self.after]
        if grads:
            self.scratch += [pltpu.SemaphoreType.DMA((self.slots,))] * 3 + [pltpu.SemaphoreType.DMA((len(grads),))]

    def bind(self, srcs, outs, scratch):
        n = len(self.plan)
        sems = scratch[3 * n :]
        holds, hops, slot = [], [], 0
        for i, (pieces, bit, turned) in enumerate(self.plan):
            landing, keep, half = scratch[i], scratch[n + i], scratch[2 * n + i]
            holds.append(halving_keep(srcs[i], keep, bit, sems[3].at[i]))
            flip = turned and landing.shape[2] % 128 == 0
            for p in range(pieces):
                move = halving_copy(srcs[i], landing, p, bit, sems[0], sems[1], slot)
                store = pltpu.make_async_copy(region(half, p, PIECE, flip), region(outs[i], p, PIECE, flip), sems[2].at[slot])
                hops.append((move, store, lambda q, j, keep=keep: keep[q, j], landing, half, p, turned))
                slot += 1
        self.holds, self.hops = holds, hops

    def targets(self):
        dp, mp = lax.axis_index("dp"), lax.axis_index("mp")
        return [(place(dp, b)[1], mp) for b in sorted({x[1] for x in self.plan})]

    def start(self):
        for hold in self.holds:
            hold.start()
        for hop in self.hops:
            hop[0].start()

    def finish(self):
        for hold in self.holds:
            hold.wait()
        for hop in self.hops:
            hop[0].wait_recv()
            halving_add(*hop[2:])
            hop[1].start()
        for hop in self.hops:
            hop[0].wait_send()
            hop[1].wait()

    def results(self, outs):
        return [Grad(a, b + 1, t) for a, (_, b, t) in zip(outs, self.plan)]


def greet(targets):
    barrier = pltpu.get_barrier_semaphore()
    for to in targets:
        pl.semaphore_signal(barrier, inc=1, device_id=to, device_id_type=MESH)
    return lambda: pl.semaphore_wait(barrier, len(targets))


def split_pair(x):
    left = lax.broadcasted_iota(jnp.int32, x.shape, 1) < HEAD
    zero = jnp.zeros_like(x)
    return jnp.concatenate([jnp.where(left, x, zero), jnp.where(left, zero, x)], 0)

def join_pair(x):
    rows = x.shape[0] // 2
    left = lax.broadcasted_iota(jnp.int32, (rows, x.shape[1]), 1) < HEAD
    return jnp.where(left, x[:rows], x[rows:])

def spot_table(spots):
    spot = lax.broadcasted_iota(jnp.int32, (spots, BQ), 0)
    inner = jnp.clip(spot - REL_LEFT, 0, REL_LEFT + REL_RIGHT)
    row = jnp.where(spot < 3 * BQ, inner, jnp.where(spot < 4 * BQ, 0, REL_LEFT + REL_RIGHT))
    return (lax.broadcasted_iota(jnp.int32, (spots, BQ), 1) == row).astype(jnp.bfloat16)


def wide_table(rel_ref, wide_ref):
    wide_ref[...] = jnp.zeros_like(wide_ref)
    turned = rel_ref[...].astype(jnp.float32)
    cols = turned.shape[1]
    wide_ref[0:HEAD, :cols] = turned
    wide_ref[HEAD : 2 * HEAD, :cols] = turned
    return wide_ref[...].T.astype(jnp.bfloat16)


def fwd_kernel(q_ref, k_ref, v_ref, relt_ref, mixed_ref, probs_ref, bias_ref, rel_ref, wide_ref):
    ib = pl.program_id(0)

    @pl.when(ib == 0)
    def _():
        rel_ref[...] = nn(spot_table(5 * BQ), wide_table(relt_ref, wide_ref)).astype(jnp.bfloat16)

    pairs = q_ref.shape[1] // 128
    nkeys = k_ref.shape[0] // BQ
    places = [pl.multiple_of(jnp.clip(jb - ib + 2, 0, 4) * BQ, BQ) for jb in range(nkeys)]
    for pr in range(pairs):
        cols = slice(pr * 128, (pr + 1) * 128)
        qs = split_pair(q_ref[:, cols] * 0.125)
        s = nt(qs, k_ref[:, cols])
        b = nt(qs, rel_ref[...])
        rows = b.shape[0] // 2
        bias_ref[pr, :, 0:BQ] = b[:, 3 * BQ : 4 * BQ]
        for h in range(2):
            r = pltpu.roll(b[h * rows : (h + 1) * rows, :WIN], 0, 1, stride=1, stride_axis=0)
            bias_ref[pr, h * rows : (h + 1) * rows, BQ : 4 * BQ] = r[:, : 3 * BQ]
        bias_ref[pr, :, 4 * BQ :] = b[:, 4 * BQ :]
        parts = [s[:, jb * BQ : (jb + 1) * BQ] + bias_ref[pr, :, pl.ds(places[jb], BQ)] for jb in range(nkeys)]
        top = functools.reduce(jnp.maximum, parts)
        m = jnp.max(top, -1, keepdims=True)
        es = [jnp.exp(p - m) for p in parts]
        tot = jnp.sum(functools.reduce(jnp.add, es), -1, keepdims=True)
        inv = 1.0 / tot
        for jb in range(nkeys):
            probs_ref[pr, :, jb * BQ : (jb + 1) * BQ] = (es[jb] * inv).astype(jnp.bfloat16)
        mixed_ref[:, cols] = join_pair(nn(probs_ref[pr], v_ref[:, cols])).astype(jnp.bfloat16)


def attend_back_block(ib, qkv_ref, probs_ref, do_ref, dq_ref, tot_ref, dkt, dvt, dta, dz_ref, hot_ref, relb_ref):
    frames, heads = qkv_ref.shape[0], qkv_ref.shape[1] // 3
    at = pl.ds(pl.multiple_of(ib * BQ, BQ), BQ)
    pairs = heads // 128
    nkeys = frames // BQ
    rows = BQ
    r2 = lax.broadcasted_iota(jnp.int32, (2 * rows, 2 * rows), 0)
    c2 = lax.broadcasted_iota(jnp.int32, (2 * rows, 2 * rows), 1)
    mirror = (r2 + c2 == jnp.where(r2 < rows, rows - 1, 3 * rows - 1)).astype(jnp.bfloat16)
    places = [pl.multiple_of(jnp.clip(jb - ib + 2, 0, 4) * BQ, BQ) for jb in range(nkeys)]
    for pr in range(pairs):
        cols = slice(pr * 128, (pr + 1) * 128)
        keys = qkv_ref[:, heads + pr * 128 : heads + (pr + 1) * 128]
        values = qkv_ref[:, 2 * heads + pr * 128 : 2 * heads + (pr + 1) * 128]
        qs = split_pair(qkv_ref[at, cols] * 0.125)
        dos = split_pair(do_ref[at, cols])
        p = probs_ref[pr]
        dprob = nt(dos, values)
        dvt[pr] += tn(dos, p)
        pf = p.astype(jnp.float32)
        acc = functools.reduce(
            jnp.add, [pf[:, jb * BQ : (jb + 1) * BQ] * dprob[:, jb * BQ : (jb + 1) * BQ] for jb in range(nkeys)]
        )
        inner = jnp.sum(acc, -1, keepdims=True)
        tot_ref[pr] = jnp.zeros(tot_ref.shape[1:], jnp.float32)
        for jb in range(nkeys):
            sl = slice(jb * BQ, (jb + 1) * BQ)
            dz = (pf[:, sl] * (dprob[:, sl] - inner)).astype(jnp.bfloat16)
            dz_ref[pr, :, sl] = dz
            tot_ref[pr, :, pl.ds(places[jb], BQ)] += dz.astype(jnp.float32)
        w = jnp.concatenate([tot_ref[pr, :, BQ : 4 * BQ].astype(jnp.bfloat16), jnp.zeros((2 * rows, BQ), jnp.bfloat16)], 1)
        w = nn(mirror, w)
        outs = [pltpu.roll(w[h * rows : (h + 1) * rows], WIN - rows + 1, 1, stride=1, stride_axis=0) for h in range(2)]
        d = nn(mirror, jnp.concatenate(outs, 0).astype(jnp.bfloat16)).astype(jnp.bfloat16)
        drel = nn(d, hot_ref[...])
        col = lax.broadcasted_iota(jnp.int32, drel.shape, 1)
        low = jnp.sum(tot_ref[pr, :, :BQ], -1, keepdims=True)
        high = jnp.sum(tot_ref[pr, :, 4 * BQ :], -1, keepdims=True)
        drel = drel + jnp.where(col == 0, low, 0.0) + jnp.where(col == REL_LEFT + REL_RIGHT, high, 0.0)
        drel = drel.astype(jnp.bfloat16)
        dz = dz_ref[pr]
        dq = nn(dz, keys) + nn(drel, relb_ref[...])
        dq_ref[at, cols] = (join_pair(dq) * 0.125).astype(jnp.bfloat16)
        dkt[pr] += tn(qs, dz)
        dta[...] += tn(drel, qs)


class Doubling:
    def __init__(self, course, refs, lands, sems, partner):
        self.course, self.items, self.sems, self.partner = course, list(zip(refs, lands)), sems, partner
        self.done = 0

    def copies(self, n):
        at = self.course[n]
        return [
            (
                pltpu.make_async_remote_copy(
                    r, l.at[n], self.sems[0].at[i, n], self.sems[1].at[i, n], device_id=self.partner(at), device_id_type=MESH
                ),
                r,
                l.at[n],
            )
            for i, (r, l) in enumerate(self.items)
            if i < 2 or not isinstance(at, str)
        ]

    def start(self, n=0):
        for cp, _, _ in self.copies(n):
            cp.start()

    def advance(self, n):
        for cp, r, l in self.copies(n):
            cp.wait()
            r[...] += l[...]
        if n + 1 < len(self.course):
            self.start(n + 1)

    def step(self):
        if self.done < len(self.course):
            self.advance(self.done)
            self.done += 1


def stage(name, cid, rows, width, count, gains, *, leave=None, enter=None, dws=(), grads=(), small=None, tail=None, attend=None, junction, row_in=(), row_out=(), sums=0):
    chunk = rows // CHUNKS
    frames = rows * 4
    bits_all = count.bit_length() - 1
    f32, bf = jnp.float32, jnp.bfloat16
    ins, vm_ins, out_shape, scratch = [], [], [], []
    known = {}

    def add_in(array, direct=False):
        if isinstance(array, str):
            return array
        if direct:
            ins.append(array)
            return len(ins) - 1
        if id(array) not in known:
            group = array if isinstance(array, tuple) else (array,)
            known[id(array)] = len(vm_ins)
            vm_ins.append((len(ins), len(group), pltpu.VMEM(flat_shape(array), group[0].dtype)))
            ins.extend(group)
        return known[id(array)]

    out_slots = [0]

    def add_scratch(item):
        scratch.append(item)
        return len(scratch) - 1

    def add_out(shape, dtype, slots, kept=True):
        if not kept:
            return -1 - add_scratch(pltpu.VMEM(shape, dtype)), None
        out_shape.append(jax.ShapeDtypeStruct(shape, dtype))
        first = out_slots[0]
        out_slots[0] += slots
        return len(out_shape) - 1, first

    add_dw = lambda where: [(add_in(d[0]), add_in(d[1])) if d[2] in where else None for d in dws]
    groups = []
    if leave:
        x_i, wl_i = add_in(leave[0]), add_in(leave[1])
        leave_s = [add_scratch(pltpu.VMEM((rows, width), f32)) for _ in range(2)]
        leave_s += [add_scratch(pltpu.VMEM((rows, width), bf)) for _ in range(6)]
        wl_s = add_scratch(pltpu.VMEM(flat_shape(leave[1])[::-1], bf)) if leave[2] else None
        groups.append(len(vm_ins))
        add_dw(("far",))
    gains_i = add_in(gains)
    gain_s = add_scratch(pltpu.VMEM((8, width), f32))
    row_i = [add_in(r) for r in row_in]
    if not leave:
        groups.append(len(vm_ins))
    add_dw(("near", "join"))
    kept = not (tail or attend)
    kept_rows = not tail
    if enter:
        we_i = add_in(enter[0])
        extra_i = [add_in(e) for e in enter[3]]
        we_s = add_scratch(pltpu.VMEM(flat_shape(enter[0])[::-1], bf)) if enter[1] else None
        all_o = add_out((frames, width), bf, 4 * CHUNKS, kept)
        e_o = [add_out((frames, c), d, 4 * CHUNKS, kept) for c, d in enter[4]]
    r_o = [add_out((rows, width), d, CHUNKS, kept_rows) for d in row_out]
    s_o = [add_out((8, width), f32, 1, kept_rows) for _ in range(sums)]
    if attend:
        qkv_i, probs_i, table_i = add_in(attend[0]), add_in(attend[1], True), add_in(attend[2])
        add_dw(("post",))
        heads = attend[0].shape[1] // 3
        pairs = heads // 128
        d_o = [add_out((frames, heads), bf, 4 * CHUNKS) for _ in range(3)] + [add_out((128, 128), f32, 1)]
        attend_s = [
            add_scratch(item)
            for item in (
                pltpu.VMEM((pairs, 2 * BQ, 5 * BQ), f32), pltpu.VMEM((pairs, 128, frames), f32), pltpu.VMEM((pairs, 128, frames), f32),
                pltpu.VMEM((128, 128), f32), pltpu.VMEM((pairs, 2 * BQ, frames), bf), pltpu.VMEM((WIN, BQ), bf), pltpu.VMEM((128, 128), bf),
            )
        ]
        wide_s = add_scratch(pltpu.VMEM((128, 128), f32))
        probs_s = add_scratch(pltpu.VMEM((2, pairs, 2 * BQ, frames), bf))
        probs_sem = add_scratch(pltpu.SemaphoreType.DMA((2,)))
    if small:
        vectors_in, table_in, taps_in = small
        vector_i = [add_in(v) for v in vectors_in]
        table_i, taps_i = add_in(table_in), add_in(taps_in)
    groups.append(len(vm_ins))
    if tail:
        add_dw(("front",))
        tw_i = add_in(tail[0])
        tw_s = add_scratch(pltpu.VMEM(flat_shape(tail[0])[::-1], bf))
        tail_i = [add_in(r) for r in tail[2]]
        add_dw(("close",))
        tail_o = [add_out((rows, width), f32, CHUNKS)]
        tail_sum = add_out((8, width), f32, 1, False)
    groups.append(len(vm_ins))
    fixed_out = len(out_shape)
    plan, dw_o = [], []
    for d in dws:
        shape = (d[6], count // 2, 2, width // count, PIECE)
        if d[2] == "join":
            dw_o.append(add_out(shape, bf, shape[0]))
        else:
            plan.append((shape, 0, d[3], bits_all if tail else min(d[4], bits_all), add_scratch(pltpu.VMEM(shape, bf)), None, None))
            dw_o.append(len(plan) - 1)
    dw_in = [(add_in(d[0]), add_in(d[1])) for d in dws]
    first_grad = len(plan)
    for g in grads:
        g, ahead = g if isinstance(g, tuple) else (g, 1)
        shape = g.array.shape
        plan.append((shape, g.bit, g.turned, bits_all if tail else min(g.bit + ahead, bits_all), None, add_in(g.array, True), add_scratch(arriving(shape))))
    chains = []
    slots = 0
    for shape, bit, turned, end, src_s, src_i, keep_s in plan:
        links = []
        pieces = shape[0]
        for b in range(bit, end):
            nxt = halved(shape, turned)
            land_s = add_scratch(arriving(shape))
            if b == end - 1:
                links.append((b, slots, land_s, None, add_out(nxt.shape, nxt.dtype, pieces)))
            else:
                links.append((b, slots, land_s, add_scratch(pltpu.VMEM(nxt.shape, nxt.dtype)), None))
            slots += pieces
            shape = nxt.shape
        chains.append((pieces, turned, src_s, src_i, keep_s, links))
    if small:
        small_shapes = [(8, width), (TABLE_ROWS, 128), taps_in.shape]
        small_o = [add_out(s, f32, 1) for s in small_shapes]
        lead_o = add_out((1, width), f32, 1)
        downward = list(range(bits_all - 1, -1, -1))
        courses = [downward[-1:] + downward[:-1] + ["sib", "far"], ["sib", "far"] + downward]
        small_l = [add_scratch(pltpu.VMEM((bits_all + 2,) + s, f32)) for s in small_shapes]
        lead_l = [add_scratch(pltpu.VMEM((bits_all + 2, 1, width), f32))]
        small_sems = [add_scratch(pltpu.SemaphoreType.DMA((3, bits_all + 2))) for _ in range(4)]
    if slots:
        grad_sems = [add_scratch(pltpu.SemaphoreType.DMA((slots,))) for _ in range(2)]
    ring_sems = [add_scratch(pltpu.SemaphoreType.DMA((6, CHUNKS))) for _ in range(2)]
    load_sem = add_scratch(pltpu.SemaphoreType.DMA((len(ins),)))
    store_sem = add_scratch(pltpu.SemaphoreType.DMA((out_slots[0],)))
    n_in, n_out = len(ins), len(out_shape)
    vm_at = [add_scratch(item[2]) for item in vm_ins]
    vo_at = [add_scratch(pltpu.VMEM(o.shape, o.dtype)) for o in out_shape]

    def kernel(*refs):
        hbm_in, hbm_out, t = refs[:n_in], refs[n_in : n_in + n_out], refs[n_in + n_out :]
        vout = lambda o: t[-1 - o[0]] if o[0] < 0 else t[vo_at[o[0]]]

        def vin(i):
            if i == "all":
                return vout(all_o)
            if i == "out":
                return vout(e_o[0])
            return t[vm_at[i]]

        waited = set()

        def load(i):
            first, parts, _ = vm_ins[i]
            if len(hbm_in[first].shape) == 3:
                slabs, _, cols = hbm_in[first].shape
                return [
                    pltpu.make_async_copy(hbm_in[first].at[n], vin(i).at[:, pl.ds(n * cols, cols)], t[load_sem].at[first])
                    for n in range(slabs)
                ]
            if parts == 1:
                return [pltpu.make_async_copy(hbm_in[first], vin(i), t[load_sem].at[first])]
            copies, at = [], 0
            for n in range(first, first + parts):
                cols = hbm_in[n].shape[1]
                copies.append(pltpu.make_async_copy(hbm_in[n], vin(i).at[:, pl.ds(at, cols)], t[load_sem].at[n]))
                at += cols
            return copies

        begun = [0]

        def begin_loads(group):
            for i in range(begun[0], groups[group]):
                for cp in load(i):
                    cp.start()
            begun[0] = max(begun[0], groups[group])

        def need(*items):
            for i in items:
                if not isinstance(i, str) and i not in waited:
                    waited.add(i)
                    for cp in load(i):
                        cp.wait()

        dp, me = lax.axis_index("dp"), lax.axis_index("mp")
        core, chip = me % 2, me // 2
        sib = chip * 2 + 1 - core
        far = (1 - chip) * 2 + core
        diag = (1 - chip) * 2 + 1 - core
        bits = sorted({link[0] for ch in chains for link in ch[5]} | set(range(bits_all) if small else ()))
        meet = greet([(dp, sib), (dp, far)] + [(place(dp, b)[1], me) for b in bits])
        begin_loads(0)

        def part(ref, block, k):
            return ref.at[pl.ds(pl.multiple_of(block * rows + k * chunk, chunk), chunk)]

        def store_rows(o, block, k):
            return pltpu.make_async_copy(
                part(vout(o), block, k), part(hbm_out[o[0]], block, k), t[store_sem].at[o[1] + block * CHUNKS + k]
            )

        def store_whole(o):
            return pltpu.make_async_copy(vout(o), hbm_out[o[0]], t[store_sem].at[o[1]])

        def store_piece(o, piece, cols, turned):
            return pltpu.make_async_copy(
                region(vout(o), piece, cols, turned), region(hbm_out[o[0]], piece, cols, turned), t[store_sem].at[o[1] + piece]
            )

        def copy(kind, k, src, dst, to):
            return pltpu.make_async_remote_copy(
                src, dst, t[ring_sems[0]].at[kind, k], t[ring_sems[1]].at[kind, k], device_id=(dp, to), device_id_type=MESH
            )

        if leave:
            px, own, sb, sr, xs, xr, ob, orv = [t[s] for s in leave_s]
        if enter:
            all_ref = vout(all_o)
            we_ref = t[we_s] if enter[1] else vin(we_i)
        pair_send = lambda k: copy(0, k, part(sb, 0, k), part(sr, 0, k), sib)
        far_send = lambda k: copy(1, k, part(xs, 0, k), part(xr, 0, k), far)
        own_send = lambda k: copy(2, k, part(ob, 0, k), part(orv, 0, k), sib)
        all_far = lambda k: copy(3, k, part(all_ref, me, k), part(all_ref, me, k), far)
        all_sib = lambda k: copy(4, k, part(all_ref, me, k), part(all_ref, me, k), sib)
        all_fwd = lambda k: copy(5, k, part(all_ref, far, k), part(all_ref, far, k), sib)
        got_far = lambda k: copy(3, k, part(all_ref, far, k), part(all_ref, far, k), far)
        got_sib = lambda k: copy(4, k, part(all_ref, sib, k), part(all_ref, sib, k), sib)
        got_diag = lambda k: copy(5, k, part(all_ref, diag, k), part(all_ref, diag, k), sib)

        def source(c, step):
            pieces, turned, src_s, src_i, keep_s, links = chains[c]
            if step:
                return t[links[step - 1][3]]
            return t[src_s] if src_s is not None else hbm_in[src_i]

        def hop(c, step, piece):
            b, slot, land_s, _, _ = chains[c][5][step]
            return halving_copy(source(c, step), t[land_s], piece, b, t[grad_sems[0]], t[grad_sems[1]], slot + piece)

        def keep(c):
            return halving_keep(hbm_in[chains[c][3]], t[chains[c][4]], chains[c][5][0][0], t[load_sem].at[chains[c][3]])

        held_back = set()

        def settle(c, step, piece):
            pieces, turned, src_s, src_i, keep_s, links = chains[c]
            b, slot, land_s, out_s, out_o = links[step]
            hop(c, step, piece).wait_recv()
            if step == 0 and src_s is None:
                if c not in held_back:
                    held_back.add(c)
                    keep(c).wait()
                held = lambda p, j: t[keep_s][p, j]
            else:
                own_bit, _ = place(dp, b)
                src = source(c, step)
                held = lambda p, j: src[p, j, own_bit]
            landing = t[land_s]
            out = t[out_s] if out_o is None else vout(out_o)
            halving_add(held, landing, out, piece, turned)
            if out_o is not None:
                store_piece(out_o, piece, PIECE, turned and landing.shape[2] % 128 == 0).start()

        def fill(k, where):
            for d, (a, b), o in zip(dws, dw_in, dw_o):
                if d[2] != where:
                    continue
                chain = None if where == "join" else o
                dw = vout(o) if chain is None else t[chains[o][2]]

                @pl.when(k < dw.shape[0])
                def _(a=a, b=b, dw=dw, chain=chain, o=o, lo=d[5]):
                    g = tn(vin(a)[...], vin(b)[:, pl.ds(pl.multiple_of((lo + k) * PIECE, PIECE), PIECE)])
                    dw[k] = g.astype(bf).reshape(dw.shape[1:])
                    if chain is None:
                        store_piece(o, k, PIECE, False).start()
                    else:
                        hop(chain, 0, k).start()

        def need_for(where):
            for d, (a, b) in zip(dws, dw_in):
                if d[2] == where:
                    need(a, b)

        def leave_phase(x_ref, wl_ref, far_fill, near_fill):
            def two(k, block_a, block_b):
                lhs = jnp.concatenate([part(x_ref, block_a, k)[...], part(x_ref, block_b, k)[...]], 0)
                return nn(lhs, wl_ref[...])

            def push(k):
                pair_send(k).wait_recv()
                part(xs, 0, k)[...] = (part(px, 0, k)[...] + part(sr, 0, k)[...].astype(f32)).astype(bf)
                far_send(k).start()

            def out_far(k, c):
                p = two(k, far, diag)
                part(px, 0, k)[...] = p[:chunk]
                part(sb, 0, k)[...] = p[chunk:].astype(bf)
                pair_send(k).start()

                @pl.when(k > 0)
                def _():
                    push(k - 1)

                fill(k, far_fill)
                return c

            lax.fori_loop(0, CHUNKS, out_far, 0)
            need_for(near_fill)

            def out_near(k, c):
                p = two(k, me, sib)
                part(own, 0, k)[...] = p[:chunk]
                part(ob, 0, k)[...] = p[chunk:].astype(bf)
                own_send(k).start()

                @pl.when(k == 0)
                def _():
                    push(CHUNKS - 1)

                fill(k, near_fill)
                return c

            lax.fori_loop(0, CHUNKS, out_near, 0)

        def leave_drain():
            def drain(k, c):
                pair_send(k).wait_send()
                far_send(k).wait_send()
                own_send(k).wait_send()
                return c

            lax.fori_loop(0, CHUNKS, drain, 0)

        def join_phase(rule, has_leave, in_refs, outs, totals, gathers):
            def join(k, c):
                fill(k, "join")
                branch = None
                if has_leave:
                    own_send(k).wait_recv()
                    far_send(k).wait_recv()
                    branch = part(own, 0, k)[...] + part(orv, 0, k)[...].astype(f32) + part(xr, 0, k)[...].astype(f32)
                fresh = rule(
                    branch, [part(r, 0, k)[...] for r in in_refs], t[gain_s], [part(vout(o), 0, k) for o in outs], [vout(o) for o in totals]
                )
                if gathers:
                    part(all_ref, me, k)[...] = fresh
                    all_far(k).start()
                    all_sib(k).start()
                for o in outs:
                    if o[0] >= 0:
                        store_rows(o, 0, k).start()
                return c

            lax.fori_loop(0, CHUNKS, join, 0)
            for o in totals:
                if o[0] >= 0:
                    store_whole(o).start()

        for o in s_o + ([tail_sum] if tail else []):
            vout(o)[...] = jnp.zeros((8, width), f32)
        meet()
        if leave:
            need(x_i, wl_i)
        begin_loads(1)
        for c in range(first_grad, len(chains)):
            for p in range(chains[c][0]):
                hop(c, 0, p).start()
        if leave:
            if leave[2]:
                t[wl_s][...] = vin(wl_i)[...].T
            need_for("far")
            leave_phase(vin(x_i), t[wl_s] if leave[2] else vin(wl_i), "far", "near")
        for c in range(first_grad, len(chains)):
            keep(c).start()
        need(gains_i, *row_i)
        for i in range(5):
            t[gain_s][i : i + 1, :] = gain_row(vin(gains_i), i, width)
        need_for("join")
        if enter and enter[1]:
            need(we_i)
            we_ref[...] = vin(we_i)[...].T
        join_phase(junction, bool(leave), [vin(r) for r in row_i], r_o, s_o, bool(enter))

        lead = [c for c in range(first_grad) if tail and dws[[i for i, o in enumerate(dw_o) if o == c][0]][2] == "far"]
        if small:
            partner = lambda at: (dp, sib) if at == "sib" else (dp, far) if at == "far" else (place(dp, at)[1], me)
            need(*vector_i, table_i, taps_i)
            rows_ref = vout(small_o[0])
            rows_ref[...] = jnp.zeros((8, width), f32)
            vectors = [vout(s_o[0])] + [vin(i) for i in vector_i]
            for i, v in enumerate(vectors[:4]):
                rows_ref[i : i + 1, :] = jnp.sum(v[...], 0, keepdims=True)
            for i, v in enumerate(vectors[4:]):
                line = jnp.sum(v[...], 0, keepdims=True)
                rows_ref[4:5, i * 128 : (i + 1) * 128] = functools.reduce(
                    jnp.add, [line[:, j * 128 : (j + 1) * 128] for j in range(width // 128)]
                )
            both = vin(table_i)[...]
            both = both + pltpu.roll(both, 64, 1)
            left = lax.broadcasted_iota(jnp.int32, (TABLE_ROWS, 128), 1) < HEAD
            vout(small_o[1])[...] = jnp.where(left, both[:TABLE_ROWS], both[TABLE_ROWS : 2 * TABLE_ROWS])
            vout(small_o[2])[...] = vin(taps_i)[...]
            wide = Doubling(courses[0], [vout(o) for o in small_o], [t[l] for l in small_l], [t[s] for s in small_sems[:2]], partner)
            wide.start()

        mid = set()

        def hasten(which):
            for c in which:
                if len(chains[c][5]) > 1:
                    mid.add(c)
                    for p in range(chains[c][0]):
                        settle(c, 0, p)
                        hop(c, 1, p).start()

        if enter:
            begin_loads(len(groups) - 1)
            need(we_i, *extra_i)

            def work(k, block_a, block_b):
                lhs = jnp.concatenate([part(all_ref, block_a, k)[...], part(all_ref, block_b, k)[...]], 0)
                h = nn(lhs, we_ref[...])
                for i, block in enumerate((block_a, block_b)):
                    view = lambda ref: part(ref, block, k)
                    enter[2](h[i * chunk : (i + 1) * chunk], [view(vin(r))[...] for r in extra_i], [view(vout(o)) for o in e_o])
                    for o in [all_o] + e_o:
                        if o[0] >= 0:
                            store_rows(o, block, k).start()

        if attend:
            tot_ref, dkt, dvt, dta, dz_ref, hot_ref, relb_ref = [t[s] for s in attend_s]
            dq, dk, dv = [vout(o) for o in d_o[:3]]
            need(qkv_i, table_i)
            need_for("post")
            for ref in (dkt, dvt, dta):
                ref[...] = jnp.zeros(ref.shape, f32)
            hot_ref[...] = spot_table(WIN)
            relb_ref[...] = wide_table(vin(table_i), t[wide_s])

            def block_of(j):
                chip_j = chip + (j // 4) * (1 - 2 * chip)
                core_j = core + (j % 2) * (1 - 2 * core)
                return (chip_j * 2 + core_j) * 2 + (j // 2) % 2

            def fetch(j):
                at = pl.ds(pl.multiple_of(block_of(j) * 2 * BQ, 2 * BQ), 2 * BQ)
                return pltpu.make_async_copy(hbm_in[probs_i].at[:, at, :], t[probs_s].at[j % 2], t[probs_sem].at[j % 2])

            fetch(0).start()

            def pass_on(*ks):
                for k in ks:
                    got_far(k).wait_recv()
                    all_fwd(k).start()

            def before(n):
                if 0 < n < 5:
                    pass_on(n - 1)
                if n == 3:
                    hasten(range(first_grad, len(chains)))
                elif n == 5:
                    hasten(range(first_grad))
                elif n == 6:
                    for k in range(CHUNKS):
                        if any(d[2] == "post" and k < d[6] for d in dws):
                            fill(k, "post")

            def rows_for(j):
                away = j // 4

                def chunk_rows(k, c):
                    @pl.when(away == 0)
                    def _():
                        got_sib(k).wait_recv()

                    @pl.when(away == 1)
                    def _():
                        got_diag(k).wait_recv()

                    there = chip + away * (1 - 2 * chip)
                    work(k, there * 2 + core, there * 2 + 1 - core)
                    return c

                first = (j // 2) % 2 * 2
                lax.fori_loop(first, first + 2, chunk_rows, 0)

            def query_block(j, c):
                for n in (1, 2, 3, 4):

                    @pl.when(j == n)
                    def _(n=n):
                        before(n)

                @pl.when(j % 2 == 0)
                def _():
                    rows_for(j)

                for n in (5, 6):

                    @pl.when(j == n)
                    def _(n=n):
                        before(n)

                @pl.when(j < 7)
                def _():
                    fetch(j + 1).start()

                fetch(j).wait()
                attend_back_block(
                    block_of(j), vin(qkv_i), t[probs_s].at[j % 2], vout(e_o[0]), dq, tot_ref, dkt, dvt, dta, dz_ref, hot_ref, relb_ref
                )
                return c

            lax.fori_loop(0, 8, query_block, 0)
            for pr in range(pairs):
                dk[:, pr * 128 : (pr + 1) * 128] = dkt[pr].T.astype(bf)
                dv[:, pr * 128 : (pr + 1) * 128] = dvt[pr].T.astype(bf)
            vout(d_o[3])[...] = dta[...]
            for o in d_o:
                store_whole(o).start()
        elif enter:

            def gather(k, c):
                got_sib(k).wait_recv()
                work(k, me, sib)
                got_far(k).wait_recv()
                all_fwd(k).start()
                got_diag(k).wait_recv()
                work(k, far, diag)
                if small:

                    for n, at in enumerate((1, CHUNKS - 1)):

                        @pl.when(k == at)
                        def _(n=n):
                            wide.advance(n)

                if lead:

                    @pl.when(k == CHUNKS - 2)
                    def _():
                        for ch in lead:
                            for p in range(chains[ch][0]):
                                settle(ch, 0, p)
                                hop(ch, 1, p).start()

                return c

            lax.fori_loop(0, CHUNKS, gather, 0)
            if small:
                wide.done = 2

        early = 0
        if tail:
            need_for("front")

            def front(k, c):
                fill(k, "front")
                return c

            lax.fori_loop(0, CHUNKS, front, 0)
            early = 1
            if lead and bits_all > 2:
                early = 2
                for ch in lead:
                    for p in range(chains[ch][0]):
                        settle(ch, 1, p)
                        hop(ch, 2, p).start()
            leave_drain()
            need(tw_i, *tail_i)
            t[tw_s][...] = vin(tw_i)[...].T
            leave_phase(vin("out"), t[tw_s], None, "close")
            wide.step()

        def close_rows():
            join_phase(tail[1], True, [vout(r_o[0])] + [vin(r) for r in tail_i], tail_o, [tail_sum], False)
            vout(lead_o)[...] = jnp.sum(vout(tail_sum)[...], 0, keepdims=True)
            final = Doubling(courses[1], [vout(lead_o)], [t[l] for l in lead_l], [t[s] for s in small_sems[2:]], partner)
            final.start()
            return final

        depth = lambda c: len(chains[c][5])
        begin = lambda c: early if c in lead else 1 if c in mid else 0
        agenda, fresh_slot = {}, 1
        for c in range(len(chains)):
            new = tail and c < first_grad and c not in lead
            for p in range(chains[c][0]):
                slot = fresh_slot if new else 0
                fresh_slot += 1 if new else 0
                for step in range(begin(c), depth(c)):
                    agenda.setdefault(slot, []).append((step, c, p))
                    slot += LAG
        final = None
        for slot in range(max(list(agenda) + [0]) + 1):
            if tail and slot == JOIN_SLOT:
                final = close_rows()
            for step, c, p in sorted(agenda.get(slot, []), key=lambda x: -x[0]):
                settle(c, step, p)
                if step + 1 < depth(c):
                    hop(c, step + 1, p).start()
            if tail and wide.done < len(courses[0]):
                wide.step()
            elif final is not None and slot > JOIN_SLOT and final.done < len(courses[1]) - 1:
                final.step()
        if tail:
            while final.done < len(courses[1]):
                final.step()
            for o in small_o + [lead_o]:
                store_whole(o).start()
        for c in range(len(chains)):
            for s in range(depth(c)):
                for p in range(chains[c][0]):
                    hop(c, s, p).wait_send()
            out_o = chains[c][5][-1][4]
            block = chains[c][5][-1][2]
            for p in range(chains[c][0]):
                store_piece(out_o, p, PIECE, chains[c][1] and t[block].shape[2] % 128 == 0).wait()
        if leave:
            leave_drain()

        def drain(k, c):
            if enter:
                all_far(k).wait_send()
                all_sib(k).wait_send()
                all_fwd(k).wait_send()
                for block in range(4):
                    for o in [all_o] + e_o:
                        if o[0] >= 0:
                            store_rows(o, block, k).wait()
            for o in r_o + (tail_o if tail else []):
                if o[0] >= 0:
                    store_rows(o, 0, k).wait()
            return c

        lax.fori_loop(0, CHUNKS, drain, 0)
        for o in s_o + (small_o + [lead_o] if tail else []) + (d_o if attend else []):
            if o[0] >= 0:
                store_whole(o).wait()
        for d, o in zip(dws, dw_o):
            if d[2] == "join":
                for p in range(d[6]):
                    store_piece(o, p, PIECE, False).wait()

    flops = 0
    if leave:
        flops += 2 * frames * flat_shape(leave[1])[1 if leave[2] else 0] * width
    if enter:
        flops += 2 * frames * width * sum(c for c, _ in enter[4])
    flops += sum(2 * frames * width * PIECE * d[6] for d in dws)
    outs = pl.pallas_call(
        kernel,
        in_specs=[in_hbm()] * n_in,
        out_specs=[in_hbm()] * n_out,
        out_shape=out_shape,
        scratch_shapes=scratch,
        compiler_params=pltpu.CompilerParams(collective_id=cid, has_side_effects=True, vmem_limit_bytes=VMEM_LIMIT),
        cost_estimate=pl.CostEstimate(flops=flops, bytes_accessed=60_000_000, transcendentals=0),
        name=name,
    )(*ins)
    fixed, rest = list(outs[:fixed_out]), list(outs[fixed_out:])
    fresh = [Grad(rest.pop(0), 0, d[3]) for d in dws if d[2] == "join"]
    for item in plan:
        fresh.append(Grad(rest.pop(0), item[3], item[2]))
    return fixed + [fresh] + rest


def publish(ends, small, sizes, rel, total):
    flat, outs, where = [], [], []
    f32 = jnp.float32
    for arrays, parts in ends:
        rows = arrays[0].shape[0]
        joined = len(arrays) > 1 and sizes[len(outs)]
        shape = (rows, sum(a.shape[1] for a in arrays)) if not joined else (sum(a.shape[0] for a in arrays), arrays[0].shape[1])
        where.append((len(flat), arrays, joined))
        flat.extend(arrays)
        if parts < 0:
            outs.append((shape, (-parts, shape[0], shape[1] // -parts)))
        else:
            outs.append((shape, (shape[0], parts, shape[1] // parts) if parts else None))
    n, m = len(flat), len(ends)
    width = small[0].shape[1]
    taps = small[3].shape
    split_at = [i for i in range(m) if ends[i][1] > 0]
    slab_at = [i for i in range(m) if ends[i][1] < 0]
    small_shapes = [(1, width)] * 5 + [(HEAD, rel), (taps[0] - 1, taps[1]), (1, taps[1]), (1, 5)]

    def kernel(*refs):
        src, small_in = refs[:n], refs[n : n + 4]
        dst, small_out = refs[n + 4 : n + 4 + m], refs[n + 4 + m : n + 13 + m]
        rest = refs[n + 13 + m :]
        held, split = rest[:m], dict(zip(split_at, rest[m:-1]))
        sem = rest[-1]
        loads, stores = [], []
        for i, (first, arrays, joined) in enumerate(where):
            at, copies = 0, []
            for k in range(len(arrays)):
                ref = src[first + k]
                size = ref.shape[0 if joined else 1]
                part = held[i].at[pl.ds(at, size)] if joined else held[i].at[:, pl.ds(at, size)]
                copies.append(pltpu.make_async_copy(ref, part, sem.at[first + k]))
                at += size
            loads.append(copies)
            if i in slab_at:
                slabs, _, cols = dst[i].shape
                stores.append(
                    [
                        pltpu.make_async_copy(held[i].at[:, pl.ds(k * cols, cols)], dst[i].at[k], sem.at[n + m + k])
                        for k in range(slabs)
                    ]
                )
            else:
                stores.append([pltpu.make_async_copy(split.get(i, held[i]), dst[i], sem.at[n + i])])
        for copies in loads:
            for cp in copies:
                cp.start()
        lead, rows, table, tap = [r[...] for r in small_in]
        small_out[0][...] = lead
        for i in range(4):
            small_out[1 + i][...] = rows[i : i + 1]
        turned = jnp.concatenate([table, jnp.zeros((128 - TABLE_ROWS, 128), f32)], 0).T
        small_out[5][:, :TABLE_ROWS] = turned[:HEAD, :TABLE_ROWS]
        small_out[5][:, TABLE_ROWS:] = turned[HEAD:, : rel - TABLE_ROWS]
        small_out[6][...] = tap[:-1]
        small_out[7][...] = tap[-1:]
        lane = lax.broadcasted_iota(jnp.int32, (1, 128), 1)
        mean = jnp.zeros((1, 128), f32)
        for i in range(5):
            mean = jnp.where(lane == i, jnp.sum(rows[4:5, i * 128 : (i + 1) * 128], -1, keepdims=True) / total, mean)
        root = jnp.sqrt(mean)
        small_out[8][...] = root[:, :5]
        for i in range(m):
            for cp in loads[i]:
                cp.wait()
            if i in split:
                cols = split[i].shape[2]
                for j in range(split[i].shape[1]):
                    split[i][:, j, :] = held[i][:, j * cols : (j + 1) * cols]
            for cp in stores[i]:
                cp.start()
        for copies in stores:
            for cp in copies:
                cp.wait()

    vm = pl.BlockSpec(memory_space=pltpu.VMEM)
    return pl.pallas_call(
        kernel,
        in_specs=[in_hbm()] * n + [vm] * 4,
        out_specs=[in_hbm()] * m + [vm] * 9,
        out_shape=[jax.ShapeDtypeStruct(o[1] or o[0], f32) for o in outs] + [jax.ShapeDtypeStruct(s, f32) for s in small_shapes],
        scratch_shapes=[pltpu.VMEM(o[0], f32) for o in outs]
        + [pltpu.VMEM(outs[i][1], f32) for i in split_at]
        + [pltpu.SemaphoreType.DMA((n + m + 4,))],
        compiler_params=pltpu.CompilerParams(vmem_limit_bytes=VMEM_LIMIT),
        name="publish",
    )(*flat, *small)


SPAN = 128


def exchange(stats, landing, send, recv):
    dp, me = lax.axis_index("dp"), lax.axis_index("mp")
    core, chip = me % 2, me // 2
    others = [chip * 2 + 1 - core, (1 - chip) * 2 + core, (1 - chip) * 2 + 1 - core]
    return [
        pltpu.make_async_remote_copy(
            stats, landing.at[i], send.at[i], recv.at[i], device_id=(dp, to), device_id_type=MESH
        )
        for i, to in enumerate(others)
    ]


def group_targets():
    dp, me = lax.axis_index("dp"), lax.axis_index("mp")
    core, chip = me % 2, me // 2
    return [(dp, chip * 2 + 1 - core), (dp, (1 - chip) * 2 + core), (dp, (1 - chip) * 2 + 1 - core)]


def to_rows(first, second):
    lane = lax.broadcasted_iota(jnp.int32, (SPAN, SPAN), 1)
    both = jnp.where(lane == 0, first, jnp.where(lane == 1, second, 0.0))
    return both.T[:8]


def to_columns(rows8):
    return jnp.concatenate([rows8, jnp.zeros((SPAN - 8, SPAN), jnp.float32)], 0).T


def shifted(window, by):
    return window if by == 0 else pltpu.roll(window, window.shape[0] - by, 0)


def depth_gain_row(ref, width, chans):
    first = 5 * width // 128
    return jnp.concatenate([ref[first + j : first + j + 1, :] for j in range(chans // 128)], 1)


def conv_mid(glu, w_depth, gains, width, cid):
    frames, chans = glu.shape
    taps = w_depth.shape[0]
    reach = taps - 1
    edge = (reach + 7) // 8 * 8
    f32, bf = jnp.float32, jnp.bfloat16
    tiles, lanes = frames // SPAN, chans // 128

    def kernel(glu_h, w_h, g_h, act_h, slope_h, unit_h, stat_h, pad, w_raw, g_raw, w_v, g_v, act, slope, unit, stat, sendbuf, landing, lsem, ssem, send, recv):
        meet = greet(group_targets())
        loads = [
            pltpu.make_async_copy(glu_h, pad.at[pl.ds(edge, frames)], lsem.at[0]),
            pltpu.make_async_copy(w_h, w_raw, lsem.at[1]),
            pltpu.make_async_copy(g_h, g_raw, lsem.at[2]),
        ]
        for cp in loads:
            cp.start()
        pad[:edge, :] = jnp.zeros((edge, chans), f32)
        for cp in loads:
            cp.wait()
        w_v[...] = w_raw[...].astype(f32)
        g_v[...] = depth_gain_row(g_raw, width, chans)

        def tile(i, c):
            at = pl.multiple_of(i * SPAN, SPAN)
            for lane in range(lanes):
                cols = slice(lane * 128, (lane + 1) * 128)
                window = pad[pl.ds(at, SPAN + edge), cols]
                total = jnp.zeros((SPAN, 128), f32)
                for by in range(8):
                    moved = shifted(window, by)
                    for base in range(0, edge + 1, 8):
                        tap = base + by - (edge - reach)
                        if 0 <= tap < taps:
                            total = total + w_v[tap : tap + 1, cols] * moved[base : base + SPAN]
                unit[pl.ds(at, SPAN), cols] = total
            depth = unit[pl.ds(at, SPAN), :]
            mean = jnp.mean(depth, -1, keepdims=True)
            centred = depth - mean
            sendbuf[:, pl.ds(at, SPAN)] = to_rows(mean, jnp.sum(centred * centred, -1, keepdims=True))
            return c

        lax.fori_loop(0, tiles, tile, 0)
        meet()
        copies = exchange(sendbuf, landing, send, recv)
        for cp in copies:
            cp.start()
        for cp in copies:
            cp.wait_recv()
        rows = [sendbuf[...]] + [landing[i] for i in range(3)]
        mean = sum(r[0:1] for r in rows) * 0.25
        spread = sum(r[1:2] + chans * (r[0:1] - mean) * (r[0:1] - mean) for r in rows) / width
        inverse = lax.rsqrt(spread + epsilon)
        row = lax.broadcasted_iota(jnp.int32, (8, frames), 0)
        stat[...] = jnp.where(row == 0, mean, jnp.where(row == 1, inverse, 0.0))
        outs = [(act, act_h), (slope, slope_h), (unit, unit_h)]

        def store(i, n):
            at = pl.ds(pl.multiple_of(i * SPAN, SPAN), SPAN)
            return pltpu.make_async_copy(outs[n][0].at[at], outs[n][1].at[at], ssem.at[n, i])

        def finish(i, c):
            at = pl.multiple_of(i * SPAN, SPAN)
            cols = to_columns(stat[:, pl.ds(at, SPAN)])
            u = (unit[pl.ds(at, SPAN), :] - cols[:, 0:1]) * cols[:, 1:2]
            a, s = silu_pair(u * g_v[...])
            unit[pl.ds(at, SPAN), :] = u
            act[pl.ds(at, SPAN), :] = a.astype(bf)
            slope[pl.ds(at, SPAN), :] = s.astype(bf)
            for n in range(3):
                store(i, n).start()
            return c

        lax.fori_loop(0, tiles, finish, 0)
        last = pltpu.make_async_copy(stat, stat_h, lsem.at[0])
        last.start()
        for cp in copies:
            cp.wait_send()
        for i in range(tiles):
            for n in range(3):
                store(i, n).wait()
        last.wait()

    S = jax.ShapeDtypeStruct
    out_shape = [S((frames, chans), bf), S((frames, chans), bf), S((frames, chans), f32), S((8, frames), f32)]
    vm = pltpu.VMEM
    return pl.pallas_call(
        kernel,
        in_specs=[in_hbm()] * 3,
        out_specs=[in_hbm()] * 4,
        out_shape=out_shape,
        scratch_shapes=[
            vm((frames + edge, chans), f32), vm(w_depth.shape, bf), vm(gains.shape, f32), vm(w_depth.shape, f32), vm((1, chans), f32),
            vm((frames, chans), bf), vm((frames, chans), bf), vm((frames, chans), f32), vm((8, frames), f32),
            vm((8, frames), f32), vm((3, 8, frames), f32),
            pltpu.SemaphoreType.DMA((3,)), pltpu.SemaphoreType.DMA((3, tiles)), pltpu.SemaphoreType.DMA((3,)), pltpu.SemaphoreType.DMA((3,)),
        ],
        compiler_params=pltpu.CompilerParams(collective_id=cid, has_side_effects=True, vmem_limit_bytes=VMEM_LIMIT),
        name="conv_mid",
    )(glu, w_depth, gains)


def conv_mid_back(grad, slope, unit, stat, glu, sig, tail, w_depth, gains, width, cid, grads):
    frames, chans = glu.shape
    taps = w_depth.shape[0]
    reach = taps - 1
    edge = (reach + 7) // 8 * 8
    f32, bf = jnp.float32, jnp.bfloat16
    tiles, lanes = frames // SPAN, chans // 128
    ins = [grad, slope, unit, stat, w_depth, gains, glu, sig, tail]
    riders = Riders(grads)
    n = len(grads)

    def kernel(*refs):
        hbm, ride_in, (pair_h, taps_h), ride_out = refs[:9], refs[9 : 9 + n], refs[9 + n : 11 + n], refs[11 + n : 11 + 2 * n]
        refs = refs[2 * n :]
        (grad_v, slope_v, unit_v, stat_v, w_raw, g_raw, pad, sig_v, tail_v, w_v, g_v, back, pair, taps_v, acc, gacc, sendbuf, landing, lsem, ssem, send, recv) = refs[11:33]
        riders.bind(ride_in, ride_out, refs[33:])
        meet = greet(group_targets() + riders.targets())
        dst = [grad_v, slope_v, unit_v, stat_v, w_raw, g_raw, pad.at[pl.ds(edge, frames)], sig_v, tail_v]
        loads = [pltpu.make_async_copy(h, d, lsem.at[i]) for i, (h, d) in enumerate(zip(hbm, dst))]
        for cp in loads:
            cp.start()
        pad[:edge, :] = jnp.zeros((edge, chans), f32)
        back[frames:, :] = jnp.zeros((edge, chans), f32)
        acc[...] = jnp.zeros_like(acc)
        gacc[...] = jnp.zeros_like(gacc)
        for cp in loads[:6]:
            cp.wait()
        w_v[...] = w_raw[...].astype(f32)
        g_v[...] = depth_gain_row(g_raw, width, chans)

        def first(i, c):
            at = pl.ds(pl.multiple_of(i * SPAN, SPAN), SPAN)
            u = unit_v[at, :]
            de = grad_v[at, :] * slope_v[at, :].astype(f32)
            gacc[...] += fold8(de * u)
            du = de * g_v[...]
            back[at, :] = du
            sendbuf[:, at] = to_rows(jnp.sum(du, -1, keepdims=True), jnp.sum(du * u, -1, keepdims=True))
            return c

        meet()
        riders.start()
        lax.fori_loop(0, tiles, first, 0)
        copies = exchange(sendbuf, landing, send, recv)
        for cp in copies:
            cp.start()
        for cp in loads[6:]:
            cp.wait()
        for cp in copies:
            cp.wait_recv()
        means = (sendbuf[...] + landing[0] + landing[1] + landing[2]) / width
        row = lax.broadcasted_iota(jnp.int32, (8, frames), 0)
        stat_v[...] = jnp.where(row == 1, stat_v[...], jnp.where(row == 0, means[0:1], jnp.where(row == 2, means[1:2], 0.0)))

        def second(i, c):
            at = pl.ds(pl.multiple_of(i * SPAN, SPAN), SPAN)
            cols = to_columns(stat_v[:, at])
            back[at, :] = cols[:, 1:2] * (back[at, :] - cols[:, 0:1] - unit_v[at, :] * cols[:, 2:3])
            return c

        lax.fori_loop(0, tiles, second, 0)

        def store(i):
            at = pl.ds(pl.multiple_of(i * SPAN, SPAN), SPAN)
            return pltpu.make_async_copy(pair.at[at], pair_h.at[at], ssem.at[i])

        def third(i, c):
            at = pl.multiple_of(i * SPAN, SPAN)
            rows = pl.ds(at, SPAN)
            for lane in range(lanes):
                cols = slice(lane * 128, (lane + 1) * 128)
                ahead = back[pl.ds(at, SPAN + edge), cols]
                total = jnp.zeros((SPAN, 128), f32)
                for by in range(8):
                    moved = shifted(ahead, by)
                    for base in range(0, edge, 8):
                        tap = reach - (base + by)
                        if 0 <= tap < taps:
                            total = total + w_v[tap : tap + 1, cols] * moved[base : base + SPAN]
                pair[rows, cols] = (total * sig_v[rows, cols].astype(f32)).astype(bf)
                pair[rows, chans + lane * 128 : chans + (lane + 1) * 128] = (total * tail_v[rows, cols].astype(f32)).astype(bf)
            store(i).start()
            for lane in range(lanes):
                cols = slice(lane * 128, (lane + 1) * 128)
                here = back[rows, cols]
                window = pad[pl.ds(at, SPAN + edge), cols]
                for by in range(8):
                    moved = shifted(window, by)
                    for base in range(0, edge + 1, 8):
                        tap = base + by - (edge - reach)
                        if 0 <= tap < taps:
                            acc[tap * 8 : tap * 8 + 8, cols] += fold8(here * moved[base : base + SPAN])
            return c

        lax.fori_loop(0, tiles, third, 0)
        for tap in range(taps):
            taps_v[tap : tap + 1, :] = jnp.sum(acc[tap * 8 : tap * 8 + 8, :], 0, keepdims=True)
        taps_v[taps : taps + 1, :] = jnp.sum(gacc[...], 0, keepdims=True)
        last = pltpu.make_async_copy(taps_v, taps_h, lsem.at[0])
        last.start()
        for cp in copies:
            cp.wait_send()
        riders.finish()
        for i in range(tiles):
            store(i).wait()
        last.wait()

    S = jax.ShapeDtypeStruct
    vm = pltpu.VMEM
    outs = pl.pallas_call(
        kernel,
        in_specs=[in_hbm()] * (9 + n),
        out_specs=[in_hbm()] * (2 + n),
        out_shape=[S((frames, 2 * chans), bf), S((taps + 1, chans), f32)] + riders.after,
        scratch_shapes=[
            vm((frames, chans), f32), vm((frames, chans), bf), vm((frames, chans), f32), vm((8, frames), f32),
            vm(w_depth.shape, bf), vm(gains.shape, f32), vm((frames + edge, chans), f32), vm((frames, chans), bf), vm((frames, chans), bf),
            vm(w_depth.shape, f32), vm((1, chans), f32),
            vm((frames + edge, chans), f32), vm((frames, 2 * chans), bf), vm((taps + 1, chans), f32), vm((taps * 8, chans), f32), vm((8, chans), f32),
            vm((8, frames), f32), vm((3, 8, frames), f32),
            pltpu.SemaphoreType.DMA((9,)), pltpu.SemaphoreType.DMA((tiles,)), pltpu.SemaphoreType.DMA((3,)), pltpu.SemaphoreType.DMA((3,)),
        ] + riders.scratch,
        compiler_params=pltpu.CompilerParams(collective_id=cid, has_side_effects=True, vmem_limit_bytes=VMEM_LIMIT),
        name="conv_mid_back",
    )(*ins, *riders.arrays)
    return outs[0], outs[1], riders.results(outs[2:])


def attn_fwd(qkv, rel):
    frames, cols = qkv.shape
    heads = cols // 3
    pairs = heads // 128
    nb = frames // BQ
    bf = jnp.bfloat16
    return pl.pallas_call(
        fwd_kernel,
        grid=(nb,),
        in_specs=[
            pl.BlockSpec((BQ, heads), lambda i: (i, 0)),
            pl.BlockSpec((frames, heads), lambda i: (0, 1)),
            pl.BlockSpec((frames, heads), lambda i: (0, 2)),
            pl.BlockSpec(rel.shape, lambda i: (0, 0)),
        ],
        out_specs=[
            pl.BlockSpec((BQ, heads), lambda i: (i, 0)),
            pl.BlockSpec((pairs, 2 * BQ, frames), lambda i: (0, i, 0)),
        ],
        out_shape=[jax.ShapeDtypeStruct((frames, heads), bf), jax.ShapeDtypeStruct((pairs, 2 * frames, frames), bf)],
        scratch_shapes=[
            pltpu.VMEM((pairs, 2 * BQ, 5 * BQ), jnp.float32), pltpu.VMEM((5 * BQ, 128), bf), pltpu.VMEM((128, 128), jnp.float32)
        ],
        compiler_params=pltpu.CompilerParams(vmem_limit_bytes=VMEM_LIMIT),
        name="attn_fwd",
    )(qkv, qkv, qkv, rel)


def body(
    features,
    w1_in,
    w1_out,
    gain_ffn1,
    w_qkv,
    w_attn_out,
    rel_table,
    gain_attn,
    w_conv_in,
    w_depth,
    gain_depth,
    w_conv_out,
    gain_conv,
    w2_in,
    w2_out,
    gain_ffn2,
    gain_final,
    cotangent,
):
    local_frames, clip_count, width = features.shape
    rows = local_frames * clip_count
    f32, bf = jnp.float32, jnp.bfloat16
    s0 = features.reshape(rows, width)
    seed = cotangent.reshape(rows, width)
    spare = jnp.zeros((width - gain_depth.shape[0],), bf)
    gains = jnp.concatenate([gain_ffn1, gain_attn, gain_conv, gain_ffn2, gain_final, gain_depth, spare])
    gains = gains.astype(f32).reshape(-1, 128)
    flat_qkv = w_qkv.transpose(1, 0, 2)
    flat_conv = w_conv_in.reshape(width, -1)
    units = w1_in.shape[1]
    half = units // PIECE // 2
    dp_count = lax.axis_size("dp")
    done = dp_count.bit_length() - 1
    pending = lambda items: [g for g in items if g.bit < done]
    chans = w_conv_out.shape[0]

    def swish_out(h, extra, outs):
        act, slope = silu_pair(h)
        outs[0][...] = act.astype(bf)
        outs[1][...] = slope.astype(bf)

    def plain_out(h, extra, outs):
        outs[0][...] = h.astype(outs[0].dtype)

    def glu_out(h, extra, outs):
        p0 = h[:, :chans]
        sig = jax.nn.sigmoid(h[:, chans:])
        glu = p0 * sig
        outs[0][...] = glu
        outs[1][...] = sig.astype(bf)
        outs[2][...] = (glu * (1.0 - sig)).astype(bf)

    def slope_out(h, extra, outs):
        outs[0][...] = (h * extra[0][...].astype(f32)).astype(bf)

    def first(branch, ins, gains, outs, sums):
        return (unit_norm(ins[0].astype(f32))[0] * gains[0:1, :]).astype(bf)

    def forward(scale, row):
        def run(branch, ins, gains, outs, sums):
            fresh = ins[0].astype(f32) + scale * branch
            outs[0][...] = fresh
            sums[0][...] += fold8(branch * branch)
            return (unit_norm(fresh)[0] * gains[row : row + 1, :]).astype(bf)
        return run

    def turn(branch, ins, gains, outs, sums):
        fresh = ins[0] + 0.5 * branch
        sums[0][...] += fold8(branch * branch)
        sums[1][...] += fold8(fresh * fresh)
        unit, inverse = unit_norm(fresh)
        outs[0][...] = unit * gains[4:5, :]
        grad = ins[1].astype(f32)
        scaled = grad * gains[4:5, :]
        mean_one = jnp.mean(scaled, -1, keepdims=True)
        mean_two = jnp.mean(scaled * unit, -1, keepdims=True)
        sums[2][...] += fold8(grad * unit)
        back = inverse * (scaled - mean_one - unit * mean_two)
        outs[1][...] = back
        return (0.5 * back).astype(bf)

    def backward(scale, row):
        def run(branch, ins, gains, outs, sums):
            pull, grad_gain = norm_pull(branch, ins[1].astype(f32), gains[row : row + 1, :])
            fresh = ins[0] + pull
            outs[0][...] = fresh
            sums[0][...] += grad_gain
            return (scale * fresh).astype(bf)
        return run

    a1, act1, slope1, _ = stage(
        "ffn1_in", 0, rows, width, dp_count, gains, enter=(w1_in, False, swish_out, (), ((units, bf), (units, bf))),
        junction=first, row_in=(s0,),
    )
    a2, qkv, s1, sq1, _ = stage(
        "ffn1_out", 1, rows, width, dp_count, gains, leave=(act1, w1_out, False),
        enter=(flat_qkv, False, plain_out, (), ((3 * w_qkv.shape[2], bf),)),
        junction=forward(0.5, 1), row_in=(s0,), row_out=(f32,), sums=1,
    )
    turned_table = rel_table.T
    mixed, probs = attn_fwd(qkv, turned_table)
    a3, glu, sig, tail, s2, sq2, _ = stage(
        "attn_out", 2, rows, width, dp_count, gains, leave=(mixed, w_attn_out, False),
        enter=(flat_conv, False, glu_out, (), ((chans, f32), (chans, bf), (chans, bf))),
        junction=forward(1.0, 2), row_in=(s1,), row_out=(f32,), sums=1,
    )
    act3, slope3, depth_unit, depth_stat = conv_mid(glu, w_depth, gains, width, 10)
    a4, act2, slope2, s3, sq3, _ = stage(
        "conv_out", 3, rows, width, dp_count, gains, leave=(act3, w_conv_out, False),
        enter=(w2_in, False, swish_out, (), ((units, bf), (units, bf))),
        junction=forward(1.0, 3), row_in=(s2,), row_out=(f32,), sums=1,
    )
    db4, dh2, output, grad4, sq4, sq5, dgf, _ = stage(
        "ffn2_out", 4, rows, width, dp_count, gains, leave=(act2, w2_out, False),
        enter=(w2_out, True, slope_out, (slope2,), ((units, bf),)),
        junction=turn, row_in=(s3, seed), row_out=(f32, f32), sums=3,
    )
    db3, de3, grad3, dg2, (ga_in, gb_in, gw2_out) = stage(
        "ffn2_back", 5, rows, width, dp_count, gains, leave=(dh2, w2_in, True),
        enter=(w_conv_out, True, plain_out, (), ((chans, f32),)), dws=(
            weight(a4, dh2, "join", False, 1, 0, half),
            weight(a4, dh2, "join", False, 1, half, units // PIECE - half),
            weight(db4, act2, "far", True),
        ),
        junction=backward(1.0, 3), row_in=(grad4, s3), row_out=(f32,), sums=1,
    )
    dpaired, tap_sums, (gw2_out, ga_in) = conv_mid_back(
        de3, slope3, depth_unit, depth_stat, glu, sig, tail, w_depth, gains, width, 11, [gw2_out, ga_in]
    )
    grad2, dgc, dq, dk, dv, dt, (gconv_in, gconv_out, gattn, gb_in, gw2_out, ga_in) = stage(
        "conv_back", 6, rows, width, dp_count, gains, leave=(dpaired, flat_conv, True),
        enter=(w_attn_out, True, plain_out, (), ((w_attn_out.shape[0], bf),)),
        dws=(
            weight(a3, dpaired, "far", False, 2),
            weight(db3, act3, "far", True, 2),
            weight("all", mixed, "post", True),
        ),
        grads=((gb_in, 2), gw2_out, (ga_in, 2)), attend=(qkv, probs, turned_table),
        junction=backward(1.0, 2), row_in=(grad3, s2), row_out=(f32,), sums=1,
    )
    dqkv = (dq, dk, dv)
    waiting = pending([gattn, gconv_in, gconv_out, ga_in, gb_in, gw2_out])
    grad0, ends, other_rows, table_end, taps_end, lead_row = stage(
        "attn_back", 7, rows, width, dp_count, gains, leave=(dqkv, flat_qkv, True),
        enter=(w1_out, True, slope_out, (slope1,), ((units, bf),)),
        dws=(
            weight(a2, dqkv, "far", False),
            weight("all", act1, "front", True),
            weight(a1, "out", "close", False, pieces=units // PIECE),
        ),
        grads=waiting, small=((dgc, dg2, dgf, sq1, sq2, sq3, sq4, sq5), dt, tap_sums),
        tail=(w1_in, backward(1.0, 0), (s0,)),
        junction=backward(0.5, 1), row_in=(grad2, s1), row_out=(f32,), sums=1,
    )
    gqkv, gw1_out, gw1_in = ends[:3]
    for item, end in zip(waiting, ends[3:]):
        item.array = end.array

    def finish(item):
        flip = item.turned and item.array.shape[0] * dp_count == width and (width // dp_count) % 128 != 0
        return item.array.T if flip else item.array

    token_total = rows * lax.axis_size("mp") * dp_count
    ends = [
        ([output], 1),
        ([grad0], 1),
        ([finish(gw1_in)], 0),
        ([finish(gw1_out)], 0),
        ([finish(gqkv)], -3),
        ([finish(gattn)], 0),
        ([finish(gconv_in)], 2),
        ([finish(gconv_out)], 0),
        ([finish(ga_in), finish(gb_in)], 0),
        ([finish(gw2_out)], 0),
    ]
    done_ends = publish(ends, [lead_row, other_rows, table_end, taps_end], {8: False}, rel_table.shape[0], float(token_total * width))
    (output, grad0, gw1_in, gw1_out, gqkv, gattn, gconv_in, gconv_out, gw2_in, gw2_out) = done_ends[:10]
    *gain_sums, table_sum, depth_sum, depth_gain_sum, rms_stats = done_ends[10:]
    gain_sums = [g[0] for g in gain_sums]
    return (
        output,
        grad0,
        gw1_in,
        gw1_out,
        gain_sums[0],
        gqkv.transpose(1, 0, 2),
        gattn,
        table_sum.T,
        gain_sums[1],
        gconv_in,
        depth_sum,
        depth_gain_sum[0],
        gconv_out,
        gain_sums[2],
        gw2_in,
        gw2_out,
        gain_sums[3],
        gain_sums[4],
        rms_stats[0],
    )


def solution(mesh):
    return jax.shard_map(
        body,
        mesh=mesh,
        in_specs=(
            P("mp", "dp", None),
            P(None, "mp"),
            P("mp", None),
            P(),
            P(None, None, "mp"),
            P("mp", None),
            P(),
            P(),
            P(None, None, "mp"),
            P(None, "mp"),
            P("mp"),
            P("mp", None),
            P(),
            P(None, "mp"),
            P("mp", None),
            P(),
            P(),
            P("mp", "dp", None),
        ),
        out_specs=(
            P("mp", "dp", None),
            P("mp", "dp", None),
            P("dp", "mp"),
            P("mp", "dp"),
            P(),
            P("dp", None, "mp"),
            P("mp", "dp"),
            P(),
            P(),
            P("dp", None, "mp"),
            P(None, "mp"),
            P("mp"),
            P("mp", "dp"),
            P(),
            P("dp", "mp"),
            P("mp", "dp"),
            P(),
            P(),
            P(),
        ),
        check_vma=False,
    )
```

```python
import functools

import jax
import jax.numpy as jnp
from jax import lax
from jax.experimental import pallas as pl
from jax.experimental.pallas import tpu as pltpu
from jax.sharding import PartitionSpec as P

HEAD = 64
REL_LEFT = 64
REL_RIGHT = 8
BQ = 128
WIN = 4 * BQ


epsilon = 1e-05


def nt(a, b):
    return lax.dot_general(a, b, (((1,), (1,)), ((), ())), preferred_element_type=jnp.float32)
def nn(a, b):
    return lax.dot_general(a, b, (((1,), (0,)), ((), ())), preferred_element_type=jnp.float32)
def tn(a, b):
    return lax.dot_general(a, b, (((0,), (0,)), ((), ())), preferred_element_type=jnp.float32)

MESH = pl.DeviceIdType.MESH
CHUNKS = 4
TABLE_ROWS = 40
LAG = 2
JOIN_SLOT = 3
PIECE = 256
VMEM_LIMIT = 58 << 20


def silu_pair(h):
    sig = jax.nn.sigmoid(h)
    act = h * sig
    return act, sig + act * (1.0 - sig)


def unit_norm(s):
    centred = s - jnp.mean(s, -1, keepdims=True)
    inverse = lax.rsqrt(jnp.mean(centred * centred, -1, keepdims=True) + epsilon)
    return centred * inverse, inverse


def fold8(x):
    return jnp.sum(x.reshape(x.shape[0] // 8, 8, x.shape[1]), 0)


def norm_pull(grad, s, gain):
    unit, inverse = unit_norm(s)
    scaled = grad * gain
    first = jnp.mean(scaled, -1, keepdims=True)
    second = jnp.mean(scaled * unit, -1, keepdims=True)
    return inverse * (scaled - first - unit * second), fold8(grad * unit)


def in_hbm():
    return pl.BlockSpec(memory_space=pltpu.HBM)


class Grad:
    def __init__(self, array, bit, turned):
        self.array, self.bit, self.turned = array, bit, turned


def halved(shape, turned):
    pieces, pairs, _, block, cols = shape
    if pairs > 1:
        return jax.ShapeDtypeStruct((pieces, pairs // 2, 2, block, cols), jnp.bfloat16)
    if turned and block % 128 == 0:
        return jax.ShapeDtypeStruct((pieces * cols, block), jnp.float32)
    return jax.ShapeDtypeStruct((block, pieces * cols), jnp.float32)


def arriving(shape):
    return pltpu.VMEM((shape[0], shape[1]) + tuple(shape[3:]), jnp.bfloat16)


def place(dp, bit):
    own = (dp // 2**bit) % 2
    return own, dp + 2**bit * (1 - 2 * own)


def halving_copy(src, landing, piece, bit, send, recv, slot):
    dp, mp = lax.axis_index("dp"), lax.axis_index("mp")
    own, partner = place(dp, bit)
    return pltpu.make_async_remote_copy(
        src.at[piece, :, 1 - own], landing.at[piece], send.at[slot], recv.at[slot],
        device_id=(partner, mp), device_id_type=MESH,
    )


def halving_keep(src, kept, bit, sem):
    own, _ = place(lax.axis_index("dp"), bit)
    return pltpu.make_async_copy(src.at[:, :, own], kept, sem)


def region(ref, piece, cols, turned):
    if len(ref.shape) > 2:
        return ref.at[piece]
    at = pl.ds(piece * cols, cols)
    return ref.at[at, :] if turned else ref.at[:, at]


def halving_add(held, landing, out, piece, turned):
    pairs, block, cols = landing.shape[1:]
    f32 = jnp.float32
    if pairs == 1:
        total = held(piece, 0).astype(f32) + landing[piece, 0].astype(f32)
        turned = turned and block % 128 == 0
        region(out, piece, cols, turned)[...] = total.T if turned else total
        return

    def add(j, c):
        total = held(piece, j).astype(f32) + landing[piece, j].astype(f32)
        out[piece, j // 2, j % 2] = total.astype(jnp.bfloat16)
        return c

    lax.fori_loop(0, pairs, add, 0)


def weight(lhs, rhs, where, turned, deep=1, lo=0, pieces=None):
    if pieces is None:
        pieces = (sum(r.shape[1] for r in rhs) if isinstance(rhs, tuple) else rhs.shape[1]) // PIECE
    return lhs, rhs, where, turned, deep, lo, pieces


def flat_shape(array):
    if isinstance(array, tuple):
        return array[0].shape[0], sum(a.shape[1] for a in array)
    if len(array.shape) == 3:
        return array.shape[1], array.shape[0] * array.shape[2]
    return array.shape


def gain_row(ref, i, width):
    first = i * width // 128
    return jnp.concatenate([ref[first + j : first + j + 1, :] for j in range(width // 128)], 1)


def pack_gains(gains, width):
    step = width // 128

    def kernel(*refs):
        out = refs[-1]
        out[...] = jnp.zeros_like(out)
        for i, ref in enumerate(refs[:-1]):
            rows = ref.shape[0] // 128
            out[i * step : i * step + rows, :] = ref[...].astype(jnp.float32).reshape(rows, 128)

    return pl.pallas_call(
        kernel,
        out_shape=jax.ShapeDtypeStruct((len(gains) * step, 128), jnp.float32),
        name="pack_gains",
    )(*gains)


class Riders:
    def __init__(self, grads):
        self.plan = [(g.array.shape[0], g.bit, g.turned) for g in grads]
        self.arrays = [g.array for g in grads]
        self.after = [halved(g.array.shape, g.turned) for g in grads]
        self.slots = sum(x[0] for x in self.plan)
        self.scratch = [arriving(g.array.shape) for g in grads] * 2 + [pltpu.VMEM(a.shape, a.dtype) for a in self.after]
        if grads:
            self.scratch += [pltpu.SemaphoreType.DMA((self.slots,))] * 3 + [pltpu.SemaphoreType.DMA((len(grads),))]

    def bind(self, srcs, outs, scratch):
        n = len(self.plan)
        sems = scratch[3 * n :]
        holds, hops, slot = [], [], 0
        for i, (pieces, bit, turned) in enumerate(self.plan):
            landing, keep, half = scratch[i], scratch[n + i], scratch[2 * n + i]
            holds.append(halving_keep(srcs[i], keep, bit, sems[3].at[i]))
            flip = turned and landing.shape[2] % 128 == 0
            for p in range(pieces):
                move = halving_copy(srcs[i], landing, p, bit, sems[0], sems[1], slot)
                store = pltpu.make_async_copy(region(half, p, PIECE, flip), region(outs[i], p, PIECE, flip), sems[2].at[slot])
                hops.append((move, store, lambda q, j, keep=keep: keep[q, j], landing, half, p, turned))
                slot += 1
        self.holds, self.hops = holds, hops

    def targets(self):
        dp, mp = lax.axis_index("dp"), lax.axis_index("mp")
        return [(place(dp, b)[1], mp) for b in sorted({x[1] for x in self.plan})]

    def start(self):
        for hold in self.holds:
            hold.start()
        for hop in self.hops:
            hop[0].start()

    def finish(self):
        for hold in self.holds:
            hold.wait()
        for hop in self.hops:
            hop[0].wait_recv()
            halving_add(*hop[2:])
            hop[1].start()
        for hop in self.hops:
            hop[0].wait_send()
            hop[1].wait()

    def results(self, outs):
        return [Grad(a, b + 1, t) for a, (_, b, t) in zip(outs, self.plan)]


def greet(targets):
    barrier = pltpu.get_barrier_semaphore()
    for to in targets:
        pl.semaphore_signal(barrier, inc=1, device_id=to, device_id_type=MESH)
    return lambda: pl.semaphore_wait(barrier, len(targets))


def split_pair(x):
    left = lax.broadcasted_iota(jnp.int32, x.shape, 1) < HEAD
    zero = jnp.zeros_like(x)
    return jnp.concatenate([jnp.where(left, x, zero), jnp.where(left, zero, x)], 0)

def join_pair(x):
    rows = x.shape[0] // 2
    left = lax.broadcasted_iota(jnp.int32, (rows, x.shape[1]), 1) < HEAD
    return jnp.where(left, x[:rows], x[rows:])

def spot_table(spots):
    spot = lax.broadcasted_iota(jnp.int32, (spots, BQ), 0)
    inner = jnp.clip(spot - REL_LEFT, 0, REL_LEFT + REL_RIGHT)
    row = jnp.where(spot < 3 * BQ, inner, jnp.where(spot < 4 * BQ, 0, REL_LEFT + REL_RIGHT))
    return (lax.broadcasted_iota(jnp.int32, (spots, BQ), 1) == row).astype(jnp.bfloat16)


def wide_table(rel_ref, wide_ref):
    wide_ref[...] = jnp.zeros_like(wide_ref)
    turned = rel_ref[...].astype(jnp.float32)
    cols = turned.shape[1]
    wide_ref[0:HEAD, :cols] = turned
    wide_ref[HEAD : 2 * HEAD, :cols] = turned
    return wide_ref[...].T.astype(jnp.bfloat16)


def attend_block(ib, qkv_ref, probs_ref, mixed_ref, bias_ref, rel_ref):
    frames, heads = qkv_ref.shape[0], qkv_ref.shape[1] // 3
    at = pl.ds(pl.multiple_of(ib * BQ, BQ), BQ)
    pairs = heads // 128
    nkeys = frames // BQ
    places = [pl.multiple_of(jnp.clip(jb - ib + 2, 0, 4) * BQ, BQ) for jb in range(nkeys)]
    for pr in range(pairs):
        cols = slice(pr * 128, (pr + 1) * 128)
        keys = qkv_ref[:, heads + pr * 128 : heads + (pr + 1) * 128]
        values = qkv_ref[:, 2 * heads + pr * 128 : 2 * heads + (pr + 1) * 128]
        qs = split_pair(qkv_ref[at, cols] * 0.125)
        s = nt(qs, keys)
        b = nt(qs, rel_ref[...])
        rows = b.shape[0] // 2
        bias_ref[pr, :, 0:BQ] = b[:, 3 * BQ : 4 * BQ]
        for h in range(2):
            r = pltpu.roll(b[h * rows : (h + 1) * rows, :WIN], 0, 1, stride=1, stride_axis=0)
            bias_ref[pr, h * rows : (h + 1) * rows, BQ : 4 * BQ] = r[:, : 3 * BQ]
        bias_ref[pr, :, 4 * BQ :] = b[:, 4 * BQ :]
        parts = [s[:, jb * BQ : (jb + 1) * BQ] + bias_ref[pr, :, pl.ds(places[jb], BQ)] for jb in range(nkeys)]
        top = functools.reduce(jnp.maximum, parts)
        m = jnp.max(top, -1, keepdims=True)
        es = [jnp.exp(p - m) for p in parts]
        tot = jnp.sum(functools.reduce(jnp.add, es), -1, keepdims=True)
        inv = 1.0 / tot
        for jb in range(nkeys):
            probs_ref[pr, :, jb * BQ : (jb + 1) * BQ] = (es[jb] * inv).astype(jnp.bfloat16)
        mixed_ref[at, cols] = join_pair(nn(probs_ref[pr], values)).astype(jnp.bfloat16)


def attend_back_block(ib, qkv_ref, probs_ref, do_ref, dq_ref, tot_ref, dkt, dvt, dta, dz_ref, hot_ref, relb_ref):
    frames, heads = qkv_ref.shape[0], qkv_ref.shape[1] // 3
    at = pl.ds(pl.multiple_of(ib * BQ, BQ), BQ)
    pairs = heads // 128
    nkeys = frames // BQ
    rows = BQ
    r2 = lax.broadcasted_iota(jnp.int32, (2 * rows, 2 * rows), 0)
    c2 = lax.broadcasted_iota(jnp.int32, (2 * rows, 2 * rows), 1)
    mirror = (r2 + c2 == jnp.where(r2 < rows, rows - 1, 3 * rows - 1)).astype(jnp.bfloat16)
    places = [pl.multiple_of(jnp.clip(jb - ib + 2, 0, 4) * BQ, BQ) for jb in range(nkeys)]
    for pr in range(pairs):
        cols = slice(pr * 128, (pr + 1) * 128)
        keys = qkv_ref[:, heads + pr * 128 : heads + (pr + 1) * 128]
        values = qkv_ref[:, 2 * heads + pr * 128 : 2 * heads + (pr + 1) * 128]
        qs = split_pair(qkv_ref[at, cols] * 0.125)
        dos = split_pair(do_ref[at, cols])
        p = probs_ref[pr]
        dprob = nt(dos, values)
        dvt[pr] += tn(dos, p)
        pf = p.astype(jnp.float32)
        acc = functools.reduce(
            jnp.add, [pf[:, jb * BQ : (jb + 1) * BQ] * dprob[:, jb * BQ : (jb + 1) * BQ] for jb in range(nkeys)]
        )
        inner = jnp.sum(acc, -1, keepdims=True)
        tot_ref[pr] = jnp.zeros(tot_ref.shape[1:], jnp.float32)
        for jb in range(nkeys):
            sl = slice(jb * BQ, (jb + 1) * BQ)
            dz = (pf[:, sl] * (dprob[:, sl] - inner)).astype(jnp.bfloat16)
            dz_ref[pr, :, sl] = dz
            tot_ref[pr, :, pl.ds(places[jb], BQ)] += dz.astype(jnp.float32)
        w = jnp.concatenate([tot_ref[pr, :, BQ : 4 * BQ].astype(jnp.bfloat16), jnp.zeros((2 * rows, BQ), jnp.bfloat16)], 1)
        w = nn(mirror, w)
        outs = [pltpu.roll(w[h * rows : (h + 1) * rows], WIN - rows + 1, 1, stride=1, stride_axis=0) for h in range(2)]
        d = nn(mirror, jnp.concatenate(outs, 0).astype(jnp.bfloat16)).astype(jnp.bfloat16)
        drel = nn(d, hot_ref[...])
        col = lax.broadcasted_iota(jnp.int32, drel.shape, 1)
        low = jnp.sum(tot_ref[pr, :, :BQ], -1, keepdims=True)
        high = jnp.sum(tot_ref[pr, :, 4 * BQ :], -1, keepdims=True)
        drel = drel + jnp.where(col == 0, low, 0.0) + jnp.where(col == REL_LEFT + REL_RIGHT, high, 0.0)
        drel = drel.astype(jnp.bfloat16)
        dz = dz_ref[pr]
        dq = nn(dz, keys) + nn(drel, relb_ref[...])
        dq_ref[at, cols] = (join_pair(dq) * 0.125).astype(jnp.bfloat16)
        dkt[pr] += tn(qs, dz)
        dta[...] += tn(drel, qs)


class Doubling:
    def __init__(self, course, refs, lands, sems, partner):
        self.course, self.items, self.sems, self.partner = course, list(zip(refs, lands)), sems, partner
        self.done = 0

    def copies(self, n):
        at = self.course[n]
        return [
            (
                pltpu.make_async_remote_copy(
                    r, l.at[n], self.sems[0].at[i, n], self.sems[1].at[i, n], device_id=self.partner(at), device_id_type=MESH
                ),
                r,
                l.at[n],
            )
            for i, (r, l) in enumerate(self.items)
            if i < 2 or not isinstance(at, str)
        ]

    def start(self, n=0):
        for cp, _, _ in self.copies(n):
            cp.start()

    def advance(self, n):
        for cp, r, l in self.copies(n):
            cp.wait()
            r[...] += l[...]
        if n + 1 < len(self.course):
            self.start(n + 1)

    def step(self):
        if self.done < len(self.course):
            self.advance(self.done)
            self.done += 1


def stage(name, cid, rows, width, count, gains, *, leave=None, enter=None, dws=(), grads=(), small=None, tail=None, attend=None, mix=None, junction, row_in=(), row_out=(), sums=0):
    chunk = rows // CHUNKS
    frames = rows * 4
    bits_all = count.bit_length() - 1
    f32, bf = jnp.float32, jnp.bfloat16
    ins, vm_ins, out_shape, scratch = [], [], [], []
    known = {}

    def add_in(array, direct=False):
        if isinstance(array, str):
            return array
        if direct:
            ins.append(array)
            return len(ins) - 1
        if id(array) not in known:
            group = array if isinstance(array, tuple) else (array,)
            known[id(array)] = len(vm_ins)
            vm_ins.append((len(ins), len(group), pltpu.VMEM(flat_shape(array), group[0].dtype)))
            ins.extend(group)
        return known[id(array)]

    out_slots = [0]

    def add_scratch(item):
        scratch.append(item)
        return len(scratch) - 1

    def add_out(shape, dtype, slots, kept=True):
        if not kept:
            return -1 - add_scratch(pltpu.VMEM(shape, dtype)), None
        out_shape.append(jax.ShapeDtypeStruct(shape, dtype))
        first = out_slots[0]
        out_slots[0] += slots
        return len(out_shape) - 1, first

    add_dw = lambda where: [(add_in(d[0]), add_in(d[1])) if d[2] in where else None for d in dws]
    groups = []
    if leave:
        if mix:
            heads = mix[0].shape[1] // 3
            pairs = heads // 128
            mix_i = [add_in(m) for m in mix]
            mixed_o = add_out((frames, heads), bf, 1)
            probs_o = add_out((pairs, 2 * frames, frames), bf, 2)
            mix_s = [
                add_scratch(item)
                for item in (
                    pltpu.VMEM((2, pairs, 2 * BQ, frames), bf), pltpu.VMEM((pairs, 2 * BQ, 5 * BQ), f32),
                    pltpu.VMEM((5 * BQ, 128), bf), pltpu.VMEM((128, 128), f32),
                )
            ]
        x_i = None if mix else add_in(leave[0])
        wl_i = add_in(leave[1])
        leave_s = [add_scratch(pltpu.VMEM((rows, width), f32)) for _ in range(2)]
        leave_s += [add_scratch(pltpu.VMEM((rows, width), bf)) for _ in range(6)]
        wl_s = add_scratch(pltpu.VMEM(flat_shape(leave[1])[::-1], bf)) if leave[2] else None
        groups.append(len(vm_ins))
        add_dw(("far",))
    gains_i = add_in(gains)
    gain_s = add_scratch(pltpu.VMEM((8, width), f32))
    row_i = [add_in(r) for r in row_in]
    if not leave:
        groups.append(len(vm_ins))
    add_dw(("near", "join"))
    kept = not (tail or attend)
    kept_rows = not tail
    if enter:
        we_i = add_in(enter[0])
        extra_i = [add_in(e) for e in enter[3]]
        we_s = add_scratch(pltpu.VMEM(flat_shape(enter[0])[::-1], bf)) if enter[1] else None
        all_o = add_out((frames, width), bf, 4 * CHUNKS, kept)
        e_o = [add_out((frames, c), d, 4 * CHUNKS, kept) for c, d in enter[4]]
    r_o = [add_out((rows, width), d, CHUNKS, kept_rows) for d in row_out]
    s_o = [add_out((8, width), f32, 1, kept_rows) for _ in range(sums)]
    if attend:
        qkv_i, probs_i, table_i = add_in(attend[0]), add_in(attend[1], True), add_in(attend[2])
        add_dw(("post",))
        heads = attend[0].shape[1] // 3
        pairs = heads // 128
        d_o = [add_out((frames, heads), bf, 4 * CHUNKS) for _ in range(3)] + [add_out((128, 128), f32, 1)]
        attend_s = [
            add_scratch(item)
            for item in (
                pltpu.VMEM((pairs, 2 * BQ, 5 * BQ), f32), pltpu.VMEM((pairs, 128, frames), f32), pltpu.VMEM((pairs, 128, frames), f32),
                pltpu.VMEM((128, 128), f32), pltpu.VMEM((pairs, 2 * BQ, frames), bf), pltpu.VMEM((WIN, BQ), bf), pltpu.VMEM((128, 128), bf),
            )
        ]
        wide_s = add_scratch(pltpu.VMEM((128, 128), f32))
        probs_s = add_scratch(pltpu.VMEM((2, pairs, 2 * BQ, frames), bf))
        probs_sem = add_scratch(pltpu.SemaphoreType.DMA((2,)))
    if small:
        vectors_in, table_in, taps_in = small
        vector_i = [add_in(v) for v in vectors_in]
        table_i, taps_i = add_in(table_in), add_in(taps_in)
    groups.append(len(vm_ins))
    if tail:
        add_dw(("front",))
        tw_i = add_in(tail[0])
        tw_s = add_scratch(pltpu.VMEM(flat_shape(tail[0])[::-1], bf))
        tail_i = [add_in(r) for r in tail[2]]
        add_dw(("close",))
        tail_o = [add_out((rows, width), f32, CHUNKS)]
        tail_sum = add_out((8, width), f32, 1, False)
    groups.append(len(vm_ins))
    fixed_out = len(out_shape)
    plan, dw_o = [], []
    for d in dws:
        shape = (d[6], count // 2, 2, width // count, PIECE)
        if d[2] == "join":
            dw_o.append(add_out(shape, bf, shape[0]))
        else:
            plan.append((shape, 0, d[3], bits_all if tail else min(d[4], bits_all), add_scratch(pltpu.VMEM(shape, bf)), None, None))
            dw_o.append(len(plan) - 1)
    dw_in = [(add_in(d[0]), add_in(d[1])) for d in dws]
    first_grad = len(plan)
    for g in grads:
        g, ahead = g if isinstance(g, tuple) else (g, 1)
        shape = g.array.shape
        plan.append((shape, g.bit, g.turned, bits_all if tail else min(g.bit + ahead, bits_all), None, add_in(g.array, True), add_scratch(arriving(shape))))
    chains = []
    slots = 0
    for shape, bit, turned, end, src_s, src_i, keep_s in plan:
        links = []
        pieces = shape[0]
        for b in range(bit, end):
            nxt = halved(shape, turned)
            land_s = add_scratch(arriving(shape))
            if b == end - 1:
                links.append((b, slots, land_s, None, add_out(nxt.shape, nxt.dtype, pieces)))
            else:
                links.append((b, slots, land_s, add_scratch(pltpu.VMEM(nxt.shape, nxt.dtype)), None))
            slots += pieces
            shape = nxt.shape
        chains.append((pieces, turned, src_s, src_i, keep_s, links))
    if small:
        small_shapes = [(8, width), (TABLE_ROWS, 128), taps_in.shape]
        small_o = [add_out(s, f32, 1) for s in small_shapes]
        lead_o = add_out((1, width), f32, 1)
        downward = list(range(bits_all - 1, -1, -1))
        courses = [downward[-1:] + downward[:-1] + ["sib", "far"], ["sib", "far"] + downward]
        small_l = [add_scratch(pltpu.VMEM((bits_all + 2,) + s, f32)) for s in small_shapes]
        lead_l = [add_scratch(pltpu.VMEM((bits_all + 2, 1, width), f32))]
        small_sems = [add_scratch(pltpu.SemaphoreType.DMA((3, bits_all + 2))) for _ in range(4)]
    if slots:
        grad_sems = [add_scratch(pltpu.SemaphoreType.DMA((slots,))) for _ in range(2)]
    ring_sems = [add_scratch(pltpu.SemaphoreType.DMA((6, CHUNKS))) for _ in range(2)]
    load_sem = add_scratch(pltpu.SemaphoreType.DMA((len(ins),)))
    store_sem = add_scratch(pltpu.SemaphoreType.DMA((out_slots[0],)))
    n_in, n_out = len(ins), len(out_shape)
    vm_at = [add_scratch(item[2]) for item in vm_ins]
    vo_at = [None if mix and i == probs_o[0] else add_scratch(pltpu.VMEM(o.shape, o.dtype)) for i, o in enumerate(out_shape)]

    def kernel(*refs):
        hbm_in, hbm_out, t = refs[:n_in], refs[n_in : n_in + n_out], refs[n_in + n_out :]
        vout = lambda o: t[-1 - o[0]] if o[0] < 0 else t[vo_at[o[0]]]

        def vin(i):
            if i == "all":
                return vout(all_o)
            if i == "out":
                return vout(e_o[0])
            return t[vm_at[i]]

        waited = set()

        def load(i):
            first, parts, _ = vm_ins[i]
            if len(hbm_in[first].shape) == 3:
                slabs, _, cols = hbm_in[first].shape
                return [
                    pltpu.make_async_copy(hbm_in[first].at[n], vin(i).at[:, pl.ds(n * cols, cols)], t[load_sem].at[first])
                    for n in range(slabs)
                ]
            if parts == 1:
                return [pltpu.make_async_copy(hbm_in[first], vin(i), t[load_sem].at[first])]
            copies, at = [], 0
            for n in range(first, first + parts):
                cols = hbm_in[n].shape[1]
                copies.append(pltpu.make_async_copy(hbm_in[n], vin(i).at[:, pl.ds(at, cols)], t[load_sem].at[n]))
                at += cols
            return copies

        begun = [0]

        def begin_loads(group):
            for i in range(begun[0], groups[group]):
                for cp in load(i):
                    cp.start()
            begun[0] = max(begun[0], groups[group])

        def need(*items):
            for i in items:
                if not isinstance(i, str) and i not in waited:
                    waited.add(i)
                    for cp in load(i):
                        cp.wait()

        dp, me = lax.axis_index("dp"), lax.axis_index("mp")
        core, chip = me % 2, me // 2
        sib = chip * 2 + 1 - core
        far = (1 - chip) * 2 + core
        diag = (1 - chip) * 2 + 1 - core
        bits = sorted({link[0] for ch in chains for link in ch[5]} | set(range(bits_all) if small else ()))
        meet = greet([(dp, sib), (dp, far)] + [(place(dp, b)[1], me) for b in bits])
        begin_loads(0)

        def part(ref, block, k):
            return ref.at[pl.ds(pl.multiple_of(block * rows + k * chunk, chunk), chunk)]

        def store_rows(o, block, k):
            return pltpu.make_async_copy(
                part(vout(o), block, k), part(hbm_out[o[0]], block, k), t[store_sem].at[o[1] + block * CHUNKS + k]
            )

        def store_whole(o):
            return pltpu.make_async_copy(vout(o), hbm_out[o[0]], t[store_sem].at[o[1]])

        def store_piece(o, piece, cols, turned):
            return pltpu.make_async_copy(
                region(vout(o), piece, cols, turned), region(hbm_out[o[0]], piece, cols, turned), t[store_sem].at[o[1] + piece]
            )

        def copy(kind, k, src, dst, to):
            return pltpu.make_async_remote_copy(
                src, dst, t[ring_sems[0]].at[kind, k], t[ring_sems[1]].at[kind, k], device_id=(dp, to), device_id_type=MESH
            )

        if leave:
            px, own, sb, sr, xs, xr, ob, orv = [t[s] for s in leave_s]
        if enter:
            all_ref = vout(all_o)
            we_ref = t[we_s] if enter[1] else vin(we_i)
        pair_send = lambda k: copy(0, k, part(sb, 0, k), part(sr, 0, k), sib)
        far_send = lambda k: copy(1, k, part(xs, 0, k), part(xr, 0, k), far)
        own_send = lambda k: copy(2, k, part(ob, 0, k), part(orv, 0, k), sib)
        all_far = lambda k: copy(3, k, part(all_ref, me, k), part(all_ref, me, k), far)
        all_sib = lambda k: copy(4, k, part(all_ref, me, k), part(all_ref, me, k), sib)
        all_fwd = lambda k: copy(5, k, part(all_ref, far, k), part(all_ref, far, k), sib)
        got_far = lambda k: copy(3, k, part(all_ref, far, k), part(all_ref, far, k), far)
        got_sib = lambda k: copy(4, k, part(all_ref, sib, k), part(all_ref, sib, k), sib)
        got_diag = lambda k: copy(5, k, part(all_ref, diag, k), part(all_ref, diag, k), sib)

        def source(c, step):
            pieces, turned, src_s, src_i, keep_s, links = chains[c]
            if step:
                return t[links[step - 1][3]]
            return t[src_s] if src_s is not None else hbm_in[src_i]

        def hop(c, step, piece):
            b, slot, land_s, _, _ = chains[c][5][step]
            return halving_copy(source(c, step), t[land_s], piece, b, t[grad_sems[0]], t[grad_sems[1]], slot + piece)

        def keep(c):
            return halving_keep(hbm_in[chains[c][3]], t[chains[c][4]], chains[c][5][0][0], t[load_sem].at[chains[c][3]])

        held_back = set()

        def settle(c, step, piece):
            pieces, turned, src_s, src_i, keep_s, links = chains[c]
            b, slot, land_s, out_s, out_o = links[step]
            hop(c, step, piece).wait_recv()
            if step == 0 and src_s is None:
                if c not in held_back:
                    held_back.add(c)
                    keep(c).wait()
                held = lambda p, j: t[keep_s][p, j]
            else:
                own_bit, _ = place(dp, b)
                src = source(c, step)
                held = lambda p, j: src[p, j, own_bit]
            landing = t[land_s]
            out = t[out_s] if out_o is None else vout(out_o)
            halving_add(held, landing, out, piece, turned)
            if out_o is not None:
                store_piece(out_o, piece, PIECE, turned and landing.shape[2] % 128 == 0).start()

        def fill(k, where):
            for d, (a, b), o in zip(dws, dw_in, dw_o):
                if d[2] != where:
                    continue
                chain = None if where == "join" else o
                dw = vout(o) if chain is None else t[chains[o][2]]

                @pl.when(k < dw.shape[0])
                def _(a=a, b=b, dw=dw, chain=chain, o=o, lo=d[5]):
                    g = tn(vin(a)[...], vin(b)[:, pl.ds(pl.multiple_of((lo + k) * PIECE, PIECE), PIECE)])
                    dw[k] = g.astype(bf).reshape(dw.shape[1:])
                    if chain is None:
                        store_piece(o, k, PIECE, False).start()
                    else:
                        hop(chain, 0, k).start()

        def need_for(where):
            for d, (a, b) in zip(dws, dw_in):
                if d[2] == where:
                    need(a, b)

        def leave_phase(x_ref, wl_ref, far_fill, near_fill):
            def two(k, block_a, block_b):
                lhs = jnp.concatenate([part(x_ref, block_a, k)[...], part(x_ref, block_b, k)[...]], 0)
                return nn(lhs, wl_ref[...])

            def push(k):
                pair_send(k).wait_recv()
                part(xs, 0, k)[...] = (part(px, 0, k)[...] + part(sr, 0, k)[...].astype(f32)).astype(bf)
                far_send(k).start()

            def out_far(k, c):
                p = two(k, far, diag)
                part(px, 0, k)[...] = p[:chunk]
                part(sb, 0, k)[...] = p[chunk:].astype(bf)
                pair_send(k).start()
                if not mix:

                    @pl.when(k > 0)
                    def _():
                        push(k - 1)

                fill(k, far_fill)
                return c

            if not mix:
                lax.fori_loop(0, CHUNKS, out_far, 0)
                need_for(near_fill)

            def out_near(k, c):
                p = two(k, me, sib)
                part(own, 0, k)[...] = p[:chunk]
                part(ob, 0, k)[...] = p[chunk:].astype(bf)
                own_send(k).start()
                if not mix:

                    @pl.when(k == 0)
                    def _():
                        push(CHUNKS - 1)

                fill(k, near_fill)
                return c

            if not mix:
                lax.fori_loop(0, CHUNKS, out_near, 0)
                return
            probs_v, bias_v, rel_v, wide_v = [t[n] for n in mix_s]
            rel_v[...] = nn(spot_table(5 * BQ), wide_table(vin(mix_i[1]), wide_v)).astype(bf)

            def spot(n):
                there = chip + (1 - n // 4) * (1 - 2 * chip)
                return (there * 2 + core + (n % 2) * (1 - 2 * core)) * 2 + (n // 2) % 2

            def store_probs(n):
                at = pl.ds(pl.multiple_of(spot(n) * 2 * BQ, 2 * BQ), 2 * BQ)
                return pltpu.make_async_copy(
                    probs_v.at[n % 2], hbm_out[probs_o[0]].at[:, at, :], t[store_sem].at[probs_o[1] + n % 2]
                )

            def quarter(s, c):
                def one(b, c):
                    n = s * 2 + b

                    @pl.when(n > 1)
                    def _():
                        store_probs(n - 2).wait()

                    attend_block(spot(n), vin(mix_i[0]), probs_v.at[n % 2], x_ref, bias_v, rel_v)
                    store_probs(n).start()
                    return c

                lax.fori_loop(0, 2, one, 0)
                first = s % 2 * 2

                @pl.when(s < 2)
                def _():
                    lax.fori_loop(first, first + 2, out_far, 0)
                    push(first)
                    push(first + 1)

                @pl.when(s > 1)
                def _():
                    lax.fori_loop(first, first + 2, out_near, 0)

                return c

            lax.fori_loop(0, 4, quarter, 0)
            store_probs(6).wait()
            store_probs(7).wait()

        def leave_drain():
            def drain(k, c):
                pair_send(k).wait_send()
                far_send(k).wait_send()
                own_send(k).wait_send()
                return c

            lax.fori_loop(0, CHUNKS, drain, 0)

        def join_phase(rule, has_leave, in_refs, outs, totals, gathers):
            def join(k, c):
                fill(k, "join")
                branch = None
                if has_leave:
                    own_send(k).wait_recv()
                    far_send(k).wait_recv()
                    branch = part(own, 0, k)[...] + part(orv, 0, k)[...].astype(f32) + part(xr, 0, k)[...].astype(f32)
                fresh = rule(
                    branch, [part(r, 0, k)[...] for r in in_refs], t[gain_s], [part(vout(o), 0, k) for o in outs], [vout(o) for o in totals]
                )
                if gathers:
                    part(all_ref, me, k)[...] = fresh
                    all_far(k).start()
                    all_sib(k).start()
                for o in outs:
                    if o[0] >= 0:
                        store_rows(o, 0, k).start()
                return c

            lax.fori_loop(0, CHUNKS, join, 0)
            for o in totals:
                if o[0] >= 0:
                    store_whole(o).start()

        for o in s_o + ([tail_sum] if tail else []):
            vout(o)[...] = jnp.zeros((8, width), f32)
        meet()
        if leave:
            need(*(mix_i if mix else [x_i]), wl_i)
        begin_loads(1)
        for c in range(first_grad, len(chains)):
            for p in range(chains[c][0]):
                hop(c, 0, p).start()
        if leave:
            if leave[2]:
                t[wl_s][...] = vin(wl_i)[...].T
            need_for("far")
            leave_phase(vout(mixed_o) if mix else vin(x_i), t[wl_s] if leave[2] else vin(wl_i), "far", "near")
            if mix:
                store_whole(mixed_o).start()
        for c in range(first_grad, len(chains)):
            keep(c).start()
        need(gains_i, *row_i)
        for i in range(5):
            t[gain_s][i : i + 1, :] = gain_row(vin(gains_i), i, width)
        need_for("join")
        if enter and enter[1]:
            need(we_i)
            we_ref[...] = vin(we_i)[...].T
        join_phase(junction, bool(leave), [vin(r) for r in row_i], r_o, s_o, bool(enter))

        lead = [c for c in range(first_grad) if tail and dws[[i for i, o in enumerate(dw_o) if o == c][0]][2] == "far"]
        if small:
            partner = lambda at: (dp, sib) if at == "sib" else (dp, far) if at == "far" else (place(dp, at)[1], me)
            need(*vector_i, table_i, taps_i)
            rows_ref = vout(small_o[0])
            rows_ref[...] = jnp.zeros((8, width), f32)
            vectors = [vout(s_o[0])] + [vin(i) for i in vector_i]
            for i, v in enumerate(vectors[:4]):
                rows_ref[i : i + 1, :] = jnp.sum(v[...], 0, keepdims=True)
            for i, v in enumerate(vectors[4:]):
                line = jnp.sum(v[...], 0, keepdims=True)
                rows_ref[4:5, i * 128 : (i + 1) * 128] = functools.reduce(
                    jnp.add, [line[:, j * 128 : (j + 1) * 128] for j in range(width // 128)]
                )
            both = vin(table_i)[...]
            both = both + pltpu.roll(both, 64, 1)
            left = lax.broadcasted_iota(jnp.int32, (TABLE_ROWS, 128), 1) < HEAD
            vout(small_o[1])[...] = jnp.where(left, both[:TABLE_ROWS], both[TABLE_ROWS : 2 * TABLE_ROWS])
            vout(small_o[2])[...] = vin(taps_i)[...]
            wide = Doubling(courses[0], [vout(o) for o in small_o], [t[l] for l in small_l], [t[s] for s in small_sems[:2]], partner)
            wide.start()

        mid = set()

        def hasten(which):
            for c in which:
                if len(chains[c][5]) > 1:
                    mid.add(c)
                    for p in range(chains[c][0]):
                        settle(c, 0, p)
                        hop(c, 1, p).start()

        if enter:
            begin_loads(len(groups) - 1)
            need(we_i, *extra_i)

            def work(k, block_a, block_b):
                lhs = jnp.concatenate([part(all_ref, block_a, k)[...], part(all_ref, block_b, k)[...]], 0)
                h = nn(lhs, we_ref[...])
                for i, block in enumerate((block_a, block_b)):
                    view = lambda ref: part(ref, block, k)
                    enter[2](h[i * chunk : (i + 1) * chunk], [view(vin(r))[...] for r in extra_i], [view(vout(o)) for o in e_o])
                    for o in [all_o] + e_o:
                        if o[0] >= 0:
                            store_rows(o, block, k).start()

        if attend:
            tot_ref, dkt, dvt, dta, dz_ref, hot_ref, relb_ref = [t[s] for s in attend_s]
            dq, dk, dv = [vout(o) for o in d_o[:3]]
            need(qkv_i, table_i)
            need_for("post")
            for ref in (dkt, dvt, dta):
                ref[...] = jnp.zeros(ref.shape, f32)
            hot_ref[...] = spot_table(WIN)
            relb_ref[...] = wide_table(vin(table_i), t[wide_s])

            def block_of(j):
                chip_j = chip + (j // 4) * (1 - 2 * chip)
                core_j = core + (j % 2) * (1 - 2 * core)
                return (chip_j * 2 + core_j) * 2 + (j // 2) % 2

            def fetch(j):
                at = pl.ds(pl.multiple_of(block_of(j) * 2 * BQ, 2 * BQ), 2 * BQ)
                return pltpu.make_async_copy(hbm_in[probs_i].at[:, at, :], t[probs_s].at[j % 2], t[probs_sem].at[j % 2])

            fetch(0).start()

            def pass_on(*ks):
                for k in ks:
                    got_far(k).wait_recv()
                    all_fwd(k).start()

            def before(n):
                if 0 < n < 5:
                    pass_on(n - 1)
                if n == 3:
                    hasten(range(first_grad, len(chains)))
                elif n == 5:
                    hasten(range(first_grad))
                elif n == 6:
                    for k in range(CHUNKS):
                        if any(d[2] == "post" and k < d[6] for d in dws):
                            fill(k, "post")

            def rows_for(j):
                away = j // 4

                def chunk_rows(k, c):
                    @pl.when(away == 0)
                    def _():
                        got_sib(k).wait_recv()

                    @pl.when(away == 1)
                    def _():
                        got_diag(k).wait_recv()

                    there = chip + away * (1 - 2 * chip)
                    work(k, there * 2 + core, there * 2 + 1 - core)
                    return c

                first = (j // 2) % 2 * 2
                lax.fori_loop(first, first + 2, chunk_rows, 0)

            def query_block(j, c):
                for n in (1, 2, 3, 4):

                    @pl.when(j == n)
                    def _(n=n):
                        before(n)

                @pl.when(j % 2 == 0)
                def _():
                    rows_for(j)

                for n in (5, 6):

                    @pl.when(j == n)
                    def _(n=n):
                        before(n)

                @pl.when(j < 7)
                def _():
                    fetch(j + 1).start()

                fetch(j).wait()
                attend_back_block(
                    block_of(j), vin(qkv_i), t[probs_s].at[j % 2], vout(e_o[0]), dq, tot_ref, dkt, dvt, dta, dz_ref, hot_ref, relb_ref
                )
                return c

            lax.fori_loop(0, 8, query_block, 0)
            for pr in range(pairs):
                dk[:, pr * 128 : (pr + 1) * 128] = dkt[pr].T.astype(bf)
                dv[:, pr * 128 : (pr + 1) * 128] = dvt[pr].T.astype(bf)
            vout(d_o[3])[...] = dta[...]
            for o in d_o:
                store_whole(o).start()
        elif enter:

            def gather(k, c):
                got_sib(k).wait_recv()
                work(k, me, sib)
                got_far(k).wait_recv()
                all_fwd(k).start()
                got_diag(k).wait_recv()
                work(k, far, diag)
                if small:

                    for n, at in enumerate((1, CHUNKS - 1)):

                        @pl.when(k == at)
                        def _(n=n):
                            wide.advance(n)

                if lead:

                    @pl.when(k == CHUNKS - 2)
                    def _():
                        for ch in lead:
                            for p in range(chains[ch][0]):
                                settle(ch, 0, p)
                                hop(ch, 1, p).start()

                return c

            lax.fori_loop(0, CHUNKS, gather, 0)
            if small:
                wide.done = 2

        early = 0
        if tail:
            need_for("front")

            def front(k, c):
                fill(k, "front")
                return c

            lax.fori_loop(0, CHUNKS, front, 0)
            early = 1
            if lead and bits_all > 2:
                early = 2
                for ch in lead:
                    for p in range(chains[ch][0]):
                        settle(ch, 1, p)
                        hop(ch, 2, p).start()
            leave_drain()
            need(tw_i, *tail_i)
            t[tw_s][...] = vin(tw_i)[...].T
            leave_phase(vin("out"), t[tw_s], None, "close")
            wide.step()

        def close_rows():
            join_phase(tail[1], True, [vout(r_o[0])] + [vin(r) for r in tail_i], tail_o, [tail_sum], False)
            vout(lead_o)[...] = jnp.sum(vout(tail_sum)[...], 0, keepdims=True)
            final = Doubling(courses[1], [vout(lead_o)], [t[l] for l in lead_l], [t[s] for s in small_sems[2:]], partner)
            final.start()
            return final

        depth = lambda c: len(chains[c][5])
        begin = lambda c: early if c in lead else 1 if c in mid else 0
        agenda, fresh_slot = {}, 1
        for c in range(len(chains)):
            new = tail and c < first_grad and c not in lead
            for p in range(chains[c][0]):
                slot = fresh_slot if new else 0
                fresh_slot += 1 if new else 0
                for step in range(begin(c), depth(c)):
                    agenda.setdefault(slot, []).append((step, c, p))
                    slot += LAG
        final = None
        for slot in range(max(list(agenda) + [0]) + 1):
            if tail and slot == JOIN_SLOT:
                final = close_rows()
            for step, c, p in sorted(agenda.get(slot, []), key=lambda x: -x[0]):
                settle(c, step, p)
                if step + 1 < depth(c):
                    hop(c, step + 1, p).start()
            if tail and wide.done < len(courses[0]):
                wide.step()
            elif final is not None and slot > JOIN_SLOT and final.done < len(courses[1]) - 1:
                final.step()
        if tail:
            while final.done < len(courses[1]):
                final.step()
            for o in small_o + [lead_o]:
                store_whole(o).start()
        for c in range(len(chains)):
            for s in range(depth(c)):
                for p in range(chains[c][0]):
                    hop(c, s, p).wait_send()
            out_o = chains[c][5][-1][4]
            block = chains[c][5][-1][2]
            for p in range(chains[c][0]):
                store_piece(out_o, p, PIECE, chains[c][1] and t[block].shape[2] % 128 == 0).wait()
        if leave:
            leave_drain()

        def drain(k, c):
            if enter:
                all_far(k).wait_send()
                all_sib(k).wait_send()
                all_fwd(k).wait_send()
                for block in range(4):
                    for o in [all_o] + e_o:
                        if o[0] >= 0:
                            store_rows(o, block, k).wait()
            for o in r_o + (tail_o if tail else []):
                if o[0] >= 0:
                    store_rows(o, 0, k).wait()
            return c

        lax.fori_loop(0, CHUNKS, drain, 0)
        for o in s_o + (small_o + [lead_o] if tail else []) + (d_o if attend else []) + ([mixed_o] if mix else []):
            if o[0] >= 0:
                store_whole(o).wait()
        for d, o in zip(dws, dw_o):
            if d[2] == "join":
                for p in range(d[6]):
                    store_piece(o, p, PIECE, False).wait()

    flops = 0
    if leave:
        flops += 2 * frames * flat_shape(leave[1])[1 if leave[2] else 0] * width
    if enter:
        flops += 2 * frames * width * sum(c for c, _ in enter[4])
    flops += sum(2 * frames * width * PIECE * d[6] for d in dws)
    outs = pl.pallas_call(
        kernel,
        in_specs=[in_hbm()] * n_in,
        out_specs=[in_hbm()] * n_out,
        out_shape=out_shape,
        scratch_shapes=scratch,
        compiler_params=pltpu.CompilerParams(collective_id=cid, has_side_effects=True, vmem_limit_bytes=VMEM_LIMIT),
        cost_estimate=pl.CostEstimate(flops=flops, bytes_accessed=60_000_000, transcendentals=0),
        name=name,
    )(*ins)
    fixed, rest = list(outs[:fixed_out]), list(outs[fixed_out:])
    fresh = [Grad(rest.pop(0), 0, d[3]) for d in dws if d[2] == "join"]
    for item in plan:
        fresh.append(Grad(rest.pop(0), item[3], item[2]))
    return fixed + [fresh] + rest


def publish(ends, small, sizes, rel, total):
    flat, outs, where = [], [], []
    f32 = jnp.float32
    for arrays, parts in ends:
        rows = arrays[0].shape[0]
        joined = len(arrays) > 1 and sizes[len(outs)]
        shape = (rows, sum(a.shape[1] for a in arrays)) if not joined else (sum(a.shape[0] for a in arrays), arrays[0].shape[1])
        where.append((len(flat), arrays, joined))
        flat.extend(arrays)
        if parts < 0:
            outs.append((shape, (-parts, shape[0], shape[1] // -parts)))
        else:
            outs.append((shape, (shape[0], parts, shape[1] // parts) if parts else None))
    n, m = len(flat), len(ends)
    width = small[0].shape[1]
    taps = small[3].shape
    split_at = [i for i in range(m) if ends[i][1] > 0]
    slab_at = [i for i in range(m) if ends[i][1] < 0]
    small_shapes = [(1, width)] * 5 + [(HEAD, rel), (taps[0] - 1, taps[1]), (1, taps[1]), (1, 5)]

    def kernel(*refs):
        src, small_in = refs[:n], refs[n : n + 4]
        dst, small_out = refs[n + 4 : n + 4 + m], refs[n + 4 + m : n + 13 + m]
        rest = refs[n + 13 + m :]
        held, split = rest[:m], dict(zip(split_at, rest[m:-1]))
        sem = rest[-1]
        loads, stores = [], []
        for i, (first, arrays, joined) in enumerate(where):
            at, copies = 0, []
            for k in range(len(arrays)):
                ref = src[first + k]
                size = ref.shape[0 if joined else 1]
                part = held[i].at[pl.ds(at, size)] if joined else held[i].at[:, pl.ds(at, size)]
                copies.append(pltpu.make_async_copy(ref, part, sem.at[first + k]))
                at += size
            loads.append(copies)
            if i in slab_at:
                slabs, _, cols = dst[i].shape
                stores.append(
                    [
                        pltpu.make_async_copy(held[i].at[:, pl.ds(k * cols, cols)], dst[i].at[k], sem.at[n + m + k])
                        for k in range(slabs)
                    ]
                )
            else:
                stores.append([pltpu.make_async_copy(split.get(i, held[i]), dst[i], sem.at[n + i])])
        for copies in loads:
            for cp in copies:
                cp.start()
        lead, rows, table, tap = [r[...] for r in small_in]
        small_out[0][...] = lead
        for i in range(4):
            small_out[1 + i][...] = rows[i : i + 1]
        turned = jnp.concatenate([table, jnp.zeros((128 - TABLE_ROWS, 128), f32)], 0).T
        small_out[5][:, :TABLE_ROWS] = turned[:HEAD, :TABLE_ROWS]
        small_out[5][:, TABLE_ROWS:] = turned[HEAD:, : rel - TABLE_ROWS]
        small_out[6][...] = tap[:-1]
        small_out[7][...] = tap[-1:]
        lane = lax.broadcasted_iota(jnp.int32, (1, 128), 1)
        mean = jnp.zeros((1, 128), f32)
        for i in range(5):
            mean = jnp.where(lane == i, jnp.sum(rows[4:5, i * 128 : (i + 1) * 128], -1, keepdims=True) / total, mean)
        root = jnp.sqrt(mean)
        small_out[8][...] = root[:, :5]
        for i in range(m):
            for cp in loads[i]:
                cp.wait()
            if i in split:
                cols = split[i].shape[2]
                for j in range(split[i].shape[1]):
                    split[i][:, j, :] = held[i][:, j * cols : (j + 1) * cols]
            for cp in stores[i]:
                cp.start()
        for copies in stores:
            for cp in copies:
                cp.wait()

    vm = pl.BlockSpec(memory_space=pltpu.VMEM)
    return pl.pallas_call(
        kernel,
        in_specs=[in_hbm()] * n + [vm] * 4,
        out_specs=[in_hbm()] * m + [vm] * 9,
        out_shape=[jax.ShapeDtypeStruct(o[1] or o[0], f32) for o in outs] + [jax.ShapeDtypeStruct(s, f32) for s in small_shapes],
        scratch_shapes=[pltpu.VMEM(o[0], f32) for o in outs]
        + [pltpu.VMEM(outs[i][1], f32) for i in split_at]
        + [pltpu.SemaphoreType.DMA((n + m + 4,))],
        compiler_params=pltpu.CompilerParams(vmem_limit_bytes=VMEM_LIMIT),
        name="publish",
    )(*flat, *small)


SPAN = 128


def exchange(stats, landing, send, recv):
    dp, me = lax.axis_index("dp"), lax.axis_index("mp")
    core, chip = me % 2, me // 2
    others = [chip * 2 + 1 - core, (1 - chip) * 2 + core, (1 - chip) * 2 + 1 - core]
    return [
        pltpu.make_async_remote_copy(
            stats, landing.at[i], send.at[i], recv.at[i], device_id=(dp, to), device_id_type=MESH
        )
        for i, to in enumerate(others)
    ]


def group_targets():
    dp, me = lax.axis_index("dp"), lax.axis_index("mp")
    core, chip = me % 2, me // 2
    return [(dp, chip * 2 + 1 - core), (dp, (1 - chip) * 2 + core), (dp, (1 - chip) * 2 + 1 - core)]


def to_rows(first, second):
    lane = lax.broadcasted_iota(jnp.int32, (SPAN, SPAN), 1)
    both = jnp.where(lane == 0, first, jnp.where(lane == 1, second, 0.0))
    return both.T[:8]


def to_columns(rows8):
    return jnp.concatenate([rows8, jnp.zeros((SPAN - 8, SPAN), jnp.float32)], 0).T


def shifted(window, by):
    return window if by == 0 else pltpu.roll(window, window.shape[0] - by, 0)


def depth_gain_row(ref, width, chans):
    first = 5 * width // 128
    return jnp.concatenate([ref[first + j : first + j + 1, :] for j in range(chans // 128)], 1)


def conv_mid(glu, w_depth, gains, width, cid):
    frames, chans = glu.shape
    taps = w_depth.shape[0]
    reach = taps - 1
    edge = (reach + 7) // 8 * 8
    f32, bf = jnp.float32, jnp.bfloat16
    tiles, lanes = frames // SPAN, chans // 128

    def kernel(glu_h, w_h, g_h, act_h, slope_h, unit_h, stat_h, pad, w_raw, g_raw, w_v, g_v, act, slope, unit, stat, sendbuf, landing, lsem, ssem, send, recv):
        meet = greet(group_targets())
        loads = [
            pltpu.make_async_copy(glu_h, pad.at[pl.ds(edge, frames)], lsem.at[0]),
            pltpu.make_async_copy(w_h, w_raw, lsem.at[1]),
            pltpu.make_async_copy(g_h, g_raw, lsem.at[2]),
        ]
        for cp in loads:
            cp.start()
        pad[:edge, :] = jnp.zeros((edge, chans), f32)
        for cp in loads:
            cp.wait()
        w_v[...] = w_raw[...].astype(f32)
        g_v[...] = depth_gain_row(g_raw, width, chans)

        def tile(i, c):
            at = pl.multiple_of(i * SPAN, SPAN)
            for lane in range(lanes):
                cols = slice(lane * 128, (lane + 1) * 128)
                window = pad[pl.ds(at, SPAN + edge), cols]
                total = jnp.zeros((SPAN, 128), f32)
                for by in range(8):
                    moved = shifted(window, by)
                    for base in range(0, edge + 1, 8):
                        tap = base + by - (edge - reach)
                        if 0 <= tap < taps:
                            total = total + w_v[tap : tap + 1, cols] * moved[base : base + SPAN]
                unit[pl.ds(at, SPAN), cols] = total
            depth = unit[pl.ds(at, SPAN), :]
            mean = jnp.mean(depth, -1, keepdims=True)
            centred = depth - mean
            sendbuf[:, pl.ds(at, SPAN)] = to_rows(mean, jnp.sum(centred * centred, -1, keepdims=True))
            return c

        lax.fori_loop(0, tiles, tile, 0)
        meet()
        copies = exchange(sendbuf, landing, send, recv)
        for cp in copies:
            cp.start()
        for cp in copies:
            cp.wait_recv()
        rows = [sendbuf[...]] + [landing[i] for i in range(3)]
        mean = sum(r[0:1] for r in rows) * 0.25
        spread = sum(r[1:2] + chans * (r[0:1] - mean) * (r[0:1] - mean) for r in rows) / width
        inverse = lax.rsqrt(spread + epsilon)
        row = lax.broadcasted_iota(jnp.int32, (8, frames), 0)
        stat[...] = jnp.where(row == 0, mean, jnp.where(row == 1, inverse, 0.0))
        outs = [(act, act_h), (slope, slope_h), (unit, unit_h)]

        def store(i, n):
            at = pl.ds(pl.multiple_of(i * SPAN, SPAN), SPAN)
            return pltpu.make_async_copy(outs[n][0].at[at], outs[n][1].at[at], ssem.at[n, i])

        def finish(i, c):
            at = pl.multiple_of(i * SPAN, SPAN)
            cols = to_columns(stat[:, pl.ds(at, SPAN)])
            u = (unit[pl.ds(at, SPAN), :] - cols[:, 0:1]) * cols[:, 1:2]
            a, s = silu_pair(u * g_v[...])
            unit[pl.ds(at, SPAN), :] = u
            act[pl.ds(at, SPAN), :] = a.astype(bf)
            slope[pl.ds(at, SPAN), :] = s.astype(bf)
            for n in range(3):
                store(i, n).start()
            return c

        lax.fori_loop(0, tiles, finish, 0)
        last = pltpu.make_async_copy(stat, stat_h, lsem.at[0])
        last.start()
        for cp in copies:
            cp.wait_send()
        for i in range(tiles):
            for n in range(3):
                store(i, n).wait()
        last.wait()

    S = jax.ShapeDtypeStruct
    out_shape = [S((frames, chans), bf), S((frames, chans), bf), S((frames, chans), f32), S((8, frames), f32)]
    vm = pltpu.VMEM
    return pl.pallas_call(
        kernel,
        in_specs=[in_hbm()] * 3,
        out_specs=[in_hbm()] * 4,
        out_shape=out_shape,
        scratch_shapes=[
            vm((frames + edge, chans), f32), vm(w_depth.shape, bf), vm(gains.shape, f32), vm(w_depth.shape, f32), vm((1, chans), f32),
            vm((frames, chans), bf), vm((frames, chans), bf), vm((frames, chans), f32), vm((8, frames), f32),
            vm((8, frames), f32), vm((3, 8, frames), f32),
            pltpu.SemaphoreType.DMA((3,)), pltpu.SemaphoreType.DMA((3, tiles)), pltpu.SemaphoreType.DMA((3,)), pltpu.SemaphoreType.DMA((3,)),
        ],
        compiler_params=pltpu.CompilerParams(collective_id=cid, has_side_effects=True, vmem_limit_bytes=VMEM_LIMIT),
        name="conv_mid",
    )(glu, w_depth, gains)


def conv_mid_back(grad, slope, unit, stat, glu, sig, tail, w_depth, gains, width, cid, grads):
    frames, chans = glu.shape
    taps = w_depth.shape[0]
    reach = taps - 1
    edge = (reach + 7) // 8 * 8
    f32, bf = jnp.float32, jnp.bfloat16
    tiles, lanes = frames // SPAN, chans // 128
    ins = [grad, slope, unit, stat, w_depth, gains, glu, sig, tail]
    riders = Riders(grads)
    n = len(grads)

    def kernel(*refs):
        hbm, ride_in, (pair_h, taps_h), ride_out = refs[:9], refs[9 : 9 + n], refs[9 + n : 11 + n], refs[11 + n : 11 + 2 * n]
        refs = refs[2 * n :]
        (grad_v, slope_v, unit_v, stat_v, w_raw, g_raw, pad, sig_v, tail_v, w_v, g_v, back, pair, taps_v, acc, gacc, sendbuf, landing, lsem, ssem, send, recv) = refs[11:33]
        riders.bind(ride_in, ride_out, refs[33:])
        meet = greet(group_targets() + riders.targets())
        dst = [grad_v, slope_v, unit_v, stat_v, w_raw, g_raw, pad.at[pl.ds(edge, frames)], sig_v, tail_v]
        loads = [pltpu.make_async_copy(h, d, lsem.at[i]) for i, (h, d) in enumerate(zip(hbm, dst))]
        for cp in loads:
            cp.start()
        pad[:edge, :] = jnp.zeros((edge, chans), f32)
        back[frames:, :] = jnp.zeros((edge, chans), f32)
        acc[...] = jnp.zeros_like(acc)
        gacc[...] = jnp.zeros_like(gacc)
        for cp in loads[:6]:
            cp.wait()
        w_v[...] = w_raw[...].astype(f32)
        g_v[...] = depth_gain_row(g_raw, width, chans)

        def first(i, c):
            at = pl.ds(pl.multiple_of(i * SPAN, SPAN), SPAN)
            u = unit_v[at, :]
            de = grad_v[at, :] * slope_v[at, :].astype(f32)
            gacc[...] += fold8(de * u)
            du = de * g_v[...]
            back[at, :] = du
            sendbuf[:, at] = to_rows(jnp.sum(du, -1, keepdims=True), jnp.sum(du * u, -1, keepdims=True))
            return c

        meet()
        riders.start()
        lax.fori_loop(0, tiles, first, 0)
        copies = exchange(sendbuf, landing, send, recv)
        for cp in copies:
            cp.start()
        for cp in loads[6:]:
            cp.wait()
        for cp in copies:
            cp.wait_recv()
        means = (sendbuf[...] + landing[0] + landing[1] + landing[2]) / width
        row = lax.broadcasted_iota(jnp.int32, (8, frames), 0)
        stat_v[...] = jnp.where(row == 1, stat_v[...], jnp.where(row == 0, means[0:1], jnp.where(row == 2, means[1:2], 0.0)))

        def second(i, c):
            at = pl.ds(pl.multiple_of(i * SPAN, SPAN), SPAN)
            cols = to_columns(stat_v[:, at])
            back[at, :] = cols[:, 1:2] * (back[at, :] - cols[:, 0:1] - unit_v[at, :] * cols[:, 2:3])
            return c

        lax.fori_loop(0, tiles, second, 0)

        def store(i):
            at = pl.ds(pl.multiple_of(i * SPAN, SPAN), SPAN)
            return pltpu.make_async_copy(pair.at[at], pair_h.at[at], ssem.at[i])

        def third(i, c):
            at = pl.multiple_of(i * SPAN, SPAN)
            rows = pl.ds(at, SPAN)
            for lane in range(lanes):
                cols = slice(lane * 128, (lane + 1) * 128)
                ahead = back[pl.ds(at, SPAN + edge), cols]
                total = jnp.zeros((SPAN, 128), f32)
                for by in range(8):
                    moved = shifted(ahead, by)
                    for base in range(0, edge, 8):
                        tap = reach - (base + by)
                        if 0 <= tap < taps:
                            total = total + w_v[tap : tap + 1, cols] * moved[base : base + SPAN]
                pair[rows, cols] = (total * sig_v[rows, cols].astype(f32)).astype(bf)
                pair[rows, chans + lane * 128 : chans + (lane + 1) * 128] = (total * tail_v[rows, cols].astype(f32)).astype(bf)
            store(i).start()
            for lane in range(lanes):
                cols = slice(lane * 128, (lane + 1) * 128)
                here = back[rows, cols]
                window = pad[pl.ds(at, SPAN + edge), cols]
                for by in range(8):
                    moved = shifted(window, by)
                    for base in range(0, edge + 1, 8):
                        tap = base + by - (edge - reach)
                        if 0 <= tap < taps:
                            acc[tap * 8 : tap * 8 + 8, cols] += fold8(here * moved[base : base + SPAN])
            return c

        lax.fori_loop(0, tiles, third, 0)
        for tap in range(taps):
            taps_v[tap : tap + 1, :] = jnp.sum(acc[tap * 8 : tap * 8 + 8, :], 0, keepdims=True)
        taps_v[taps : taps + 1, :] = jnp.sum(gacc[...], 0, keepdims=True)
        last = pltpu.make_async_copy(taps_v, taps_h, lsem.at[0])
        last.start()
        for cp in copies:
            cp.wait_send()
        riders.finish()
        for i in range(tiles):
            store(i).wait()
        last.wait()

    S = jax.ShapeDtypeStruct
    vm = pltpu.VMEM
    outs = pl.pallas_call(
        kernel,
        in_specs=[in_hbm()] * (9 + n),
        out_specs=[in_hbm()] * (2 + n),
        out_shape=[S((frames, 2 * chans), bf), S((taps + 1, chans), f32)] + riders.after,
        scratch_shapes=[
            vm((frames, chans), f32), vm((frames, chans), bf), vm((frames, chans), f32), vm((8, frames), f32),
            vm(w_depth.shape, bf), vm(gains.shape, f32), vm((frames + edge, chans), f32), vm((frames, chans), bf), vm((frames, chans), bf),
            vm(w_depth.shape, f32), vm((1, chans), f32),
            vm((frames + edge, chans), f32), vm((frames, 2 * chans), bf), vm((taps + 1, chans), f32), vm((taps * 8, chans), f32), vm((8, chans), f32),
            vm((8, frames), f32), vm((3, 8, frames), f32),
            pltpu.SemaphoreType.DMA((9,)), pltpu.SemaphoreType.DMA((tiles,)), pltpu.SemaphoreType.DMA((3,)), pltpu.SemaphoreType.DMA((3,)),
        ] + riders.scratch,
        compiler_params=pltpu.CompilerParams(collective_id=cid, has_side_effects=True, vmem_limit_bytes=VMEM_LIMIT),
        name="conv_mid_back",
    )(*ins, *riders.arrays)
    return outs[0], outs[1], riders.results(outs[2:])


def body(
    features,
    w1_in,
    w1_out,
    gain_ffn1,
    w_qkv,
    w_attn_out,
    rel_table,
    gain_attn,
    w_conv_in,
    w_depth,
    gain_depth,
    w_conv_out,
    gain_conv,
    w2_in,
    w2_out,
    gain_ffn2,
    gain_final,
    cotangent,
):
    local_frames, clip_count, width = features.shape
    rows = local_frames * clip_count
    f32, bf = jnp.float32, jnp.bfloat16
    s0 = features.reshape(rows, width)
    seed = cotangent.reshape(rows, width)
    gains = pack_gains((gain_ffn1, gain_attn, gain_conv, gain_ffn2, gain_final, gain_depth), width)
    flat_qkv = w_qkv.transpose(1, 0, 2)
    flat_conv = w_conv_in.reshape(width, -1)
    units = w1_in.shape[1]
    half = units // PIECE // 2
    dp_count = lax.axis_size("dp")
    done = dp_count.bit_length() - 1
    pending = lambda items: [g for g in items if g.bit < done]
    chans = w_conv_out.shape[0]

    def swish_out(h, extra, outs):
        act, slope = silu_pair(h)
        outs[0][...] = act.astype(bf)
        outs[1][...] = slope.astype(bf)

    def plain_out(h, extra, outs):
        outs[0][...] = h.astype(outs[0].dtype)

    def glu_out(h, extra, outs):
        p0 = h[:, :chans]
        sig = jax.nn.sigmoid(h[:, chans:])
        glu = p0 * sig
        outs[0][...] = glu
        outs[1][...] = sig.astype(bf)
        outs[2][...] = (glu * (1.0 - sig)).astype(bf)

    def slope_out(h, extra, outs):
        outs[0][...] = (h * extra[0][...].astype(f32)).astype(bf)

    def first(branch, ins, gains, outs, sums):
        return (unit_norm(ins[0].astype(f32))[0] * gains[0:1, :]).astype(bf)

    def forward(scale, row):
        def run(branch, ins, gains, outs, sums):
            fresh = ins[0].astype(f32) + scale * branch
            outs[0][...] = fresh
            sums[0][...] += fold8(branch * branch)
            return (unit_norm(fresh)[0] * gains[row : row + 1, :]).astype(bf)
        return run

    def turn(branch, ins, gains, outs, sums):
        fresh = ins[0] + 0.5 * branch
        sums[0][...] += fold8(branch * branch)
        sums[1][...] += fold8(fresh * fresh)
        unit, inverse = unit_norm(fresh)
        outs[0][...] = unit * gains[4:5, :]
        grad = ins[1].astype(f32)
        scaled = grad * gains[4:5, :]
        mean_one = jnp.mean(scaled, -1, keepdims=True)
        mean_two = jnp.mean(scaled * unit, -1, keepdims=True)
        sums[2][...] += fold8(grad * unit)
        back = inverse * (scaled - mean_one - unit * mean_two)
        outs[1][...] = back
        return (0.5 * back).astype(bf)

    def backward(scale, row):
        def run(branch, ins, gains, outs, sums):
            pull, grad_gain = norm_pull(branch, ins[1].astype(f32), gains[row : row + 1, :])
            fresh = ins[0] + pull
            outs[0][...] = fresh
            sums[0][...] += grad_gain
            return (scale * fresh).astype(bf)
        return run

    a1, act1, slope1, _ = stage(
        "ffn1_in", 0, rows, width, dp_count, gains, enter=(w1_in, False, swish_out, (), ((units, bf), (units, bf))),
        junction=first, row_in=(s0,),
    )
    a2, qkv, s1, sq1, _ = stage(
        "ffn1_out", 1, rows, width, dp_count, gains, leave=(act1, w1_out, False),
        enter=(flat_qkv, False, plain_out, (), ((3 * w_qkv.shape[2], bf),)),
        junction=forward(0.5, 1), row_in=(s0,), row_out=(f32,), sums=1,
    )
    turned_table = rel_table.T
    mixed, probs, a3, glu, sig, tail, s2, sq2, _ = stage(
        "attn_out", 2, rows, width, dp_count, gains, leave=(None, w_attn_out, False), mix=(qkv, turned_table),
        enter=(flat_conv, False, glu_out, (), ((chans, f32), (chans, bf), (chans, bf))),
        junction=forward(1.0, 2), row_in=(s1,), row_out=(f32,), sums=1,
    )
    act3, slope3, depth_unit, depth_stat = conv_mid(glu, w_depth, gains, width, 10)
    a4, act2, slope2, s3, sq3, _ = stage(
        "conv_out", 3, rows, width, dp_count, gains, leave=(act3, w_conv_out, False),
        enter=(w2_in, False, swish_out, (), ((units, bf), (units, bf))),
        junction=forward(1.0, 3), row_in=(s2,), row_out=(f32,), sums=1,
    )
    db4, dh2, output, grad4, sq4, sq5, dgf, _ = stage(
        "ffn2_out", 4, rows, width, dp_count, gains, leave=(act2, w2_out, False),
        enter=(w2_out, True, slope_out, (slope2,), ((units, bf),)),
        junction=turn, row_in=(s3, seed), row_out=(f32, f32), sums=3,
    )
    db3, de3, grad3, dg2, (ga_in, gb_in, gw2_out) = stage(
        "ffn2_back", 5, rows, width, dp_count, gains, leave=(dh2, w2_in, True),
        enter=(w_conv_out, True, plain_out, (), ((chans, f32),)), dws=(
            weight(a4, dh2, "join", False, 1, 0, half),
            weight(a4, dh2, "join", False, 1, half, units // PIECE - half),
            weight(db4, act2, "far", True),
        ),
        junction=backward(1.0, 3), row_in=(grad4, s3), row_out=(f32,), sums=1,
    )
    dpaired, tap_sums, (gw2_out, ga_in) = conv_mid_back(
        de3, slope3, depth_unit, depth_stat, glu, sig, tail, w_depth, gains, width, 11, [gw2_out, ga_in]
    )
    grad2, dgc, dq, dk, dv, dt, (gconv_in, gconv_out, gattn, gb_in, gw2_out, ga_in) = stage(
        "conv_back", 6, rows, width, dp_count, gains, leave=(dpaired, flat_conv, True),
        enter=(w_attn_out, True, plain_out, (), ((w_attn_out.shape[0], bf),)),
        dws=(
            weight(a3, dpaired, "far", False, 2),
            weight(db3, act3, "far", True, 2),
            weight("all", mixed, "post", True),
        ),
        grads=((gb_in, 2), gw2_out, (ga_in, 2)), attend=(qkv, probs, turned_table),
        junction=backward(1.0, 2), row_in=(grad3, s2), row_out=(f32,), sums=1,
    )
    dqkv = (dq, dk, dv)
    waiting = pending([gattn, gconv_in, gconv_out, ga_in, gb_in, gw2_out])
    grad0, ends, other_rows, table_end, taps_end, lead_row = stage(
        "attn_back", 7, rows, width, dp_count, gains, leave=(dqkv, flat_qkv, True),
        enter=(w1_out, True, slope_out, (slope1,), ((units, bf),)),
        dws=(
            weight(a2, dqkv, "far", False),
            weight("all", act1, "front", True),
            weight(a1, "out", "close", False, pieces=units // PIECE),
        ),
        grads=waiting, small=((dgc, dg2, dgf, sq1, sq2, sq3, sq4, sq5), dt, tap_sums),
        tail=(w1_in, backward(1.0, 0), (s0,)),
        junction=backward(0.5, 1), row_in=(grad2, s1), row_out=(f32,), sums=1,
    )
    gqkv, gw1_out, gw1_in = ends[:3]
    for item, end in zip(waiting, ends[3:]):
        item.array = end.array

    def finish(item):
        flip = item.turned and item.array.shape[0] * dp_count == width and (width // dp_count) % 128 != 0
        return item.array.T if flip else item.array

    token_total = rows * lax.axis_size("mp") * dp_count
    ends = [
        ([output], 1),
        ([grad0], 1),
        ([finish(gw1_in)], 0),
        ([finish(gw1_out)], 0),
        ([finish(gqkv)], -3),
        ([finish(gattn)], 0),
        ([finish(gconv_in)], 2),
        ([finish(gconv_out)], 0),
        ([finish(ga_in), finish(gb_in)], 0),
        ([finish(gw2_out)], 0),
    ]
    done_ends = publish(ends, [lead_row, other_rows, table_end, taps_end], {8: False}, rel_table.shape[0], float(token_total * width))
    (output, grad0, gw1_in, gw1_out, gqkv, gattn, gconv_in, gconv_out, gw2_in, gw2_out) = done_ends[:10]
    *gain_sums, table_sum, depth_sum, depth_gain_sum, rms_stats = done_ends[10:]
    gain_sums = [g[0] for g in gain_sums]
    return (
        output,
        grad0,
        gw1_in,
        gw1_out,
        gain_sums[0],
        gqkv.transpose(1, 0, 2),
        gattn,
        table_sum.T,
        gain_sums[1],
        gconv_in,
        depth_sum,
        depth_gain_sum[0],
        gconv_out,
        gain_sums[2],
        gw2_in,
        gw2_out,
        gain_sums[3],
        gain_sums[4],
        rms_stats[0],
    )


def solution(mesh):
    return jax.shard_map(
        body,
        mesh=mesh,
        in_specs=(
            P("mp", "dp", None),
            P(None, "mp"),
            P("mp", None),
            P(),
            P(None, None, "mp"),
            P("mp", None),
            P(),
            P(),
            P(None, None, "mp"),
            P(None, "mp"),
            P("mp"),
            P("mp", None),
            P(),
            P(None, "mp"),
            P("mp", None),
            P(),
            P(),
            P("mp", "dp", None),
        ),
        out_specs=(
            P("mp", "dp", None),
            P("mp", "dp", None),
            P("dp", "mp"),
            P("mp", "dp"),
            P(),
            P("dp", None, "mp"),
            P("mp", "dp"),
            P(),
            P(),
            P("dp", None, "mp"),
            P(None, "mp"),
            P("mp"),
            P("mp", "dp"),
            P(),
            P("dp", "mp"),
            P("mp", "dp"),
            P(),
            P(),
            P(),
        ),
        check_vma=False,
    )
```

```python
import functools

import jax
import jax.numpy as jnp
from jax import lax
from jax.experimental import pallas as pl
from jax.experimental.pallas import tpu as pltpu
from jax.sharding import PartitionSpec as P

HEAD = 64
REL_LEFT = 64
REL_RIGHT = 8
BQ = 128
WIN = 4 * BQ


epsilon = 1e-05


def nt(a, b):
    return lax.dot_general(a, b, (((1,), (1,)), ((), ())), preferred_element_type=jnp.float32)
def nn(a, b):
    return lax.dot_general(a, b, (((1,), (0,)), ((), ())), preferred_element_type=jnp.float32)
def tn(a, b):
    return lax.dot_general(a, b, (((0,), (0,)), ((), ())), preferred_element_type=jnp.float32)

MESH = pl.DeviceIdType.MESH
CHUNKS = 4
TABLE_ROWS = 40
LAG = 2
JOIN_SLOT = 3
PIECE = 256
VMEM_LIMIT = 58 << 20


def silu_pair(h):
    sig = jax.nn.sigmoid(h)
    act = h * sig
    return act, sig + act * (1.0 - sig)


def unit_norm(s):
    centred = s - jnp.mean(s, -1, keepdims=True)
    inverse = lax.rsqrt(jnp.mean(centred * centred, -1, keepdims=True) + epsilon)
    return centred * inverse, inverse


def fold8(x):
    return jnp.sum(x.reshape(x.shape[0] // 8, 8, x.shape[1]), 0)


def norm_pull(grad, s, gain):
    unit, inverse = unit_norm(s)
    scaled = grad * gain
    first = jnp.mean(scaled, -1, keepdims=True)
    second = jnp.mean(scaled * unit, -1, keepdims=True)
    return inverse * (scaled - first - unit * second), fold8(grad * unit)


def in_hbm():
    return pl.BlockSpec(memory_space=pltpu.HBM)


class Grad:
    def __init__(self, array, bit, turned):
        self.array, self.bit, self.turned = array, bit, turned


def halved(shape, turned):
    pieces, pairs, _, block, cols = shape
    if pairs > 1:
        return jax.ShapeDtypeStruct((pieces, pairs // 2, 2, block, cols), jnp.bfloat16)
    if turned and block % 128 == 0:
        return jax.ShapeDtypeStruct((pieces * cols, block), jnp.float32)
    return jax.ShapeDtypeStruct((block, pieces * cols), jnp.float32)


def arriving(shape):
    return pltpu.VMEM((shape[0], shape[1]) + tuple(shape[3:]), jnp.bfloat16)


def place(dp, bit):
    own = (dp // 2**bit) % 2
    return own, dp + 2**bit * (1 - 2 * own)


def halving_copy(src, landing, piece, bit, send, recv, slot):
    dp, mp = lax.axis_index("dp"), lax.axis_index("mp")
    own, partner = place(dp, bit)
    return pltpu.make_async_remote_copy(
        src.at[piece, :, 1 - own], landing.at[piece], send.at[slot], recv.at[slot],
        device_id=(partner, mp), device_id_type=MESH,
    )


def halving_keep(src, kept, bit, sem):
    own, _ = place(lax.axis_index("dp"), bit)
    return pltpu.make_async_copy(src.at[:, :, own], kept, sem)


def region(ref, piece, cols, turned):
    if len(ref.shape) > 2:
        return ref.at[piece]
    at = pl.ds(piece * cols, cols)
    return ref.at[at, :] if turned else ref.at[:, at]


def halving_add(held, landing, out, piece, turned):
    pairs, block, cols = landing.shape[1:]
    f32 = jnp.float32
    if pairs == 1:
        total = held(piece, 0).astype(f32) + landing[piece, 0].astype(f32)
        turned = turned and block % 128 == 0
        region(out, piece, cols, turned)[...] = total.T if turned else total
        return

    def add(j, c):
        total = held(piece, j).astype(f32) + landing[piece, j].astype(f32)
        out[piece, j // 2, j % 2] = total.astype(jnp.bfloat16)
        return c

    lax.fori_loop(0, pairs, add, 0)


def weight(lhs, rhs, where, turned, deep=1, lo=0, pieces=None, order=None):
    if pieces is None:
        pieces = (sum(r.shape[1] for r in rhs) if isinstance(rhs, tuple) else rhs.shape[1]) // PIECE
    return lhs, rhs, where, turned, deep, lo, pieces, order


def flat_shape(array):
    if isinstance(array, tuple):
        return array[0].shape[0], sum(a.shape[1] for a in array)
    if len(array.shape) == 3:
        return array.shape[1], array.shape[0] * array.shape[2]
    return array.shape


def gain_row(ref, i, width):
    first = i * width // 128
    return jnp.concatenate([ref[first + j : first + j + 1, :] for j in range(width // 128)], 1)


def pack_gains(gains, width):
    step = width // 128

    def kernel(*refs):
        out = refs[-1]
        out[...] = jnp.zeros_like(out)
        for i, ref in enumerate(refs[:-1]):
            rows = ref.shape[0] // 128
            out[i * step : i * step + rows, :] = ref[...].astype(jnp.float32).reshape(rows, 128)

    return pl.pallas_call(
        kernel,
        out_shape=jax.ShapeDtypeStruct((len(gains) * step, 128), jnp.float32),
        name="pack_gains",
    )(*gains)


class Riders:
    def __init__(self, grads):
        self.plan = [(g.array.shape[0], g.bit, g.turned) for g in grads]
        self.arrays = [g.array for g in grads]
        self.after = [halved(g.array.shape, g.turned) for g in grads]
        self.slots = sum(x[0] for x in self.plan)
        self.scratch = [arriving(g.array.shape) for g in grads] * 2 + [pltpu.VMEM(a.shape, a.dtype) for a in self.after]
        if grads:
            self.scratch += [pltpu.SemaphoreType.DMA((self.slots,))] * 3 + [pltpu.SemaphoreType.DMA((len(grads),))]

    def bind(self, srcs, outs, scratch):
        n = len(self.plan)
        sems = scratch[3 * n :]
        holds, hops, slot = [], [], 0
        for i, (pieces, bit, turned) in enumerate(self.plan):
            landing, keep, half = scratch[i], scratch[n + i], scratch[2 * n + i]
            holds.append(halving_keep(srcs[i], keep, bit, sems[3].at[i]))
            flip = turned and landing.shape[2] % 128 == 0
            for p in range(pieces):
                move = halving_copy(srcs[i], landing, p, bit, sems[0], sems[1], slot)
                store = pltpu.make_async_copy(region(half, p, PIECE, flip), region(outs[i], p, PIECE, flip), sems[2].at[slot])
                hops.append((move, store, lambda q, j, keep=keep: keep[q, j], landing, half, p, turned))
                slot += 1
        self.holds, self.hops = holds, hops

    def targets(self):
        dp, mp = lax.axis_index("dp"), lax.axis_index("mp")
        return [(place(dp, b)[1], mp) for b in sorted({x[1] for x in self.plan})]

    def start(self):
        for hold in self.holds:
            hold.start()
        for hop in self.hops:
            hop[0].start()

    def finish(self):
        for hold in self.holds:
            hold.wait()
        for hop in self.hops:
            hop[0].wait_recv()
            halving_add(*hop[2:])
            hop[1].start()
        for hop in self.hops:
            hop[0].wait_send()
            hop[1].wait()

    def results(self, outs):
        return [Grad(a, b + 1, t) for a, (_, b, t) in zip(outs, self.plan)]


def greet(targets):
    barrier = pltpu.get_barrier_semaphore()
    for to in targets:
        pl.semaphore_signal(barrier, inc=1, device_id=to, device_id_type=MESH)
    return lambda: pl.semaphore_wait(barrier, len(targets))


def split_pair(x):
    left = lax.broadcasted_iota(jnp.int32, x.shape, 1) < HEAD
    zero = jnp.zeros_like(x)
    return jnp.concatenate([jnp.where(left, x, zero), jnp.where(left, zero, x)], 0)

def join_pair(x):
    rows = x.shape[0] // 2
    left = lax.broadcasted_iota(jnp.int32, (rows, x.shape[1]), 1) < HEAD
    return jnp.where(left, x[:rows], x[rows:])

def spot_table(spots):
    spot = lax.broadcasted_iota(jnp.int32, (spots, BQ), 0)
    inner = jnp.clip(spot - REL_LEFT, 0, REL_LEFT + REL_RIGHT)
    row = jnp.where(spot < 3 * BQ, inner, jnp.where(spot < 4 * BQ, 0, REL_LEFT + REL_RIGHT))
    return (lax.broadcasted_iota(jnp.int32, (spots, BQ), 1) == row).astype(jnp.bfloat16)


def wide_table(rel_ref, wide_ref):
    wide_ref[...] = jnp.zeros_like(wide_ref)
    turned = rel_ref[...].astype(jnp.float32)
    cols = turned.shape[1]
    wide_ref[0:HEAD, :cols] = turned
    wide_ref[HEAD : 2 * HEAD, :cols] = turned
    return wide_ref[...].T.astype(jnp.bfloat16)


def attend_block(ib, qkv_ref, probs_ref, mixed_ref, bias_ref, rel_ref):
    frames, heads = qkv_ref.shape[0], qkv_ref.shape[1] // 3
    at = pl.ds(pl.multiple_of(ib * BQ, BQ), BQ)
    pairs = heads // 128
    nkeys = frames // BQ
    places = [pl.multiple_of(jnp.clip(jb - ib + 2, 0, 4) * BQ, BQ) for jb in range(nkeys)]
    for pr in range(pairs):
        cols = slice(pr * 128, (pr + 1) * 128)
        keys = qkv_ref[:, heads + pr * 128 : heads + (pr + 1) * 128]
        values = qkv_ref[:, 2 * heads + pr * 128 : 2 * heads + (pr + 1) * 128]
        qs = split_pair(qkv_ref[at, cols] * 0.125)
        s = nt(qs, keys)
        b = nt(qs, rel_ref[...])
        rows = b.shape[0] // 2
        bias_ref[pr, :, 0:BQ] = b[:, 3 * BQ : 4 * BQ]
        for h in range(2):
            r = pltpu.roll(b[h * rows : (h + 1) * rows, :WIN], 0, 1, stride=1, stride_axis=0)
            bias_ref[pr, h * rows : (h + 1) * rows, BQ : 4 * BQ] = r[:, : 3 * BQ]
        bias_ref[pr, :, 4 * BQ :] = b[:, 4 * BQ :]
        parts = [s[:, jb * BQ : (jb + 1) * BQ] + bias_ref[pr, :, pl.ds(places[jb], BQ)] for jb in range(nkeys)]
        top = functools.reduce(jnp.maximum, parts)
        m = jnp.max(top, -1, keepdims=True)
        es = [jnp.exp(p - m) for p in parts]
        tot = jnp.sum(functools.reduce(jnp.add, es), -1, keepdims=True)
        inv = 1.0 / tot
        for jb in range(nkeys):
            probs_ref[pr, :, jb * BQ : (jb + 1) * BQ] = (es[jb] * inv).astype(jnp.bfloat16)
        mixed_ref[at, cols] = join_pair(nn(probs_ref[pr], values)).astype(jnp.bfloat16)


def attend_back_block(ib, qkv_ref, probs_ref, do_ref, dq_ref, tot_ref, dkt, dvt, dta, dz_ref, hot_ref, relb_ref):
    frames, heads = qkv_ref.shape[0], qkv_ref.shape[1] // 3
    at = pl.ds(pl.multiple_of(ib * BQ, BQ), BQ)
    pairs = heads // 128
    nkeys = frames // BQ
    rows = BQ
    r2 = lax.broadcasted_iota(jnp.int32, (2 * rows, 2 * rows), 0)
    c2 = lax.broadcasted_iota(jnp.int32, (2 * rows, 2 * rows), 1)
    mirror = (r2 + c2 == jnp.where(r2 < rows, rows - 1, 3 * rows - 1)).astype(jnp.bfloat16)
    places = [pl.multiple_of(jnp.clip(jb - ib + 2, 0, 4) * BQ, BQ) for jb in range(nkeys)]
    for pr in range(pairs):
        cols = slice(pr * 128, (pr + 1) * 128)
        keys = qkv_ref[:, heads + pr * 128 : heads + (pr + 1) * 128]
        values = qkv_ref[:, 2 * heads + pr * 128 : 2 * heads + (pr + 1) * 128]
        qs = split_pair(qkv_ref[at, cols] * 0.125)
        dos = split_pair(do_ref[at, cols])
        p = probs_ref[pr]
        dprob = nt(dos, values)
        dvt[pr] += tn(dos, p)
        pf = p.astype(jnp.float32)
        acc = functools.reduce(
            jnp.add, [pf[:, jb * BQ : (jb + 1) * BQ] * dprob[:, jb * BQ : (jb + 1) * BQ] for jb in range(nkeys)]
        )
        inner = jnp.sum(acc, -1, keepdims=True)
        tot_ref[pr] = jnp.zeros(tot_ref.shape[1:], jnp.float32)
        for jb in range(nkeys):
            sl = slice(jb * BQ, (jb + 1) * BQ)
            dz = (pf[:, sl] * (dprob[:, sl] - inner)).astype(jnp.bfloat16)
            dz_ref[pr, :, sl] = dz
            tot_ref[pr, :, pl.ds(places[jb], BQ)] += dz.astype(jnp.float32)
        w = jnp.concatenate([tot_ref[pr, :, BQ : 4 * BQ].astype(jnp.bfloat16), jnp.zeros((2 * rows, BQ), jnp.bfloat16)], 1)
        w = nn(mirror, w)
        outs = [pltpu.roll(w[h * rows : (h + 1) * rows], WIN - rows + 1, 1, stride=1, stride_axis=0) for h in range(2)]
        d = nn(mirror, jnp.concatenate(outs, 0).astype(jnp.bfloat16)).astype(jnp.bfloat16)
        drel = nn(d, hot_ref[...])
        col = lax.broadcasted_iota(jnp.int32, drel.shape, 1)
        low = jnp.sum(tot_ref[pr, :, :BQ], -1, keepdims=True)
        high = jnp.sum(tot_ref[pr, :, 4 * BQ :], -1, keepdims=True)
        drel = drel + jnp.where(col == 0, low, 0.0) + jnp.where(col == REL_LEFT + REL_RIGHT, high, 0.0)
        drel = drel.astype(jnp.bfloat16)
        dz = dz_ref[pr]
        dq = nn(dz, keys) + nn(drel, relb_ref[...])
        dq_ref[at, cols] = (join_pair(dq) * 0.125).astype(jnp.bfloat16)
        dkt[pr] += tn(qs, dz)
        dta[...] += tn(drel, qs)


class Doubling:
    def __init__(self, course, refs, lands, sems, partner):
        self.course, self.items, self.sems, self.partner = course, list(zip(refs, lands)), sems, partner
        self.done = 0

    def copies(self, n):
        at = self.course[n]
        return [
            (
                pltpu.make_async_remote_copy(
                    r, l.at[n], self.sems[0].at[i, n], self.sems[1].at[i, n], device_id=self.partner(at), device_id_type=MESH
                ),
                r,
                l.at[n],
            )
            for i, (r, l) in enumerate(self.items)
            if i < 2 or not isinstance(at, str)
        ]

    def start(self, n=0):
        for cp, _, _ in self.copies(n):
            cp.start()

    def advance(self, n):
        for cp, r, l in self.copies(n):
            cp.wait()
            r[...] += l[...]
        if n + 1 < len(self.course):
            self.start(n + 1)

    def step(self):
        if self.done < len(self.course):
            self.advance(self.done)
            self.done += 1


def stage(name, cid, rows, width, count, gains, *, leave=None, enter=None, dws=(), grads=(), small=None, tail=None, attend=None, mix=None, pre=None, junction, row_in=(), row_out=(), sums=0):
    chunk = rows // CHUNKS
    frames = rows * 4
    bits_all = count.bit_length() - 1
    f32, bf = jnp.float32, jnp.bfloat16
    ins, vm_ins, out_shape, scratch = [], [], [], []
    known = {}

    def add_in(array, direct=False):
        if isinstance(array, str):
            return array
        if direct:
            ins.append(array)
            return len(ins) - 1
        if id(array) not in known:
            group = array if isinstance(array, tuple) else (array,)
            known[id(array)] = len(vm_ins)
            vm_ins.append((len(ins), len(group), pltpu.VMEM(flat_shape(array), group[0].dtype)))
            ins.extend(group)
        return known[id(array)]

    out_slots = [0]

    def add_scratch(item):
        scratch.append(item)
        return len(scratch) - 1

    def add_out(shape, dtype, slots, kept=True):
        if not kept:
            return -1 - add_scratch(pltpu.VMEM(shape, dtype)), None
        out_shape.append(jax.ShapeDtypeStruct(shape, dtype))
        first = out_slots[0]
        out_slots[0] += slots
        return len(out_shape) - 1, first

    add_dw = lambda where: [(add_in(d[0]), add_in(d[1])) if d[2] in where else None for d in dws]
    groups = []
    if leave:
        if mix:
            heads = mix[0].shape[1] // 3
            pairs = heads // 128
            mix_i = [add_in(m) for m in mix]
            mixed_o = add_out((frames, heads), bf, 1)
            probs_o = add_out((pairs, 2 * frames, frames), bf, 2)
            mix_s = [
                add_scratch(item)
                for item in (
                    pltpu.VMEM((2, pairs, 2 * BQ, frames), bf), pltpu.VMEM((pairs, 2 * BQ, 5 * BQ), f32),
                    pltpu.VMEM((5 * BQ, 128), bf), pltpu.VMEM((128, 128), f32),
                )
            ]
        if pre:
            pre_i = [add_in(a, True) for a in pre[0]]
            pre_o = [add_out(o.shape, o.dtype, 0) for o in pre[1]]
            pre_s = [add_scratch(item) for item in pre[2]]
        x_i = None if mix or pre else add_in(leave[0])
        wl_i = add_in(leave[1])
        leave_s = [add_scratch(pltpu.VMEM((rows, width), f32)) for _ in range(2)]
        leave_s += [add_scratch(pltpu.VMEM((rows, width), bf)) for _ in range(6)]
        wl_s = add_scratch(pltpu.VMEM(flat_shape(leave[1])[::-1], bf)) if leave[2] else None
        groups.append(len(vm_ins))
        add_dw(("far",))
    gains_i = add_in(gains)
    gain_s = add_scratch(pltpu.VMEM((8, width), f32))
    row_i = [add_in(r) for r in row_in]
    if not leave:
        groups.append(len(vm_ins))
    add_dw(("near", "join"))
    kept = not (tail or attend)
    kept_rows = not tail
    if enter:
        we_i = add_in(enter[0])
        extra_i = [add_in(e) for e in enter[3]]
        we_s = add_scratch(pltpu.VMEM(flat_shape(enter[0])[::-1], bf)) if enter[1] else None
        all_o = add_out((frames, width), bf, 4 * CHUNKS, kept)
        e_o = [add_out((frames, c), d, 4 * CHUNKS, kept) for c, d in enter[4]]
    r_o = [add_out((rows, width), d, CHUNKS, kept_rows) for d in row_out]
    s_o = [add_out((8, width), f32, 1, kept_rows) for _ in range(sums)]
    if attend:
        qkv_i, probs_i, table_i = add_in(attend[0]), add_in(attend[1], True), add_in(attend[2])
        add_dw(("post",))
        heads = attend[0].shape[1] // 3
        pairs = heads // 128
        d_o = [add_out((frames, heads), bf, 4 * CHUNKS) for _ in range(3)] + [add_out((128, 128), f32, 1)]
        attend_s = [
            add_scratch(item)
            for item in (
                pltpu.VMEM((pairs, 2 * BQ, 5 * BQ), f32), pltpu.VMEM((pairs, 128, frames), f32), pltpu.VMEM((pairs, 128, frames), f32),
                pltpu.VMEM((128, 128), f32), pltpu.VMEM((pairs, 2 * BQ, frames), bf), pltpu.VMEM((WIN, BQ), bf), pltpu.VMEM((128, 128), bf),
            )
        ]
        wide_s = add_scratch(pltpu.VMEM((128, 128), f32))
        probs_s = add_scratch(pltpu.VMEM((2, pairs, 2 * BQ, frames), bf))
        probs_sem = add_scratch(pltpu.SemaphoreType.DMA((2,)))
    if small:
        vectors_in, table_in, taps_in = small
        vector_i = [add_in(v) for v in vectors_in]
        table_i, taps_i = add_in(table_in), add_in(taps_in)
    groups.append(len(vm_ins))
    if tail:
        add_dw(("front",))
        tw_i = add_in(tail[0])
        tw_s = add_scratch(pltpu.VMEM(flat_shape(tail[0])[::-1], bf))
        tail_i = [add_in(r) for r in tail[2]]
        add_dw(("close",))
        tail_o = [add_out((rows, width), f32, CHUNKS)]
        tail_sum = add_out((8, width), f32, 1, False)
    groups.append(len(vm_ins))
    fixed_out = len(out_shape)
    plan, dw_o = [], []
    for d in dws:
        shape = (d[6], count // 2, 2, width // count, PIECE)
        if d[2] == "join":
            dw_o.append(add_out(shape, bf, shape[0]))
        else:
            plan.append((shape, d[7] or 0, d[3], bits_all if tail else min(d[4], bits_all), add_scratch(pltpu.VMEM(shape, bf)), None, None))
            dw_o.append(len(plan) - 1)
    dw_in = [(add_in(d[0]), add_in(d[1])) for d in dws]
    first_grad = len(plan)
    for g in grads:
        g, ahead = g if isinstance(g, tuple) else (g, 1)
        shape = g.array.shape
        plan.append((shape, g.bit, g.turned, bits_all if tail else min(g.bit + ahead, bits_all), None, add_in(g.array, True), add_scratch(arriving(shape))))
    chains = []
    slots = 0
    for shape, bit, turned, end, src_s, src_i, keep_s in plan:
        links = []
        pieces = shape[0]
        course = bit if isinstance(bit, tuple) else tuple(range(bit, end))
        for b in course:
            nxt = halved(shape, turned)
            land_s = add_scratch(arriving(shape))
            if b == course[-1]:
                links.append((b, slots, land_s, None, add_out(nxt.shape, nxt.dtype, pieces)))
            else:
                links.append((b, slots, land_s, add_scratch(pltpu.VMEM(nxt.shape, nxt.dtype)), None))
            slots += pieces
            shape = nxt.shape
        chains.append((pieces, turned, src_s, src_i, keep_s, links))
    if small:
        small_shapes = [(8, width), (TABLE_ROWS, 128), taps_in.shape]
        small_o = [add_out(s, f32, 1) for s in small_shapes]
        lead_o = add_out((1, width), f32, 1)
        downward = list(range(bits_all - 1, -1, -1))
        courses = [downward[-1:] + downward[:-1] + ["sib", "far"], ["sib", "far"] + downward]
        small_l = [add_scratch(pltpu.VMEM((bits_all + 2,) + s, f32)) for s in small_shapes]
        lead_l = [add_scratch(pltpu.VMEM((bits_all + 2, 1, width), f32))]
        small_sems = [add_scratch(pltpu.SemaphoreType.DMA((3, bits_all + 2))) for _ in range(4)]
    if slots:
        grad_sems = [add_scratch(pltpu.SemaphoreType.DMA((slots,))) for _ in range(2)]
    ring_sems = [add_scratch(pltpu.SemaphoreType.DMA((6, CHUNKS))) for _ in range(2)]
    load_sem = add_scratch(pltpu.SemaphoreType.DMA((len(ins),)))
    store_sem = add_scratch(pltpu.SemaphoreType.DMA((out_slots[0],)))
    n_in, n_out = len(ins), len(out_shape)
    vm_at = [add_scratch(item[2]) for item in vm_ins]
    vo_at = [None if (mix and i == probs_o[0]) or (pre and i < len(pre[1])) else add_scratch(pltpu.VMEM(o.shape, o.dtype)) for i, o in enumerate(out_shape)]

    def kernel(*refs):
        hbm_in, hbm_out, t = refs[:n_in], refs[n_in : n_in + n_out], refs[n_in + n_out :]
        vout = lambda o: t[-1 - o[0]] if o[0] < 0 else t[vo_at[o[0]]]

        def vin(i):
            if i == "all":
                return vout(all_o)
            if i == "out":
                return vout(e_o[0])
            return t[vm_at[i]]

        waited = set()

        def load(i):
            first, parts, _ = vm_ins[i]
            if len(hbm_in[first].shape) == 3:
                slabs, _, cols = hbm_in[first].shape
                return [
                    pltpu.make_async_copy(hbm_in[first].at[n], vin(i).at[:, pl.ds(n * cols, cols)], t[load_sem].at[first])
                    for n in range(slabs)
                ]
            if parts == 1:
                return [pltpu.make_async_copy(hbm_in[first], vin(i), t[load_sem].at[first])]
            copies, at = [], 0
            for n in range(first, first + parts):
                cols = hbm_in[n].shape[1]
                copies.append(pltpu.make_async_copy(hbm_in[n], vin(i).at[:, pl.ds(at, cols)], t[load_sem].at[n]))
                at += cols
            return copies

        begun = [0]

        def begin_loads(group):
            for i in range(begun[0], groups[group]):
                for cp in load(i):
                    cp.start()
            begun[0] = max(begun[0], groups[group])

        def need(*items):
            for i in items:
                if not isinstance(i, str) and i not in waited:
                    waited.add(i)
                    for cp in load(i):
                        cp.wait()

        dp, me = lax.axis_index("dp"), lax.axis_index("mp")
        core, chip = me % 2, me // 2
        sib = chip * 2 + 1 - core
        far = (1 - chip) * 2 + core
        diag = (1 - chip) * 2 + 1 - core
        bits = sorted({link[0] for ch in chains for link in ch[5]} | set(range(bits_all) if small else ()))
        meet = greet([(dp, sib), (dp, far)] + ([(dp, diag)] if pre else []) + [(place(dp, b)[1], me) for b in bits])
        begin_loads(0)

        def part(ref, block, k):
            return ref.at[pl.ds(pl.multiple_of(block * rows + k * chunk, chunk), chunk)]

        def store_rows(o, block, k):
            return pltpu.make_async_copy(
                part(vout(o), block, k), part(hbm_out[o[0]], block, k), t[store_sem].at[o[1] + block * CHUNKS + k]
            )

        def store_whole(o):
            return pltpu.make_async_copy(vout(o), hbm_out[o[0]], t[store_sem].at[o[1]])

        def store_piece(o, piece, cols, turned):
            return pltpu.make_async_copy(
                region(vout(o), piece, cols, turned), region(hbm_out[o[0]], piece, cols, turned), t[store_sem].at[o[1] + piece]
            )

        def copy(kind, k, src, dst, to):
            return pltpu.make_async_remote_copy(
                src, dst, t[ring_sems[0]].at[kind, k], t[ring_sems[1]].at[kind, k], device_id=(dp, to), device_id_type=MESH
            )

        if leave:
            px, own, sb, sr, xs, xr, ob, orv = [t[s] for s in leave_s]
        if enter:
            all_ref = vout(all_o)
            we_ref = t[we_s] if enter[1] else vin(we_i)
        pair_send = lambda k: copy(0, k, part(sb, 0, k), part(sr, 0, k), sib)
        far_send = lambda k: copy(1, k, part(xs, 0, k), part(xr, 0, k), far)
        own_send = lambda k: copy(2, k, part(ob, 0, k), part(orv, 0, k), sib)
        all_far = lambda k: copy(3, k, part(all_ref, me, k), part(all_ref, me, k), far)
        all_sib = lambda k: copy(4, k, part(all_ref, me, k), part(all_ref, me, k), sib)
        all_fwd = lambda k: copy(5, k, part(all_ref, far, k), part(all_ref, far, k), sib)
        got_far = lambda k: copy(3, k, part(all_ref, far, k), part(all_ref, far, k), far)
        got_sib = lambda k: copy(4, k, part(all_ref, sib, k), part(all_ref, sib, k), sib)
        got_diag = lambda k: copy(5, k, part(all_ref, diag, k), part(all_ref, diag, k), sib)

        def source(c, step):
            pieces, turned, src_s, src_i, keep_s, links = chains[c]
            if step:
                return t[links[step - 1][3]]
            return t[src_s] if src_s is not None else hbm_in[src_i]

        def hop(c, step, piece):
            b, slot, land_s, _, _ = chains[c][5][step]
            return halving_copy(source(c, step), t[land_s], piece, b, t[grad_sems[0]], t[grad_sems[1]], slot + piece)

        def keep(c):
            return halving_keep(hbm_in[chains[c][3]], t[chains[c][4]], chains[c][5][0][0], t[load_sem].at[chains[c][3]])

        held_back = set()

        def settle(c, step, piece):
            pieces, turned, src_s, src_i, keep_s, links = chains[c]
            b, slot, land_s, out_s, out_o = links[step]
            hop(c, step, piece).wait_recv()
            if step == 0 and src_s is None:
                if c not in held_back:
                    held_back.add(c)
                    keep(c).wait()
                held = lambda p, j: t[keep_s][p, j]
            else:
                own_bit, _ = place(dp, b)
                src = source(c, step)
                held = lambda p, j: src[p, j, own_bit]
            landing = t[land_s]
            out = t[out_s] if out_o is None else vout(out_o)
            halving_add(held, landing, out, piece, turned)
            if out_o is not None:
                store_piece(out_o, piece, PIECE, turned and landing.shape[2] % 128 == 0).start()

        def fill(k, where):
            for d, (a, b), o in zip(dws, dw_in, dw_o):
                if d[2] != where:
                    continue
                chain = None if where == "join" else o
                dw = vout(o) if chain is None else t[chains[o][2]]

                @pl.when(k < dw.shape[0])
                def _(a=a, b=b, dw=dw, chain=chain, o=o, lo=d[5], order=d[7]):
                    g = tn(vin(a)[...], vin(b)[:, pl.ds(pl.multiple_of((lo + k) * PIECE, PIECE), PIECE)]).astype(bf)
                    if order:
                        size = width // count
                        for blk in range(count):
                            at = sum((blk >> bit & 1) << n for n, bit in enumerate(order))
                            dw[k, at // 2, at % 2] = g[blk * size : (blk + 1) * size]
                    else:
                        dw[k] = g.reshape(dw.shape[1:])
                    if chain is None:
                        store_piece(o, k, PIECE, False).start()
                    else:
                        hop(chain, 0, k).start()

        def need_for(where):
            for d, (a, b) in zip(dws, dw_in):
                if d[2] == where:
                    need(a, b)

        def leave_phase(x_ref, wl_ref, far_fill, near_fill):
            def two(k, block_a, block_b):
                lhs = jnp.concatenate([part(x_ref, block_a, k)[...], part(x_ref, block_b, k)[...]], 0)
                return nn(lhs, wl_ref[...])

            def push(k):
                pair_send(k).wait_recv()
                part(xs, 0, k)[...] = (part(px, 0, k)[...] + part(sr, 0, k)[...].astype(f32)).astype(bf)
                far_send(k).start()

            def out_far(k, c):
                p = two(k, far, diag)
                part(px, 0, k)[...] = p[:chunk]
                part(sb, 0, k)[...] = p[chunk:].astype(bf)
                pair_send(k).start()
                if not mix:

                    @pl.when(k > 0)
                    def _():
                        push(k - 1)

                fill(k, far_fill)
                return c

            if not mix:
                lax.fori_loop(0, CHUNKS, out_far, 0)
                need_for(near_fill)

            def out_near(k, c):
                p = two(k, me, sib)
                part(own, 0, k)[...] = p[:chunk]
                part(ob, 0, k)[...] = p[chunk:].astype(bf)
                own_send(k).start()
                if not mix:

                    @pl.when(k == 0)
                    def _():
                        push(CHUNKS - 1)

                fill(k, near_fill)
                return c

            if not mix:
                lax.fori_loop(0, CHUNKS, out_near, 0)
                return
            probs_v, bias_v, rel_v, wide_v = [t[n] for n in mix_s]
            rel_v[...] = nn(spot_table(5 * BQ), wide_table(vin(mix_i[1]), wide_v)).astype(bf)

            def spot(n):
                there = chip + (1 - n // 4) * (1 - 2 * chip)
                return (there * 2 + core + (n % 2) * (1 - 2 * core)) * 2 + (n // 2) % 2

            def store_probs(n):
                at = pl.ds(pl.multiple_of(spot(n) * 2 * BQ, 2 * BQ), 2 * BQ)
                return pltpu.make_async_copy(
                    probs_v.at[n % 2], hbm_out[probs_o[0]].at[:, at, :], t[store_sem].at[probs_o[1] + n % 2]
                )

            def quarter(s, c):
                def one(b, c):
                    n = s * 2 + b

                    @pl.when(n > 1)
                    def _():
                        store_probs(n - 2).wait()

                    attend_block(spot(n), vin(mix_i[0]), probs_v.at[n % 2], x_ref, bias_v, rel_v)
                    store_probs(n).start()
                    return c

                lax.fori_loop(0, 2, one, 0)
                first = s % 2 * 2

                @pl.when(s < 2)
                def _():
                    lax.fori_loop(first, first + 2, out_far, 0)
                    push(first)
                    push(first + 1)

                @pl.when(s > 1)
                def _():
                    lax.fori_loop(first, first + 2, out_near, 0)

                return c

            lax.fori_loop(0, 4, quarter, 0)
            store_probs(6).wait()
            store_probs(7).wait()

        def leave_drain():
            def drain(k, c):
                pair_send(k).wait_send()
                far_send(k).wait_send()
                own_send(k).wait_send()
                return c

            lax.fori_loop(0, CHUNKS, drain, 0)

        def join_phase(rule, has_leave, in_refs, outs, totals, gathers):
            def join(k, c):
                fill(k, "join")
                branch = None
                if has_leave:
                    own_send(k).wait_recv()
                    far_send(k).wait_recv()
                    branch = part(own, 0, k)[...] + part(orv, 0, k)[...].astype(f32) + part(xr, 0, k)[...].astype(f32)
                fresh = rule(
                    branch, [part(r, 0, k)[...] for r in in_refs], t[gain_s], [part(vout(o), 0, k) for o in outs], [vout(o) for o in totals]
                )
                if gathers:
                    part(all_ref, me, k)[...] = fresh
                    all_far(k).start()
                    all_sib(k).start()
                for o in outs:
                    if o[0] >= 0:
                        store_rows(o, 0, k).start()
                return c

            lax.fori_loop(0, CHUNKS, join, 0)
            for o in totals:
                if o[0] >= 0:
                    store_whole(o).start()

        for o in s_o + ([tail_sum] if tail else []):
            vout(o)[...] = jnp.zeros((8, width), f32)
        if pre:
            steps = pre[3](*[hbm_in[i] for i in pre_i], *[hbm_out[o[0]] for o in pre_o], *[t[n] for n in pre_s])
            next(steps)
        meet()
        if pre:
            pre_x = next(steps)
        if leave:
            need(*(mix_i if mix else [] if pre else [x_i]), wl_i)
        begin_loads(1)
        for c in range(first_grad, len(chains)):
            for p in range(chains[c][0]):
                hop(c, 0, p).start()
        if leave:
            if leave[2]:
                t[wl_s][...] = vin(wl_i)[...].T
            need_for("far")
            leave_phase(vout(mixed_o) if mix else pre_x if pre else vin(x_i), t[wl_s] if leave[2] else vin(wl_i), "far", "near")
            if mix:
                store_whole(mixed_o).start()
        for c in range(first_grad, len(chains)):
            keep(c).start()
        need(gains_i, *row_i)
        for i in range(5):
            t[gain_s][i : i + 1, :] = gain_row(vin(gains_i), i, width)
        need_for("join")
        if enter and enter[1]:
            need(we_i)
            we_ref[...] = vin(we_i)[...].T
        join_phase(junction, bool(leave), [vin(r) for r in row_i], r_o, s_o, bool(enter))

        lead = [c for c in range(first_grad) if tail and dws[[i for i, o in enumerate(dw_o) if o == c][0]][2] == "far"]
        if small:
            partner = lambda at: (dp, sib) if at == "sib" else (dp, far) if at == "far" else (place(dp, at)[1], me)
            need(*vector_i, table_i, taps_i)
            rows_ref = vout(small_o[0])
            rows_ref[...] = jnp.zeros((8, width), f32)
            vectors = [vout(s_o[0])] + [vin(i) for i in vector_i]
            for i, v in enumerate(vectors[:4]):
                rows_ref[i : i + 1, :] = jnp.sum(v[...], 0, keepdims=True)
            for i, v in enumerate(vectors[4:]):
                line = jnp.sum(v[...], 0, keepdims=True)
                rows_ref[4:5, i * 128 : (i + 1) * 128] = functools.reduce(
                    jnp.add, [line[:, j * 128 : (j + 1) * 128] for j in range(width // 128)]
                )
            both = vin(table_i)[...]
            both = both + pltpu.roll(both, 64, 1)
            left = lax.broadcasted_iota(jnp.int32, (TABLE_ROWS, 128), 1) < HEAD
            vout(small_o[1])[...] = jnp.where(left, both[:TABLE_ROWS], both[TABLE_ROWS : 2 * TABLE_ROWS])
            vout(small_o[2])[...] = vin(taps_i)[...]
            wide = Doubling(courses[0], [vout(o) for o in small_o], [t[l] for l in small_l], [t[s] for s in small_sems[:2]], partner)
            wide.start()

        mid = set()

        def hasten(which):
            for c in which:
                if len(chains[c][5]) > 1:
                    mid.add(c)
                    for p in range(chains[c][0]):
                        settle(c, 0, p)
                        hop(c, 1, p).start()

        if enter:
            begin_loads(len(groups) - 1)
            need(we_i, *extra_i)

            def work(k, block_a, block_b):
                lhs = jnp.concatenate([part(all_ref, block_a, k)[...], part(all_ref, block_b, k)[...]], 0)
                h = nn(lhs, we_ref[...])
                for i, block in enumerate((block_a, block_b)):
                    view = lambda ref: part(ref, block, k)
                    enter[2](h[i * chunk : (i + 1) * chunk], [view(vin(r))[...] for r in extra_i], [view(vout(o)) for o in e_o])
                    for o in [all_o] + e_o:
                        if o[0] >= 0:
                            store_rows(o, block, k).start()

        if attend:
            tot_ref, dkt, dvt, dta, dz_ref, hot_ref, relb_ref = [t[s] for s in attend_s]
            dq, dk, dv = [vout(o) for o in d_o[:3]]
            need(qkv_i, table_i)
            need_for("post")
            for ref in (dkt, dvt, dta):
                ref[...] = jnp.zeros(ref.shape, f32)
            hot_ref[...] = spot_table(WIN)
            relb_ref[...] = wide_table(vin(table_i), t[wide_s])

            def block_of(j):
                chip_j = chip + (j // 4) * (1 - 2 * chip)
                core_j = core + (j % 2) * (1 - 2 * core)
                return (chip_j * 2 + core_j) * 2 + (j // 2) % 2

            def fetch(j):
                at = pl.ds(pl.multiple_of(block_of(j) * 2 * BQ, 2 * BQ), 2 * BQ)
                return pltpu.make_async_copy(hbm_in[probs_i].at[:, at, :], t[probs_s].at[j % 2], t[probs_sem].at[j % 2])

            fetch(0).start()

            def pass_on(*ks):
                for k in ks:
                    got_far(k).wait_recv()
                    all_fwd(k).start()

            def before(n):
                if 0 < n < 5:
                    pass_on(n - 1)
                if n == 3:
                    hasten(range(first_grad, len(chains)))
                elif n == 5:
                    hasten(range(first_grad))
                elif n == 6:
                    for k in range(CHUNKS):
                        if any(d[2] == "post" and k < d[6] for d in dws):
                            fill(k, "post")

            def rows_for(j):
                away = j // 4

                def chunk_rows(k, c):
                    @pl.when(away == 0)
                    def _():
                        got_sib(k).wait_recv()

                    @pl.when(away == 1)
                    def _():
                        got_diag(k).wait_recv()

                    there = chip + away * (1 - 2 * chip)
                    work(k, there * 2 + core, there * 2 + 1 - core)
                    return c

                first = (j // 2) % 2 * 2
                lax.fori_loop(first, first + 2, chunk_rows, 0)

            def query_block(j, c):
                for n in (1, 2, 3, 4):

                    @pl.when(j == n)
                    def _(n=n):
                        before(n)

                @pl.when(j % 2 == 0)
                def _():
                    rows_for(j)

                for n in (5, 6):

                    @pl.when(j == n)
                    def _(n=n):
                        before(n)

                @pl.when(j < 7)
                def _():
                    fetch(j + 1).start()

                fetch(j).wait()
                attend_back_block(
                    block_of(j), vin(qkv_i), t[probs_s].at[j % 2], vout(e_o[0]), dq, tot_ref, dkt, dvt, dta, dz_ref, hot_ref, relb_ref
                )
                return c

            lax.fori_loop(0, 8, query_block, 0)
            for pr in range(pairs):
                dk[:, pr * 128 : (pr + 1) * 128] = dkt[pr].T.astype(bf)
                dv[:, pr * 128 : (pr + 1) * 128] = dvt[pr].T.astype(bf)
            vout(d_o[3])[...] = dta[...]
            for o in d_o:
                store_whole(o).start()
        elif enter:

            def gather(k, c):
                got_sib(k).wait_recv()
                work(k, me, sib)
                got_far(k).wait_recv()
                all_fwd(k).start()
                got_diag(k).wait_recv()
                work(k, far, diag)
                if small:

                    for n, at in enumerate((1, CHUNKS - 1)):

                        @pl.when(k == at)
                        def _(n=n):
                            wide.advance(n)

                if lead:

                    @pl.when(k == CHUNKS - 2)
                    def _():
                        for ch in lead:
                            for p in range(chains[ch][0]):
                                settle(ch, 0, p)
                                hop(ch, 1, p).start()

                return c

            lax.fori_loop(0, CHUNKS, gather, 0)
            if small:
                wide.done = 2

        early = 0
        if tail:
            need_for("front")

            def front(k, c):
                fill(k, "front")
                return c

            lax.fori_loop(0, CHUNKS, front, 0)
            early = 1
            if lead and bits_all > 2:
                early = 2
                for ch in lead:
                    for p in range(chains[ch][0]):
                        settle(ch, 1, p)
                        hop(ch, 2, p).start()
            leave_drain()
            need(tw_i, *tail_i)
            t[tw_s][...] = vin(tw_i)[...].T
            leave_phase(vin("out"), t[tw_s], None, "close")
            wide.step()

        def close_rows():
            join_phase(tail[1], True, [vout(r_o[0])] + [vin(r) for r in tail_i], tail_o, [tail_sum], False)
            vout(lead_o)[...] = jnp.sum(vout(tail_sum)[...], 0, keepdims=True)
            final = Doubling(courses[1], [vout(lead_o)], [t[l] for l in lead_l], [t[s] for s in small_sems[2:]], partner)
            final.start()
            return final

        depth = lambda c: len(chains[c][5])
        begin = lambda c: early if c in lead else 1 if c in mid else 0
        agenda, fresh_slot, late = {}, 1, []
        for c in range(len(chains)):
            new = tail and c < first_grad and c not in lead
            if isinstance(plan[c][1], tuple):
                for p in range(chains[c][0]):
                    for step in range(depth(c) - 1):
                        agenda.setdefault(1 + LAG * step, []).append((step, c, p))
                    late.append((depth(c) - 1, c, p))
                continue
            for p in range(chains[c][0]):
                slot = fresh_slot if new else 0
                fresh_slot += 1 if new else 0
                for step in range(begin(c), depth(c)):
                    agenda.setdefault(slot, []).append((step, c, p))
                    slot += LAG
        final = None
        agenda.setdefault(max(list(agenda) + [0]), []).extend(late)
        for slot in range(max(list(agenda) + [0]) + 1):
            if tail and slot == JOIN_SLOT:
                final = close_rows()
            for step, c, p in sorted(agenda.get(slot, []), key=lambda x: -x[0]):
                settle(c, step, p)
                if step + 1 < depth(c):
                    hop(c, step + 1, p).start()
            if tail and wide.done < len(courses[0]):
                wide.step()
            elif final is not None and slot > JOIN_SLOT and final.done < len(courses[1]) - 1:
                final.step()
        if tail:
            while final.done < len(courses[1]):
                final.step()
            for o in small_o + [lead_o]:
                store_whole(o).start()
        for c in range(len(chains)):
            for s in range(depth(c)):
                for p in range(chains[c][0]):
                    hop(c, s, p).wait_send()
            out_o = chains[c][5][-1][4]
            block = chains[c][5][-1][2]
            for p in range(chains[c][0]):
                store_piece(out_o, p, PIECE, chains[c][1] and t[block].shape[2] % 128 == 0).wait()
        if leave:
            leave_drain()
        if pre:
            next(steps)

        def drain(k, c):
            if enter:
                all_far(k).wait_send()
                all_sib(k).wait_send()
                all_fwd(k).wait_send()
                for block in range(4):
                    for o in [all_o] + e_o:
                        if o[0] >= 0:
                            store_rows(o, block, k).wait()
            for o in r_o + (tail_o if tail else []):
                if o[0] >= 0:
                    store_rows(o, 0, k).wait()
            return c

        lax.fori_loop(0, CHUNKS, drain, 0)
        for o in s_o + (small_o + [lead_o] if tail else []) + (d_o if attend else []) + ([mixed_o] if mix else []):
            if o[0] >= 0:
                store_whole(o).wait()
        for d, o in zip(dws, dw_o):
            if d[2] == "join":
                for p in range(d[6]):
                    store_piece(o, p, PIECE, False).wait()

    flops = 0
    if leave:
        flops += 2 * frames * flat_shape(leave[1])[1 if leave[2] else 0] * width
    if enter:
        flops += 2 * frames * width * sum(c for c, _ in enter[4])
    flops += sum(2 * frames * width * PIECE * d[6] for d in dws)
    outs = pl.pallas_call(
        kernel,
        in_specs=[in_hbm()] * n_in,
        out_specs=[in_hbm()] * n_out,
        out_shape=out_shape,
        scratch_shapes=scratch,
        compiler_params=pltpu.CompilerParams(collective_id=cid, has_side_effects=True, vmem_limit_bytes=VMEM_LIMIT),
        cost_estimate=pl.CostEstimate(flops=flops, bytes_accessed=60_000_000, transcendentals=0),
        name=name,
    )(*ins)
    fixed, rest = list(outs[:fixed_out]), list(outs[fixed_out:])
    fresh = [Grad(rest.pop(0), 0, d[3]) for d in dws if d[2] == "join"]
    for item in plan:
        fresh.append(Grad(rest.pop(0), item[3], item[2]))
    return fixed + [fresh] + rest


def publish(ends, small, sizes, rel, total):
    flat, outs, where = [], [], []
    f32 = jnp.float32
    for arrays, parts in ends:
        rows = arrays[0].shape[0]
        joined = len(arrays) > 1 and sizes[len(outs)]
        shape = (rows, sum(a.shape[1] for a in arrays)) if not joined else (sum(a.shape[0] for a in arrays), arrays[0].shape[1])
        where.append((len(flat), arrays, joined))
        flat.extend(arrays)
        if parts < 0:
            outs.append((shape, (-parts, shape[0], shape[1] // -parts)))
        else:
            outs.append((shape, (shape[0], parts, shape[1] // parts) if parts else None))
    n, m = len(flat), len(ends)
    width = small[0].shape[1]
    taps = small[3].shape
    split_at = [i for i in range(m) if ends[i][1] > 0]
    slab_at = [i for i in range(m) if ends[i][1] < 0]
    small_shapes = [(1, width)] * 5 + [(HEAD, rel), (taps[0] - 1, taps[1]), (1, taps[1]), (1, 5)]

    def kernel(*refs):
        src, small_in = refs[:n], refs[n : n + 4]
        dst, small_out = refs[n + 4 : n + 4 + m], refs[n + 4 + m : n + 13 + m]
        rest = refs[n + 13 + m :]
        held, split = rest[:m], dict(zip(split_at, rest[m:-1]))
        sem = rest[-1]
        loads, stores = [], []
        for i, (first, arrays, joined) in enumerate(where):
            at, copies = 0, []
            for k in range(len(arrays)):
                ref = src[first + k]
                size = ref.shape[0 if joined else 1]
                part = held[i].at[pl.ds(at, size)] if joined else held[i].at[:, pl.ds(at, size)]
                copies.append(pltpu.make_async_copy(ref, part, sem.at[first + k]))
                at += size
            loads.append(copies)
            if i in slab_at:
                slabs, _, cols = dst[i].shape
                stores.append(
                    [
                        pltpu.make_async_copy(held[i].at[:, pl.ds(k * cols, cols)], dst[i].at[k], sem.at[n + m + k])
                        for k in range(slabs)
                    ]
                )
            else:
                stores.append([pltpu.make_async_copy(split.get(i, held[i]), dst[i], sem.at[n + i])])
        for copies in loads:
            for cp in copies:
                cp.start()
        lead, rows, table, tap = [r[...] for r in small_in]
        small_out[0][...] = lead
        for i in range(4):
            small_out[1 + i][...] = rows[i : i + 1]
        turned = jnp.concatenate([table, jnp.zeros((128 - TABLE_ROWS, 128), f32)], 0).T
        small_out[5][:, :TABLE_ROWS] = turned[:HEAD, :TABLE_ROWS]
        small_out[5][:, TABLE_ROWS:] = turned[HEAD:, : rel - TABLE_ROWS]
        small_out[6][...] = tap[:-1]
        small_out[7][...] = tap[-1:]
        lane = lax.broadcasted_iota(jnp.int32, (1, 128), 1)
        mean = jnp.zeros((1, 128), f32)
        for i in range(5):
            mean = jnp.where(lane == i, jnp.sum(rows[4:5, i * 128 : (i + 1) * 128], -1, keepdims=True) / total, mean)
        root = jnp.sqrt(mean)
        small_out[8][...] = root[:, :5]
        for i in range(m):
            for cp in loads[i]:
                cp.wait()
            if i in split:
                cols = split[i].shape[2]
                for j in range(split[i].shape[1]):
                    split[i][:, j, :] = held[i][:, j * cols : (j + 1) * cols]
            for cp in stores[i]:
                cp.start()
        for copies in stores:
            for cp in copies:
                cp.wait()

    vm = pl.BlockSpec(memory_space=pltpu.VMEM)
    return pl.pallas_call(
        kernel,
        in_specs=[in_hbm()] * n + [vm] * 4,
        out_specs=[in_hbm()] * m + [vm] * 9,
        out_shape=[jax.ShapeDtypeStruct(o[1] or o[0], f32) for o in outs] + [jax.ShapeDtypeStruct(s, f32) for s in small_shapes],
        scratch_shapes=[pltpu.VMEM(o[0], f32) for o in outs]
        + [pltpu.VMEM(outs[i][1], f32) for i in split_at]
        + [pltpu.SemaphoreType.DMA((n + m + 4,))],
        compiler_params=pltpu.CompilerParams(vmem_limit_bytes=VMEM_LIMIT),
        name="publish",
    )(*flat, *small)


SPAN = 128


def exchange(stats, landing, send, recv):
    dp, me = lax.axis_index("dp"), lax.axis_index("mp")
    core, chip = me % 2, me // 2
    others = [chip * 2 + 1 - core, (1 - chip) * 2 + core, (1 - chip) * 2 + 1 - core]
    return [
        pltpu.make_async_remote_copy(
            stats, landing.at[i], send.at[i], recv.at[i], device_id=(dp, to), device_id_type=MESH
        )
        for i, to in enumerate(others)
    ]


def group_targets():
    dp, me = lax.axis_index("dp"), lax.axis_index("mp")
    core, chip = me % 2, me // 2
    return [(dp, chip * 2 + 1 - core), (dp, (1 - chip) * 2 + core), (dp, (1 - chip) * 2 + 1 - core)]


def to_rows(first, second):
    lane = lax.broadcasted_iota(jnp.int32, (SPAN, SPAN), 1)
    both = jnp.where(lane == 0, first, jnp.where(lane == 1, second, 0.0))
    return both.T[:8]


def to_columns(rows8):
    return jnp.concatenate([rows8, jnp.zeros((SPAN - 8, SPAN), jnp.float32)], 0).T


def shifted(window, by):
    return window if by == 0 else pltpu.roll(window, window.shape[0] - by, 0)


def depth_gain_row(ref, width, chans):
    first = 5 * width // 128
    return jnp.concatenate([ref[first + j : first + j + 1, :] for j in range(chans // 128)], 1)


def conv_mid(glu, w_depth, gains, width):
    frames, chans = glu.shape
    taps = w_depth.shape[0]
    reach = taps - 1
    edge = (reach + 7) // 8 * 8
    f32, bf = jnp.float32, jnp.bfloat16
    tiles, lanes = frames // SPAN, chans // 128

    def run(glu_h, w_h, g_h, act_h, slope_h, unit_h, stat_h, pad, w_raw, g_raw, w_v, g_v, act, slope, unit, stat, sendbuf, landing, lsem, ssem, send, recv):
        loads = [
            pltpu.make_async_copy(glu_h, pad.at[pl.ds(edge, frames)], lsem.at[0]),
            pltpu.make_async_copy(w_h, w_raw, lsem.at[1]),
            pltpu.make_async_copy(g_h, g_raw, lsem.at[2]),
        ]
        for cp in loads:
            cp.start()
        pad[:edge, :] = jnp.zeros((edge, chans), f32)
        yield None
        for cp in loads:
            cp.wait()
        w_v[...] = w_raw[...].astype(f32)
        g_v[...] = depth_gain_row(g_raw, width, chans)

        def tile(i, c):
            at = pl.multiple_of(i * SPAN, SPAN)
            for lane in range(lanes):
                cols = slice(lane * 128, (lane + 1) * 128)
                window = pad[pl.ds(at, SPAN + edge), cols]
                total = jnp.zeros((SPAN, 128), f32)
                for by in range(8):
                    moved = shifted(window, by)
                    for base in range(0, edge + 1, 8):
                        tap = base + by - (edge - reach)
                        if 0 <= tap < taps:
                            total = total + w_v[tap : tap + 1, cols] * moved[base : base + SPAN]
                unit[pl.ds(at, SPAN), cols] = total
            depth = unit[pl.ds(at, SPAN), :]
            mean = jnp.mean(depth, -1, keepdims=True)
            centred = depth - mean
            sendbuf[:, pl.ds(at, SPAN)] = to_rows(mean, jnp.sum(centred * centred, -1, keepdims=True))
            return c

        lax.fori_loop(0, tiles, tile, 0)
        copies = exchange(sendbuf, landing, send, recv)
        for cp in copies:
            cp.start()
        for cp in copies:
            cp.wait_recv()
        rows = [sendbuf[...]] + [landing[i] for i in range(3)]
        mean = sum(r[0:1] for r in rows) * 0.25
        spread = sum(r[1:2] + chans * (r[0:1] - mean) * (r[0:1] - mean) for r in rows) / width
        inverse = lax.rsqrt(spread + epsilon)
        row = lax.broadcasted_iota(jnp.int32, (8, frames), 0)
        stat[...] = jnp.where(row == 0, mean, jnp.where(row == 1, inverse, 0.0))
        outs = [(act, act_h), (slope, slope_h), (unit, unit_h)]

        def store(i, n):
            at = pl.ds(pl.multiple_of(i * SPAN, SPAN), SPAN)
            return pltpu.make_async_copy(outs[n][0].at[at], outs[n][1].at[at], ssem.at[n, i])

        def finish(i, c):
            at = pl.multiple_of(i * SPAN, SPAN)
            cols = to_columns(stat[:, pl.ds(at, SPAN)])
            u = (unit[pl.ds(at, SPAN), :] - cols[:, 0:1]) * cols[:, 1:2]
            a, s = silu_pair(u * g_v[...])
            unit[pl.ds(at, SPAN), :] = u
            act[pl.ds(at, SPAN), :] = a.astype(bf)
            slope[pl.ds(at, SPAN), :] = s.astype(bf)
            for n in range(3):
                store(i, n).start()
            return c

        lax.fori_loop(0, tiles, finish, 0)
        last = pltpu.make_async_copy(stat, stat_h, lsem.at[0])
        last.start()
        yield act
        for cp in copies:
            cp.wait_send()
        for i in range(tiles):
            for n in range(3):
                store(i, n).wait()
        last.wait()
        yield None

    S = jax.ShapeDtypeStruct
    out_shape = [S((frames, chans), bf), S((frames, chans), bf), S((frames, chans), f32), S((8, frames), f32)]
    vm = pltpu.VMEM
    scratch = [
        vm((frames + edge, chans), f32), vm(w_depth.shape, bf), vm(gains.shape, f32), vm(w_depth.shape, f32), vm((1, chans), f32),
        vm((frames, chans), bf), vm((frames, chans), bf), vm((frames, chans), f32), vm((8, frames), f32),
        vm((8, frames), f32), vm((3, 8, frames), f32),
        pltpu.SemaphoreType.DMA((3,)), pltpu.SemaphoreType.DMA((3, tiles)), pltpu.SemaphoreType.DMA((3,)), pltpu.SemaphoreType.DMA((3,)),
    ]
    return [glu, w_depth, gains], out_shape, scratch, run


def conv_mid_back(grad, slope, unit, stat, glu, sig, tail, w_depth, gains, width, cid, grads):
    frames, chans = glu.shape
    taps = w_depth.shape[0]
    reach = taps - 1
    edge = (reach + 7) // 8 * 8
    f32, bf = jnp.float32, jnp.bfloat16
    tiles, lanes = frames // SPAN, chans // 128
    ins = [grad, slope, unit, stat, w_depth, gains, glu, sig, tail]
    riders = Riders(grads)
    n = len(grads)

    def kernel(*refs):
        hbm, ride_in, (pair_h, taps_h), ride_out = refs[:9], refs[9 : 9 + n], refs[9 + n : 11 + n], refs[11 + n : 11 + 2 * n]
        refs = refs[2 * n :]
        (grad_v, slope_v, unit_v, stat_v, w_raw, g_raw, pad, sig_v, tail_v, w_v, g_v, back, pair, taps_v, acc, gacc, sendbuf, landing, lsem, ssem, send, recv) = refs[11:33]
        riders.bind(ride_in, ride_out, refs[33:])
        meet = greet(group_targets() + riders.targets())
        dst = [grad_v, slope_v, unit_v, stat_v, w_raw, g_raw, pad.at[pl.ds(edge, frames)], sig_v, tail_v]
        loads = [pltpu.make_async_copy(h, d, lsem.at[i]) for i, (h, d) in enumerate(zip(hbm, dst))]
        for cp in loads:
            cp.start()
        pad[:edge, :] = jnp.zeros((edge, chans), f32)
        back[frames:, :] = jnp.zeros((edge, chans), f32)
        acc[...] = jnp.zeros_like(acc)
        gacc[...] = jnp.zeros_like(gacc)
        for cp in loads[:6]:
            cp.wait()
        w_v[...] = w_raw[...].astype(f32)
        g_v[...] = depth_gain_row(g_raw, width, chans)

        def first(i, c):
            at = pl.ds(pl.multiple_of(i * SPAN, SPAN), SPAN)
            u = unit_v[at, :]
            de = grad_v[at, :] * slope_v[at, :].astype(f32)
            gacc[...] += fold8(de * u)
            du = de * g_v[...]
            back[at, :] = du
            sendbuf[:, at] = to_rows(jnp.sum(du, -1, keepdims=True), jnp.sum(du * u, -1, keepdims=True))
            return c

        meet()
        riders.start()
        lax.fori_loop(0, tiles, first, 0)
        copies = exchange(sendbuf, landing, send, recv)
        for cp in copies:
            cp.start()
        for cp in loads[6:]:
            cp.wait()
        for cp in copies:
            cp.wait_recv()
        means = (sendbuf[...] + landing[0] + landing[1] + landing[2]) / width
        row = lax.broadcasted_iota(jnp.int32, (8, frames), 0)
        stat_v[...] = jnp.where(row == 1, stat_v[...], jnp.where(row == 0, means[0:1], jnp.where(row == 2, means[1:2], 0.0)))

        def second(i, c):
            at = pl.ds(pl.multiple_of(i * SPAN, SPAN), SPAN)
            cols = to_columns(stat_v[:, at])
            back[at, :] = cols[:, 1:2] * (back[at, :] - cols[:, 0:1] - unit_v[at, :] * cols[:, 2:3])
            return c

        lax.fori_loop(0, tiles, second, 0)

        def store(i):
            at = pl.ds(pl.multiple_of(i * SPAN, SPAN), SPAN)
            return pltpu.make_async_copy(pair.at[at], pair_h.at[at], ssem.at[i])

        def third(i, c):
            at = pl.multiple_of(i * SPAN, SPAN)
            rows = pl.ds(at, SPAN)
            for lane in range(lanes):
                cols = slice(lane * 128, (lane + 1) * 128)
                ahead = back[pl.ds(at, SPAN + edge), cols]
                total = jnp.zeros((SPAN, 128), f32)
                for by in range(8):
                    moved = shifted(ahead, by)
                    for base in range(0, edge, 8):
                        tap = reach - (base + by)
                        if 0 <= tap < taps:
                            total = total + w_v[tap : tap + 1, cols] * moved[base : base + SPAN]
                pair[rows, cols] = (total * sig_v[rows, cols].astype(f32)).astype(bf)
                pair[rows, chans + lane * 128 : chans + (lane + 1) * 128] = (total * tail_v[rows, cols].astype(f32)).astype(bf)
            store(i).start()
            for lane in range(lanes):
                cols = slice(lane * 128, (lane + 1) * 128)
                here = back[rows, cols]
                window = pad[pl.ds(at, SPAN + edge), cols]
                for by in range(8):
                    moved = shifted(window, by)
                    for base in range(0, edge + 1, 8):
                        tap = base + by - (edge - reach)
                        if 0 <= tap < taps:
                            acc[tap * 8 : tap * 8 + 8, cols] += fold8(here * moved[base : base + SPAN])
            return c

        lax.fori_loop(0, tiles, third, 0)
        for tap in range(taps):
            taps_v[tap : tap + 1, :] = jnp.sum(acc[tap * 8 : tap * 8 + 8, :], 0, keepdims=True)
        taps_v[taps : taps + 1, :] = jnp.sum(gacc[...], 0, keepdims=True)
        last = pltpu.make_async_copy(taps_v, taps_h, lsem.at[0])
        last.start()
        for cp in copies:
            cp.wait_send()
        riders.finish()
        for i in range(tiles):
            store(i).wait()
        last.wait()

    S = jax.ShapeDtypeStruct
    vm = pltpu.VMEM
    outs = pl.pallas_call(
        kernel,
        in_specs=[in_hbm()] * (9 + n),
        out_specs=[in_hbm()] * (2 + n),
        out_shape=[S((frames, 2 * chans), bf), S((taps + 1, chans), f32)] + riders.after,
        scratch_shapes=[
            vm((frames, chans), f32), vm((frames, chans), bf), vm((frames, chans), f32), vm((8, frames), f32),
            vm(w_depth.shape, bf), vm(gains.shape, f32), vm((frames + edge, chans), f32), vm((frames, chans), bf), vm((frames, chans), bf),
            vm(w_depth.shape, f32), vm((1, chans), f32),
            vm((frames + edge, chans), f32), vm((frames, 2 * chans), bf), vm((taps + 1, chans), f32), vm((taps * 8, chans), f32), vm((8, chans), f32),
            vm((8, frames), f32), vm((3, 8, frames), f32),
            pltpu.SemaphoreType.DMA((9,)), pltpu.SemaphoreType.DMA((tiles,)), pltpu.SemaphoreType.DMA((3,)), pltpu.SemaphoreType.DMA((3,)),
        ] + riders.scratch,
        compiler_params=pltpu.CompilerParams(collective_id=cid, has_side_effects=True, vmem_limit_bytes=VMEM_LIMIT),
        name="conv_mid_back",
    )(*ins, *riders.arrays)
    return outs[0], outs[1], riders.results(outs[2:])


def body(
    features,
    w1_in,
    w1_out,
    gain_ffn1,
    w_qkv,
    w_attn_out,
    rel_table,
    gain_attn,
    w_conv_in,
    w_depth,
    gain_depth,
    w_conv_out,
    gain_conv,
    w2_in,
    w2_out,
    gain_ffn2,
    gain_final,
    cotangent,
):
    local_frames, clip_count, width = features.shape
    rows = local_frames * clip_count
    f32, bf = jnp.float32, jnp.bfloat16
    s0 = features.reshape(rows, width)
    seed = cotangent.reshape(rows, width)
    gains = pack_gains((gain_ffn1, gain_attn, gain_conv, gain_ffn2, gain_final, gain_depth), width)
    flat_qkv = w_qkv.transpose(1, 0, 2)
    flat_conv = w_conv_in.reshape(width, -1)
    units = w1_in.shape[1]
    half = units // PIECE // 2
    dp_count = lax.axis_size("dp")
    done = dp_count.bit_length() - 1
    pending = lambda items: [g for g in items if g.bit < done]
    chans = w_conv_out.shape[0]

    def swish_out(h, extra, outs):
        act, slope = silu_pair(h)
        outs[0][...] = act.astype(bf)
        outs[1][...] = slope.astype(bf)

    def plain_out(h, extra, outs):
        outs[0][...] = h.astype(outs[0].dtype)

    def glu_out(h, extra, outs):
        p0 = h[:, :chans]
        sig = jax.nn.sigmoid(h[:, chans:])
        glu = p0 * sig
        outs[0][...] = glu
        outs[1][...] = sig.astype(bf)
        outs[2][...] = (glu * (1.0 - sig)).astype(bf)

    def slope_out(h, extra, outs):
        outs[0][...] = (h * extra[0][...].astype(f32)).astype(bf)

    def first(branch, ins, gains, outs, sums):
        return (unit_norm(ins[0].astype(f32))[0] * gains[0:1, :]).astype(bf)

    def forward(scale, row):
        def run(branch, ins, gains, outs, sums):
            fresh = ins[0].astype(f32) + scale * branch
            outs[0][...] = fresh
            sums[0][...] += fold8(branch * branch)
            return (unit_norm(fresh)[0] * gains[row : row + 1, :]).astype(bf)
        return run

    def turn(branch, ins, gains, outs, sums):
        fresh = ins[0] + 0.5 * branch
        sums[0][...] += fold8(branch * branch)
        sums[1][...] += fold8(fresh * fresh)
        unit, inverse = unit_norm(fresh)
        outs[0][...] = unit * gains[4:5, :]
        grad = ins[1].astype(f32)
        scaled = grad * gains[4:5, :]
        mean_one = jnp.mean(scaled, -1, keepdims=True)
        mean_two = jnp.mean(scaled * unit, -1, keepdims=True)
        sums[2][...] += fold8(grad * unit)
        back = inverse * (scaled - mean_one - unit * mean_two)
        outs[1][...] = back
        return (0.5 * back).astype(bf)

    def backward(scale, row):
        def run(branch, ins, gains, outs, sums):
            pull, grad_gain = norm_pull(branch, ins[1].astype(f32), gains[row : row + 1, :])
            fresh = ins[0] + pull
            outs[0][...] = fresh
            sums[0][...] += grad_gain
            return (scale * fresh).astype(bf)
        return run

    a1, act1, slope1, _ = stage(
        "ffn1_in", 0, rows, width, dp_count, gains, enter=(w1_in, False, swish_out, (), ((units, bf), (units, bf))),
        junction=first, row_in=(s0,),
    )
    a2, qkv, s1, sq1, _ = stage(
        "ffn1_out", 1, rows, width, dp_count, gains, leave=(act1, w1_out, False),
        enter=(flat_qkv, False, plain_out, (), ((3 * w_qkv.shape[2], bf),)),
        junction=forward(0.5, 1), row_in=(s0,), row_out=(f32,), sums=1,
    )
    turned_table = rel_table.T
    mixed, probs, a3, glu, sig, tail, s2, sq2, _ = stage(
        "attn_out", 2, rows, width, dp_count, gains, leave=(None, w_attn_out, False), mix=(qkv, turned_table),
        enter=(flat_conv, False, glu_out, (), ((chans, f32), (chans, bf), (chans, bf))),
        junction=forward(1.0, 2), row_in=(s1,), row_out=(f32,), sums=1,
    )
    act3, slope3, depth_unit, depth_stat, a4, act2, slope2, s3, sq3, _ = stage(
        "conv_out", 3, rows, width, dp_count, gains, leave=(None, w_conv_out, False), pre=conv_mid(glu, w_depth, gains, width),
        enter=(w2_in, False, swish_out, (), ((units, bf), (units, bf))),
        junction=forward(1.0, 3), row_in=(s2,), row_out=(f32,), sums=1,
    )
    db4, dh2, output, grad4, sq4, sq5, dgf, _ = stage(
        "ffn2_out", 4, rows, width, dp_count, gains, leave=(act2, w2_out, False),
        enter=(w2_out, True, slope_out, (slope2,), ((units, bf),)),
        junction=turn, row_in=(s3, seed), row_out=(f32, f32), sums=3,
    )
    db3, de3, grad3, dg2, (ga_in, gb_in, gw2_out) = stage(
        "ffn2_back", 5, rows, width, dp_count, gains, leave=(dh2, w2_in, True),
        enter=(w_conv_out, True, plain_out, (), ((chans, f32),)), dws=(
            weight(a4, dh2, "join", False, 1, 0, half),
            weight(a4, dh2, "join", False, 1, half, units // PIECE - half),
            weight(db4, act2, "far", True),
        ),
        junction=backward(1.0, 3), row_in=(grad4, s3), row_out=(f32,), sums=1,
    )
    dpaired, tap_sums, (gw2_out, ga_in) = conv_mid_back(
        de3, slope3, depth_unit, depth_stat, glu, sig, tail, w_depth, gains, width, 11, [gw2_out, ga_in]
    )
    grad2, dgc, dq, dk, dv, dt, (gconv_in, gconv_out, gattn, gb_in, gw2_out, ga_in) = stage(
        "conv_back", 6, rows, width, dp_count, gains, leave=(dpaired, flat_conv, True),
        enter=(w_attn_out, True, plain_out, (), ((w_attn_out.shape[0], bf),)),
        dws=(
            weight(a3, dpaired, "far", False, 2),
            weight(db3, act3, "far", True, 2),
            weight("all", mixed, "post", True),
        ),
        grads=((gb_in, 2), gw2_out, (ga_in, 2)), attend=(qkv, probs, turned_table),
        junction=backward(1.0, 2), row_in=(grad3, s2), row_out=(f32,), sums=1,
    )
    dqkv = (dq, dk, dv)
    waiting = pending([gattn, gconv_in, gconv_out, ga_in, gb_in, gw2_out])
    grad0, ends, other_rows, table_end, taps_end, lead_row = stage(
        "attn_back", 7, rows, width, dp_count, gains, leave=(dqkv, flat_qkv, True),
        enter=(w1_out, True, slope_out, (slope1,), ((units, bf),)),
        dws=(
            weight(a2, dqkv, "far", False),
            weight("all", act1, "front", True, 1, 0, 1, tuple(range(1, done)) + (0,)),
            weight("all", act1, "front", True, 1, 1, units // PIECE - 1),
            weight(a1, "out", "close", False, pieces=units // PIECE),
        ),
        grads=waiting, small=((dgc, dg2, dgf, sq1, sq2, sq3, sq4, sq5), dt, tap_sums),
        tail=(w1_in, backward(1.0, 0), (s0,)),
        junction=backward(0.5, 1), row_in=(grad2, s1), row_out=(f32,), sums=1,
    )
    gqkv, gw1_head, gw1_out, gw1_in = ends[:4]
    for item, end in zip(waiting, ends[4:]):
        item.array = end.array

    def finish(item):
        flip = item.turned and item.array.shape[0] * dp_count == width and (width // dp_count) % 128 != 0
        return item.array.T if flip else item.array

    token_total = rows * lax.axis_size("mp") * dp_count
    ends = [
        ([output], 1),
        ([grad0], 1),
        ([finish(gw1_in)], 0),
        ([finish(gw1_head), finish(gw1_out)], 0),
        ([finish(gqkv)], -3),
        ([finish(gattn)], 0),
        ([finish(gconv_in)], 2),
        ([finish(gconv_out)], 0),
        ([finish(ga_in), finish(gb_in)], 0),
        ([finish(gw2_out)], 0),
    ]
    done_ends = publish(ends, [lead_row, other_rows, table_end, taps_end], {3: True, 8: False}, rel_table.shape[0], float(token_total * width))
    (output, grad0, gw1_in, gw1_out, gqkv, gattn, gconv_in, gconv_out, gw2_in, gw2_out) = done_ends[:10]
    *gain_sums, table_sum, depth_sum, depth_gain_sum, rms_stats = done_ends[10:]
    gain_sums = [g[0] for g in gain_sums]
    return (
        output,
        grad0,
        gw1_in,
        gw1_out,
        gain_sums[0],
        gqkv.transpose(1, 0, 2),
        gattn,
        table_sum.T,
        gain_sums[1],
        gconv_in,
        depth_sum,
        depth_gain_sum[0],
        gconv_out,
        gain_sums[2],
        gw2_in,
        gw2_out,
        gain_sums[3],
        gain_sums[4],
        rms_stats[0],
    )


def solution(mesh):
    return jax.shard_map(
        body,
        mesh=mesh,
        in_specs=(
            P("mp", "dp", None),
            P(None, "mp"),
            P("mp", None),
            P(),
            P(None, None, "mp"),
            P("mp", None),
            P(),
            P(),
            P(None, None, "mp"),
            P(None, "mp"),
            P("mp"),
            P("mp", None),
            P(),
            P(None, "mp"),
            P("mp", None),
            P(),
            P(),
            P("mp", "dp", None),
        ),
        out_specs=(
            P("mp", "dp", None),
            P("mp", "dp", None),
            P("dp", "mp"),
            P("mp", "dp"),
            P(),
            P("dp", None, "mp"),
            P("mp", "dp"),
            P(),
            P(),
            P("dp", None, "mp"),
            P(None, "mp"),
            P("mp"),
            P("mp", "dp"),
            P(),
            P("dp", "mp"),
            P("mp", "dp"),
            P(),
            P(),
            P(),
        ),
        check_vma=False,
    )
```
